32 devices in a mesh: dp: 4 (over y, x), seq: 8 (over z, core).
Axes of the slice: x: 2, y: 2, z: 4, core: 2. Of those that a mesh axis runs over, the one named last changes fastest.
Arguments:
- tokens: bfloat16 [4096, 768], P(('dp', 'seq')), may hold values from -6 to 6
- w_qkv: bfloat16 [768, 2304], P(('dp', 'seq')), may hold values from -0.21875 to 0.21875
- w_attn_out: bfloat16 [768, 768], P(('dp', 'seq')), may hold values from -0.875 to 0.875
- gain_attn: bfloat16 [768], P(('dp', 'seq')), may hold values from 0.5 to 1.5
- gain_moe: bfloat16 [768], P(('dp', 'seq')), may hold values from 0.5 to 1.5
- w_router: bfloat16 [768, 16], P(('dp', 'seq')), may hold values from -0.15625 to 0.15625
- rel_bias: float32 [32, 12], replicated, may hold values from -4 to 4
- w_in: bfloat16 [16, 768, 3072], P('seq', 'dp'), may hold values from -0.21875 to 0.21875
- w_out: bfloat16 [16, 3072, 768], P('seq', 'dp'), may hold values from -0.15625 to 0.15625
- teacher: bfloat16 [4096, 768], P(('dp', 'seq')), may hold values from -6 to 6
- routes: int32 [4096, 2], P(('dp', 'seq')), may hold values from 0 to 15, all different within a row; in each aligned block of 128 rows (0 to 127, 128 to 255, ...) at most 32 rows name the same one
- valid: int32 [4096], P(('dp', 'seq')), may hold values from 0 to 1, as said below
- buckets: int32 [1024], replicated, may hold values from 0 to 31, never falling along the last dimension, each value on 1 to 128 neighbouring positions
Outputs:
- output: float32 [4096, 768], P(('dp', 'seq'))
- loss: float32 [], replicated
- grad_tokens: float32 [4096, 768], P(('dp', 'seq'))
- grad_w_qkv: float32 [768, 2304], P(('dp', 'seq'))
- grad_w_attn_out: float32 [768, 768], P(('dp', 'seq'))
- grad_gain_attn: float32 [768], P(('dp', 'seq'))
- grad_gain_moe: float32 [768], P(('dp', 'seq'))
- grad_w_router: float32 [768, 16], P(('dp', 'seq'))
- grad_rel_bias: float32 [32, 12], replicated
- grad_w_in: float32 [16, 768, 3072], P('seq', 'dp')
- grad_w_out: float32 [16, 3072, 768], P('seq', 'dp')
The draws below stay inside these ranges and needn't reach their ends.
Inputs may be any that keep to these rules, and one draw needn't show every extreme that they name: `routes`: each row names two different experts; the rows of one device name one expert at most 32 times, a bound that some block reaches. Every token whose row index is 3 modulo 4 has valid = 1. `buckets`: never falls as the distance grows; every bucket covers 1 to 128 distances.
All inputs are finite; a program needn't handle non-finite values.
Results may differ from the reference program's by a relative error of at most 0.017.
Values may be sent and summed in bfloat16 or wider, within the bound.
A program may use at most 192 MiB of HBM per device.

```python
import math
import jax
import jax.numpy as jnp
import numpy as np
from jax import lax

D = 768
H = 12
HEAD = 64
FF = 3072
BUCKETS = 32
TOK_DEV = 128
EXPERTS = 16
LENGTH = 1024
TOKENS = 4096
CAP = 32


def draw_valid(key, part):
    position = jnp.arange(TOKENS, dtype=jnp.int32)
    threshold = 50 + 900 * position // TOKENS
    ticket = jax.random.randint(key, (TOKENS,), 0, 1000, dtype=jnp.int32)
    return jnp.where((ticket < threshold) | (position % 4 == 3), 1, 0).astype(jnp.int32)


def steps_of(rng, dims, pieces, smallest, top_value):
    level, own = 1.0, jax.random.fold_in(rng, 6)
    for dim, parts in pieces:
        heights = jnp.exp(jax.random.uniform(jax.random.fold_in(own, dim), (parts,), jnp.float32, smallest / len(pieces), top_value / len(pieces)))
        level = level * jnp.repeat(heights, dims[dim] // parts).reshape([-1 if axis == dim else 1 for axis in range(len(dims))])
    return level


def length_profile(amount, total, reach, lean):
    portions = [(1 << 20) // math.isqrt(rank ** lean) + 1 for rank in range(2, amount + 1)]
    surplus, given = total - reach - (amount - 1), [1] * (amount - 1)
    while surplus > 0:
        free = [i for i in range(amount - 1) if given[i] < reach]
        mass, left = sum([portions[i] for i in free]), surplus
        for i in free:
            addition = min(reach - given[i], max(1, left * portions[i] // mass), surplus)
            given[i] = given[i] + addition
            surplus = surplus - addition
    return np.array([reach] + given)


def ragged_sizes(own_key, count, total, reach, skew):
    if count == 2:
        one = jax.random.randint(own_key, (), max(1, total - reach), min(reach, total - 1) + 1)
        return jnp.stack([one, total - one])
    tallies = jnp.asarray(length_profile(count, total, reach, skew), jnp.int32)
    twos = (count - 1) // 2
    donor, sink = tallies[1:1 + 2 * twos:2], tallies[2:2 + 2 * twos:2]
    margin = jnp.minimum(donor - 1, reach - sink)
    passed = jax.random.randint(jax.random.fold_in(own_key, 1), (twos,), 0, 1 << 20) % (margin + 1)
    tallies = tallies.at[1:1 + 2 * twos:2].set(donor - passed).at[2:2 + 2 * twos:2].set(sink + passed)
    return tallies[jax.random.permutation(jax.random.fold_in(own_key, 2), count)]


def assign_block(stream_key, own, number, rows, number_of, top, bound, slope):
    sequence = jax.random.permutation(stream_key, number_of)
    heavy_load, ordinary = shares(number_of, rows * top, bound, slope, True), shares(number_of, rows * top, bound, slope, False)
    places = jnp.arange(number_of)

    def named(sizes, turn):
        used = int((sizes > 0).sum())
        fixed = max(1, used // 4)
        passed = fixed + (places - fixed + turn * (used - fixed)) % max(1, number_of - fixed)
        return jnp.zeros((number_of,), jnp.int32).at[sequence[jnp.where(places < fixed, places, passed)]].set(jnp.asarray(sizes, jnp.int32))

    sizes = jnp.where(number % 4 == 0, named(heavy_load, number // 4), named(ordinary, number - number // 4 - 1))
    mixed = jax.random.permutation(jax.random.fold_in(own, 3), number_of)
    source_of, taker = mixed[0:number_of // 2 * 2:2], mixed[1:number_of // 2 * 2:2]
    room = jnp.minimum(sizes[source_of] - 1, bound - sizes[taker]) // 2
    room = jnp.where((source_of == sequence[0]) | (taker == sequence[0]) | (sizes[taker] == 0), 0, jnp.maximum(room, 0))
    passed = jax.random.randint(jax.random.fold_in(own, 4), (number_of // 2,), 0, 1 << 20) % (room + 1)
    sizes = sizes.at[source_of].add(-passed).at[taker].add(passed)
    items = jnp.searchsorted(jnp.cumsum(sizes), jnp.arange(rows * top), side="right").astype(jnp.int32)
    grid = items.reshape(top, rows).T
    grid = grid[jax.random.permutation(jax.random.fold_in(own, 1), rows)]
    turn = jax.random.randint(jax.random.fold_in(own, 2), (rows, 1), 0, top)
    return jnp.take_along_axis(grid, (jnp.arange(top)[None, :] + turn) % top, axis=1)


def shares(amount, total, reach, skew, full):
    portions = [(1 << 20) // math.isqrt(grade ** skew) + 1 for grade in range(1, amount + 1)]
    largest = reach if full else min(reach, max(-(-total // amount), total * portions[0] // sum(portions)))
    least = 1 if total - largest >= amount - 1 else 0
    holding, surplus = [largest] + [least] * (amount - 1), total - largest - least * (amount - 1)
    while surplus > 0:
        candidates = [i for i in range(1, amount) if holding[i] < largest] or [i for i in range(1, amount) if holding[i] < reach]
        pool, budget = sum([portions[i] for i in candidates]), surplus
        for i in candidates:
            addition = min(reach - holding[i], max(1, budget * portions[i] // pool), surplus)
            holding[i] = holding[i] + addition
            surplus = surplus - addition
    return np.array(holding)


def normal_values(rng, shape, scale, limit, split=(), held_as=jnp.bfloat16):
    entries = jax.random.normal(rng, shape, jnp.float32) * scale
    if len(split) > 0:
        entries = steps_of(rng, shape, split, -0.22, 0.18) * entries
    return jnp.clip(entries, min=-limit, max=limit).astype(held_as)


def setup_inputs(seed: int = 0) -> dict:
    keys = jax.random.split(jax.random.key(seed), 14)
    tokens = normal_values(keys[0], (TOKENS, D), 1.0, 6.0, ((0, 32),))
    w_qkv = normal_values(keys[1], (D, 3 * D), D ** -0.5, 0.21875, ((0, 32),))
    w_attn_out = normal_values(keys[2], (D, D), (D // 16) ** -0.5, 0.875, ((0, 32),))
    gain_attn = jnp.clip(1.0 + 0.1 * jax.random.normal(keys[3], (D,), jnp.float32), 0.5, 1.5).astype(jnp.bfloat16)
    gain_moe = jnp.clip(1.0 + 0.1 * jax.random.normal(keys[4], (D,), jnp.float32), 0.5, 1.5).astype(jnp.bfloat16)
    w_router = normal_values(keys[5], (D, EXPERTS), (2 * D) ** -0.5, 0.15625, ((0, 32),))
    rel_bias = normal_values(keys[6], (BUCKETS, H), 1.0, 4.0, (), jnp.float32)
    w_in = normal_values(keys[7], (EXPERTS, D, FF), D ** -0.5, 0.21875, ((0, 8), (1, 4)))
    w_out = normal_values(keys[8], (EXPERTS, FF, D), (FF // 2) ** -0.5, 0.15625, ((0, 8), (1, 4)))
    teacher = normal_values(keys[9], (TOKENS, D), 1.0, 6.0, ((0, 32),))
    routes_keys = jax.random.split(jax.random.fold_in(keys[10], 1), TOKENS // TOK_DEV)
    routes_turns = jax.random.permutation(jax.random.fold_in(keys[10], 3), TOKENS // TOK_DEV)
    routes = jax.vmap(lambda own, number: assign_block(jax.random.fold_in(keys[10], 2), own, number, TOK_DEV, EXPERTS, 2, CAP, 1))(routes_keys, routes_turns).reshape((TOKENS, 2))
    valid = draw_valid(jax.random.fold_in(keys[13], 71), 0)
    buckets = jnp.searchsorted(jnp.cumsum(ragged_sizes(keys[12], BUCKETS, LENGTH, LENGTH // 8, 1)), jnp.arange(LENGTH), side="right").astype(jnp.int32)
    return dict(tokens=tokens, w_qkv=w_qkv, w_attn_out=w_attn_out, gain_attn=gain_attn, gain_moe=gain_moe, w_router=w_router, rel_bias=rel_bias, w_in=w_in, w_out=w_out, teacher=teacher, routes=routes, valid=valid, buckets=buckets)


EPS = 1e-06
NEG = -1e+30
HIGH = lax.Precision.HIGHEST

@jax.custom_vjp
def low(v):
    return lax.optimization_barrier(v.astype(jnp.bfloat16)).astype(jnp.float32)

@jax.custom_vjp
def low_back(v):
    return v

def low_keep(v):
    return (low(v), None)

def low_pass(kept, grad):
    return (grad,)

def back_keep(v):
    return (v, None)

def back_low(kept, grad):
    return (low(grad),)
low.defvjp(low_keep, low_pass)
low_back.defvjp(back_keep, back_low)

def matmul(left, right):
    return jnp.dot(left, right, precision=HIGH)

def normalize(values, gain):
    return values * lax.rsqrt(lax.optimization_barrier(jnp.mean(values * values, axis=-1, keepdims=True)) + EPS) * gain

def attend(queries, key_rows, value_rows, dist_bias):
    length = queries.shape[0]
    section = 512 if length % 512 == 0 else length
    positions = jnp.arange(length, dtype=jnp.int32)

    def one_block(first_row):
        query_rows = lax.dynamic_slice_in_dim(queries, first_row, section, 0)
        distance = (first_row + jnp.arange(section, dtype=jnp.int32))[:, None] - positions[None, :]
        allowed = distance >= 0
        bias_term = jnp.transpose(jnp.take(dist_bias, jnp.clip(distance, 0, length - 1), axis=0), (2, 0, 1))
        raw_scores = jnp.einsum('qhd,khd->hqk', query_rows, key_rows, precision=HIGH) * HEAD ** (-0.5) + bias_term
        scores = low_back(raw_scores)
        masked = jnp.where(allowed[None], scores, NEG)
        maximum = lax.optimization_barrier(jnp.max(masked, axis=2, keepdims=True))
        weights = jnp.where(allowed[None], jnp.exp(masked - maximum), 0.0)
        attn_weights = weights / lax.optimization_barrier(jnp.sum(weights, axis=2, keepdims=True))
        return jnp.einsum('hqk,khd->qhd', low(attn_weights), value_rows, precision=HIGH)
    first_rows = jnp.arange(length // section, dtype=jnp.int32) * section
    mixed_rows = lax.map(jax.checkpoint(one_block), first_rows)
    return mixed_rows.reshape(length, H * HEAD)

def experts_mix(moe_rows, seq_routes, gate_weights, weight_in, weight_out):
    length = moe_rows.shape[0]
    room = 4 * length // EXPERTS
    padded_rows = jnp.concatenate([moe_rows, jnp.zeros((1, moe_rows.shape[1]), jnp.float32)], axis=0)

    def one_expert(running, entry_pair):
        expert, matrix_in, matrix_out = entry_pair
        picked = seq_routes == expert
        coeff = lax.optimization_barrier(jnp.sum(jnp.where(picked, gate_weights, 0.0), axis=1))
        member = jnp.any(picked, axis=1)
        row_index = jnp.nonzero(member, size=room, fill_value=length)[0].astype(jnp.int32)
        entry = low_back(padded_rows[row_index])
        preact = low_back(matmul(entry, matrix_in))
        hidden = low(jax.nn.gelu(preact))
        result = low_back(low(matmul(hidden, matrix_out)))
        coeff_rows = jnp.concatenate([coeff, jnp.zeros((1,), jnp.float32)])[row_index]
        return (running.at[row_index].add(coeff_rows[:, None] * result), None)
    start_sum = jnp.zeros((length + 1, moe_rows.shape[1]), jnp.float32)
    expert_ids = jnp.arange(EXPERTS, dtype=jnp.int32)
    summed, _ = lax.scan(jax.checkpoint(one_expert), start_sum, (expert_ids, weight_in, weight_out))
    return summed[:length]

def reference(tokens, w_qkv, w_attn_out, gain_attn, gain_moe, w_router, rel_bias, w_in, w_out, teacher, routes, valid, buckets):
    float_type = jnp.float32
    params = (tokens.astype(float_type), w_qkv.astype(float_type), w_attn_out.astype(float_type), gain_attn.astype(float_type), gain_moe.astype(float_type), w_router.astype(float_type), rel_bias.astype(float_type), w_in.astype(float_type), w_out.astype(float_type))
    valid_float = valid.astype(float_type)
    count_all = jnp.sum(valid_float)
    one_hot = (buckets[:, None] == jnp.arange(BUCKETS, dtype=jnp.int32)[None, :]).astype(float_type)
    seq_total = TOKENS // LENGTH
    width = H * HEAD

    def forward(inputs, mat_qkv, mat_attn, gain_one, gain_two, mat_router, bias_table, mat_in, mat_out):
        dist_bias = matmul(one_hot, bias_table)

        def one_seq(loss_sum, entry_pair):
            seq_inputs, seq_routes, seq_teacher, seq_valid = entry_pair
            normed_in = low(normalize(seq_inputs, gain_one))
            qkv_rows = matmul(normed_in, mat_qkv)
            queries = low_back(low(qkv_rows[:, :width])).reshape(LENGTH, H, HEAD)
            key_rows = low_back(low(qkv_rows[:, width:2 * width])).reshape(LENGTH, H, HEAD)
            value_rows = low_back(low(qkv_rows[:, 2 * width:])).reshape(LENGTH, H, HEAD)
            attn_rows = attend(queries, key_rows, value_rows, dist_bias)
            attn_low = low_back(low(attn_rows))
            hidden_state = seq_inputs + low_back(matmul(attn_low, mat_attn))
            moe_rows = low(normalize(hidden_state, gain_two))
            logits = low_back(matmul(moe_rows, mat_router))
            chosen = jnp.take_along_axis(logits, seq_routes, axis=1)
            gate_weights = jax.nn.softmax(chosen, axis=1)
            mixture = experts_mix(moe_rows, seq_routes, gate_weights, mat_in, mat_out)
            result_rows = hidden_state + mixture
            error_rows = result_rows - seq_teacher
            return (loss_sum + jnp.sum(seq_valid[:, None] * error_rows * error_rows), result_rows)
        scanned = (inputs.reshape(seq_total, LENGTH, width), routes.reshape(seq_total, LENGTH, 2), teacher.astype(float_type).reshape(seq_total, LENGTH, width), valid_float.reshape(seq_total, LENGTH))
        loss_sum, result_rows = lax.scan(one_seq, jnp.zeros((), float_type), scanned)
        return (result_rows.reshape(TOKENS, width), loss_sum / (count_all * D))
    (output, loss), backward = jax.vjp(forward, *params)
    grads = backward((jnp.zeros_like(output), jnp.asarray(TOKENS * D, dtype=float_type)))
    return (output, loss, grads[0], grads[1], grads[2], grads[3], grads[4], grads[5], grads[6], grads[7], grads[8])
```

```python
import functools

import jax
import jax.numpy as jnp
from jax import lax
from jax.experimental import pallas as pl
from jax.experimental.pallas import tpu as pltpu
from jax.sharding import PartitionSpec as P

H = 12
HEAD = 64
BUCKETS = 32


EPS = 1e-06
NEG = -1e30
SECTION = 512
HIGH = lax.Precision.HIGHEST
FLOAT_TYPE = jnp.float32
HALF_TYPE = jnp.bfloat16


def normalize(values, gain):
    factor = lax.rsqrt(jnp.mean(values * values, axis=-1, keepdims=True) + EPS)
    return (values * factor * gain, factor)


def norm_back(values, factor, gain, grad_norm):
    scaled = grad_norm * gain
    mean_term = jnp.mean(scaled * values, axis=-1, keepdims=True)
    grad_values = factor * scaled - values * (factor * factor * factor) * mean_term
    return (grad_values, jnp.sum(grad_norm * values * factor, axis=0))


def gelu_grad(preact, grad_hidden):
    _, gelu_back = jax.vjp(jax.nn.gelu, preact)
    return gelu_back(grad_hidden)[0]


def in_sections(advance, running, shards):
    row_count = shards[0].shape[0]
    sections = row_count // SECTION
    stacked = tuple((member.reshape((sections, SECTION) + member.shape[1:]) for member in shards))

    def one_section(inner_state, entry_pair):
        return (advance(inner_state, entry_pair[1], entry_pair[0] * SECTION), None)

    final_state, _ = lax.scan(
        one_section, running, (jnp.arange(sections, dtype=jnp.int32), stacked)
    )
    return final_state


def score_block(queries, key_rows, query_start, key_start, rel_bias, edges):
    query_count = queries.shape[0]
    key_count = key_rows.shape[0]
    distance = (query_start + jnp.arange(query_count, dtype=jnp.int32))[:, None] - (
        key_start + jnp.arange(key_count, dtype=jnp.int32)
    )[None, :]
    allowed = distance >= 0
    bucket_hot = (
        (distance[:, :, None] >= edges[None, None, :-1])
        & (distance[:, :, None] < edges[None, None, 1:])
    ).astype(FLOAT_TYPE)
    bias_term = jnp.einsum("qkb,bh->hqk", bucket_hot, rel_bias, precision=HIGH)
    raw_scores = (
        jnp.einsum("qhd,khd->hqk", queries, key_rows, preferred_element_type=FLOAT_TYPE)
        * queries.shape[2] ** (-0.5)
        + bias_term
    )
    return (raw_scores, allowed, bucket_hot)


def split_three(values):
    upper = lax.optimization_barrier(values.astype(HALF_TYPE))
    remainder = values - upper.astype(FLOAT_TYPE)
    middle = lax.optimization_barrier(remainder.astype(HALF_TYPE))
    bottom = (remainder - middle.astype(FLOAT_TYPE)).astype(HALF_TYPE)
    return jnp.stack([upper, middle, bottom], axis=1)


def join_three(packed):
    as_float = packed.astype(FLOAT_TYPE)
    return as_float[:, 0] + as_float[:, 1] + as_float[:, 2]


def on_device(
    tokens,
    w_qkv,
    w_attn_out,
    gain_attn,
    gain_moe,
    w_router,
    rel_bias,
    w_in,
    w_out,
    teacher,
    routes,
    valid,
    buckets,
):
    tok_rows = tokens.shape[0]
    width = tokens.shape[1]
    seq_count = lax.axis_size("seq")
    my_start = lax.axis_index("seq") * tok_rows
    local_experts = w_in.shape[0]
    experts_all = local_experts * seq_count
    capacity = 4 * tok_rows // experts_all
    slot_rows = seq_count * capacity
    scale = HEAD ** (-0.5)
    qkv_full, attn_full, router_full, gain_one, gain_two, valid_all = (
        lax.all_gather(w_qkv, ("dp", "seq"), axis=0, tiled=True),
        lax.all_gather(w_attn_out, ("dp", "seq"), axis=0, tiled=True),
        lax.all_gather(w_router, ("dp", "seq"), axis=0, tiled=True),
        lax.all_gather(gain_attn, ("dp", "seq"), axis=0, tiled=True),
        lax.all_gather(gain_moe, ("dp", "seq"), axis=0, tiled=True),
        lax.all_gather(valid.astype(HALF_TYPE), ("dp", "seq"), axis=0, tiled=True),
    )
    valid_float = valid.astype(FLOAT_TYPE)
    count_all = jnp.sum(valid_all.astype(FLOAT_TYPE))
    tokens_all = tok_rows * lax.axis_size("dp") * seq_count
    edges = jnp.sum(
        (buckets[None, :] < jnp.arange(BUCKETS + 1, dtype=jnp.int32)[:, None]).astype(jnp.int32),
        axis=1,
    )
    inputs = tokens.astype(FLOAT_TYPE)
    gain_first = gain_one.astype(FLOAT_TYPE)
    gain_second = gain_two.astype(FLOAT_TYPE)
    normed_one, factor_one = normalize(inputs, gain_first)
    normed_in = normed_one.astype(HALF_TYPE)
    qkv_rows = jnp.dot(normed_in, qkv_full, preferred_element_type=FLOAT_TYPE)
    query_low = qkv_rows[:, :width].astype(HALF_TYPE)
    key_low = qkv_rows[:, width : 2 * width].astype(HALF_TYPE)
    value_low = qkv_rows[:, 2 * width :].astype(HALF_TYPE)
    heads_q = query_low.reshape(tok_rows, H, HEAD)
    heads_k = key_low.reshape(tok_rows, H, HEAD)
    heads_v = value_low.reshape(tok_rows, H, HEAD)
    last_row = my_start + tok_rows - 1

    def forward_step(running, shards, offset):
        key_rows = shards[0].reshape(shards[0].shape[0], H, HEAD)
        value_rows = shards[1].reshape(shards[1].shape[0], H, HEAD)

        def work(inner_state):
            maximum, denom, mixture = inner_state
            raw_scores, allowed, _ = score_block(
                heads_q, key_rows, my_start, offset, rel_bias, edges
            )
            masked = jnp.where(allowed[None], raw_scores, NEG)
            new_max = jnp.maximum(maximum, jnp.max(masked, axis=2))
            weights = jnp.where(allowed[None], jnp.exp(masked - new_max[:, :, None]), 0.0)
            rescale = jnp.exp(maximum - new_max)
            addend = jnp.einsum(
                "hqk,khd->hqd",
                weights.astype(HALF_TYPE),
                value_rows,
                preferred_element_type=FLOAT_TYPE,
            )
            return (
                new_max,
                denom * rescale + jnp.sum(weights, axis=2),
                mixture * rescale[:, :, None] + addend,
            )

        return lax.cond(offset <= last_row, work, lambda inner_state: inner_state, running)

    start_state = (
        jnp.full((H, tok_rows), NEG, FLOAT_TYPE),
        jnp.zeros((H, tok_rows), FLOAT_TYPE),
        jnp.zeros((H, tok_rows, HEAD), FLOAT_TYPE),
    )
    maximum, denom, mixture = in_sections(
        forward_step,
        start_state,
        (
            lax.all_gather(key_low, "seq", axis=0, tiled=True),
            lax.all_gather(value_low, "seq", axis=0, tiled=True),
        ),
    )
    log_total = maximum + jnp.log(denom)
    attn_heads = mixture / denom[:, :, None]
    attn_rows = jnp.transpose(attn_heads, (1, 0, 2)).reshape(tok_rows, width)
    attn_low = attn_rows.astype(HALF_TYPE)
    hidden_state = inputs + jnp.dot(attn_low, attn_full, preferred_element_type=FLOAT_TYPE)
    normed_two, factor_two = normalize(hidden_state, gain_second)
    moe_in = normed_two.astype(HALF_TYPE)
    logits = jnp.dot(moe_in, router_full, preferred_element_type=FLOAT_TYPE)
    chosen = jnp.take_along_axis(logits, routes, axis=1)
    gate_weights = jax.nn.softmax(chosen, axis=1)
    flat_routes = routes.reshape(-1)
    matches = (flat_routes[:, None] == jnp.arange(experts_all, dtype=jnp.int32)[None, :]).astype(
        jnp.int32
    )
    slot_index = jnp.sum((jnp.cumsum(matches, axis=0) - matches) * matches, axis=1)
    target_dev = flat_routes // local_experts
    target_local = flat_routes % local_experts
    position = (target_dev * capacity + slot_index) * local_experts + target_local
    dispatch_map = (
        jnp.arange(experts_all * capacity, dtype=jnp.int32)[:, None] == position[None, :]
    ).astype(HALF_TYPE)
    dispatch_map = dispatch_map.reshape(experts_all * capacity, tok_rows, 2)
    outgoing = jnp.einsum(
        "prk,rd->pd", dispatch_map, moe_in, preferred_element_type=FLOAT_TYPE
    ).astype(HALF_TYPE)
    arrived = lax.all_to_all(
        outgoing.reshape(seq_count, capacity * local_experts, width),
        "seq",
        split_axis=0,
        concat_axis=0,
        tiled=True,
    )
    arrived_rows = arrived.reshape(slot_rows, local_experts, width)
    in_full, out_full = (
        lax.all_gather(w_in, "dp", axis=1, tiled=True),
        lax.all_gather(w_out, "dp", axis=1, tiled=True),
    )
    preact = jnp.einsum("mld,ldf->mlf", arrived_rows, in_full, preferred_element_type=FLOAT_TYPE)
    hidden = jax.nn.gelu(preact).astype(HALF_TYPE)
    result = jnp.einsum("mlf,lfd->mld", hidden, out_full, preferred_element_type=FLOAT_TYPE).astype(
        HALF_TYPE
    )
    returned = lax.all_to_all(
        result.reshape(seq_count, capacity * local_experts, width),
        "seq",
        split_axis=0,
        concat_axis=0,
        tiled=True,
    )
    returned = returned.reshape(experts_all * capacity, width)
    combined = jnp.einsum("prk,pd->krd", dispatch_map, returned, preferred_element_type=FLOAT_TYPE)
    output = hidden_state + gate_weights[:, 0:1] * combined[0] + gate_weights[:, 1:2] * combined[1]
    error_rows = output - teacher.astype(FLOAT_TYPE)
    loss_local = jnp.sum(valid_float[:, None] * error_rows * error_rows)
    grad_out = 2.0 * tokens_all / count_all * valid_float[:, None] * error_rows
    grad_gate = jnp.einsum("krd,rd->rk", combined, grad_out)
    grad_chosen = gate_weights * (
        grad_gate - jnp.sum(gate_weights * grad_gate, axis=1, keepdims=True)
    )
    pick = (routes[:, :, None] == jnp.arange(experts_all, dtype=jnp.int32)[None, None, :]).astype(
        FLOAT_TYPE
    )
    grad_logits = jnp.sum(pick * grad_chosen[:, :, None], axis=1).astype(HALF_TYPE)
    grad_router = jnp.einsum("rd,re->de", moe_in, grad_logits, preferred_element_type=FLOAT_TYPE)
    grad_result = (jnp.transpose(gate_weights)[:, :, None] * grad_out[None]).astype(HALF_TYPE)
    grad_slots = jnp.einsum(
        "prk,krd->pd", dispatch_map, grad_result, preferred_element_type=FLOAT_TYPE
    ).astype(HALF_TYPE)
    grad_arrived = lax.all_to_all(
        grad_slots.reshape(seq_count, capacity * local_experts, width),
        "seq",
        split_axis=0,
        concat_axis=0,
        tiled=True,
    )
    grad_rows = grad_arrived.reshape(slot_rows, local_experts, width)
    grad_hidden = jnp.einsum("mld,lfd->mlf", grad_rows, out_full, preferred_element_type=FLOAT_TYPE)
    grad_preact = gelu_grad(preact, grad_hidden).astype(HALF_TYPE)
    grad_out_local = jnp.einsum(
        "mlf,mld->lfd", hidden, grad_rows, preferred_element_type=FLOAT_TYPE
    )
    grad_in_local = jnp.einsum(
        "mld,mlf->ldf", arrived_rows, grad_preact, preferred_element_type=FLOAT_TYPE
    )
    grad_entry = jnp.einsum(
        "mlf,ldf->mld", grad_preact, in_full, preferred_element_type=FLOAT_TYPE
    ).astype(HALF_TYPE)
    grad_w_in, grad_w_out = (
        lax.psum_scatter(
            grad_in_local.astype(jnp.bfloat16), "dp", scatter_dimension=1, tiled=True
        ).astype(jnp.float32),
        lax.psum_scatter(
            grad_out_local.astype(jnp.bfloat16), "dp", scatter_dimension=1, tiled=True
        ).astype(jnp.float32),
    )
    grad_back = lax.all_to_all(
        grad_entry.reshape(seq_count, capacity * local_experts, width),
        "seq",
        split_axis=0,
        concat_axis=0,
        tiled=True,
    )
    grad_back = grad_back.reshape(experts_all * capacity, width)
    grad_moe_in = jnp.einsum(
        "prk,pd->rd", dispatch_map, grad_back, preferred_element_type=FLOAT_TYPE
    )
    grad_moe_in = grad_moe_in + jnp.einsum(
        "re,de->rd", grad_logits, router_full, preferred_element_type=FLOAT_TYPE
    )
    grad_hidden_norm, grad_gain_second = norm_back(
        hidden_state, factor_two, gain_second, grad_moe_in
    )
    grad_state = grad_out + grad_hidden_norm
    grad_state_low = grad_state.astype(HALF_TYPE)
    grad_attn_w = jnp.einsum(
        "rd,re->de", attn_low, grad_state_low, preferred_element_type=FLOAT_TYPE
    )
    grad_attn_low = jnp.einsum(
        "re,de->rd", grad_state_low, attn_full, preferred_element_type=FLOAT_TYPE
    ).astype(HALF_TYPE)
    heads_dout = grad_attn_low.reshape(tok_rows, H, HEAD)
    softmax_dot = jnp.sum(
        jnp.transpose(heads_dout, (1, 0, 2)).astype(FLOAT_TYPE) * attn_heads, axis=2
    )
    row_stats = split_three(
        jnp.stack([jnp.transpose(log_total), jnp.transpose(softmax_dot)], axis=1)
    )

    def backward_step(running, shards, offset):
        key_rows = shards[0].reshape(shards[0].shape[0], H, HEAD)
        value_rows = shards[1].reshape(shards[1].shape[0], H, HEAD)
        query_rows = shards[2].reshape(shards[2].shape[0], H, HEAD)
        dout_rows = shards[3].reshape(shards[3].shape[0], H, HEAD)
        stats_rows = join_three(shards[4])
        piece_total = jnp.transpose(stats_rows[:, 0, :])
        piece_dot = jnp.transpose(stats_rows[:, 1, :])
        grad_query, grad_table, grad_key, grad_value = running

        def query_work(inner_state):
            inner_query, inner_table = inner_state
            raw_scores, allowed, bucket_hot = score_block(
                heads_q, key_rows, my_start, offset, rel_bias, edges
            )
            weights = jnp.where(allowed[None], jnp.exp(raw_scores - log_total[:, :, None]), 0.0)
            grad_prob = jnp.einsum(
                "qhd,khd->hqk", heads_dout, value_rows, preferred_element_type=FLOAT_TYPE
            )
            grad_score = (weights * (grad_prob - softmax_dot[:, :, None])).astype(HALF_TYPE)
            inner_query = (
                inner_query
                + jnp.einsum(
                    "hqk,khd->hqd", grad_score, key_rows, preferred_element_type=FLOAT_TYPE
                )
                * scale
            )
            inner_table = inner_table + jnp.einsum(
                "hqk,qkb->bh", grad_score.astype(FLOAT_TYPE), bucket_hot, precision=HIGH
            )
            return (inner_query, inner_table)

        def key_work(inner_state):
            inner_key, inner_value = inner_state
            raw_scores, allowed, _ = score_block(
                query_rows, heads_k, offset, my_start, rel_bias, edges
            )
            weights = jnp.where(allowed[None], jnp.exp(raw_scores - piece_total[:, :, None]), 0.0)
            inner_value = inner_value + jnp.einsum(
                "hqk,qhd->khd",
                weights.astype(HALF_TYPE),
                dout_rows,
                preferred_element_type=FLOAT_TYPE,
            )
            grad_prob = jnp.einsum(
                "qhd,khd->hqk", dout_rows, heads_v, preferred_element_type=FLOAT_TYPE
            )
            grad_score = (weights * (grad_prob - piece_dot[:, :, None])).astype(HALF_TYPE)
            inner_key = (
                inner_key
                + jnp.einsum(
                    "hqk,qhd->khd", grad_score, query_rows, preferred_element_type=FLOAT_TYPE
                )
                * scale
            )
            return (inner_key, inner_value)

        grad_query, grad_table = lax.cond(
            offset <= last_row,
            query_work,
            lambda inner_state: inner_state,
            (grad_query, grad_table),
        )
        grad_key, grad_value = lax.cond(
            offset + shards[0].shape[0] - 1 >= my_start,
            key_work,
            lambda inner_state: inner_state,
            (grad_key, grad_value),
        )
        return (grad_query, grad_table, grad_key, grad_value)

    back_start = (
        jnp.zeros((H, tok_rows, HEAD), FLOAT_TYPE),
        jnp.zeros((BUCKETS, H), FLOAT_TYPE),
        jnp.zeros((tok_rows, H, HEAD), FLOAT_TYPE),
        jnp.zeros((tok_rows, H, HEAD), FLOAT_TYPE),
    )
    grad_query, grad_table_local, grad_key, grad_value = in_sections(
        backward_step,
        back_start,
        (
            lax.all_gather(key_low, "seq", axis=0, tiled=True),
            lax.all_gather(value_low, "seq", axis=0, tiled=True),
            lax.all_gather(query_low, "seq", axis=0, tiled=True),
            lax.all_gather(grad_attn_low, "seq", axis=0, tiled=True),
            lax.all_gather(row_stats, "seq", axis=0, tiled=True),
        ),
    )
    grad_qkv_low = jnp.concatenate(
        [
            jnp.transpose(grad_query, (1, 0, 2)).reshape(tok_rows, width),
            grad_key.reshape(tok_rows, width),
            grad_value.reshape(tok_rows, width),
        ],
        axis=1,
    ).astype(HALF_TYPE)
    grad_qkv_w = jnp.einsum("rd,re->de", normed_in, grad_qkv_low, preferred_element_type=FLOAT_TYPE)
    grad_normed_one = jnp.einsum(
        "re,de->rd", grad_qkv_low, qkv_full, preferred_element_type=FLOAT_TYPE
    )
    grad_in_norm, grad_gain_first = norm_back(inputs, factor_one, gain_first, grad_normed_one)
    grad_tokens = grad_state + grad_in_norm
    grad_qkv_own, grad_attn_own, grad_router_own, grad_gain_attn, grad_gain_moe = (
        lax.psum_scatter(grad_qkv_w, ("dp", "seq"), scatter_dimension=0, tiled=True),
        lax.psum_scatter(grad_attn_w, ("dp", "seq"), scatter_dimension=0, tiled=True),
        lax.psum_scatter(grad_router, ("dp", "seq"), scatter_dimension=0, tiled=True),
        lax.psum_scatter(grad_gain_first, ("dp", "seq"), scatter_dimension=0, tiled=True),
        lax.psum_scatter(grad_gain_second, ("dp", "seq"), scatter_dimension=0, tiled=True),
    )
    loss_sum, grad_table = lax.psum((loss_local, grad_table_local), ("dp", "seq"))
    loss = loss_sum / (count_all * width)
    return (
        output,
        loss,
        grad_tokens,
        grad_qkv_own,
        grad_attn_own,
        grad_gain_attn,
        grad_gain_moe,
        grad_router_own,
        grad_table,
        grad_w_in,
        grad_w_out,
    )


MESH = pl.DeviceIdType.MESH
ANY = pl.BlockSpec(memory_space=pl.ANY)
VM = pl.BlockSpec(memory_space=pltpu.VMEM)
ROLL = 1280
GW = 1152


def remote(src, dst, send, recv, dev):
    return pltpu.make_async_remote_copy(
        src_ref=src, dst_ref=dst, send_sem=send, recv_sem=recv, device_id=dev, device_id_type=MESH
    )


def place():
    d = lax.axis_index("dp")
    s = lax.axis_index("seq")
    return d, s, s // 2, lax.rem(s, 2)


def greet(peers):
    barrier = pltpu.get_barrier_semaphore()
    for peer in peers:
        pl.semaphore_signal(barrier, inc=1, device_id=peer, device_id_type=MESH)
    pl.semaphore_wait(barrier, len(peers))


def comm_call(body, outs, n_in, cid, scratch, name, in_specs=None, out_specs=None, vmem=None):
    return pl.pallas_call(
        body,
        out_shape=outs,
        in_specs=in_specs or [ANY] * n_in,
        out_specs=out_specs or [ANY] * len(outs),
        scratch_shapes=scratch,
        compiler_params=pltpu.CompilerParams(
            collective_id=cid, has_side_effects=True, vmem_limit_bytes=vmem
        ),
        name=name,
    )


def sds(shape, dtype=jnp.bfloat16):
    return jax.ShapeDtypeStruct(shape, dtype)


def gather_kernel(x, wq, wr, win, wout, xs, wqf, wrf, winf, woutf, ss, rs, xe, re, ls):
    d, s, z, c = place()
    sib = (d, s + 1 - 2 * c)
    plane = [(lax.rem(d + k, 4), s) for k in (1, 2, 3)]
    plane_other = [(lax.rem(d + k, 4), s + 1 - 2 * c) for k in (1, 2, 3)]
    zs = [(d, 2 * lax.rem(z + k, 4) + c) for k in (1, 2, 3)]
    greet(plane + plane_other + zs + [sib])
    local = [
        pltpu.make_async_copy(wq.at[z], wqf.at[d, z, c], ls.at[0]),
        pltpu.make_async_copy(wr, wrf.at[d, z, c], ls.at[1]),
        pltpu.make_async_copy(x, xs.at[z], ls.at[2]),
    ]
    for cp in local:
        cp.start()
    stage1 = []
    for i, k in enumerate((1, 2, 3)):
        zt = lax.rem(z + k, 4)
        stage1.append(remote(wq.at[zt], wqf.at[d, z, c], ss.at[i], rs.at[i], zs[i]))
        stage1.append(remote(wr, wrf.at[d, z, c], ss.at[3 + i], rs.at[3 + i], zs[i]))
    for cp in stage1:
        cp.start()
    stage_x = []
    for i in range(3):
        cp = remote(x, xs.at[z], ss.at[6 + i], rs.at[6 + i], zs[i])
        cp.start()
        stage_x.append(cp)
    for m, (src, dst) in enumerate(((win, winf), (wout, woutf))):
        for k in (1, 2, 3):
            j = lax.rem(d + k, 4)

            @pl.when(j // 2 == c)
            def _(src=src, dst=dst, m=m, k=k, j=j):
                for half in range(2):
                    remote(
                        src.at[lax.rem(j, 2), half],
                        dst.at[d, half],
                        xe.at[m, k, half],
                        re.at[m, k],
                        (j, 2 * z + half),
                    ).start()

        @pl.when(d // 2 == c)
        def _(src=src, dst=dst, m=m):
            mine = src.at[lax.rem(d, 2)]
            pltpu.make_async_copy(mine, dst.at[d], ls.at[3 + m]).start()
            remote(mine, dst.at[d], xe.at[m, 0, 0], re.at[m, 4], sib).start()

    for cp in local:
        cp.wait()
    for cp in stage1:
        cp.wait_recv()
    stage2 = []
    for i, k in enumerate((1, 2, 3)):
        stage2.append(
            remote(wqf.at[d, :, c], wqf.at[d, :, c], ss.at[9 + i], rs.at[9 + i], plane[i])
        )
        stage2.append(
            remote(wrf.at[d, :, c], wrf.at[d, :, c], ss.at[12 + i], rs.at[12 + i], plane[i])
        )
    for cp in stage2:
        cp.start()
    stage3 = []

    def forward(array, dd, i):
        cp = remote(array.at[dd, :, c], array.at[dd, :, c], ss.at[i], rs.at[i], sib)
        cp.start()
        stage3.append(cp)

    forward(wqf, d, 15)
    forward(wrf, d, 16)
    for i, k in enumerate((1, 2, 3)):
        dd = lax.rem(d + 4 - k, 4)
        stage2[2 * i].wait_recv()
        forward(wqf, dd, 17 + 2 * i)
        stage2[2 * i + 1].wait_recv()
        forward(wrf, dd, 18 + 2 * i)
    for cp in stage_x:
        cp.wait_recv()
    for cp in stage3:
        cp.wait_recv()
    passed = []
    for m, (src, dst) in enumerate(((win, winf), (wout, woutf))):
        for k in (1, 2, 3):
            dd = lax.rem(d + 4 - k, 4)
            cp = remote(dst.at[dd, c], dst.at[dd, c], xe.at[m, k, 2], re.at[m, 4 + k], sib)
            remote(dst.at[dd, c], dst.at[dd, c], xe.at[m, k, 2], re.at[m, k], sib).wait_recv()
            cp.start()
            passed.append(cp)
    for cp in passed:
        cp.wait_recv()
    for m, (src, dst) in enumerate(((win, winf), (wout, woutf))):

        @pl.when(d // 2 == c)
        def _(src=src, dst=dst, m=m):
            mine = src.at[lax.rem(d, 2)]
            pltpu.make_async_copy(mine, dst.at[d], ls.at[3 + m]).wait()
            remote(mine, dst.at[d], xe.at[m, 0, 0], re.at[m, 4], sib).wait_send()

        @pl.when(d // 2 != c)
        def _(src=src, dst=dst, m=m):
            mine = src.at[lax.rem(d, 2)]
            remote(mine, dst.at[d], xe.at[m, 0, 0], re.at[m, 4], sib).wait_recv()

        for k in (1, 2, 3):
            j = lax.rem(d + k, 4)

            @pl.when(j // 2 == c)
            def _(src=src, dst=dst, m=m, k=k, j=j):
                for half in range(2):
                    remote(
                        src.at[lax.rem(j, 2), half],
                        dst.at[d, half],
                        xe.at[m, k, half],
                        re.at[m, k],
                        (j, 2 * z + half),
                    ).wait_send()

    for cp in stage1 + stage_x + stage2 + stage3 + passed:
        cp.wait_send()


def head_mask(h):
    lane = lax.broadcasted_iota(jnp.int32, (1, 192), 1)
    return lane // HEAD == h


def bias_kernel(e_ref, g_ref):
    for h in range(3):
        row = jnp.broadcast_to(e_ref[h : h + 1, :], (128, ROLL))
        g_ref[h] = pltpu.roll(row, 0, 1, stride=1, stride_axis=0)[:, 128:]


def dot_t(a, b):
    return lax.dot_general(a, b, (((1,), (1,)), ((), ())), preferred_element_type=jnp.float32)


def dot_l(a, b):
    return lax.dot_general(a, b, (((0,), (0,)), ((), ())), preferred_element_type=jnp.float32)


def dot_n(a, b):
    return jnp.dot(a, b, preferred_element_type=jnp.float32)


def soft_rows(q, keys, g_ref, h, start, width):
    s = dot_t(q, keys) * HEAD ** (-0.5) + g_ref[h, :, pl.ds(start, width)]
    m = jnp.max(s, axis=1, keepdims=True)
    p = jnp.exp(s - m)
    return p / jnp.sum(p, axis=1, keepdims=True)


def attend_kernel(q, k, v, g, attn, kf, vf, out, ss, rs):
    d, s, z, c = place()
    sib = (d, s + 1 - 2 * c)
    zs = [(d, 2 * lax.rem(z + i, 4) + c) for i in (1, 2, 3)]
    greet(zs + [sib])
    kf[:, pl.ds(c, 1)] = k[...][:, None]
    vf[:, pl.ds(c, 1)] = v[...][:, None]
    swap = [
        remote(k, kf.at[:, c], ss.at[4], rs.at[4], sib),
        remote(v, vf.at[:, c], ss.at[5], rs.at[5], sib),
    ]
    for cp in swap:
        cp.start()
    for cp in swap:
        cp.wait_recv()
    for zb in (3, 2, 1, 0):
        width = 256 * (zb + 1)
        start = pl.multiple_of(128 * (7 - 2 * zb) - 128 * c, 128)
        keys = kf[: zb + 1].reshape(width, 192)
        values = vf[: zb + 1].reshape(width, 192)
        acc = jnp.zeros((128, 192), jnp.float32)
        for h in range(3):
            qh = jnp.where(head_mask(h), q[zb], jnp.zeros((), jnp.bfloat16))
            p = soft_rows(qh, keys, g, h, start, width).astype(jnp.bfloat16)
            acc = acc + jnp.where(head_mask(h), dot_n(p, values), 0.0)
        out[zb] = acc.astype(jnp.bfloat16)

        @pl.when(z != zb)
        def _(zb=zb):
            remote(out.at[zb], attn.at[z], ss.at[zb], rs.at[z], (d, 2 * zb + c)).start()

        @pl.when(z == zb)
        def _(zb=zb):
            attn[pl.ds(z, 1)] = out[zb][None]

    for zb in range(4):

        @pl.when(z != zb)
        def _(zb=zb):
            cp = remote(out.at[zb], attn.at[zb], ss.at[zb], rs.at[zb], (d, 2 * zb + c))
            cp.wait_send()
            cp.wait_recv()

    for cp in swap:
        cp.wait_send()


def attend_back_kernel(q, k, v, g, do, dq, dk, dv, db, kacc, vacc, gacc):
    c = lax.rem(lax.axis_index("seq"), 2)
    kacc[...] = jnp.zeros_like(kacc)
    vacc[...] = jnp.zeros_like(vacc)
    gacc[...] = jnp.zeros_like(gacc)
    for zb in (3, 2, 1, 0):
        width = 256 * (zb + 1)
        start = pl.multiple_of(128 * (7 - 2 * zb) - 128 * c, 128)
        keys = k[: zb + 1].reshape(width, 192)
        values = v[: zb + 1].reshape(width, 192)
        acc = jnp.zeros((128, 192), jnp.float32)
        for h in range(3):
            mask = head_mask(h)
            qh = jnp.where(mask, q[zb], jnp.zeros((), jnp.bfloat16))
            doh = jnp.where(mask, do[zb], jnp.zeros((), jnp.bfloat16))
            p = soft_rows(qh, keys, g, h, start, width)
            vacc[:width] += dot_l(p.astype(jnp.bfloat16), doh)
            dp = dot_t(doh, values)
            dot = jnp.sum(p * dp, axis=1, keepdims=True)
            ds = (p * (dp - dot)).astype(jnp.bfloat16)
            gacc[h, :, pl.ds(start, width)] += ds.astype(jnp.float32)
            acc = acc + jnp.where(mask, dot_n(ds, keys), 0.0)
            kacc[:width] += dot_l(ds, qh)
        dq[zb] = (acc * HEAD ** (-0.5)).astype(jnp.bfloat16)
    dk[...] = (kacc[...] * HEAD ** (-0.5)).reshape(4, 2, 128, 192)
    dv[...] = vacc[...].reshape(4, 2, 128, 192)
    row = lax.broadcasted_iota(jnp.int32, (128, 1), 0)
    for h in range(3):
        y = jnp.concatenate([jnp.zeros((128, ROLL - GW), jnp.float32), gacc[h]], axis=1)
        for bit in range(7):
            y = jnp.where((row >> bit) & 1 == 1, pltpu.roll(y, ROLL - (1 << bit), 1), y)
        db[h : h + 1, :] = jnp.sum(y, axis=0, keepdims=True)


def spread_kernel(src, dst, ss, rs, ls):
    d, s, z, c = place()
    me = z * 4 + d
    peers = []
    for k in range(1, 16):
        t = lax.rem(me + k, 16)
        peers.append((lax.rem(t, 4), 2 * (t // 4) + c))
    greet(peers)
    own = pltpu.make_async_copy(src.at[me], dst.at[me], ls)
    own.start()
    sent = []
    for k in range(1, 16):
        t = lax.rem(me + k, 16)
        cp = remote(src.at[t], dst.at[me], ss.at[k - 1], rs.at[k - 1], peers[k - 1])
        cp.start()
        sent.append(cp)
    for cp in sent:
        cp.wait()
    own.wait()


def spread(x, cid, name):
    return comm_call(
        spread_kernel,
        [sds(x.shape, x.dtype)],
        1,
        cid,
        [
            pltpu.SemaphoreType.DMA((15,)),
            pltpu.SemaphoreType.DMA((15,)),
            pltpu.SemaphoreType.DMA,
        ],
        name,
    )(x)[0]


def columns_kernel(src, dst, ss, rs, ls):
    d, s, z, c = place()
    peers = [(d, 2 * lax.rem(z + k, 4) + c) for k in (1, 2, 3)]
    greet(peers)
    own = pltpu.make_async_copy(src.at[z], dst.at[z], ls)
    own.start()
    sent = []
    for i, k in enumerate((1, 2, 3)):
        t = lax.rem(z + k, 4)
        cp = remote(src.at[t], dst.at[z], ss.at[i], rs.at[i], peers[i])
        cp.start()
        sent.append(cp)
    for cp in sent:
        cp.wait()
    own.wait()


def columns(x, cid, name):
    return comm_call(
        columns_kernel,
        [sds(x.shape, x.dtype)],
        1,
        cid,
        [pltpu.SemaphoreType.DMA((3,)), pltpu.SemaphoreType.DMA((3,)), pltpu.SemaphoreType.DMA],
        name,
    )(x)[0]


def swap_kernel(n, *refs):
    ins, outs, ss, rs = refs[:n], refs[n : 2 * n], refs[2 * n], refs[2 * n + 1]
    d, s, z, c = place()
    sib = (d, s + 1 - 2 * c)
    greet([sib])
    sent = [remote(a, b, ss.at[i], rs.at[i], sib) for i, (a, b) in enumerate(zip(ins, outs))]
    for cp in sent:
        cp.start()
    for cp in sent:
        cp.wait()


def swap(arrays, cid, name):
    n = len(arrays)
    return comm_call(
        functools.partial(swap_kernel, n),
        [sds(a.shape, a.dtype) for a in arrays],
        n,
        cid,
        [pltpu.SemaphoreType.DMA((n,)), pltpu.SemaphoreType.DMA((n,))],
        name,
    )(*arrays)


def owners_kernel(gin, gout, oin, oout, ss, rs, ls):
    d, s, z, c = place()
    peers = []
    for k in (1, 2, 3):
        for core in range(2):
            peers.append((lax.rem(d + k, 4), 2 * z + core))
    peers.append((d, s + 1 - 2 * c))
    greet(peers)
    pairs = ((gin, oin), (gout, oout))
    sent = []
    for m, (src, dst) in enumerate(pairs):
        for i, k in enumerate((1, 2, 3)):
            dd = lax.rem(d + k, 4)
            cp = remote(
                src.at[dd],
                dst.at[lax.rem(d, 2), c],
                ss.at[m, i],
                rs.at[m, lax.rem(d, 2), c],
                (dd, 2 * z + d // 2),
            )
            cp.start()
            sent.append(cp)

        @pl.when(d // 2 == c)
        def _(src=src, dst=dst, m=m):
            pltpu.make_async_copy(src.at[d], dst.at[lax.rem(d, 2), c], ls.at[m]).start()

        @pl.when(d // 2 != c)
        def _(src=src, dst=dst, m=m):
            remote(
                src.at[d],
                dst.at[lax.rem(d, 2), c],
                ss.at[m, 3],
                rs.at[m, lax.rem(d, 2), c],
                (d, s + 1 - 2 * c),
            ).start()

    for m, (src, dst) in enumerate(pairs):
        for l in range(2):
            for half in range(2):
                here = (2 * c + l == d) & (c == half)

                @pl.when(jnp.logical_not(here))
                def _(src=src, dst=dst, m=m, l=l, half=half):
                    remote(
                        src.at[0], dst.at[l, half], ss.at[m, 0], rs.at[m, l, half], peers[0]
                    ).wait_recv()

        @pl.when(d // 2 == c)
        def _(src=src, dst=dst, m=m):
            pltpu.make_async_copy(src.at[d], dst.at[lax.rem(d, 2), c], ls.at[m]).wait()

        @pl.when(d // 2 != c)
        def _(src=src, dst=dst, m=m):
            remote(
                src.at[d],
                dst.at[lax.rem(d, 2), c],
                ss.at[m, 3],
                rs.at[m, lax.rem(d, 2), c],
                (d, s + 1 - 2 * c),
            ).wait_send()

    for cp in sent:
        cp.wait_send()


def share_kernel(src, dst, ss, rs, ls):
    d, s, z, c = place()
    peers = []
    for k in range(1, 32):
        peers.append((lax.rem(d + k // 8, 4), lax.rem(s + lax.rem(k, 8), 8)))
    greet(peers)
    me = d * 8 + s
    own = pltpu.make_async_copy(src, dst.at[me], ls)
    own.start()
    sent = []
    for k in range(1, 32):
        cp = remote(src, dst.at[me], ss.at[k - 1], rs.at[k - 1], peers[k - 1])
        cp.start()
        sent.append(cp)
    for cp in sent:
        cp.wait()
    own.wait()


def fast_path(
    tokens,
    w_qkv,
    w_attn_out,
    gain_attn,
    gain_moe,
    w_router,
    rel_bias,
    w_in,
    w_out,
    teacher,
    routes,
    valid,
    buckets,
):
    f32, bf16 = jnp.float32, jnp.bfloat16
    d = lax.axis_index("dp")
    s = lax.axis_index("seq")
    z, c = s // 2, s % 2
    sections = [pltpu.SemaphoreType.DMA((26,)), pltpu.SemaphoreType.DMA((26,))]
    wq = w_qkv.reshape(24, 3, 4, 192).transpose(2, 0, 1, 3).reshape(4, 24, 576)
    valid_float = valid.astype(f32)
    misc = jnp.concatenate(
        [
            w_attn_out,
            w_router,
            gain_attn[:, None],
            gain_moe[:, None],
            jnp.full((24, 1), jnp.sum(valid_float)).astype(bf16),
            jnp.zeros((24, 109), bf16),
        ],
        axis=1,
    )
    xs, wqf, wrf, winf, woutf = comm_call(
        gather_kernel,
        [
            sds((4, 128, 768)),
            sds((4, 4, 2, 24, 576)),
            sds((4, 4, 2, 24, 896)),
            sds((4, 2, 96, 3072)),
            sds((4, 2, 384, 768)),
        ],
        5,
        1,
        sections
        + [
            pltpu.SemaphoreType.DMA((2, 4, 3)),
            pltpu.SemaphoreType.DMA((2, 8)),
            pltpu.SemaphoreType.DMA((5,)),
        ],
        "gather_all",
    )(tokens, wq, misc, w_in.reshape(2, 2, 96, 3072), w_out.reshape(2, 2, 384, 768))
    wqf = wqf.reshape(768, 576)
    wrf = wrf.reshape(768, 896)
    winf = winf.reshape(768, 3072)
    woutf = woutf.reshape(3072, 768)
    attn_full = wrf[:, :768]
    router_full = wrf[:, 768:784]
    gain_first = wrf[:, 784].astype(f32)
    gain_second = wrf[:, 785].astype(f32)
    count_all = jnp.sum(wrf.reshape(32, 24, 896)[:, 0, 786].astype(f32))
    tokens_all = 4096.0

    one_hot = (buckets[None, :] == jnp.arange(BUCKETS, dtype=jnp.int32)[:, None]).astype(f32)
    my_bias = lax.dynamic_slice_in_dim(rel_bias, 3 * z, 3, 1)
    table = jnp.einsum("bh,bt->ht", my_bias, one_hot, precision=HIGH)
    line = jnp.concatenate(
        [
            jnp.full((3, 1), NEG, f32),
            table[:, ::-1],
            jnp.full((3, ROLL - 1025), NEG, f32),
        ],
        axis=1,
    )
    bias = pl.pallas_call(bias_kernel, out_shape=sds((3, 128, GW), f32), name="bias_tiles")(line)

    inputs_s = xs.reshape(512, 768).astype(f32)
    normed_s, factor_s = normalize(inputs_s, gain_first)
    n1s = normed_s.astype(bf16)
    qkv = dot_n(n1s, wqf).astype(bf16).reshape(4, 128, 576)
    q, k, v = qkv[:, :, :192], qkv[:, :, 192:384], qkv[:, :, 384:]
    attn, kf, vf = comm_call(
        attend_kernel,
        [sds((4, 128, 192)), sds((4, 2, 128, 192)), sds((4, 2, 128, 192))],
        4,
        2,
        [
            pltpu.VMEM((4, 128, 192), bf16),
            pltpu.SemaphoreType.DMA((6,)),
            pltpu.SemaphoreType.DMA((6,)),
        ],
        "attend",
        in_specs=[VM] * 4,
        out_specs=[VM] * 3,
        vmem=50 << 20,
    )(q, k, v, bias)
    attn_low = attn.transpose(1, 0, 2).reshape(128, 768)
    inputs = tokens.astype(f32)
    hidden_state = inputs + dot_n(attn_low, attn_full)
    normed_two, factor_two = normalize(hidden_state, gain_second)
    moe_in = normed_two.astype(bf16)
    logits = dot_n(moe_in, router_full)
    pick = (routes[:, :, None] == jnp.arange(16, dtype=jnp.int32)[None, None, :]).astype(f32)
    chosen = jnp.sum(pick * logits[:, None, :], axis=2)
    gate_weights = jax.nn.softmax(chosen, axis=1)
    matches = jnp.sum(pick, axis=1)
    lower = (
        jnp.arange(128, dtype=jnp.int32)[:, None] > jnp.arange(128, dtype=jnp.int32)[None, :]
    ).astype(bf16)
    before = dot_n(lower, matches.astype(bf16))
    slot = jnp.sum(pick * before[:, None, :], axis=2).astype(jnp.int32)
    position = routes * 32 + slot
    maps = [
        (jnp.arange(512, dtype=jnp.int32)[:, None] == position[None, :, i]).astype(bf16)
        for i in range(2)
    ]
    outgoing = dot_n(maps[0] + maps[1], moe_in).astype(bf16)
    arrived = spread(outgoing.reshape(16, 32, 768), 3, "dispatch").reshape(512, 768)
    preact = dot_n(arrived, winf)
    hidden = jax.nn.gelu(preact).astype(bf16)
    result = dot_n(hidden, woutf).astype(bf16)
    returned = spread(result.reshape(16, 32, 768), 4, "results").reshape(512, 768)
    combined = [dot_l(m, returned) for m in maps]
    output = hidden_state + gate_weights[:, 0:1] * combined[0] + gate_weights[:, 1:2] * combined[1]
    error_rows = output - teacher.astype(f32)
    loss_local = jnp.sum(valid_float[:, None] * error_rows * error_rows)
    grad_out = 2.0 * tokens_all / count_all * valid_float[:, None] * error_rows
    grad_gate = jnp.stack([jnp.sum(m * grad_out, axis=1) for m in combined], axis=1)
    grad_chosen = gate_weights * (
        grad_gate - jnp.sum(gate_weights * grad_gate, axis=1, keepdims=True)
    )
    grad_logits = jnp.sum(pick * grad_chosen[:, :, None], axis=1).astype(bf16)
    grad_slots = sum(
        dot_n(maps[i], (gate_weights[:, i : i + 1] * grad_out).astype(bf16)) for i in range(2)
    ).astype(bf16)
    grad_rows = spread(grad_slots.reshape(16, 32, 768), 5, "grads_in").reshape(512, 768)
    grad_hidden = dot_t(grad_rows, woutf)
    grad_preact = gelu_grad(preact, grad_hidden).astype(bf16)
    grad_entry = dot_t(grad_preact, winf).astype(bf16)
    grad_back = spread(grad_entry.reshape(16, 32, 768), 6, "grads_out").reshape(512, 768)
    grad_out_local = dot_l(hidden, grad_rows).astype(bf16).reshape(4, 2, 384, 768)
    grad_in_local = dot_l(arrived, grad_preact).astype(bf16).reshape(4, 2, 96, 3072)

    grad_moe_in = dot_l(maps[0] + maps[1], grad_back) + dot_t(grad_logits, router_full)
    grad_hidden_norm, grad_gain_second = norm_back(
        hidden_state, factor_two, gain_second, grad_moe_in
    )
    grad_state = grad_out + grad_hidden_norm
    grad_state_low = grad_state.astype(bf16)
    dout = dot_t(grad_state_low, attn_full).astype(bf16)
    dout_s = columns(dout.reshape(128, 4, 192).transpose(1, 0, 2), 7, "grads_heads")

    grad_attn_w = dot_l(attn_low, grad_state_low)
    grad_router = dot_l(moe_in, grad_logits)
    grad_rest = jnp.concatenate(
        [grad_attn_w, grad_router, grad_gain_second[:, None], jnp.zeros((768, 111), f32)], axis=1
    ).reshape(4, 4, 2, 24, 896)

    dq, dk, dv, db = pl.pallas_call(
        attend_back_kernel,
        out_shape=[
            sds((4, 128, 192)),
            sds((4, 2, 128, 192), f32),
            sds((4, 2, 128, 192), f32),
            sds((3, ROLL), f32),
        ],
        in_specs=[VM] * 5,
        out_specs=[VM] * 4,
        scratch_shapes=[
            pltpu.VMEM((1024, 192), f32),
            pltpu.VMEM((1024, 192), f32),
            pltpu.VMEM((3, 128, GW), f32),
        ],
        compiler_params=pltpu.CompilerParams(vmem_limit_bytes=50 << 20),
        name="attend_back",
    )(q, kf, vf, bias, dout_s)

    def mine(a, axis):
        return lax.dynamic_index_in_dim(a, c, axis, keepdims=False)

    def theirs(a, axis):
        return lax.dynamic_index_in_dim(a, 1 - c, axis, keepdims=False).astype(bf16)

    dk_in, dv_in, rest_in, gin_in, gout_in = swap(
        [
            theirs(dk, 1),
            theirs(dv, 1),
            theirs(grad_rest, 2),
            theirs(grad_in_local, 1),
            theirs(grad_out_local, 1),
        ],
        8,
        "core_swap",
    )
    dk_own = (mine(dk, 1) + dk_in.astype(f32)).astype(bf16)
    dv_own = (mine(dv, 1) + dv_in.astype(f32)).astype(bf16)
    rest_own = (mine(grad_rest, 2) + rest_in.astype(f32)).astype(bf16)
    gin_own = (mine(grad_in_local, 1).astype(f32) + gin_in.astype(f32)).astype(bf16)
    gout_own = (mine(grad_out_local, 1).astype(f32) + gout_in.astype(f32)).astype(bf16)

    dqkv = jnp.concatenate([dq, dk_own, dv_own], axis=2).reshape(512, 576)
    dn1_part = dot_t(dqkv, wqf)
    gain_part = jnp.sum(dn1_part * inputs_s * factor_s, axis=0)
    dn1_all = columns(dn1_part.astype(bf16).reshape(4, 128, 768), 9, "grads_tokens")
    grad_qkv = dot_l(n1s, dqkv).reshape(4, 4, 2, 24, 576)
    (qkv_in,) = swap([theirs(grad_qkv, 2)], 10, "core_swap_qkv")
    qkv_own = (mine(grad_qkv, 2) + qkv_in.astype(f32)).astype(bf16)
    weights = jnp.concatenate([qkv_own, rest_own], axis=3)
    weights = weights.transpose(1, 0, 2, 3).reshape(16, 24, 1472)
    shards = spread(weights, 11, "grads_owner").astype(f32).reshape(4, 4, 24, 1472)
    grad_w_qkv = jnp.sum(shards[:, :, :, :576], axis=1)
    grad_w_qkv = grad_w_qkv.reshape(4, 24, 3, 192).transpose(1, 2, 0, 3).reshape(24, 2304)
    rest = jnp.sum(shards[:, :, :, 576:], axis=(0, 1))
    grad_w_attn = rest[:, :768]
    grad_w_router = rest[:, 768:784]
    grad_gain_moe = rest[:, 784]

    oin, oout = comm_call(
        owners_kernel,
        [sds((2, 2, 96, 3072)), sds((2, 2, 384, 768))],
        2,
        12,
        [
            pltpu.SemaphoreType.DMA((2, 4)),
            pltpu.SemaphoreType.DMA((2, 2, 2)),
            pltpu.SemaphoreType.DMA((2,)),
        ],
        "grads_experts",
    )(gin_own, gout_own)

    dn1 = jnp.sum(dn1_all.astype(f32), axis=0)
    _, factor_one = normalize(inputs, gain_first)
    grad_in_norm, _ = norm_back(inputs, factor_one, gain_first, dn1)
    grad_tokens = grad_state + grad_in_norm

    distance_sums = db[:, 1:1025][:, ::-1]
    table_part = jnp.einsum("ht,bt->hb", distance_sums, one_hot, precision=HIGH)
    small = jnp.zeros((16, 128), f32)
    small = small.at[:6].set(gain_part.reshape(6, 128))
    small = small.at[6:9, :32].set(table_part)
    small = small.at[9, 0].set(loss_local)
    small_all = comm_call(
        share_kernel,
        [sds((32, 16, 128), f32)],
        1,
        13,
        [
            pltpu.SemaphoreType.DMA((31,)),
            pltpu.SemaphoreType.DMA((31,)),
            pltpu.SemaphoreType.DMA,
        ],
        "share_small",
    )(small)[0]
    small_sum = jnp.sum(small_all, axis=0)
    grad_gain_attn = lax.dynamic_slice_in_dim(small_sum[:6].reshape(768), (d * 8 + s) * 24, 24, 0)
    loss = small_sum[9, 0] / (count_all * 768)
    by_z = jnp.sum(small_all.reshape(4, 4, 2, 16, 128)[:, :, :, 6:9, :32], axis=(0, 2))
    grad_table = by_z.reshape(12, 32).T
    return (
        output,
        loss,
        grad_tokens,
        grad_w_qkv,
        grad_w_attn,
        grad_gain_attn,
        grad_gain_moe,
        grad_w_router,
        grad_table,
        oin.reshape(2, 192, 3072).astype(f32),
        oout.reshape(2, 768, 768).astype(f32),
    )


def choose(*arrays):
    tokens, w_in, rel_bias, buckets = arrays[0], arrays[7], arrays[6], arrays[12]
    fits = (
        lax.axis_size("dp") == 4
        and lax.axis_size("seq") == 8
        and tokens.shape == (128, 768)
        and w_in.shape == (2, 192, 3072)
        and rel_bias.shape == (32, 12)
        and buckets.shape == (1024,)
    )
    return fast_path(*arrays) if fits else on_device(*arrays)


def solution(mesh):
    in_specs = (
        P(("dp", "seq"), None),
        P(("dp", "seq"), None),
        P(("dp", "seq"), None),
        P(("dp", "seq")),
        P(("dp", "seq")),
        P(("dp", "seq"), None),
        P(),
        P("seq", "dp", None),
        P("seq", "dp", None),
        P(("dp", "seq"), None),
        P(("dp", "seq"), None),
        P(("dp", "seq")),
        P(),
    )
    out_specs = (
        P(("dp", "seq"), None),
        P(),
        P(("dp", "seq"), None),
        P(("dp", "seq"), None),
        P(("dp", "seq"), None),
        P(("dp", "seq")),
        P(("dp", "seq")),
        P(("dp", "seq"), None),
        P(),
        P("seq", "dp", None),
        P("seq", "dp", None),
    )
    return jax.shard_map(
        choose, mesh=mesh, in_specs=in_specs, out_specs=out_specs, check_vma=False
    )
```

```python
import functools

import jax
import jax.numpy as jnp
from jax import lax
from jax.experimental import pallas as pl
from jax.experimental.pallas import tpu as pltpu
from jax.sharding import PartitionSpec as P

H = 12
HEAD = 64
BUCKETS = 32


EPS = 1e-06
NEG = -1e30
SECTION = 512
HIGH = lax.Precision.HIGHEST
FLOAT_TYPE = jnp.float32
HALF_TYPE = jnp.bfloat16


def normalize(values, gain):
    factor = lax.rsqrt(jnp.mean(values * values, axis=-1, keepdims=True) + EPS)
    return (values * factor * gain, factor)


def norm_back(values, factor, gain, grad_norm):
    scaled = grad_norm * gain
    mean_term = jnp.mean(scaled * values, axis=-1, keepdims=True)
    grad_values = factor * scaled - values * (factor * factor * factor) * mean_term
    return (grad_values, jnp.sum(grad_norm * values * factor, axis=0))


def gelu_grad(preact, grad_hidden):
    _, gelu_back = jax.vjp(jax.nn.gelu, preact)
    return gelu_back(grad_hidden)[0]


def in_sections(advance, running, shards):
    row_count = shards[0].shape[0]
    sections = row_count // SECTION
    stacked = tuple((member.reshape((sections, SECTION) + member.shape[1:]) for member in shards))

    def one_section(inner_state, entry_pair):
        return (advance(inner_state, entry_pair[1], entry_pair[0] * SECTION), None)

    final_state, _ = lax.scan(
        one_section, running, (jnp.arange(sections, dtype=jnp.int32), stacked)
    )
    return final_state


def score_block(queries, key_rows, query_start, key_start, rel_bias, edges):
    query_count = queries.shape[0]
    key_count = key_rows.shape[0]
    distance = (query_start + jnp.arange(query_count, dtype=jnp.int32))[:, None] - (
        key_start + jnp.arange(key_count, dtype=jnp.int32)
    )[None, :]
    allowed = distance >= 0
    bucket_hot = (
        (distance[:, :, None] >= edges[None, None, :-1])
        & (distance[:, :, None] < edges[None, None, 1:])
    ).astype(FLOAT_TYPE)
    bias_term = jnp.einsum("qkb,bh->hqk", bucket_hot, rel_bias, precision=HIGH)
    raw_scores = (
        jnp.einsum("qhd,khd->hqk", queries, key_rows, preferred_element_type=FLOAT_TYPE)
        * queries.shape[2] ** (-0.5)
        + bias_term
    )
    return (raw_scores, allowed, bucket_hot)


def split_three(values):
    upper = lax.optimization_barrier(values.astype(HALF_TYPE))
    remainder = values - upper.astype(FLOAT_TYPE)
    middle = lax.optimization_barrier(remainder.astype(HALF_TYPE))
    bottom = (remainder - middle.astype(FLOAT_TYPE)).astype(HALF_TYPE)
    return jnp.stack([upper, middle, bottom], axis=1)


def join_three(packed):
    as_float = packed.astype(FLOAT_TYPE)
    return as_float[:, 0] + as_float[:, 1] + as_float[:, 2]


def on_device(
    tokens,
    w_qkv,
    w_attn_out,
    gain_attn,
    gain_moe,
    w_router,
    rel_bias,
    w_in,
    w_out,
    teacher,
    routes,
    valid,
    buckets,
):
    tok_rows = tokens.shape[0]
    width = tokens.shape[1]
    seq_count = lax.axis_size("seq")
    my_start = lax.axis_index("seq") * tok_rows
    local_experts = w_in.shape[0]
    experts_all = local_experts * seq_count
    capacity = 4 * tok_rows // experts_all
    slot_rows = seq_count * capacity
    scale = HEAD ** (-0.5)
    qkv_full, attn_full, router_full, gain_one, gain_two, valid_all = (
        lax.all_gather(w_qkv, ("dp", "seq"), axis=0, tiled=True),
        lax.all_gather(w_attn_out, ("dp", "seq"), axis=0, tiled=True),
        lax.all_gather(w_router, ("dp", "seq"), axis=0, tiled=True),
        lax.all_gather(gain_attn, ("dp", "seq"), axis=0, tiled=True),
        lax.all_gather(gain_moe, ("dp", "seq"), axis=0, tiled=True),
        lax.all_gather(valid.astype(HALF_TYPE), ("dp", "seq"), axis=0, tiled=True),
    )
    valid_float = valid.astype(FLOAT_TYPE)
    count_all = jnp.sum(valid_all.astype(FLOAT_TYPE))
    tokens_all = tok_rows * lax.axis_size("dp") * seq_count
    edges = jnp.sum(
        (buckets[None, :] < jnp.arange(BUCKETS + 1, dtype=jnp.int32)[:, None]).astype(jnp.int32),
        axis=1,
    )
    inputs = tokens.astype(FLOAT_TYPE)
    gain_first = gain_one.astype(FLOAT_TYPE)
    gain_second = gain_two.astype(FLOAT_TYPE)
    normed_one, factor_one = normalize(inputs, gain_first)
    normed_in = normed_one.astype(HALF_TYPE)
    qkv_rows = jnp.dot(normed_in, qkv_full, preferred_element_type=FLOAT_TYPE)
    query_low = qkv_rows[:, :width].astype(HALF_TYPE)
    key_low = qkv_rows[:, width : 2 * width].astype(HALF_TYPE)
    value_low = qkv_rows[:, 2 * width :].astype(HALF_TYPE)
    heads_q = query_low.reshape(tok_rows, H, HEAD)
    heads_k = key_low.reshape(tok_rows, H, HEAD)
    heads_v = value_low.reshape(tok_rows, H, HEAD)
    last_row = my_start + tok_rows - 1

    def forward_step(running, shards, offset):
        key_rows = shards[0].reshape(shards[0].shape[0], H, HEAD)
        value_rows = shards[1].reshape(shards[1].shape[0], H, HEAD)

        def work(inner_state):
            maximum, denom, mixture = inner_state
            raw_scores, allowed, _ = score_block(
                heads_q, key_rows, my_start, offset, rel_bias, edges
            )
            masked = jnp.where(allowed[None], raw_scores, NEG)
            new_max = jnp.maximum(maximum, jnp.max(masked, axis=2))
            weights = jnp.where(allowed[None], jnp.exp(masked - new_max[:, :, None]), 0.0)
            rescale = jnp.exp(maximum - new_max)
            addend = jnp.einsum(
                "hqk,khd->hqd",
                weights.astype(HALF_TYPE),
                value_rows,
                preferred_element_type=FLOAT_TYPE,
            )
            return (
                new_max,
                denom * rescale + jnp.sum(weights, axis=2),
                mixture * rescale[:, :, None] + addend,
            )

        return lax.cond(offset <= last_row, work, lambda inner_state: inner_state, running)

    start_state = (
        jnp.full((H, tok_rows), NEG, FLOAT_TYPE),
        jnp.zeros((H, tok_rows), FLOAT_TYPE),
        jnp.zeros((H, tok_rows, HEAD), FLOAT_TYPE),
    )
    maximum, denom, mixture = in_sections(
        forward_step,
        start_state,
        (
            lax.all_gather(key_low, "seq", axis=0, tiled=True),
            lax.all_gather(value_low, "seq", axis=0, tiled=True),
        ),
    )
    log_total = maximum + jnp.log(denom)
    attn_heads = mixture / denom[:, :, None]
    attn_rows = jnp.transpose(attn_heads, (1, 0, 2)).reshape(tok_rows, width)
    attn_low = attn_rows.astype(HALF_TYPE)
    hidden_state = inputs + jnp.dot(attn_low, attn_full, preferred_element_type=FLOAT_TYPE)
    normed_two, factor_two = normalize(hidden_state, gain_second)
    moe_in = normed_two.astype(HALF_TYPE)
    logits = jnp.dot(moe_in, router_full, preferred_element_type=FLOAT_TYPE)
    chosen = jnp.take_along_axis(logits, routes, axis=1)
    gate_weights = jax.nn.softmax(chosen, axis=1)
    flat_routes = routes.reshape(-1)
    matches = (flat_routes[:, None] == jnp.arange(experts_all, dtype=jnp.int32)[None, :]).astype(
        jnp.int32
    )
    slot_index = jnp.sum((jnp.cumsum(matches, axis=0) - matches) * matches, axis=1)
    target_dev = flat_routes // local_experts
    target_local = flat_routes % local_experts
    position = (target_dev * capacity + slot_index) * local_experts + target_local
    dispatch_map = (
        jnp.arange(experts_all * capacity, dtype=jnp.int32)[:, None] == position[None, :]
    ).astype(HALF_TYPE)
    dispatch_map = dispatch_map.reshape(experts_all * capacity, tok_rows, 2)
    outgoing = jnp.einsum(
        "prk,rd->pd", dispatch_map, moe_in, preferred_element_type=FLOAT_TYPE
    ).astype(HALF_TYPE)
    arrived = lax.all_to_all(
        outgoing.reshape(seq_count, capacity * local_experts, width),
        "seq",
        split_axis=0,
        concat_axis=0,
        tiled=True,
    )
    arrived_rows = arrived.reshape(slot_rows, local_experts, width)
    in_full, out_full = (
        lax.all_gather(w_in, "dp", axis=1, tiled=True),
        lax.all_gather(w_out, "dp", axis=1, tiled=True),
    )
    preact = jnp.einsum("mld,ldf->mlf", arrived_rows, in_full, preferred_element_type=FLOAT_TYPE)
    hidden = jax.nn.gelu(preact).astype(HALF_TYPE)
    result = jnp.einsum("mlf,lfd->mld", hidden, out_full, preferred_element_type=FLOAT_TYPE).astype(
        HALF_TYPE
    )
    returned = lax.all_to_all(
        result.reshape(seq_count, capacity * local_experts, width),
        "seq",
        split_axis=0,
        concat_axis=0,
        tiled=True,
    )
    returned = returned.reshape(experts_all * capacity, width)
    combined = jnp.einsum("prk,pd->krd", dispatch_map, returned, preferred_element_type=FLOAT_TYPE)
    output = hidden_state + gate_weights[:, 0:1] * combined[0] + gate_weights[:, 1:2] * combined[1]
    error_rows = output - teacher.astype(FLOAT_TYPE)
    loss_local = jnp.sum(valid_float[:, None] * error_rows * error_rows)
    grad_out = 2.0 * tokens_all / count_all * valid_float[:, None] * error_rows
    grad_gate = jnp.einsum("krd,rd->rk", combined, grad_out)
    grad_chosen = gate_weights * (
        grad_gate - jnp.sum(gate_weights * grad_gate, axis=1, keepdims=True)
    )
    pick = (routes[:, :, None] == jnp.arange(experts_all, dtype=jnp.int32)[None, None, :]).astype(
        FLOAT_TYPE
    )
    grad_logits = jnp.sum(pick * grad_chosen[:, :, None], axis=1).astype(HALF_TYPE)
    grad_router = jnp.einsum("rd,re->de", moe_in, grad_logits, preferred_element_type=FLOAT_TYPE)
    grad_result = (jnp.transpose(gate_weights)[:, :, None] * grad_out[None]).astype(HALF_TYPE)
    grad_slots = jnp.einsum(
        "prk,krd->pd", dispatch_map, grad_result, preferred_element_type=FLOAT_TYPE
    ).astype(HALF_TYPE)
    grad_arrived = lax.all_to_all(
        grad_slots.reshape(seq_count, capacity * local_experts, width),
        "seq",
        split_axis=0,
        concat_axis=0,
        tiled=True,
    )
    grad_rows = grad_arrived.reshape(slot_rows, local_experts, width)
    grad_hidden = jnp.einsum("mld,lfd->mlf", grad_rows, out_full, preferred_element_type=FLOAT_TYPE)
    grad_preact = gelu_grad(preact, grad_hidden).astype(HALF_TYPE)
    grad_out_local = jnp.einsum(
        "mlf,mld->lfd", hidden, grad_rows, preferred_element_type=FLOAT_TYPE
    )
    grad_in_local = jnp.einsum(
        "mld,mlf->ldf", arrived_rows, grad_preact, preferred_element_type=FLOAT_TYPE
    )
    grad_entry = jnp.einsum(
        "mlf,ldf->mld", grad_preact, in_full, preferred_element_type=FLOAT_TYPE
    ).astype(HALF_TYPE)
    grad_w_in, grad_w_out = (
        lax.psum_scatter(
            grad_in_local.astype(jnp.bfloat16), "dp", scatter_dimension=1, tiled=True
        ).astype(jnp.float32),
        lax.psum_scatter(
            grad_out_local.astype(jnp.bfloat16), "dp", scatter_dimension=1, tiled=True
        ).astype(jnp.float32),
    )
    grad_back = lax.all_to_all(
        grad_entry.reshape(seq_count, capacity * local_experts, width),
        "seq",
        split_axis=0,
        concat_axis=0,
        tiled=True,
    )
    grad_back = grad_back.reshape(experts_all * capacity, width)
    grad_moe_in = jnp.einsum(
        "prk,pd->rd", dispatch_map, grad_back, preferred_element_type=FLOAT_TYPE
    )
    grad_moe_in = grad_moe_in + jnp.einsum(
        "re,de->rd", grad_logits, router_full, preferred_element_type=FLOAT_TYPE
    )
    grad_hidden_norm, grad_gain_second = norm_back(
        hidden_state, factor_two, gain_second, grad_moe_in
    )
    grad_state = grad_out + grad_hidden_norm
    grad_state_low = grad_state.astype(HALF_TYPE)
    grad_attn_w = jnp.einsum(
        "rd,re->de", attn_low, grad_state_low, preferred_element_type=FLOAT_TYPE
    )
    grad_attn_low = jnp.einsum(
        "re,de->rd", grad_state_low, attn_full, preferred_element_type=FLOAT_TYPE
    ).astype(HALF_TYPE)
    heads_dout = grad_attn_low.reshape(tok_rows, H, HEAD)
    softmax_dot = jnp.sum(
        jnp.transpose(heads_dout, (1, 0, 2)).astype(FLOAT_TYPE) * attn_heads, axis=2
    )
    row_stats = split_three(
        jnp.stack([jnp.transpose(log_total), jnp.transpose(softmax_dot)], axis=1)
    )

    def backward_step(running, shards, offset):
        key_rows = shards[0].reshape(shards[0].shape[0], H, HEAD)
        value_rows = shards[1].reshape(shards[1].shape[0], H, HEAD)
        query_rows = shards[2].reshape(shards[2].shape[0], H, HEAD)
        dout_rows = shards[3].reshape(shards[3].shape[0], H, HEAD)
        stats_rows = join_three(shards[4])
        piece_total = jnp.transpose(stats_rows[:, 0, :])
        piece_dot = jnp.transpose(stats_rows[:, 1, :])
        grad_query, grad_table, grad_key, grad_value = running

        def query_work(inner_state):
            inner_query, inner_table = inner_state
            raw_scores, allowed, bucket_hot = score_block(
                heads_q, key_rows, my_start, offset, rel_bias, edges
            )
            weights = jnp.where(allowed[None], jnp.exp(raw_scores - log_total[:, :, None]), 0.0)
            grad_prob = jnp.einsum(
                "qhd,khd->hqk", heads_dout, value_rows, preferred_element_type=FLOAT_TYPE
            )
            grad_score = (weights * (grad_prob - softmax_dot[:, :, None])).astype(HALF_TYPE)
            inner_query = (
                inner_query
                + jnp.einsum(
                    "hqk,khd->hqd", grad_score, key_rows, preferred_element_type=FLOAT_TYPE
                )
                * scale
            )
            inner_table = inner_table + jnp.einsum(
                "hqk,qkb->bh", grad_score.astype(FLOAT_TYPE), bucket_hot, precision=HIGH
            )
            return (inner_query, inner_table)

        def key_work(inner_state):
            inner_key, inner_value = inner_state
            raw_scores, allowed, _ = score_block(
                query_rows, heads_k, offset, my_start, rel_bias, edges
            )
            weights = jnp.where(allowed[None], jnp.exp(raw_scores - piece_total[:, :, None]), 0.0)
            inner_value = inner_value + jnp.einsum(
                "hqk,qhd->khd",
                weights.astype(HALF_TYPE),
                dout_rows,
                preferred_element_type=FLOAT_TYPE,
            )
            grad_prob = jnp.einsum(
                "qhd,khd->hqk", dout_rows, heads_v, preferred_element_type=FLOAT_TYPE
            )
            grad_score = (weights * (grad_prob - piece_dot[:, :, None])).astype(HALF_TYPE)
            inner_key = (
                inner_key
                + jnp.einsum(
                    "hqk,qhd->khd", grad_score, query_rows, preferred_element_type=FLOAT_TYPE
                )
                * scale
            )
            return (inner_key, inner_value)

        grad_query, grad_table = lax.cond(
            offset <= last_row,
            query_work,
            lambda inner_state: inner_state,
            (grad_query, grad_table),
        )
        grad_key, grad_value = lax.cond(
            offset + shards[0].shape[0] - 1 >= my_start,
            key_work,
            lambda inner_state: inner_state,
            (grad_key, grad_value),
        )
        return (grad_query, grad_table, grad_key, grad_value)

    back_start = (
        jnp.zeros((H, tok_rows, HEAD), FLOAT_TYPE),
        jnp.zeros((BUCKETS, H), FLOAT_TYPE),
        jnp.zeros((tok_rows, H, HEAD), FLOAT_TYPE),
        jnp.zeros((tok_rows, H, HEAD), FLOAT_TYPE),
    )
    grad_query, grad_table_local, grad_key, grad_value = in_sections(
        backward_step,
        back_start,
        (
            lax.all_gather(key_low, "seq", axis=0, tiled=True),
            lax.all_gather(value_low, "seq", axis=0, tiled=True),
            lax.all_gather(query_low, "seq", axis=0, tiled=True),
            lax.all_gather(grad_attn_low, "seq", axis=0, tiled=True),
            lax.all_gather(row_stats, "seq", axis=0, tiled=True),
        ),
    )
    grad_qkv_low = jnp.concatenate(
        [
            jnp.transpose(grad_query, (1, 0, 2)).reshape(tok_rows, width),
            grad_key.reshape(tok_rows, width),
            grad_value.reshape(tok_rows, width),
        ],
        axis=1,
    ).astype(HALF_TYPE)
    grad_qkv_w = jnp.einsum("rd,re->de", normed_in, grad_qkv_low, preferred_element_type=FLOAT_TYPE)
    grad_normed_one = jnp.einsum(
        "re,de->rd", grad_qkv_low, qkv_full, preferred_element_type=FLOAT_TYPE
    )
    grad_in_norm, grad_gain_first = norm_back(inputs, factor_one, gain_first, grad_normed_one)
    grad_tokens = grad_state + grad_in_norm
    grad_qkv_own, grad_attn_own, grad_router_own, grad_gain_attn, grad_gain_moe = (
        lax.psum_scatter(grad_qkv_w, ("dp", "seq"), scatter_dimension=0, tiled=True),
        lax.psum_scatter(grad_attn_w, ("dp", "seq"), scatter_dimension=0, tiled=True),
        lax.psum_scatter(grad_router, ("dp", "seq"), scatter_dimension=0, tiled=True),
        lax.psum_scatter(grad_gain_first, ("dp", "seq"), scatter_dimension=0, tiled=True),
        lax.psum_scatter(grad_gain_second, ("dp", "seq"), scatter_dimension=0, tiled=True),
    )
    loss_sum, grad_table = lax.psum((loss_local, grad_table_local), ("dp", "seq"))
    loss = loss_sum / (count_all * width)
    return (
        output,
        loss,
        grad_tokens,
        grad_qkv_own,
        grad_attn_own,
        grad_gain_attn,
        grad_gain_moe,
        grad_router_own,
        grad_table,
        grad_w_in,
        grad_w_out,
    )


MESH = pl.DeviceIdType.MESH
ANY = pl.BlockSpec(memory_space=pl.ANY)
VM = pl.BlockSpec(memory_space=pltpu.VMEM)
ROLL = 1280
GW = 1152


def remote(src, dst, send, recv, dev):
    return pltpu.make_async_remote_copy(
        src_ref=src, dst_ref=dst, send_sem=send, recv_sem=recv, device_id=dev, device_id_type=MESH
    )


def place():
    d = lax.axis_index("dp")
    s = lax.axis_index("seq")
    return d, s, s // 2, lax.rem(s, 2)


def greet(peers):
    barrier = pltpu.get_barrier_semaphore()
    for peer in peers:
        pl.semaphore_signal(barrier, inc=1, device_id=peer, device_id_type=MESH)
    pl.semaphore_wait(barrier, len(peers))


def comm_call(body, outs, n_in, cid, scratch, name, in_specs=None, out_specs=None, vmem=None):
    return pl.pallas_call(
        body,
        out_shape=outs,
        in_specs=in_specs or [ANY] * n_in,
        out_specs=out_specs or [ANY] * len(outs),
        scratch_shapes=scratch,
        compiler_params=pltpu.CompilerParams(
            collective_id=cid, has_side_effects=True, vmem_limit_bytes=vmem
        ),
        name=name,
    )


def sds(shape, dtype=jnp.bfloat16):
    return jax.ShapeDtypeStruct(shape, dtype)


def gather_kernel(x, wq, wr, win, wout, xs, wqf, wrf, winf, woutf, ss, rs, xe, re, ls):
    d, s, z, c = place()
    sib = (d, s + 1 - 2 * c)
    plane = [(lax.rem(d + k, 4), s) for k in (1, 2, 3)]
    plane_other = [(lax.rem(d + k, 4), s + 1 - 2 * c) for k in (1, 2, 3)]
    zs = [(d, 2 * lax.rem(z + k, 4) + c) for k in (1, 2, 3)]
    greet(plane + plane_other + zs + [sib])
    local = [
        pltpu.make_async_copy(wq.at[z], wqf.at[d, z, c], ls.at[0]),
        pltpu.make_async_copy(wr, wrf.at[d, z, c], ls.at[1]),
        pltpu.make_async_copy(x, xs.at[z], ls.at[2]),
    ]
    for cp in local:
        cp.start()
    stage1 = []
    for i, k in enumerate((1, 2, 3)):
        zt = lax.rem(z + k, 4)
        stage1.append(remote(wq.at[zt], wqf.at[d, z, c], ss.at[i], rs.at[i], zs[i]))
        stage1.append(remote(wr, wrf.at[d, z, c], ss.at[3 + i], rs.at[3 + i], zs[i]))
    for cp in stage1:
        cp.start()
    stage_x = []
    for i in range(3):
        cp = remote(x, xs.at[z], ss.at[6 + i], rs.at[6 + i], zs[i])
        cp.start()
        stage_x.append(cp)
    for m, (src, dst) in enumerate(((win, winf), (wout, woutf))):
        for k in (1, 2, 3):
            j = lax.rem(d + k, 4)

            @pl.when(j // 2 == c)
            def _(src=src, dst=dst, m=m, k=k, j=j):
                for half in range(2):
                    remote(
                        src.at[lax.rem(j, 2), half],
                        dst.at[d, half],
                        xe.at[m, k, half],
                        re.at[m, k],
                        (j, 2 * z + half),
                    ).start()

        @pl.when(d // 2 == c)
        def _(src=src, dst=dst, m=m):
            mine = src.at[lax.rem(d, 2)]
            pltpu.make_async_copy(mine, dst.at[d], ls.at[3 + m]).start()
            remote(mine, dst.at[d], xe.at[m, 0, 0], re.at[m, 4], sib).start()

    for cp in local:
        cp.wait()
    for cp in stage1:
        cp.wait_recv()
    stage2 = []
    for i, k in enumerate((1, 2, 3)):
        stage2.append(
            remote(wqf.at[d, :, c], wqf.at[d, :, c], ss.at[9 + i], rs.at[9 + i], plane[i])
        )
        stage2.append(
            remote(wrf.at[d, :, c], wrf.at[d, :, c], ss.at[12 + i], rs.at[12 + i], plane[i])
        )
    for cp in stage2:
        cp.start()
    stage3 = []

    def forward(array, dd, i):
        cp = remote(array.at[dd, :, c], array.at[dd, :, c], ss.at[i], rs.at[i], sib)
        cp.start()
        stage3.append(cp)

    forward(wqf, d, 15)
    forward(wrf, d, 16)
    for i, k in enumerate((1, 2, 3)):
        dd = lax.rem(d + 4 - k, 4)
        stage2[2 * i].wait_recv()
        forward(wqf, dd, 17 + 2 * i)
        stage2[2 * i + 1].wait_recv()
        forward(wrf, dd, 18 + 2 * i)
    for cp in stage_x:
        cp.wait_recv()
    for cp in stage3:
        cp.wait_recv()
    passed = []
    for m, (src, dst) in enumerate(((win, winf), (wout, woutf))):
        for k in (1, 2, 3):
            dd = lax.rem(d + 4 - k, 4)
            cp = remote(dst.at[dd, c], dst.at[dd, c], xe.at[m, k, 2], re.at[m, 4 + k], sib)
            remote(dst.at[dd, c], dst.at[dd, c], xe.at[m, k, 2], re.at[m, k], sib).wait_recv()
            cp.start()
            passed.append(cp)
    for cp in passed:
        cp.wait_recv()
    for m, (src, dst) in enumerate(((win, winf), (wout, woutf))):

        @pl.when(d // 2 == c)
        def _(src=src, dst=dst, m=m):
            mine = src.at[lax.rem(d, 2)]
            pltpu.make_async_copy(mine, dst.at[d], ls.at[3 + m]).wait()
            remote(mine, dst.at[d], xe.at[m, 0, 0], re.at[m, 4], sib).wait_send()

        @pl.when(d // 2 != c)
        def _(src=src, dst=dst, m=m):
            mine = src.at[lax.rem(d, 2)]
            remote(mine, dst.at[d], xe.at[m, 0, 0], re.at[m, 4], sib).wait_recv()

        for k in (1, 2, 3):
            j = lax.rem(d + k, 4)

            @pl.when(j // 2 == c)
            def _(src=src, dst=dst, m=m, k=k, j=j):
                for half in range(2):
                    remote(
                        src.at[lax.rem(j, 2), half],
                        dst.at[d, half],
                        xe.at[m, k, half],
                        re.at[m, k],
                        (j, 2 * z + half),
                    ).wait_send()

    for cp in stage1 + stage_x + stage2 + stage3 + passed:
        cp.wait_send()


def head_mask(h):
    lane = lax.broadcasted_iota(jnp.int32, (1, 192), 1)
    return lane // HEAD == h


def bias_kernel(e_ref, g_ref):
    for h in range(3):
        row = jnp.broadcast_to(e_ref[h : h + 1, :], (128, ROLL))
        g_ref[h] = pltpu.roll(row, 0, 1, stride=1, stride_axis=0)[:, 128:]


def dot_t(a, b):
    return lax.dot_general(a, b, (((1,), (1,)), ((), ())), preferred_element_type=jnp.float32)


def dot_l(a, b):
    return lax.dot_general(a, b, (((0,), (0,)), ((), ())), preferred_element_type=jnp.float32)


def dot_n(a, b):
    return jnp.dot(a, b, preferred_element_type=jnp.float32)


def soft_rows(q, keys, g_ref, h, start, width):
    s = dot_t(q, keys) * HEAD ** (-0.5) + g_ref[h, :, pl.ds(start, width)]
    m = jnp.max(s, axis=1, keepdims=True)
    p = jnp.exp(s - m)
    return p / jnp.sum(p, axis=1, keepdims=True)


def attend_kernel(q, k, v, g, attn, kf, vf, out, ss, rs):
    d, s, z, c = place()
    sib = (d, s + 1 - 2 * c)
    zs = [(d, 2 * lax.rem(z + i, 4) + c) for i in (1, 2, 3)]
    greet(zs + [sib])
    kf[:, pl.ds(c, 1)] = k[...][:, None]
    vf[:, pl.ds(c, 1)] = v[...][:, None]
    swap = [
        remote(k, kf.at[:, c], ss.at[4], rs.at[4], sib),
        remote(v, vf.at[:, c], ss.at[5], rs.at[5], sib),
    ]
    for cp in swap:
        cp.start()
    for cp in swap:
        cp.wait_recv()
    for zb in (3, 2, 1, 0):
        width = 256 * (zb + 1)
        start = pl.multiple_of(128 * (7 - 2 * zb) - 128 * c, 128)
        keys = kf[: zb + 1].reshape(width, 192)
        values = vf[: zb + 1].reshape(width, 192)
        acc = jnp.zeros((128, 192), jnp.float32)
        for h in range(3):
            qh = jnp.where(head_mask(h), q[zb], jnp.zeros((), jnp.bfloat16))
            p = soft_rows(qh, keys, g, h, start, width).astype(jnp.bfloat16)
            acc = acc + jnp.where(head_mask(h), dot_n(p, values), 0.0)
        out[zb] = acc.astype(jnp.bfloat16)

        @pl.when(z != zb)
        def _(zb=zb):
            remote(out.at[zb], attn.at[z], ss.at[zb], rs.at[z], (d, 2 * zb + c)).start()

        @pl.when(z == zb)
        def _(zb=zb):
            attn[pl.ds(z, 1)] = out[zb][None]

    for zb in range(4):

        @pl.when(z != zb)
        def _(zb=zb):
            cp = remote(out.at[zb], attn.at[zb], ss.at[zb], rs.at[zb], (d, 2 * zb + c))
            cp.wait_send()
            cp.wait_recv()

    for cp in swap:
        cp.wait_send()


def attend_back_kernel(q, k, v, g, do, dq, dk, dv, db, kacc, vacc, gacc):
    c = lax.rem(lax.axis_index("seq"), 2)
    kacc[...] = jnp.zeros_like(kacc)
    vacc[...] = jnp.zeros_like(vacc)
    gacc[...] = jnp.zeros_like(gacc)
    for zb in (3, 2, 1, 0):
        width = 256 * (zb + 1)
        start = pl.multiple_of(128 * (7 - 2 * zb) - 128 * c, 128)
        keys = k[: zb + 1].reshape(width, 192)
        values = v[: zb + 1].reshape(width, 192)
        acc = jnp.zeros((128, 192), jnp.float32)
        for h in range(3):
            mask = head_mask(h)
            qh = jnp.where(mask, q[zb], jnp.zeros((), jnp.bfloat16))
            doh = jnp.where(mask, do[zb], jnp.zeros((), jnp.bfloat16))
            p = soft_rows(qh, keys, g, h, start, width)
            vacc[:width] += dot_l(p.astype(jnp.bfloat16), doh)
            dp = dot_t(doh, values)
            dot = jnp.sum(p * dp, axis=1, keepdims=True)
            ds = (p * (dp - dot)).astype(jnp.bfloat16)
            gacc[h, :, pl.ds(start, width)] += ds.astype(jnp.float32)
            acc = acc + jnp.where(mask, dot_n(ds, keys), 0.0)
            kacc[:width] += dot_l(ds, qh)
        dq[zb] = (acc * HEAD ** (-0.5)).astype(jnp.bfloat16)
    dk[...] = (kacc[...] * HEAD ** (-0.5)).reshape(4, 2, 128, 192)
    dv[...] = vacc[...].reshape(4, 2, 128, 192)
    row = lax.broadcasted_iota(jnp.int32, (128, 1), 0)
    for h in range(3):
        y = jnp.concatenate([jnp.zeros((128, ROLL - GW), jnp.float32), gacc[h]], axis=1)
        for bit in range(7):
            y = jnp.where((row >> bit) & 1 == 1, pltpu.roll(y, ROLL - (1 << bit), 1), y)
        db[h : h + 1, :] = jnp.sum(y, axis=0, keepdims=True)


class Sems:
    def __init__(self, send, recv):
        self.send, self.recv, self.n = send, recv, 0

    def copy(self, src, dst, dev):
        cp = remote(src, dst, self.send.at[self.n], self.recv.at[self.n], dev)
        self.n += 1
        return cp


def run(copies):
    for cp in copies:
        cp.start()
    return copies


def received(copies):
    for cp in copies:
        cp.wait_recv()


def sent(copies):
    for cp in copies:
        cp.wait_send()


def chips():
    d, s, z, c = place()
    me = z * 4 + d
    numbers = [lax.rem(me + k, 16) for k in range(1, 16)]
    return me, numbers, [(lax.rem(t, 4), 2 * (t // 4) + c) for t in numbers]


def rms(v):
    return lax.rsqrt(jnp.mean(v * v, axis=1, keepdims=True) + EPS)


def forward_kernel(
    x,
    wq,
    wr,
    line,
    routes,
    win,
    wout,
    arrived,
    win_a,
    win_b,
    wout_a,
    wout_b,
    wqf,
    wrf,
    xs,
    n1s,
    q,
    kf,
    vf,
    bias,
    attn,
    h_out,
    n2_out,
    pos_out,
    gate_out,
    gains_out,
    out_v,
    going,
    ss,
    rs,
    xe,
    re,
    ls,
):
    d, s, z, c = place()
    sib = (d, s + 1 - 2 * c)
    across = (d + 1 - 2 * lax.rem(d, 2), lax.rem(d + 2, 4), 3 - d)
    plane = [(j, s) for j in across]
    plane_other = [(j, s + 1 - 2 * c) for j in across]
    zs = [(d, 2 * lax.rem(z + k, 4) + c) for k in (1, 2, 3)]
    me, numbers, others = chips()
    greet(others + plane_other + [sib])
    sems = Sems(ss, rs)

    def rows_of(ref, dd, zz, cc):
        return ref.at[pl.ds(pl.multiple_of(((dd * 4 + zz) * 2 + cc) * 24, 8), 24)]

    def column_rows(ref, dd, dev):
        copies = []
        for zz in range(4):
            part = rows_of(ref, dd, zz, c)
            copies.append(sems.copy(part, part, dev))
        return run(copies)

    local = [
        pltpu.make_async_copy(wq.at[z], rows_of(wqf, d, z, c), ls.at[0]),
        pltpu.make_async_copy(wr, rows_of(wrf, d, z, c), ls.at[1]),
        pltpu.make_async_copy(x, xs.at[z], ls.at[2]),
    ]
    run(local)
    stage1 = run(
        [
            sems.copy(wq.at[lax.rem(z + k, 4)], rows_of(wqf, d, z, c), zs[i])
            for i, k in enumerate((1, 2, 3))
        ]
    )
    bulk = []

    def expert_send(m, i, half):
        src, dst = ((win, win_a), (wout, wout_a))[m]
        j = across[i]

        def make():
            return remote(
                src.at[lax.rem(j, 2), half],
                dst.at[d],
                xe.at[m, i, half],
                re.at[m, i],
                (j, 2 * z + half),
            )

        @pl.when(j // 2 == c)
        def _():
            make().start()

        bulk.append((j // 2 == c, make))

    def expert_own(m):
        src, dst = ((win, win_a), (wout, wout_a))[m]

        def make():
            return remote(
                src.at[lax.rem(d, 2), 1 - c], dst.at[d], xe.at[m, 3, 0], re.at[m, 3], sib
            )

        @pl.when(d // 2 == c)
        def _():
            pltpu.make_async_copy(src.at[lax.rem(d, 2), c], dst.at[d], ls.at[3 + m]).start()
            make().start()

        bulk.append((d // 2 == c, make))

    def expert_pass(m, i):
        src, half, other = ((win, win_a, win_b), (wout, wout_a, wout_b))[m]
        if i < 3:
            dd = across[i]
            remote(half.at[dd], half.at[dd], xe.at[m, i, 0], re.at[m, i], sib).wait_recv()
        else:
            dd = d

            @pl.when(d // 2 == c)
            def _():
                pltpu.make_async_copy(src.at[lax.rem(d, 2), c], half.at[d], ls.at[3 + m]).wait()

            @pl.when(d // 2 != c)
            def _():
                remote(half.at[d], half.at[d], xe.at[m, 3, 0], re.at[m, 3], sib).wait_recv()

        passed.extend(run([sems.copy(half.at[dd], other.at[dd], sib)]))

    passed = []
    expert_send(0, 0, 0)
    expert_send(0, 1, 0)
    rest1 = run([sems.copy(wr, rows_of(wrf, d, z, c), zs[i]) for i in range(3)])
    rows = run([sems.copy(x, xs.at[z], zs[i]) for i in range(3)])
    for h in range(3):
        row = jnp.broadcast_to(line[h : h + 1, :], (128, ROLL))
        bias[h] = pltpu.roll(row, 0, 1, stride=1, stride_axis=0)[:, 128:]
    for cp in local:
        cp.wait()
    received(stage1)
    stage2 = [column_rows(wqf, d, dev) for dev in plane]
    stage3 = column_rows(wqf, d, sib)
    received(rest1)
    rest2 = [column_rows(wrf, d, dev) for dev in plane]
    rest3 = column_rows(wrf, d, sib)
    for i, k in ((0, 1), (1, 1), (2, 0), (2, 1)):
        expert_send(0, i, k)
    expert_own(0)
    expert_own(1)
    for i, dd in enumerate(across):
        received(stage2[i])
        stage3 += column_rows(wqf, dd, sib)
    received(stage3)
    misc = jnp.transpose(wqf[:, 576:704].astype(jnp.float32))
    gains_out[...] = misc[16:24]
    gain_first = misc[16:17]
    gain_second = misc[17:18]

    pairs = []
    for i in range(4):
        zb = lax.rem(z + 4 - i, 4)
        if i > 0:
            rows[i - 1].wait_recv()
        xf = xs[zb].astype(jnp.float32)
        n1 = (xf * rms(xf) * gain_first).astype(jnp.bfloat16)
        n1s[zb] = n1
        qkv = dot_n(n1, wqf[:, :576]).astype(jnp.bfloat16)
        q[zb] = qkv[:, :192]
        kf[zb, c] = qkv[:, 192:384]
        vf[zb, c] = qkv[:, 384:]
        pairs += run(
            [
                sems.copy(kf.at[zb, c], kf.at[zb, c], sib),
                sems.copy(vf.at[zb, c], vf.at[zb, c], sib),
            ]
        )
    for i, dd in enumerate(across):
        received(rest2[i])
        rest3 += column_rows(wrf, dd, sib)
    expert_send(1, 0, 0)
    expert_send(1, 1, 0)
    received(pairs)
    first = sems.n
    sems.n += 4
    for zb in (3, 2, 1, 0):
        width = 256 * (zb + 1)
        start = pl.multiple_of(128 * (7 - 2 * zb) - 128 * c, 128)
        keys = kf[: zb + 1].reshape(width, 192)
        values = vf[: zb + 1].reshape(width, 192)
        acc = jnp.zeros((128, 192), jnp.float32)
        for h in range(3):
            qh = jnp.where(head_mask(h), q[zb], jnp.zeros((), jnp.bfloat16))
            p = soft_rows(qh, keys, bias, h, start, width).astype(jnp.bfloat16)
            acc = acc + jnp.where(head_mask(h), dot_n(p, values), 0.0)
        out_v[zb] = acc.astype(jnp.bfloat16)

        @pl.when(z != zb)
        def _(zb=zb):
            remote(
                out_v.at[zb], attn.at[z], ss.at[first + zb], rs.at[first + z], (d, 2 * zb + c)
            ).start()

        @pl.when(z == zb)
        def _(zb=zb):
            attn[zb] = out_v[zb]

    received(rest3)
    for zb in range(4):

        @pl.when(z != zb)
        def _(zb=zb):
            remote(
                out_v.at[zb], attn.at[zb], ss.at[first + zb], rs.at[first + zb], (d, 2 * zb + c)
            ).wait()

    hidden = x[...].astype(jnp.float32)
    for zb in range(4):
        hidden = hidden + dot_n(attn[zb], wrf[192 * zb : 192 * (zb + 1), :])
    h_out[...] = hidden
    n2 = (hidden * rms(hidden) * gain_second).astype(jnp.bfloat16)
    n2_out[...] = n2
    logits = dot_n(n2, wqf[:, 576:704])
    lane = lax.broadcasted_iota(jnp.int32, (128, 128), 1)
    picks = [(lane == routes[:, i : i + 1]).astype(jnp.float32) for i in range(2)]
    chosen = [jnp.sum(jnp.where(lane == routes[:, i : i + 1], logits, 0.0), axis=1, keepdims=True) for i in range(2)]
    top = jnp.maximum(chosen[0], chosen[1])
    powers = [jnp.exp(v - top) for v in chosen]
    gates = [v / (powers[0] + powers[1]) for v in powers]
    lower = (lax.broadcasted_iota(jnp.int32, (128, 128), 0) > lane).astype(jnp.bfloat16)
    before = dot_n(lower, (picks[0] + picks[1]).astype(jnp.bfloat16))
    wide = lax.broadcasted_iota(jnp.int32, (128, 512), 1)
    chart = jnp.zeros((128, 512), jnp.float32)
    for i in range(2):
        slot = jnp.sum(picks[i] * before, axis=1, keepdims=True).astype(jnp.int32)
        position = routes[:, i : i + 1] * 32 + slot
        pos_out[:, i : i + 1] = position
        gate_out[:, i : i + 1] = gates[i]
        chart = chart + (wide == position).astype(jnp.float32)
    going[...] = dot_l(chart.astype(jnp.bfloat16), n2).astype(jnp.bfloat16).reshape(16, 32, 768)
    out = run([sems.copy(going.at[t], arrived.at[me], dev) for t, dev in zip(numbers, others)])
    own = pltpu.make_async_copy(going.at[me], arrived.at[me], ls.at[7])
    own.start()

    for i, k in ((0, 1), (1, 1), (2, 0), (2, 1)):
        expert_send(1, i, k)
    for m in range(2):
        for i in (3, 0, 1, 2):
            expert_pass(m, i)
    received(out)
    received(passed)
    own.wait()
    sent(stage1 + rows + rest1 + stage3 + pairs + rest3 + out + passed + sum(stage2 + rest2, []))
    for held, make in bulk:

        @pl.when(held)
        def _(make=make):
            make().wait_send()


CHUNK = 768
GELU_A = 0.7978845608028654
GELU_B = 0.044715


def experts_kernel(
    arrived,
    h,
    position,
    gates,
    routes,
    teacher,
    valid,
    gains,
    win_a,
    win_b,
    wout_a,
    wout_b,
    grad_back,
    output,
    grad_out,
    grad_logits,
    loss,
    gin_sum,
    gout_sum,
    win,
    wout,
    slope,
    hid,
    acc,
    leave,
    back,
    gback,
    din,
    dout,
    gin_in,
    gout_in,
    ss,
    rs,
    ls,
):
    f32, bf16 = jnp.float32, jnp.bfloat16
    d, s, z, c = place()
    sib = (d, s + 1 - 2 * c)
    me, numbers, others = chips()
    loads = []
    for j in range(4):
        for half, (a, b) in enumerate(((win_a, wout_a), (win_b, wout_b))):
            core = c if half == 0 else 1 - c
            r_in = pl.multiple_of(j * 192 + core * 96, 32)
            r_out = pl.multiple_of(j * 768 + core * 384, 128)
            loads.append(pltpu.make_async_copy(a.at[j], win.at[pl.ds(r_in, 96)], ls.at[0, j, half]))
            loads.append(
                pltpu.make_async_copy(b.at[j], wout.at[pl.ds(r_out, 384)], ls.at[1, j, half])
            )
    run(loads)
    greet(others + [sib])
    sems = Sems(ss, rs)

    def spread_rows(src, dst):
        copies = run([sems.copy(src.at[t], dst.at[me], dev) for t, dev in zip(numbers, others)])
        dst[pl.ds(me, 1)] = src[pl.ds(me, 1)]
        return copies

    rows_in = arrived[...].reshape(512, 768)
    for cp in loads:
        cp.wait()
    acc[...] = jnp.zeros_like(acc)

    def forward_step(f, carry):
        at = pl.multiple_of(f * CHUNK, CHUNK)
        for r in (0, 256):
            pre = dot_n(arrived[r // 32 : r // 32 + 8].reshape(256, 768), win[:, pl.ds(at, CHUNK)])
            t = jnp.tanh(GELU_A * (pre + GELU_B * pre * pre * pre))
            half = 0.5 * (1.0 + t)
            hd = (pre * half).astype(bf16)
            slope[r : r + 256, pl.ds(at, CHUNK)] = half + 0.5 * pre * (1.0 - t * t) * (
                GELU_A * (1.0 + 3.0 * GELU_B * pre * pre)
            )
            hid[r : r + 256, pl.ds(at, CHUNK)] = hd
            acc[r : r + 256] += dot_n(hd, wout[pl.ds(at, CHUNK), :])
        return carry

    lax.fori_loop(0, 4, forward_step, 0)
    leave[...] = acc[...].astype(bf16).reshape(16, 32, 768)
    results = spread_rows(leave, back)
    count = jnp.sum(gains[2:3, :], axis=1, keepdims=True) / 24.0
    wide = lax.broadcasted_iota(jnp.int32, (128, 512), 1)
    maps = [(wide == position[:, i : i + 1]).astype(f32).astype(bf16) for i in range(2)]
    received(results)
    sent(results)
    combined = [dot_n(m, back[...].reshape(512, 768)) for m in maps]
    gate = [gates[:, i : i + 1] for i in range(2)]
    out = h[...] + gate[0] * combined[0] + gate[1] * combined[1]
    output[...] = out
    error = out - teacher[...].astype(f32)
    masked = valid[...] * error
    loss[...] = jnp.broadcast_to(jnp.sum(masked * error, keepdims=True), (8, 128))
    gout = (2.0 * 4096.0) / count * masked
    grad_out[...] = gout
    leave[...] = (
        (
            dot_l(maps[0], (gate[0] * gout).astype(bf16))
            + dot_l(maps[1], (gate[1] * gout).astype(bf16))
        )
        .astype(bf16)
        .reshape(16, 32, 768)
    )
    grads = spread_rows(leave, gback)
    dgate = [jnp.sum(m * gout, axis=1, keepdims=True) for m in combined]
    mean = gate[0] * dgate[0] + gate[1] * dgate[1]
    lane = lax.broadcasted_iota(jnp.int32, (128, 128), 1)
    total = jnp.zeros((128, 128), f32)
    for i in range(2):
        total = total + jnp.where(lane == routes[:, i : i + 1], gate[i] * (dgate[i] - mean), 0.0)
    grad_logits[...] = total.astype(bf16)
    received(grads)
    sent(grads)
    acc[...] = jnp.zeros_like(acc)

    def backward_step(f, carry):
        at = pl.multiple_of(f * CHUNK, CHUNK)
        for r in (0, 256):
            dh = dot_t(gback[r // 32 : r // 32 + 8].reshape(256, 768), wout[pl.ds(at, CHUNK), :])
            dp = (dh * slope[r : r + 256, pl.ds(at, CHUNK)]).astype(bf16)
            slope[r : r + 256, pl.ds(at, CHUNK)] = dp.astype(f32)
            acc[r : r + 256] += dot_t(dp, win[:, pl.ds(at, CHUNK)])
        return carry

    lax.fori_loop(0, 4, backward_step, 0)
    leave[...] = acc[...].astype(bf16).reshape(16, 32, 768)
    entries = run([sems.copy(leave.at[t], grad_back.at[me], dev) for t, dev in zip(numbers, others)])
    own = pltpu.make_async_copy(leave.at[me], grad_back.at[me], ls.at[2, 0, 0])
    own.start()

    def weights_step(f, carry):
        at = pl.multiple_of(f * CHUNK, CHUNK)
        rows = gback[...].reshape(512, 768)
        dout[f] = dot_l(hid[:, pl.ds(at, CHUNK)], rows).astype(bf16).reshape(2, 384, 768)
        remote(
            dout.at[f, 1 - c], gout_in.at[f], ss.at[50 + f], rs.at[50 + f], sib
        ).start()
        dp = slope[:, pl.ds(at, CHUNK)].astype(bf16)
        din[:, :, :, pl.ds(at, CHUNK)] = (
            dot_l(rows_in, dp).astype(bf16).reshape(4, 2, 96, CHUNK)
        )
        return carry

    lax.fori_loop(0, 4, weights_step, 0)
    inner = remote(din.at[:, 1 - c], gin_in, ss.at[54], rs.at[54], sib)
    inner.start()
    for f in range(4):
        remote(dout.at[f, 1 - c], gout_in.at[f], ss.at[50 + f], rs.at[50 + f], sib).wait()
        gout_in[f] = (dout[f, c].astype(f32) + gout_in[f].astype(f32)).astype(bf16)
    stores = run([pltpu.make_async_copy(gout_in, gout_sum, ls.at[2, 1, 0])])
    inner.wait()
    for j in range(4):
        gin_in[j] = (din[j, c].astype(f32) + gin_in[j].astype(f32)).astype(bf16)
    stores += run([pltpu.make_async_copy(gin_in, gin_sum, ls.at[2, 2, 0])])
    received(entries)
    sent(entries)
    own.wait()
    for cp in stores:
        cp.wait()


def spread_kernel(src, dst, ss, rs, ls):
    d, s, z, c = place()
    me = z * 4 + d
    peers = []
    for k in range(1, 16):
        t = lax.rem(me + k, 16)
        peers.append((lax.rem(t, 4), 2 * (t // 4) + c))
    greet(peers)
    own = pltpu.make_async_copy(src.at[me], dst.at[me], ls)
    own.start()
    sent = []
    for k in range(1, 16):
        t = lax.rem(me + k, 16)
        cp = remote(src.at[t], dst.at[me], ss.at[k - 1], rs.at[k - 1], peers[k - 1])
        cp.start()
        sent.append(cp)
    for cp in sent:
        cp.wait()
    own.wait()


def spread(x, cid, name):
    return comm_call(
        spread_kernel,
        [sds(x.shape, x.dtype)],
        1,
        cid,
        [
            pltpu.SemaphoreType.DMA((15,)),
            pltpu.SemaphoreType.DMA((15,)),
            pltpu.SemaphoreType.DMA,
        ],
        name,
    )(x)[0]


def columns_kernel(src, dst, ss, rs, ls):
    d, s, z, c = place()
    peers = [(d, 2 * lax.rem(z + k, 4) + c) for k in (1, 2, 3)]
    greet(peers)
    own = pltpu.make_async_copy(src.at[z], dst.at[z], ls)
    own.start()
    sent = []
    for i, k in enumerate((1, 2, 3)):
        t = lax.rem(z + k, 4)
        cp = remote(src.at[t], dst.at[z], ss.at[i], rs.at[i], peers[i])
        cp.start()
        sent.append(cp)
    for cp in sent:
        cp.wait()
    own.wait()


def columns(x, cid, name):
    return comm_call(
        columns_kernel,
        [sds(x.shape, x.dtype)],
        1,
        cid,
        [pltpu.SemaphoreType.DMA((3,)), pltpu.SemaphoreType.DMA((3,)), pltpu.SemaphoreType.DMA],
        name,
    )(x)[0]


def swap_kernel(n, *refs):
    ins, outs, ss, rs = refs[:n], refs[n : 2 * n], refs[2 * n], refs[2 * n + 1]
    d, s, z, c = place()
    sib = (d, s + 1 - 2 * c)
    greet([sib])
    sent = [remote(a, b, ss.at[i], rs.at[i], sib) for i, (a, b) in enumerate(zip(ins, outs))]
    for cp in sent:
        cp.start()
    for cp in sent:
        cp.wait()


def swap(arrays, cid, name):
    n = len(arrays)
    return comm_call(
        functools.partial(swap_kernel, n),
        [sds(a.shape, a.dtype) for a in arrays],
        n,
        cid,
        [pltpu.SemaphoreType.DMA((n,)), pltpu.SemaphoreType.DMA((n,))],
        name,
    )(*arrays)


def owners_kernel(gin, gout, oin, oout, ss, rs, ls):
    d, s, z, c = place()
    peers = []
    for k in (1, 2, 3):
        for core in range(2):
            peers.append((lax.rem(d + k, 4), 2 * z + core))
    peers.append((d, s + 1 - 2 * c))
    greet(peers)
    pairs = ((gin, oin), (gout, oout))
    sent = []
    for m, (src, dst) in enumerate(pairs):
        for i, k in enumerate((1, 2, 3)):
            dd = lax.rem(d + k, 4)
            cp = remote(
                src.at[dd],
                dst.at[lax.rem(d, 2), c],
                ss.at[m, i],
                rs.at[m, lax.rem(d, 2), c],
                (dd, 2 * z + d // 2),
            )
            cp.start()
            sent.append(cp)

        @pl.when(d // 2 == c)
        def _(src=src, dst=dst, m=m):
            pltpu.make_async_copy(src.at[d], dst.at[lax.rem(d, 2), c], ls.at[m]).start()

        @pl.when(d // 2 != c)
        def _(src=src, dst=dst, m=m):
            remote(
                src.at[d],
                dst.at[lax.rem(d, 2), c],
                ss.at[m, 3],
                rs.at[m, lax.rem(d, 2), c],
                (d, s + 1 - 2 * c),
            ).start()

    for m, (src, dst) in enumerate(pairs):
        for l in range(2):
            for half in range(2):
                here = (2 * c + l == d) & (c == half)

                @pl.when(jnp.logical_not(here))
                def _(src=src, dst=dst, m=m, l=l, half=half):
                    remote(
                        src.at[0], dst.at[l, half], ss.at[m, 0], rs.at[m, l, half], peers[0]
                    ).wait_recv()

        @pl.when(d // 2 == c)
        def _(src=src, dst=dst, m=m):
            pltpu.make_async_copy(src.at[d], dst.at[lax.rem(d, 2), c], ls.at[m]).wait()

        @pl.when(d // 2 != c)
        def _(src=src, dst=dst, m=m):
            remote(
                src.at[d],
                dst.at[lax.rem(d, 2), c],
                ss.at[m, 3],
                rs.at[m, lax.rem(d, 2), c],
                (d, s + 1 - 2 * c),
            ).wait_send()

    for cp in sent:
        cp.wait_send()


def share_kernel(src, dst, ss, rs, ls):
    d, s, z, c = place()
    peers = []
    for k in range(1, 32):
        peers.append((lax.rem(d + k // 8, 4), lax.rem(s + lax.rem(k, 8), 8)))
    greet(peers)
    me = d * 8 + s
    own = pltpu.make_async_copy(src, dst.at[me], ls)
    own.start()
    sent = []
    for k in range(1, 32):
        cp = remote(src, dst.at[me], ss.at[k - 1], rs.at[k - 1], peers[k - 1])
        cp.start()
        sent.append(cp)
    for cp in sent:
        cp.wait()
    own.wait()


def fast_path(
    tokens,
    w_qkv,
    w_attn_out,
    gain_attn,
    gain_moe,
    w_router,
    rel_bias,
    w_in,
    w_out,
    teacher,
    routes,
    valid,
    buckets,
):
    f32, bf16 = jnp.float32, jnp.bfloat16
    d = lax.axis_index("dp")
    s = lax.axis_index("seq")
    z, c = s // 2, s % 2
    wq = w_qkv.reshape(24, 3, 4, 192).transpose(2, 0, 1, 3).reshape(4, 24, 576)
    valid_float = valid.astype(f32)
    misc = jnp.concatenate(
        [
            w_router,
            gain_attn[:, None],
            gain_moe[:, None],
            jnp.full((24, 1), jnp.sum(valid_float)).astype(bf16),
            jnp.zeros((24, 109), bf16),
        ],
        axis=1,
    )
    wq = jnp.concatenate([wq, jnp.broadcast_to(misc[None], (4, 24, 128))], axis=2)
    one_hot = (buckets[None, :] == jnp.arange(BUCKETS, dtype=jnp.int32)[:, None]).astype(f32)
    my_bias = lax.dynamic_slice_in_dim(rel_bias, 3 * z, 3, 1)
    table = jnp.einsum("bh,bt->ht", my_bias, one_hot, precision=HIGH)
    line = jnp.concatenate(
        [
            jnp.full((3, 1), NEG, f32),
            table[:, ::-1],
            jnp.full((3, ROLL - 1025), NEG, f32),
        ],
        axis=1,
    )
    (
        arrived,
        win_a,
        win_b,
        wout_a,
        wout_b,
        wqf,
        wrf,
        xs,
        n1s,
        q,
        kf,
        vf,
        bias,
        attn,
        hidden_state,
        moe_in,
        position,
        gate_weights,
        gains,
    ) = comm_call(
        forward_kernel,
        [
            sds((16, 32, 768)),
            sds((4, 96, 3072)),
            sds((4, 96, 3072)),
            sds((4, 384, 768)),
            sds((4, 384, 768)),
            sds((768, 704)),
            sds((768, 768)),
            sds((4, 128, 768)),
            sds((4, 128, 768)),
            sds((4, 128, 192)),
            sds((4, 2, 128, 192)),
            sds((4, 2, 128, 192)),
            sds((3, 128, GW), f32),
            sds((4, 128, 192)),
            sds((128, 768), f32),
            sds((128, 768)),
            sds((128, 2), jnp.int32),
            sds((128, 2), f32),
            sds((8, 768), f32),
        ],
        7,
        1,
        [
            pltpu.VMEM((4, 128, 192), bf16),
            pltpu.VMEM((16, 32, 768), bf16),
            pltpu.SemaphoreType.DMA((120,)),
            pltpu.SemaphoreType.DMA((120,)),
            pltpu.SemaphoreType.DMA((2, 4, 2)),
            pltpu.SemaphoreType.DMA((2, 4)),
            pltpu.SemaphoreType.DMA((8,)),
        ],
        "forward",
        in_specs=[VM, ANY, ANY, VM, VM, ANY, ANY],
        out_specs=[ANY] * 5 + [VM] * 14,
        vmem=50 << 20,
    )(
        tokens,
        wq,
        w_attn_out,
        line,
        routes,
        w_in.reshape(2, 2, 96, 3072),
        w_out.reshape(2, 2, 384, 768),
    )
    router_full = wqf[:, 576:592]
    wqf = wqf[:, :576]
    attn_full = wrf
    (
        grad_back,
        output,
        grad_out,
        grad_logits,
        loss_rows,
        gin_own,
        gout_own,
    ) = comm_call(
        experts_kernel,
        [
            sds((16, 32, 768)),
            sds((128, 768), f32),
            sds((128, 768), f32),
            sds((128, 128)),
            sds((8, 128), f32),
            sds((4, 96, 3072)),
            sds((4, 384, 768)),
        ],
        12,
        2,
        [
            pltpu.VMEM((768, 3072), bf16),
            pltpu.VMEM((3072, 768), bf16),
            pltpu.VMEM((512, 3072), f32),
            pltpu.VMEM((512, 3072), bf16),
            pltpu.VMEM((512, 768), f32),
            pltpu.VMEM((16, 32, 768), bf16),
            pltpu.VMEM((16, 32, 768), bf16),
            pltpu.VMEM((16, 32, 768), bf16),
            pltpu.VMEM((4, 2, 96, 3072), bf16),
            pltpu.VMEM((4, 2, 384, 768), bf16),
            pltpu.VMEM((4, 96, 3072), bf16),
            pltpu.VMEM((4, 384, 768), bf16),
            pltpu.SemaphoreType.DMA((56,)),
            pltpu.SemaphoreType.DMA((56,)),
            pltpu.SemaphoreType.DMA((3, 4, 2)),
        ],
        "experts",
        in_specs=[VM] * 8 + [ANY] * 4,
        out_specs=[ANY] + [VM] * 4 + [ANY] * 2,
        vmem=60 << 20,
    )(
        arrived,
        hidden_state,
        position,
        gate_weights,
        routes,
        teacher,
        valid_float[:, None],
        gains,
        win_a,
        win_b,
        wout_a,
        wout_b,
    )
    loss_local = loss_rows[0, 0]
    grad_logits = grad_logits[:, :16]
    grad_back = grad_back.reshape(512, 768)
    gain_first, gain_second = gains[0], gains[1]
    count_all = jnp.sum(gains[2]) / 24.0
    tokens_all = 4096.0
    inputs_s = xs.reshape(512, 768).astype(f32)
    factor_s = lax.rsqrt(jnp.mean(inputs_s * inputs_s, axis=-1, keepdims=True) + EPS)
    n1s = n1s.reshape(512, 768)
    attn_low = attn.transpose(1, 0, 2).reshape(128, 768)
    inputs = tokens.astype(f32)
    _, factor_two = normalize(hidden_state, gain_second)
    maps = [
        (jnp.arange(512, dtype=jnp.int32)[:, None] == position[None, :, i]).astype(bf16)
        for i in range(2)
    ]
    grad_moe_in = dot_l(maps[0] + maps[1], grad_back) + dot_t(grad_logits, router_full)
    grad_hidden_norm, grad_gain_second = norm_back(
        hidden_state, factor_two, gain_second, grad_moe_in
    )
    grad_state = grad_out + grad_hidden_norm
    grad_state_low = grad_state.astype(bf16)
    dout = dot_t(grad_state_low, attn_full).astype(bf16)
    dout_s = columns(dout.reshape(128, 4, 192).transpose(1, 0, 2), 7, "grads_heads")

    grad_attn_w = dot_l(attn_low, grad_state_low)
    grad_router = dot_l(moe_in, grad_logits)
    grad_rest = jnp.concatenate(
        [grad_attn_w, grad_router, grad_gain_second[:, None], jnp.zeros((768, 111), f32)], axis=1
    ).reshape(4, 4, 2, 24, 896)

    dq, dk, dv, db = pl.pallas_call(
        attend_back_kernel,
        out_shape=[
            sds((4, 128, 192)),
            sds((4, 2, 128, 192), f32),
            sds((4, 2, 128, 192), f32),
            sds((3, ROLL), f32),
        ],
        in_specs=[VM] * 5,
        out_specs=[VM] * 4,
        scratch_shapes=[
            pltpu.VMEM((1024, 192), f32),
            pltpu.VMEM((1024, 192), f32),
            pltpu.VMEM((3, 128, GW), f32),
        ],
        compiler_params=pltpu.CompilerParams(vmem_limit_bytes=50 << 20),
        name="attend_back",
    )(q, kf, vf, bias, dout_s)

    def mine(a, axis):
        return lax.dynamic_index_in_dim(a, c, axis, keepdims=False)

    def theirs(a, axis):
        return lax.dynamic_index_in_dim(a, 1 - c, axis, keepdims=False).astype(bf16)

    dk_in, dv_in, rest_in = swap(
        [
            theirs(dk, 1),
            theirs(dv, 1),
            theirs(grad_rest, 2),
        ],
        8,
        "core_swap",
    )
    dk_own = (mine(dk, 1) + dk_in.astype(f32)).astype(bf16)
    dv_own = (mine(dv, 1) + dv_in.astype(f32)).astype(bf16)
    rest_own = (mine(grad_rest, 2) + rest_in.astype(f32)).astype(bf16)
    dqkv = jnp.concatenate([dq, dk_own, dv_own], axis=2).reshape(512, 576)
    dn1_part = dot_t(dqkv, wqf)
    gain_part = jnp.sum(dn1_part * inputs_s * factor_s, axis=0)
    dn1_all = columns(dn1_part.astype(bf16).reshape(4, 128, 768), 9, "grads_tokens")
    grad_qkv = dot_l(n1s, dqkv).reshape(4, 4, 2, 24, 576)
    (qkv_in,) = swap([theirs(grad_qkv, 2)], 10, "core_swap_qkv")
    qkv_own = (mine(grad_qkv, 2) + qkv_in.astype(f32)).astype(bf16)
    weights = jnp.concatenate([qkv_own, rest_own], axis=3)
    weights = weights.transpose(1, 0, 2, 3).reshape(16, 24, 1472)
    shards = spread(weights, 11, "grads_owner").astype(f32).reshape(4, 4, 24, 1472)
    grad_w_qkv = jnp.sum(shards[:, :, :, :576], axis=1)
    grad_w_qkv = grad_w_qkv.reshape(4, 24, 3, 192).transpose(1, 2, 0, 3).reshape(24, 2304)
    rest = jnp.sum(shards[:, :, :, 576:], axis=(0, 1))
    grad_w_attn = rest[:, :768]
    grad_w_router = rest[:, 768:784]
    grad_gain_moe = rest[:, 784]

    oin, oout = comm_call(
        owners_kernel,
        [sds((2, 2, 96, 3072)), sds((2, 2, 384, 768))],
        2,
        12,
        [
            pltpu.SemaphoreType.DMA((2, 4)),
            pltpu.SemaphoreType.DMA((2, 2, 2)),
            pltpu.SemaphoreType.DMA((2,)),
        ],
        "grads_experts",
    )(gin_own, gout_own)

    dn1 = jnp.sum(dn1_all.astype(f32), axis=0)
    _, factor_one = normalize(inputs, gain_first)
    grad_in_norm, _ = norm_back(inputs, factor_one, gain_first, dn1)
    grad_tokens = grad_state + grad_in_norm

    distance_sums = db[:, 1:1025][:, ::-1]
    table_part = jnp.einsum("ht,bt->hb", distance_sums, one_hot, precision=HIGH)
    small = jnp.zeros((16, 128), f32)
    small = small.at[:6].set(gain_part.reshape(6, 128))
    small = small.at[6:9, :32].set(table_part)
    small = small.at[9, 0].set(loss_local)
    small_all = comm_call(
        share_kernel,
        [sds((32, 16, 128), f32)],
        1,
        13,
        [
            pltpu.SemaphoreType.DMA((31,)),
            pltpu.SemaphoreType.DMA((31,)),
            pltpu.SemaphoreType.DMA,
        ],
        "share_small",
    )(small)[0]
    small_sum = jnp.sum(small_all, axis=0)
    grad_gain_attn = lax.dynamic_slice_in_dim(small_sum[:6].reshape(768), (d * 8 + s) * 24, 24, 0)
    loss = small_sum[9, 0] / (count_all * 768)
    by_z = jnp.sum(small_all.reshape(4, 4, 2, 16, 128)[:, :, :, 6:9, :32], axis=(0, 2))
    grad_table = by_z.reshape(12, 32).T
    return (
        output,
        loss,
        grad_tokens,
        grad_w_qkv,
        grad_w_attn,
        grad_gain_attn,
        grad_gain_moe,
        grad_w_router,
        grad_table,
        oin.reshape(2, 192, 3072).astype(f32),
        oout.reshape(2, 768, 768).astype(f32),
    )


def choose(*arrays):
    tokens, w_in, rel_bias, buckets = arrays[0], arrays[7], arrays[6], arrays[12]
    fits = (
        lax.axis_size("dp") == 4
        and lax.axis_size("seq") == 8
        and tokens.shape == (128, 768)
        and w_in.shape == (2, 192, 3072)
        and rel_bias.shape == (32, 12)
        and buckets.shape == (1024,)
    )
    return fast_path(*arrays) if fits else on_device(*arrays)


def solution(mesh):
    in_specs = (
        P(("dp", "seq"), None),
        P(("dp", "seq"), None),
        P(("dp", "seq"), None),
        P(("dp", "seq")),
        P(("dp", "seq")),
        P(("dp", "seq"), None),
        P(),
        P("seq", "dp", None),
        P("seq", "dp", None),
        P(("dp", "seq"), None),
        P(("dp", "seq"), None),
        P(("dp", "seq")),
        P(),
    )
    out_specs = (
        P(("dp", "seq"), None),
        P(),
        P(("dp", "seq"), None),
        P(("dp", "seq"), None),
        P(("dp", "seq"), None),
        P(("dp", "seq")),
        P(("dp", "seq")),
        P(("dp", "seq"), None),
        P(),
        P("seq", "dp", None),
        P("seq", "dp", None),
    )
    return jax.shard_map(
        choose, mesh=mesh, in_specs=in_specs, out_specs=out_specs, check_vma=False
    )
```

```python
import functools

import jax
import jax.numpy as jnp
from jax import lax
from jax.experimental import pallas as pl
from jax.experimental.pallas import tpu as pltpu
from jax.sharding import PartitionSpec as P

H = 12
HEAD = 64
BUCKETS = 32


EPS = 1e-06
NEG = -1e30
SECTION = 512
HIGH = lax.Precision.HIGHEST
FLOAT_TYPE = jnp.float32
HALF_TYPE = jnp.bfloat16


def normalize(values, gain):
    factor = lax.rsqrt(jnp.mean(values * values, axis=-1, keepdims=True) + EPS)
    return (values * factor * gain, factor)


def norm_back(values, factor, gain, grad_norm):
    scaled = grad_norm * gain
    mean_term = jnp.mean(scaled * values, axis=-1, keepdims=True)
    grad_values = factor * scaled - values * (factor * factor * factor) * mean_term
    return (grad_values, jnp.sum(grad_norm * values * factor, axis=0))


def gelu_grad(preact, grad_hidden):
    _, gelu_back = jax.vjp(jax.nn.gelu, preact)
    return gelu_back(grad_hidden)[0]


def in_sections(advance, running, shards):
    row_count = shards[0].shape[0]
    sections = row_count // SECTION
    stacked = tuple((member.reshape((sections, SECTION) + member.shape[1:]) for member in shards))

    def one_section(inner_state, entry_pair):
        return (advance(inner_state, entry_pair[1], entry_pair[0] * SECTION), None)

    final_state, _ = lax.scan(
        one_section, running, (jnp.arange(sections, dtype=jnp.int32), stacked)
    )
    return final_state


def score_block(queries, key_rows, query_start, key_start, rel_bias, edges):
    query_count = queries.shape[0]
    key_count = key_rows.shape[0]
    distance = (query_start + jnp.arange(query_count, dtype=jnp.int32))[:, None] - (
        key_start + jnp.arange(key_count, dtype=jnp.int32)
    )[None, :]
    allowed = distance >= 0
    bucket_hot = (
        (distance[:, :, None] >= edges[None, None, :-1])
        & (distance[:, :, None] < edges[None, None, 1:])
    ).astype(FLOAT_TYPE)
    bias_term = jnp.einsum("qkb,bh->hqk", bucket_hot, rel_bias, precision=HIGH)
    raw_scores = (
        jnp.einsum("qhd,khd->hqk", queries, key_rows, preferred_element_type=FLOAT_TYPE)
        * queries.shape[2] ** (-0.5)
        + bias_term
    )
    return (raw_scores, allowed, bucket_hot)


def split_three(values):
    upper = lax.optimization_barrier(values.astype(HALF_TYPE))
    remainder = values - upper.astype(FLOAT_TYPE)
    middle = lax.optimization_barrier(remainder.astype(HALF_TYPE))
    bottom = (remainder - middle.astype(FLOAT_TYPE)).astype(HALF_TYPE)
    return jnp.stack([upper, middle, bottom], axis=1)


def join_three(packed):
    as_float = packed.astype(FLOAT_TYPE)
    return as_float[:, 0] + as_float[:, 1] + as_float[:, 2]


def on_device(
    tokens,
    w_qkv,
    w_attn_out,
    gain_attn,
    gain_moe,
    w_router,
    rel_bias,
    w_in,
    w_out,
    teacher,
    routes,
    valid,
    buckets,
):
    tok_rows = tokens.shape[0]
    width = tokens.shape[1]
    seq_count = lax.axis_size("seq")
    my_start = lax.axis_index("seq") * tok_rows
    local_experts = w_in.shape[0]
    experts_all = local_experts * seq_count
    capacity = 4 * tok_rows // experts_all
    slot_rows = seq_count * capacity
    scale = HEAD ** (-0.5)
    qkv_full, attn_full, router_full, gain_one, gain_two, valid_all = (
        lax.all_gather(w_qkv, ("dp", "seq"), axis=0, tiled=True),
        lax.all_gather(w_attn_out, ("dp", "seq"), axis=0, tiled=True),
        lax.all_gather(w_router, ("dp", "seq"), axis=0, tiled=True),
        lax.all_gather(gain_attn, ("dp", "seq"), axis=0, tiled=True),
        lax.all_gather(gain_moe, ("dp", "seq"), axis=0, tiled=True),
        lax.all_gather(valid.astype(HALF_TYPE), ("dp", "seq"), axis=0, tiled=True),
    )
    valid_float = valid.astype(FLOAT_TYPE)
    count_all = jnp.sum(valid_all.astype(FLOAT_TYPE))
    tokens_all = tok_rows * lax.axis_size("dp") * seq_count
    edges = jnp.sum(
        (buckets[None, :] < jnp.arange(BUCKETS + 1, dtype=jnp.int32)[:, None]).astype(jnp.int32),
        axis=1,
    )
    inputs = tokens.astype(FLOAT_TYPE)
    gain_first = gain_one.astype(FLOAT_TYPE)
    gain_second = gain_two.astype(FLOAT_TYPE)
    normed_one, factor_one = normalize(inputs, gain_first)
    normed_in = normed_one.astype(HALF_TYPE)
    qkv_rows = jnp.dot(normed_in, qkv_full, preferred_element_type=FLOAT_TYPE)
    query_low = qkv_rows[:, :width].astype(HALF_TYPE)
    key_low = qkv_rows[:, width : 2 * width].astype(HALF_TYPE)
    value_low = qkv_rows[:, 2 * width :].astype(HALF_TYPE)
    heads_q = query_low.reshape(tok_rows, H, HEAD)
    heads_k = key_low.reshape(tok_rows, H, HEAD)
    heads_v = value_low.reshape(tok_rows, H, HEAD)
    last_row = my_start + tok_rows - 1

    def forward_step(running, shards, offset):
        key_rows = shards[0].reshape(shards[0].shape[0], H, HEAD)
        value_rows = shards[1].reshape(shards[1].shape[0], H, HEAD)

        def work(inner_state):
            maximum, denom, mixture = inner_state
            raw_scores, allowed, _ = score_block(
                heads_q, key_rows, my_start, offset, rel_bias, edges
            )
            masked = jnp.where(allowed[None], raw_scores, NEG)
            new_max = jnp.maximum(maximum, jnp.max(masked, axis=2))
            weights = jnp.where(allowed[None], jnp.exp(masked - new_max[:, :, None]), 0.0)
            rescale = jnp.exp(maximum - new_max)
            addend = jnp.einsum(
                "hqk,khd->hqd",
                weights.astype(HALF_TYPE),
                value_rows,
                preferred_element_type=FLOAT_TYPE,
            )
            return (
                new_max,
                denom * rescale + jnp.sum(weights, axis=2),
                mixture * rescale[:, :, None] + addend,
            )

        return lax.cond(offset <= last_row, work, lambda inner_state: inner_state, running)

    start_state = (
        jnp.full((H, tok_rows), NEG, FLOAT_TYPE),
        jnp.zeros((H, tok_rows), FLOAT_TYPE),
        jnp.zeros((H, tok_rows, HEAD), FLOAT_TYPE),
    )
    maximum, denom, mixture = in_sections(
        forward_step,
        start_state,
        (
            lax.all_gather(key_low, "seq", axis=0, tiled=True),
            lax.all_gather(value_low, "seq", axis=0, tiled=True),
        ),
    )
    log_total = maximum + jnp.log(denom)
    attn_heads = mixture / denom[:, :, None]
    attn_rows = jnp.transpose(attn_heads, (1, 0, 2)).reshape(tok_rows, width)
    attn_low = attn_rows.astype(HALF_TYPE)
    hidden_state = inputs + jnp.dot(attn_low, attn_full, preferred_element_type=FLOAT_TYPE)
    normed_two, factor_two = normalize(hidden_state, gain_second)
    moe_in = normed_two.astype(HALF_TYPE)
    logits = jnp.dot(moe_in, router_full, preferred_element_type=FLOAT_TYPE)
    chosen = jnp.take_along_axis(logits, routes, axis=1)
    gate_weights = jax.nn.softmax(chosen, axis=1)
    flat_routes = routes.reshape(-1)
    matches = (flat_routes[:, None] == jnp.arange(experts_all, dtype=jnp.int32)[None, :]).astype(
        jnp.int32
    )
    slot_index = jnp.sum((jnp.cumsum(matches, axis=0) - matches) * matches, axis=1)
    target_dev = flat_routes // local_experts
    target_local = flat_routes % local_experts
    position = (target_dev * capacity + slot_index) * local_experts + target_local
    dispatch_map = (
        jnp.arange(experts_all * capacity, dtype=jnp.int32)[:, None] == position[None, :]
    ).astype(HALF_TYPE)
    dispatch_map = dispatch_map.reshape(experts_all * capacity, tok_rows, 2)
    outgoing = jnp.einsum(
        "prk,rd->pd", dispatch_map, moe_in, preferred_element_type=FLOAT_TYPE
    ).astype(HALF_TYPE)
    arrived = lax.all_to_all(
        outgoing.reshape(seq_count, capacity * local_experts, width),
        "seq",
        split_axis=0,
        concat_axis=0,
        tiled=True,
    )
    arrived_rows = arrived.reshape(slot_rows, local_experts, width)
    in_full, out_full = (
        lax.all_gather(w_in, "dp", axis=1, tiled=True),
        lax.all_gather(w_out, "dp", axis=1, tiled=True),
    )
    preact = jnp.einsum("mld,ldf->mlf", arrived_rows, in_full, preferred_element_type=FLOAT_TYPE)
    hidden = jax.nn.gelu(preact).astype(HALF_TYPE)
    result = jnp.einsum("mlf,lfd->mld", hidden, out_full, preferred_element_type=FLOAT_TYPE).astype(
        HALF_TYPE
    )
    returned = lax.all_to_all(
        result.reshape(seq_count, capacity * local_experts, width),
        "seq",
        split_axis=0,
        concat_axis=0,
        tiled=True,
    )
    returned = returned.reshape(experts_all * capacity, width)
    combined = jnp.einsum("prk,pd->krd", dispatch_map, returned, preferred_element_type=FLOAT_TYPE)
    output = hidden_state + gate_weights[:, 0:1] * combined[0] + gate_weights[:, 1:2] * combined[1]
    error_rows = output - teacher.astype(FLOAT_TYPE)
    loss_local = jnp.sum(valid_float[:, None] * error_rows * error_rows)
    grad_out = 2.0 * tokens_all / count_all * valid_float[:, None] * error_rows
    grad_gate = jnp.einsum("krd,rd->rk", combined, grad_out)
    grad_chosen = gate_weights * (
        grad_gate - jnp.sum(gate_weights * grad_gate, axis=1, keepdims=True)
    )
    pick = (routes[:, :, None] == jnp.arange(experts_all, dtype=jnp.int32)[None, None, :]).astype(
        FLOAT_TYPE
    )
    grad_logits = jnp.sum(pick * grad_chosen[:, :, None], axis=1).astype(HALF_TYPE)
    grad_router = jnp.einsum("rd,re->de", moe_in, grad_logits, preferred_element_type=FLOAT_TYPE)
    grad_result = (jnp.transpose(gate_weights)[:, :, None] * grad_out[None]).astype(HALF_TYPE)
    grad_slots = jnp.einsum(
        "prk,krd->pd", dispatch_map, grad_result, preferred_element_type=FLOAT_TYPE
    ).astype(HALF_TYPE)
    grad_arrived = lax.all_to_all(
        grad_slots.reshape(seq_count, capacity * local_experts, width),
        "seq",
        split_axis=0,
        concat_axis=0,
        tiled=True,
    )
    grad_rows = grad_arrived.reshape(slot_rows, local_experts, width)
    grad_hidden = jnp.einsum("mld,lfd->mlf", grad_rows, out_full, preferred_element_type=FLOAT_TYPE)
    grad_preact = gelu_grad(preact, grad_hidden).astype(HALF_TYPE)
    grad_out_local = jnp.einsum(
        "mlf,mld->lfd", hidden, grad_rows, preferred_element_type=FLOAT_TYPE
    )
    grad_in_local = jnp.einsum(
        "mld,mlf->ldf", arrived_rows, grad_preact, preferred_element_type=FLOAT_TYPE
    )
    grad_entry = jnp.einsum(
        "mlf,ldf->mld", grad_preact, in_full, preferred_element_type=FLOAT_TYPE
    ).astype(HALF_TYPE)
    grad_w_in, grad_w_out = (
        lax.psum_scatter(
            grad_in_local.astype(jnp.bfloat16), "dp", scatter_dimension=1, tiled=True
        ).astype(jnp.float32),
        lax.psum_scatter(
            grad_out_local.astype(jnp.bfloat16), "dp", scatter_dimension=1, tiled=True
        ).astype(jnp.float32),
    )
    grad_back = lax.all_to_all(
        grad_entry.reshape(seq_count, capacity * local_experts, width),
        "seq",
        split_axis=0,
        concat_axis=0,
        tiled=True,
    )
    grad_back = grad_back.reshape(experts_all * capacity, width)
    grad_moe_in = jnp.einsum(
        "prk,pd->rd", dispatch_map, grad_back, preferred_element_type=FLOAT_TYPE
    )
    grad_moe_in = grad_moe_in + jnp.einsum(
        "re,de->rd", grad_logits, router_full, preferred_element_type=FLOAT_TYPE
    )
    grad_hidden_norm, grad_gain_second = norm_back(
        hidden_state, factor_two, gain_second, grad_moe_in
    )
    grad_state = grad_out + grad_hidden_norm
    grad_state_low = grad_state.astype(HALF_TYPE)
    grad_attn_w = jnp.einsum(
        "rd,re->de", attn_low, grad_state_low, preferred_element_type=FLOAT_TYPE
    )
    grad_attn_low = jnp.einsum(
        "re,de->rd", grad_state_low, attn_full, preferred_element_type=FLOAT_TYPE
    ).astype(HALF_TYPE)
    heads_dout = grad_attn_low.reshape(tok_rows, H, HEAD)
    softmax_dot = jnp.sum(
        jnp.transpose(heads_dout, (1, 0, 2)).astype(FLOAT_TYPE) * attn_heads, axis=2
    )
    row_stats = split_three(
        jnp.stack([jnp.transpose(log_total), jnp.transpose(softmax_dot)], axis=1)
    )

    def backward_step(running, shards, offset):
        key_rows = shards[0].reshape(shards[0].shape[0], H, HEAD)
        value_rows = shards[1].reshape(shards[1].shape[0], H, HEAD)
        query_rows = shards[2].reshape(shards[2].shape[0], H, HEAD)
        dout_rows = shards[3].reshape(shards[3].shape[0], H, HEAD)
        stats_rows = join_three(shards[4])
        piece_total = jnp.transpose(stats_rows[:, 0, :])
        piece_dot = jnp.transpose(stats_rows[:, 1, :])
        grad_query, grad_table, grad_key, grad_value = running

        def query_work(inner_state):
            inner_query, inner_table = inner_state
            raw_scores, allowed, bucket_hot = score_block(
                heads_q, key_rows, my_start, offset, rel_bias, edges
            )
            weights = jnp.where(allowed[None], jnp.exp(raw_scores - log_total[:, :, None]), 0.0)
            grad_prob = jnp.einsum(
                "qhd,khd->hqk", heads_dout, value_rows, preferred_element_type=FLOAT_TYPE
            )
            grad_score = (weights * (grad_prob - softmax_dot[:, :, None])).astype(HALF_TYPE)
            inner_query = (
                inner_query
                + jnp.einsum(
                    "hqk,khd->hqd", grad_score, key_rows, preferred_element_type=FLOAT_TYPE
                )
                * scale
            )
            inner_table = inner_table + jnp.einsum(
                "hqk,qkb->bh", grad_score.astype(FLOAT_TYPE), bucket_hot, precision=HIGH
            )
            return (inner_query, inner_table)

        def key_work(inner_state):
            inner_key, inner_value = inner_state
            raw_scores, allowed, _ = score_block(
                query_rows, heads_k, offset, my_start, rel_bias, edges
            )
            weights = jnp.where(allowed[None], jnp.exp(raw_scores - piece_total[:, :, None]), 0.0)
            inner_value = inner_value + jnp.einsum(
                "hqk,qhd->khd",
                weights.astype(HALF_TYPE),
                dout_rows,
                preferred_element_type=FLOAT_TYPE,
            )
            grad_prob = jnp.einsum(
                "qhd,khd->hqk", dout_rows, heads_v, preferred_element_type=FLOAT_TYPE
            )
            grad_score = (weights * (grad_prob - piece_dot[:, :, None])).astype(HALF_TYPE)
            inner_key = (
                inner_key
                + jnp.einsum(
                    "hqk,qhd->khd", grad_score, query_rows, preferred_element_type=FLOAT_TYPE
                )
                * scale
            )
            return (inner_key, inner_value)

        grad_query, grad_table = lax.cond(
            offset <= last_row,
            query_work,
            lambda inner_state: inner_state,
            (grad_query, grad_table),
        )
        grad_key, grad_value = lax.cond(
            offset + shards[0].shape[0] - 1 >= my_start,
            key_work,
            lambda inner_state: inner_state,
            (grad_key, grad_value),
        )
        return (grad_query, grad_table, grad_key, grad_value)

    back_start = (
        jnp.zeros((H, tok_rows, HEAD), FLOAT_TYPE),
        jnp.zeros((BUCKETS, H), FLOAT_TYPE),
        jnp.zeros((tok_rows, H, HEAD), FLOAT_TYPE),
        jnp.zeros((tok_rows, H, HEAD), FLOAT_TYPE),
    )
    grad_query, grad_table_local, grad_key, grad_value = in_sections(
        backward_step,
        back_start,
        (
            lax.all_gather(key_low, "seq", axis=0, tiled=True),
            lax.all_gather(value_low, "seq", axis=0, tiled=True),
            lax.all_gather(query_low, "seq", axis=0, tiled=True),
            lax.all_gather(grad_attn_low, "seq", axis=0, tiled=True),
            lax.all_gather(row_stats, "seq", axis=0, tiled=True),
        ),
    )
    grad_qkv_low = jnp.concatenate(
        [
            jnp.transpose(grad_query, (1, 0, 2)).reshape(tok_rows, width),
            grad_key.reshape(tok_rows, width),
            grad_value.reshape(tok_rows, width),
        ],
        axis=1,
    ).astype(HALF_TYPE)
    grad_qkv_w = jnp.einsum("rd,re->de", normed_in, grad_qkv_low, preferred_element_type=FLOAT_TYPE)
    grad_normed_one = jnp.einsum(
        "re,de->rd", grad_qkv_low, qkv_full, preferred_element_type=FLOAT_TYPE
    )
    grad_in_norm, grad_gain_first = norm_back(inputs, factor_one, gain_first, grad_normed_one)
    grad_tokens = grad_state + grad_in_norm
    grad_qkv_own, grad_attn_own, grad_router_own, grad_gain_attn, grad_gain_moe = (
        lax.psum_scatter(grad_qkv_w, ("dp", "seq"), scatter_dimension=0, tiled=True),
        lax.psum_scatter(grad_attn_w, ("dp", "seq"), scatter_dimension=0, tiled=True),
        lax.psum_scatter(grad_router, ("dp", "seq"), scatter_dimension=0, tiled=True),
        lax.psum_scatter(grad_gain_first, ("dp", "seq"), scatter_dimension=0, tiled=True),
        lax.psum_scatter(grad_gain_second, ("dp", "seq"), scatter_dimension=0, tiled=True),
    )
    loss_sum, grad_table = lax.psum((loss_local, grad_table_local), ("dp", "seq"))
    loss = loss_sum / (count_all * width)
    return (
        output,
        loss,
        grad_tokens,
        grad_qkv_own,
        grad_attn_own,
        grad_gain_attn,
        grad_gain_moe,
        grad_router_own,
        grad_table,
        grad_w_in,
        grad_w_out,
    )


MESH = pl.DeviceIdType.MESH
ANY = pl.BlockSpec(memory_space=pl.ANY)
VM = pl.BlockSpec(memory_space=pltpu.VMEM)
ROLL = 1280
GW = 1152


def remote(src, dst, send, recv, dev):
    return pltpu.make_async_remote_copy(
        src_ref=src, dst_ref=dst, send_sem=send, recv_sem=recv, device_id=dev, device_id_type=MESH
    )


def place():
    d = lax.axis_index("dp")
    s = lax.axis_index("seq")
    return d, s, s // 2, lax.rem(s, 2)


def greet(peers):
    barrier = pltpu.get_barrier_semaphore()
    for peer in peers:
        pl.semaphore_signal(barrier, inc=1, device_id=peer, device_id_type=MESH)
    pl.semaphore_wait(barrier, len(peers))


def comm_call(body, outs, n_in, cid, scratch, name, in_specs=None, out_specs=None, vmem=None):
    return pl.pallas_call(
        body,
        out_shape=outs,
        in_specs=in_specs or [ANY] * n_in,
        out_specs=out_specs or [ANY] * len(outs),
        scratch_shapes=scratch,
        compiler_params=pltpu.CompilerParams(
            collective_id=cid, has_side_effects=True, vmem_limit_bytes=vmem
        ),
        name=name,
    )


def sds(shape, dtype=jnp.bfloat16):
    return jax.ShapeDtypeStruct(shape, dtype)


def head_mask(h):
    lane = lax.broadcasted_iota(jnp.int32, (1, 192), 1)
    return lane // HEAD == h


def dot_t(a, b):
    return lax.dot_general(a, b, (((1,), (1,)), ((), ())), preferred_element_type=jnp.float32)


def dot_l(a, b):
    return lax.dot_general(a, b, (((0,), (0,)), ((), ())), preferred_element_type=jnp.float32)


def dot_n(a, b):
    return jnp.dot(a, b, preferred_element_type=jnp.float32)


def soft_rows(q, keys, g_ref, h, start, width):
    s = dot_t(q, keys) * HEAD ** (-0.5) + g_ref[h, :, pl.ds(start, width)]
    m = jnp.max(s, axis=1, keepdims=True)
    p = jnp.exp(s - m)
    return p / jnp.sum(p, axis=1, keepdims=True)


class Sems:
    def __init__(self, send, recv):
        self.send, self.recv, self.n = send, recv, 0

    def copy(self, src, dst, dev):
        cp = remote(src, dst, self.send.at[self.n], self.recv.at[self.n], dev)
        self.n += 1
        return cp


def run(copies):
    for cp in copies:
        cp.start()
    return copies


def received(copies):
    for cp in copies:
        cp.wait_recv()


def sent(copies):
    for cp in copies:
        cp.wait_send()


def chips():
    d, s, z, c = place()
    me = z * 4 + d
    numbers = [lax.rem(me + k, 16) for k in range(1, 16)]
    return me, numbers, [(lax.rem(t, 4), 2 * (t // 4) + c) for t in numbers]


def rms(v):
    return lax.rsqrt(jnp.mean(v * v, axis=1, keepdims=True) + EPS)


def forward_kernel(
    x,
    wq,
    wr,
    line,
    routes,
    win,
    wout,
    arrived,
    win_a,
    win_b,
    wout_a,
    wout_b,
    wqf,
    wrf,
    xs,
    n1s,
    q,
    kf,
    vf,
    bias,
    attn,
    h_out,
    n2_out,
    pos_out,
    gate_out,
    gains_out,
    out_v,
    going,
    ss,
    rs,
    xe,
    re,
    ls,
):
    d, s, z, c = place()
    sib = (d, s + 1 - 2 * c)
    across = (d + 1 - 2 * lax.rem(d, 2), lax.rem(d + 2, 4), 3 - d)
    plane = [(j, s) for j in across]
    plane_other = [(j, s + 1 - 2 * c) for j in across]
    zs = [(d, 2 * lax.rem(z + k, 4) + c) for k in (1, 2, 3)]
    me, numbers, others = chips()
    greet(others + plane_other + [sib])
    sems = Sems(ss, rs)

    def rows_of(ref, dd, zz, cc):
        return ref.at[pl.ds(pl.multiple_of(((dd * 4 + zz) * 2 + cc) * 24, 8), 24)]

    def column_rows(ref, dd, dev):
        copies = []
        for zz in range(4):
            part = rows_of(ref, dd, zz, c)
            copies.append(sems.copy(part, part, dev))
        return run(copies)

    local = [
        pltpu.make_async_copy(wq.at[z], rows_of(wqf, d, z, c), ls.at[0]),
        pltpu.make_async_copy(wr, rows_of(wrf, d, z, c), ls.at[1]),
        pltpu.make_async_copy(x, xs.at[z], ls.at[2]),
    ]
    run(local)
    stage1 = run(
        [
            sems.copy(wq.at[lax.rem(z + k, 4)], rows_of(wqf, d, z, c), zs[i])
            for i, k in enumerate((1, 2, 3))
        ]
    )
    bulk = []

    def expert_send(m, i, half):
        src, dst = ((win, win_a), (wout, wout_a))[m]
        j = across[i]

        def make():
            return remote(
                src.at[lax.rem(j, 2), half],
                dst.at[d],
                xe.at[m, i, half],
                re.at[m, i],
                (j, 2 * z + half),
            )

        @pl.when(j // 2 == c)
        def _():
            make().start()

        bulk.append((j // 2 == c, make))

    def expert_own(m):
        src, dst = ((win, win_a), (wout, wout_a))[m]

        def make():
            return remote(
                src.at[lax.rem(d, 2), 1 - c], dst.at[d], xe.at[m, 3, 0], re.at[m, 3], sib
            )

        @pl.when(d // 2 == c)
        def _():
            pltpu.make_async_copy(src.at[lax.rem(d, 2), c], dst.at[d], ls.at[3 + m]).start()
            make().start()

        bulk.append((d // 2 == c, make))

    def expert_pass(m, i):
        src, half, other = ((win, win_a, win_b), (wout, wout_a, wout_b))[m]
        if i < 3:
            dd = across[i]
            remote(half.at[dd], half.at[dd], xe.at[m, i, 0], re.at[m, i], sib).wait_recv()
        else:
            dd = d

            @pl.when(d // 2 == c)
            def _():
                pltpu.make_async_copy(src.at[lax.rem(d, 2), c], half.at[d], ls.at[3 + m]).wait()

            @pl.when(d // 2 != c)
            def _():
                remote(half.at[d], half.at[d], xe.at[m, 3, 0], re.at[m, 3], sib).wait_recv()

        passed.extend(run([sems.copy(half.at[dd], other.at[dd], sib)]))

    passed = []
    expert_send(0, 0, 0)
    expert_send(0, 1, 0)
    rest1 = run([sems.copy(wr, rows_of(wrf, d, z, c), zs[i]) for i in range(3)])
    rows = run([sems.copy(x, xs.at[z], zs[i]) for i in range(3)])
    for h in range(3):
        row = jnp.broadcast_to(line[h : h + 1, :], (128, ROLL))
        bias[h] = pltpu.roll(row, 0, 1, stride=1, stride_axis=0)[:, 128:]
    for cp in local:
        cp.wait()
    received(stage1)
    stage2 = [column_rows(wqf, d, dev) for dev in plane]
    stage3 = column_rows(wqf, d, sib)
    received(rest1)
    rest2 = [column_rows(wrf, d, dev) for dev in plane]
    rest3 = column_rows(wrf, d, sib)
    for i, k in ((0, 1), (1, 1), (2, 0), (2, 1)):
        expert_send(0, i, k)
    expert_own(0)
    expert_own(1)
    for i, dd in enumerate(across):
        received(stage2[i])
        stage3 += column_rows(wqf, dd, sib)
    received(stage3)
    misc = jnp.transpose(wqf[:, 576:704].astype(jnp.float32))
    gains_out[...] = misc[16:24]
    gain_first = misc[16:17]
    gain_second = misc[17:18]

    pairs = []
    for i in range(4):
        zb = lax.rem(z + 4 - i, 4)
        if i > 0:
            rows[i - 1].wait_recv()
        xf = xs[zb].astype(jnp.float32)
        n1 = (xf * rms(xf) * gain_first).astype(jnp.bfloat16)
        n1s[zb] = n1
        qkv = dot_n(n1, wqf[:, :576]).astype(jnp.bfloat16)
        q[zb] = qkv[:, :192]
        kf[zb, c] = qkv[:, 192:384]
        vf[zb, c] = qkv[:, 384:]
        pairs += run(
            [
                sems.copy(kf.at[zb, c], kf.at[zb, c], sib),
                sems.copy(vf.at[zb, c], vf.at[zb, c], sib),
            ]
        )
    for i, dd in enumerate(across):
        received(rest2[i])
        rest3 += column_rows(wrf, dd, sib)
    expert_send(1, 0, 0)
    expert_send(1, 1, 0)
    received(pairs)
    first = sems.n
    sems.n += 4
    for zb in (3, 2, 1, 0):
        width = 256 * (zb + 1)
        start = pl.multiple_of(128 * (7 - 2 * zb) - 128 * c, 128)
        keys = kf[: zb + 1].reshape(width, 192)
        values = vf[: zb + 1].reshape(width, 192)
        acc = jnp.zeros((128, 192), jnp.float32)
        for h in range(3):
            qh = jnp.where(head_mask(h), q[zb], jnp.zeros((), jnp.bfloat16))
            p = soft_rows(qh, keys, bias, h, start, width).astype(jnp.bfloat16)
            acc = acc + jnp.where(head_mask(h), dot_n(p, values), 0.0)
        out_v[zb] = acc.astype(jnp.bfloat16)

        @pl.when(z != zb)
        def _(zb=zb):
            remote(
                out_v.at[zb], attn.at[z], ss.at[first + zb], rs.at[first + z], (d, 2 * zb + c)
            ).start()

        @pl.when(z == zb)
        def _(zb=zb):
            attn[zb] = out_v[zb]

    received(rest3)
    for zb in range(4):

        @pl.when(z != zb)
        def _(zb=zb):
            remote(
                out_v.at[zb], attn.at[zb], ss.at[first + zb], rs.at[first + zb], (d, 2 * zb + c)
            ).wait()

    hidden = x[...].astype(jnp.float32)
    for zb in range(4):
        hidden = hidden + dot_n(attn[zb], wrf[192 * zb : 192 * (zb + 1), :])
    h_out[...] = hidden
    n2 = (hidden * rms(hidden) * gain_second).astype(jnp.bfloat16)
    n2_out[...] = n2
    logits = dot_n(n2, wqf[:, 576:704])
    lane = lax.broadcasted_iota(jnp.int32, (128, 128), 1)
    picks = [(lane == routes[:, i : i + 1]).astype(jnp.float32) for i in range(2)]
    chosen = [jnp.sum(jnp.where(lane == routes[:, i : i + 1], logits, 0.0), axis=1, keepdims=True) for i in range(2)]
    top = jnp.maximum(chosen[0], chosen[1])
    powers = [jnp.exp(v - top) for v in chosen]
    gates = [v / (powers[0] + powers[1]) for v in powers]
    lower = (lax.broadcasted_iota(jnp.int32, (128, 128), 0) > lane).astype(jnp.bfloat16)
    before = dot_n(lower, (picks[0] + picks[1]).astype(jnp.bfloat16))
    wide = lax.broadcasted_iota(jnp.int32, (128, 512), 1)
    chart = jnp.zeros((128, 512), jnp.float32)
    for i in range(2):
        slot = jnp.sum(picks[i] * before, axis=1, keepdims=True).astype(jnp.int32)
        position = routes[:, i : i + 1] * 32 + slot
        pos_out[:, i : i + 1] = position
        gate_out[:, i : i + 1] = gates[i]
        chart = chart + (wide == position).astype(jnp.float32)
    going[...] = dot_l(chart.astype(jnp.bfloat16), n2).astype(jnp.bfloat16).reshape(16, 32, 768)
    out = run([sems.copy(going.at[t], arrived.at[me], dev) for t, dev in zip(numbers, others)])
    own = pltpu.make_async_copy(going.at[me], arrived.at[me], ls.at[7])
    own.start()

    for i, k in ((0, 1), (1, 1), (2, 0), (2, 1)):
        expert_send(1, i, k)
    for m in range(2):
        for i in (3, 0, 1, 2):
            expert_pass(m, i)
    received(out)
    received(passed)
    own.wait()
    sent(stage1 + rows + rest1 + stage3 + pairs + rest3 + out + passed + sum(stage2 + rest2, []))
    for held, make in bulk:

        @pl.when(held)
        def _(make=make):
            make().wait_send()


CHUNK = 768
GELU_A = 0.7978845608028654
GELU_B = 0.044715


def experts_kernel(
    arrived,
    h,
    position,
    gates,
    routes,
    teacher,
    valid,
    gains,
    win_a,
    win_b,
    wout_a,
    wout_b,
    grad_back,
    output,
    grad_out,
    grad_logits,
    loss,
    gin_sum,
    gout_sum,
    win,
    wout,
    slope,
    hid,
    acc,
    leave,
    back,
    gback,
    din,
    dout,
    gin_in,
    gout_in,
    ss,
    rs,
    ls,
):
    f32, bf16 = jnp.float32, jnp.bfloat16
    d, s, z, c = place()
    sib = (d, s + 1 - 2 * c)
    me, numbers, others = chips()
    loads = []
    for j in range(4):
        for half, (a, b) in enumerate(((win_a, wout_a), (win_b, wout_b))):
            core = c if half == 0 else 1 - c
            r_in = pl.multiple_of(j * 192 + core * 96, 32)
            r_out = pl.multiple_of(j * 768 + core * 384, 128)
            loads.append(pltpu.make_async_copy(a.at[j], win.at[pl.ds(r_in, 96)], ls.at[0, j, half]))
            loads.append(
                pltpu.make_async_copy(b.at[j], wout.at[pl.ds(r_out, 384)], ls.at[1, j, half])
            )
    run(loads)
    greet(others + [sib])
    sems = Sems(ss, rs)

    def spread_rows(src, dst):
        copies = run([sems.copy(src.at[t], dst.at[me], dev) for t, dev in zip(numbers, others)])
        dst[pl.ds(me, 1)] = src[pl.ds(me, 1)]
        return copies

    rows_in = arrived[...].reshape(512, 768)
    for cp in loads:
        cp.wait()
    acc[...] = jnp.zeros_like(acc)

    def forward_step(f, carry):
        at = pl.multiple_of(f * CHUNK, CHUNK)
        for r in (0, 256):
            pre = dot_n(arrived[r // 32 : r // 32 + 8].reshape(256, 768), win[:, pl.ds(at, CHUNK)])
            t = jnp.tanh(GELU_A * (pre + GELU_B * pre * pre * pre))
            half = 0.5 * (1.0 + t)
            hd = (pre * half).astype(bf16)
            slope[r : r + 256, pl.ds(at, CHUNK)] = half + 0.5 * pre * (1.0 - t * t) * (
                GELU_A * (1.0 + 3.0 * GELU_B * pre * pre)
            )
            hid[r : r + 256, pl.ds(at, CHUNK)] = hd
            acc[r : r + 256] += dot_n(hd, wout[pl.ds(at, CHUNK), :])
        return carry

    lax.fori_loop(0, 4, forward_step, 0)
    leave[...] = acc[...].astype(bf16).reshape(16, 32, 768)
    results = spread_rows(leave, back)
    count = jnp.sum(gains[2:3, :], axis=1, keepdims=True) / 24.0
    wide = lax.broadcasted_iota(jnp.int32, (128, 512), 1)
    maps = [(wide == position[:, i : i + 1]).astype(f32).astype(bf16) for i in range(2)]
    received(results)
    sent(results)
    combined = [dot_n(m, back[...].reshape(512, 768)) for m in maps]
    gate = [gates[:, i : i + 1] for i in range(2)]
    out = h[...] + gate[0] * combined[0] + gate[1] * combined[1]
    output[...] = out
    error = out - teacher[...].astype(f32)
    masked = valid[...] * error
    loss[...] = jnp.broadcast_to(jnp.sum(masked * error, keepdims=True), (8, 128))
    gout = (2.0 * 4096.0) / count * masked
    grad_out[...] = gout
    leave[...] = (
        (
            dot_l(maps[0], (gate[0] * gout).astype(bf16))
            + dot_l(maps[1], (gate[1] * gout).astype(bf16))
        )
        .astype(bf16)
        .reshape(16, 32, 768)
    )
    grads = spread_rows(leave, gback)
    dgate = [jnp.sum(m * gout, axis=1, keepdims=True) for m in combined]
    mean = gate[0] * dgate[0] + gate[1] * dgate[1]
    lane = lax.broadcasted_iota(jnp.int32, (128, 128), 1)
    total = jnp.zeros((128, 128), f32)
    for i in range(2):
        total = total + jnp.where(lane == routes[:, i : i + 1], gate[i] * (dgate[i] - mean), 0.0)
    grad_logits[...] = total.astype(bf16)
    received(grads)
    sent(grads)
    acc[...] = jnp.zeros_like(acc)

    def backward_step(f, carry):
        at = pl.multiple_of(f * CHUNK, CHUNK)
        for r in (0, 256):
            dh = dot_t(gback[r // 32 : r // 32 + 8].reshape(256, 768), wout[pl.ds(at, CHUNK), :])
            dp = (dh * slope[r : r + 256, pl.ds(at, CHUNK)]).astype(bf16)
            slope[r : r + 256, pl.ds(at, CHUNK)] = dp.astype(f32)
            acc[r : r + 256] += dot_t(dp, win[:, pl.ds(at, CHUNK)])
        return carry

    lax.fori_loop(0, 4, backward_step, 0)
    leave[...] = acc[...].astype(bf16).reshape(16, 32, 768)
    entries = run([sems.copy(leave.at[t], grad_back.at[me], dev) for t, dev in zip(numbers, others)])
    own = pltpu.make_async_copy(leave.at[me], grad_back.at[me], ls.at[2, 0, 0])
    own.start()

    def weights_step(f, carry):
        at = pl.multiple_of(f * CHUNK, CHUNK)
        rows = gback[...].reshape(512, 768)
        dout[f] = dot_l(hid[:, pl.ds(at, CHUNK)], rows).astype(bf16).reshape(2, 384, 768)
        remote(
            dout.at[f, 1 - c], gout_in.at[f], ss.at[50 + f], rs.at[50 + f], sib
        ).start()
        dp = slope[:, pl.ds(at, CHUNK)].astype(bf16)
        din[:, :, :, pl.ds(at, CHUNK)] = (
            dot_l(rows_in, dp).astype(bf16).reshape(4, 2, 96, CHUNK)
        )
        return carry

    lax.fori_loop(0, 4, weights_step, 0)
    inner = remote(din.at[:, 1 - c], gin_in, ss.at[54], rs.at[54], sib)
    inner.start()
    for f in range(4):
        remote(dout.at[f, 1 - c], gout_in.at[f], ss.at[50 + f], rs.at[50 + f], sib).wait()
        gout_in[f] = (dout[f, c].astype(f32) + gout_in[f].astype(f32)).astype(bf16)
    stores = run([pltpu.make_async_copy(gout_in, gout_sum, ls.at[2, 1, 0])])
    inner.wait()
    for j in range(4):
        gin_in[j] = (din[j, c].astype(f32) + gin_in[j].astype(f32)).astype(bf16)
    stores += run([pltpu.make_async_copy(gin_in, gin_sum, ls.at[2, 2, 0])])
    received(entries)
    sent(entries)
    own.wait()
    for cp in stores:
        cp.wait()


def backward_kernel(
    grad_back,
    position,
    h,
    gains,
    grad_out,
    grad_logits,
    loss,
    n2,
    x,
    attn,
    hot,
    wqf_h,
    wrf_h,
    q_h,
    kf_h,
    vf_h,
    bias_h,
    n1s_h,
    xs_h,
    gin,
    gout,
    grad_tokens,
    grad_qkv,
    grad_rest,
    oin,
    oout,
    shared,
    wqf,
    wrf,
    q,
    kf,
    vf,
    bias,
    n1s,
    xs,
    do_out,
    do,
    rest,
    rest_in,
    rest_got,
    kacc,
    vacc,
    gacc,
    dk_out,
    dv_out,
    dk_in,
    dv_in,
    dqkv,
    part,
    parts,
    wpart,
    wpart_in,
    wgot,
    small,
    ss,
    rs,
    xe,
    re,
    ls,
):
    f32, bf16 = jnp.float32, jnp.bfloat16
    d, s, z, c = place()
    sib = (d, s + 1 - 2 * c)
    across = (d + 1 - 2 * lax.rem(d, 2), lax.rem(d + 2, 4), 3 - d)
    zs = [(d, 2 * lax.rem(z + k, 4) + c) for k in (1, 2, 3)]
    me, numbers, others = chips()
    device = d * 8 + s
    everyone = [
        (lax.rem(d + k // 8, 4), lax.rem(s + k % 8, 8)) for k in range(1, 32)
    ]
    loads = [
        pltpu.make_async_copy(a, b, ls.at[i])
        for i, (a, b) in enumerate(
            (
                (wqf_h, wqf),
                (wrf_h, wrf),
                (q_h, q),
                (kf_h, kf),
                (vf_h, vf),
                (bias_h, bias),
                (n1s_h, n1s),
                (xs_h, xs),
            )
        )
    ]
    run(loads)
    greet(everyone)
    sems = Sems(ss, rs)
    bulk = []

    def owner_send(m, i):
        src, dst = ((gin, oin), (gout, oout))[m]
        cp = remote(
            src.at[across[i]],
            dst.at[lax.rem(d, 2), c],
            xe.at[m, i],
            re.at[m, lax.rem(d, 2), c],
            (across[i], 2 * z + d // 2),
        )
        cp.start()
        bulk.append(cp)

    def owner_local(m):
        src, dst = ((gin, oin), (gout, oout))[m]

        @pl.when(d // 2 == c)
        def _():
            pltpu.make_async_copy(src.at[d], dst.at[lax.rem(d, 2), c], ls.at[8 + m]).start()

        @pl.when(d // 2 != c)
        def _():
            remote(
                src.at[d],
                dst.at[lax.rem(d, 2), c],
                xe.at[m, 3],
                re.at[m, lax.rem(d, 2), c],
                sib,
            ).start()

    def rows_of(ref, t):
        return ref.at[pl.ds(pl.multiple_of(((lax.rem(t, 4) * 4 + t // 4) * 2 + c) * 24, 8), 24)]

    def to_owners(src, dst):
        mine = dst.at[pl.ds(pl.multiple_of(me * 24, 8), 24)]
        return run([sems.copy(rows_of(src, t), mine, dev) for t, dev in zip(numbers, others)])

    for i in range(3):
        owner_send(1, i)
    owner_local(0)
    owner_local(1)

    wide = lax.broadcasted_iota(jnp.int32, (128, 512), 1)
    chart = (wide == position[:, 0:1]).astype(f32) + (wide == position[:, 1:2]).astype(f32)
    loads[0].wait()
    dn2 = dot_n(chart.astype(bf16), grad_back[...].reshape(512, 768))
    dn2 = dn2 + dot_t(grad_logits[...], wqf[:, 576:704])
    hidden = h[...]
    r2 = rms(hidden)
    scaled = dn2 * gains[1:2]
    mean = jnp.mean(scaled * hidden, axis=1, keepdims=True)
    dh = grad_out[...] + r2 * scaled - hidden * (r2 * r2 * r2) * mean
    dh_low = dh.astype(bf16)
    loads[1].wait()
    for zb in range(4):
        do_out[zb] = dot_t(dh_low, wrf[192 * zb : 192 * (zb + 1), :]).astype(bf16)
    heads = run([sems.copy(do_out.at[lax.rem(z + k, 4)], do.at[z], zs[i]) for i, k in enumerate((1, 2, 3))])
    do[pl.ds(z, 1)] = do_out[pl.ds(z, 1)]

    for zb in range(4):
        rest[192 * zb : 192 * (zb + 1), :768] = dot_l(attn[zb], dh_low).astype(bf16)
    gain_rows = jnp.broadcast_to(jnp.sum(dn2 * hidden * r2, axis=0, keepdims=True), (128, 768))
    lane = lax.broadcasted_iota(jnp.int32, (768, 128), 1)
    rest[:, 768:] = jnp.where(
        lane == 16, jnp.transpose(gain_rows), dot_l(n2[...], grad_logits[...])
    ).astype(bf16)
    rest_swap = run([sems.copy(rest, rest_in, sib)])
    grad_tokens[...] = dh
    kacc[...] = jnp.zeros_like(kacc)
    vacc[...] = jnp.zeros_like(vacc)
    gacc[...] = jnp.zeros_like(gacc)
    received(rest_swap)
    sent(rest_swap)
    rest_in[...] = (rest[...].astype(f32) + rest_in[...].astype(f32)).astype(bf16)
    rest_sent = to_owners(rest_in, rest_got)
    for i in range(3):
        owner_send(0, i)
    for cp in loads[2:6]:
        cp.wait()
    received(heads)
    for zb in (3, 2, 1, 0):
        width = 256 * (zb + 1)
        start = pl.multiple_of(128 * (7 - 2 * zb) - 128 * c, 128)
        keys = kf[: zb + 1].reshape(width, 192)
        values = vf[: zb + 1].reshape(width, 192)
        acc = jnp.zeros((128, 192), f32)
        for hd in range(3):
            mask = head_mask(hd)
            qh = jnp.where(mask, q[zb], jnp.zeros((), bf16))
            doh = jnp.where(mask, do[zb], jnp.zeros((), bf16))
            p = soft_rows(qh, keys, bias, hd, start, width)
            vacc[:width] += dot_l(p.astype(bf16), doh)
            dp = dot_t(doh, values)
            dot = jnp.sum(p * dp, axis=1, keepdims=True)
            ds = (p * (dp - dot)).astype(bf16)
            gacc[hd, :, pl.ds(start, width)] += ds.astype(f32)
            acc = acc + jnp.where(mask, dot_n(ds, keys), 0.0)
            kacc[:width] += dot_l(ds, qh)
        dqkv[zb, :, :192] = (acc * HEAD ** (-0.5)).astype(bf16)
    scale = HEAD ** (-0.5)
    for zb in range(4):
        there = pl.ds(pl.multiple_of((2 * zb + 1 - c) * 128, 128), 128)
        dk_out[zb] = (kacc[there] * scale).astype(bf16)
        dv_out[zb] = vacc[there].astype(bf16)
    pairs = run([sems.copy(dk_out, dk_in, sib), sems.copy(dv_out, dv_in, sib)])

    row = lax.broadcasted_iota(jnp.int32, (128, 1), 0)
    sums = []
    for hd in range(3):
        y = jnp.concatenate([jnp.zeros((128, ROLL - GW), f32), gacc[hd]], axis=1)
        for bit in range(7):
            y = jnp.where((row >> bit) & 1 == 1, pltpu.roll(y, ROLL - (1 << bit), 1), y)
        sums.append(jnp.sum(y, axis=0, keepdims=True))
    lines = jnp.concatenate(sums + [jnp.zeros((5, ROLL), f32)], axis=0)
    table = lax.dot_general(
        lines, hot[...], (((1,), (1,)), ((), ())), precision=HIGH, preferred_element_type=f32
    )
    index = lax.broadcasted_iota(jnp.int32, (8, 128), 0)
    small[...] = jnp.where(index == 3, loss[...], table)
    shares = run([sems.copy(small, shared.at[device], dev) for dev in everyone])
    own_share = pltpu.make_async_copy(small, shared.at[device], ls.at[10])
    own_share.start()

    for cp in loads[6:]:
        cp.wait()
    received(pairs)
    first = sems.n
    sems.n += 4
    gain_first = gains[0:1]
    gain_part = jnp.zeros((1, 768), f32)
    for zb in (3, 2, 1, 0):
        here = pl.ds(pl.multiple_of((2 * zb + c) * 128, 128), 128)
        dqkv[zb, :, 192:384] = (kacc[here] * scale + dk_in[zb].astype(f32)).astype(bf16)
        dqkv[zb, :, 384:] = (vacc[here] + dv_in[zb].astype(f32)).astype(bf16)
        dn1 = dot_t(dqkv[zb], wqf[:, :576])
        part[zb] = dn1.astype(bf16)

        @pl.when(z != zb)
        def _(zb=zb):
            remote(
                part.at[zb], parts.at[z], ss.at[first + zb], rs.at[first + z], (d, 2 * zb + c)
            ).start()

        @pl.when(z == zb)
        def _(zb=zb):
            parts[zb] = part[zb]

        xf = xs[zb].astype(f32)
        gain_part = gain_part + jnp.sum(dn1 * xf * rms(xf), axis=0, keepdims=True)
    wpart[:, :576] = dot_l(n1s[...].reshape(512, 768), dqkv[...].reshape(512, 576)).astype(bf16)
    wpart[:, 576:] = jnp.transpose(jnp.broadcast_to(gain_part, (128, 768))).astype(bf16)
    wswap = run([sems.copy(wpart, wpart_in, sib)])
    received(wswap)
    sent(wswap)
    wpart_in[...] = (wpart[...].astype(f32) + wpart_in[...].astype(f32)).astype(bf16)
    wsent = to_owners(wpart_in, wgot)

    for zb in range(4):

        @pl.when(z != zb)
        def _(zb=zb):
            remote(
                part.at[zb], parts.at[zb], ss.at[first + zb], rs.at[first + zb], (d, 2 * zb + c)
            ).wait()

    dn1 = (
        parts[0].astype(f32) + parts[1].astype(f32) + parts[2].astype(f32) + parts[3].astype(f32)
    )
    xf = x[...].astype(f32)
    r1 = rms(xf)
    scaled = dn1 * gain_first
    mean = jnp.mean(scaled * xf, axis=1, keepdims=True)
    grad_tokens[...] += r1 * scaled - xf * (r1 * r1 * r1) * mean

    mine = pl.ds(pl.multiple_of(me * 24, 8), 24)
    own_rows = [
        pltpu.make_async_copy(rows_of(rest_in, me), rest_got.at[mine], ls.at[11]),
        pltpu.make_async_copy(rows_of(wpart_in, me), wgot.at[mine], ls.at[12]),
    ]
    run(own_rows)
    received(rest_sent)
    received(wsent)
    for cp in own_rows:
        cp.wait()
    total = jnp.zeros((24, 896), f32)
    gain_total = jnp.zeros((24, 128), f32)
    for zb in range(4):
        block = jnp.zeros((24, 576), f32)
        for dd in range(4):
            r = (zb * 4 + dd) * 24
            total = total + rest_got[r : r + 24, :].astype(f32)
            block = block + wgot[r : r + 24, :576].astype(f32)
            gain_total = gain_total + wgot[r : r + 24, 576:].astype(f32)
        for i in range(3):
            at = i * 768 + zb * 192
            grad_qkv[:, at : at + 192] = block[:, i * 192 : (i + 1) * 192]
    grad_rest[:, :896] = total
    grad_rest[:, 896:] = gain_total

    received(shares)
    own_share.wait()
    for m, (src, dst) in enumerate(((gin, oin), (gout, oout))):
        for l in range(2):
            for half in range(2):
                here = (2 * c + l == d) & (c == half)

                @pl.when(jnp.logical_not(here))
                def _(src=src, dst=dst, m=m, l=l, half=half):
                    remote(
                        src.at[0], dst.at[l, half], xe.at[m, 3], re.at[m, l, half], sib
                    ).wait_recv()

        @pl.when(d // 2 == c)
        def _(src=src, dst=dst, m=m):
            pltpu.make_async_copy(src.at[d], dst.at[lax.rem(d, 2), c], ls.at[8 + m]).wait()

        @pl.when(d // 2 != c)
        def _(src=src, dst=dst, m=m):
            remote(
                src.at[d],
                dst.at[lax.rem(d, 2), c],
                xe.at[m, 3],
                re.at[m, lax.rem(d, 2), c],
                sib,
            ).wait_send()

    sent(heads + rest_sent + pairs + shares + wsent + bulk)


def fast_path(
    tokens,
    w_qkv,
    w_attn_out,
    gain_attn,
    gain_moe,
    w_router,
    rel_bias,
    w_in,
    w_out,
    teacher,
    routes,
    valid,
    buckets,
):
    f32, bf16 = jnp.float32, jnp.bfloat16
    d = lax.axis_index("dp")
    s = lax.axis_index("seq")
    z, c = s // 2, s % 2
    wq = w_qkv.reshape(24, 3, 4, 192).transpose(2, 0, 1, 3).reshape(4, 24, 576)
    valid_float = valid.astype(f32)
    misc = jnp.concatenate(
        [
            w_router,
            gain_attn[:, None],
            gain_moe[:, None],
            jnp.full((24, 1), jnp.sum(valid_float)).astype(bf16),
            jnp.zeros((24, 109), bf16),
        ],
        axis=1,
    )
    wq = jnp.concatenate([wq, jnp.broadcast_to(misc[None], (4, 24, 128))], axis=2)
    one_hot = (buckets[None, :] == jnp.arange(BUCKETS, dtype=jnp.int32)[:, None]).astype(f32)
    my_bias = lax.dynamic_slice_in_dim(rel_bias, 3 * z, 3, 1)
    table = jnp.einsum("bh,bt->ht", my_bias, one_hot, precision=HIGH)
    line = jnp.concatenate(
        [
            jnp.full((3, 1), NEG, f32),
            table[:, ::-1],
            jnp.full((3, ROLL - 1025), NEG, f32),
        ],
        axis=1,
    )
    (
        arrived,
        win_a,
        win_b,
        wout_a,
        wout_b,
        wqf,
        wrf,
        xs,
        n1s,
        q,
        kf,
        vf,
        bias,
        attn,
        hidden_state,
        moe_in,
        position,
        gate_weights,
        gains,
    ) = comm_call(
        forward_kernel,
        [
            sds((16, 32, 768)),
            sds((4, 96, 3072)),
            sds((4, 96, 3072)),
            sds((4, 384, 768)),
            sds((4, 384, 768)),
            sds((768, 704)),
            sds((768, 768)),
            sds((4, 128, 768)),
            sds((4, 128, 768)),
            sds((4, 128, 192)),
            sds((4, 2, 128, 192)),
            sds((4, 2, 128, 192)),
            sds((3, 128, GW), f32),
            sds((4, 128, 192)),
            sds((128, 768), f32),
            sds((128, 768)),
            sds((128, 2), jnp.int32),
            sds((128, 2), f32),
            sds((8, 768), f32),
        ],
        7,
        1,
        [
            pltpu.VMEM((4, 128, 192), bf16),
            pltpu.VMEM((16, 32, 768), bf16),
            pltpu.SemaphoreType.DMA((120,)),
            pltpu.SemaphoreType.DMA((120,)),
            pltpu.SemaphoreType.DMA((2, 4, 2)),
            pltpu.SemaphoreType.DMA((2, 4)),
            pltpu.SemaphoreType.DMA((8,)),
        ],
        "forward",
        in_specs=[VM, ANY, ANY, VM, VM, ANY, ANY],
        out_specs=[ANY] * 5 + [VM] * 14,
        vmem=50 << 20,
    )(
        tokens,
        wq,
        w_attn_out,
        line,
        routes,
        w_in.reshape(2, 2, 96, 3072),
        w_out.reshape(2, 2, 384, 768),
    )
    (
        grad_back,
        output,
        grad_out,
        grad_logits,
        loss_rows,
        gin_own,
        gout_own,
    ) = comm_call(
        experts_kernel,
        [
            sds((16, 32, 768)),
            sds((128, 768), f32),
            sds((128, 768), f32),
            sds((128, 128)),
            sds((8, 128), f32),
            sds((4, 96, 3072)),
            sds((4, 384, 768)),
        ],
        12,
        2,
        [
            pltpu.VMEM((768, 3072), bf16),
            pltpu.VMEM((3072, 768), bf16),
            pltpu.VMEM((512, 3072), f32),
            pltpu.VMEM((512, 3072), bf16),
            pltpu.VMEM((512, 768), f32),
            pltpu.VMEM((16, 32, 768), bf16),
            pltpu.VMEM((16, 32, 768), bf16),
            pltpu.VMEM((16, 32, 768), bf16),
            pltpu.VMEM((4, 2, 96, 3072), bf16),
            pltpu.VMEM((4, 2, 384, 768), bf16),
            pltpu.VMEM((4, 96, 3072), bf16),
            pltpu.VMEM((4, 384, 768), bf16),
            pltpu.SemaphoreType.DMA((56,)),
            pltpu.SemaphoreType.DMA((56,)),
            pltpu.SemaphoreType.DMA((3, 4, 2)),
        ],
        "experts",
        in_specs=[VM] * 8 + [ANY] * 4,
        out_specs=[ANY] + [VM] * 4 + [ANY] * 2,
        vmem=60 << 20,
    )(
        arrived,
        hidden_state,
        position,
        gate_weights,
        routes,
        teacher,
        valid_float[:, None],
        gains,
        win_a,
        win_b,
        wout_a,
        wout_b,
    )
    hot = jnp.concatenate(
        [jnp.zeros((32, 1), f32), one_hot[:, ::-1], jnp.zeros((32, ROLL - 1025), f32)], axis=1
    )
    hot = jnp.concatenate([hot, jnp.zeros((96, ROLL), f32)], axis=0)
    grad_tokens, grad_w_qkv, grad_rest, oin, oout, shared = comm_call(
        backward_kernel,
        [
            sds((128, 768), f32),
            sds((24, 2304), f32),
            sds((24, 1024), f32),
            sds((2, 2, 96, 3072)),
            sds((2, 2, 384, 768)),
            sds((32, 8, 128), f32),
        ],
        21,
        3,
        [
            pltpu.VMEM((768, 704), bf16),
            pltpu.VMEM((768, 768), bf16),
            pltpu.VMEM((4, 128, 192), bf16),
            pltpu.VMEM((4, 2, 128, 192), bf16),
            pltpu.VMEM((4, 2, 128, 192), bf16),
            pltpu.VMEM((3, 128, GW), f32),
            pltpu.VMEM((4, 128, 768), bf16),
            pltpu.VMEM((4, 128, 768), bf16),
            pltpu.VMEM((4, 128, 192), bf16),
            pltpu.VMEM((4, 128, 192), bf16),
            pltpu.VMEM((768, 896), bf16),
            pltpu.VMEM((768, 896), bf16),
            pltpu.VMEM((384, 896), bf16),
            pltpu.VMEM((1024, 192), f32),
            pltpu.VMEM((1024, 192), f32),
            pltpu.VMEM((3, 128, GW), f32),
            pltpu.VMEM((4, 128, 192), bf16),
            pltpu.VMEM((4, 128, 192), bf16),
            pltpu.VMEM((4, 128, 192), bf16),
            pltpu.VMEM((4, 128, 192), bf16),
            pltpu.VMEM((4, 128, 576), bf16),
            pltpu.VMEM((4, 128, 768), bf16),
            pltpu.VMEM((4, 128, 768), bf16),
            pltpu.VMEM((768, 704), bf16),
            pltpu.VMEM((768, 704), bf16),
            pltpu.VMEM((384, 704), bf16),
            pltpu.VMEM((8, 128), f32),
            pltpu.SemaphoreType.DMA((90,)),
            pltpu.SemaphoreType.DMA((90,)),
            pltpu.SemaphoreType.DMA((2, 4)),
            pltpu.SemaphoreType.DMA((2, 2, 2)),
            pltpu.SemaphoreType.DMA((13,)),
        ],
        "backward",
        in_specs=[VM] * 11 + [ANY] * 10,
        out_specs=[VM] * 3 + [ANY] * 3,
        vmem=60 << 20,
    )(
        grad_back,
        position,
        hidden_state,
        gains,
        grad_out,
        grad_logits,
        loss_rows,
        moe_in,
        tokens,
        attn,
        hot,
        wqf,
        wrf,
        q,
        kf,
        vf,
        bias,
        n1s,
        xs,
        gin_own,
        gout_own,
    )
    count_all = jnp.sum(gains[2]) / 24.0
    by_z = jnp.sum(shared.reshape(4, 4, 2, 8, 128), axis=(0, 2))
    loss = jnp.sum(by_z[:, 3, 0]) / (count_all * 768)
    grad_table = by_z[:, :3, :32].reshape(12, 32).T
    return (
        output,
        loss,
        grad_tokens,
        grad_w_qkv,
        grad_rest[:, :768],
        grad_rest[:, 896],
        grad_rest[:, 784],
        grad_rest[:, 768:784],
        grad_table,
        oin.reshape(2, 192, 3072).astype(f32),
        oout.reshape(2, 768, 768).astype(f32),
    )


def choose(*arrays):
    tokens, w_in, rel_bias, buckets = arrays[0], arrays[7], arrays[6], arrays[12]
    fits = (
        lax.axis_size("dp") == 4
        and lax.axis_size("seq") == 8
        and tokens.shape == (128, 768)
        and w_in.shape == (2, 192, 3072)
        and rel_bias.shape == (32, 12)
        and buckets.shape == (1024,)
    )
    return fast_path(*arrays) if fits else on_device(*arrays)


def solution(mesh):
    in_specs = (
        P(("dp", "seq"), None),
        P(("dp", "seq"), None),
        P(("dp", "seq"), None),
        P(("dp", "seq")),
        P(("dp", "seq")),
        P(("dp", "seq"), None),
        P(),
        P("seq", "dp", None),
        P("seq", "dp", None),
        P(("dp", "seq"), None),
        P(("dp", "seq"), None),
        P(("dp", "seq")),
        P(),
    )
    out_specs = (
        P(("dp", "seq"), None),
        P(),
        P(("dp", "seq"), None),
        P(("dp", "seq"), None),
        P(("dp", "seq"), None),
        P(("dp", "seq")),
        P(("dp", "seq")),
        P(("dp", "seq"), None),
        P(),
        P("seq", "dp", None),
        P("seq", "dp", None),
    )
    return jax.shard_map(
        choose, mesh=mesh, in_specs=in_specs, out_specs=out_specs, check_vma=False
    )
```

```python
import functools

import jax
import jax.numpy as jnp
from jax import lax
from jax.experimental import pallas as pl
from jax.experimental.pallas import tpu as pltpu
from jax.sharding import PartitionSpec as P

H = 12
HEAD = 64
BUCKETS = 32


EPS = 1e-06
NEG = -1e30
SECTION = 512
HIGH = lax.Precision.HIGHEST
FLOAT_TYPE = jnp.float32
HALF_TYPE = jnp.bfloat16


def normalize(values, gain):
    factor = lax.rsqrt(jnp.mean(values * values, axis=-1, keepdims=True) + EPS)
    return (values * factor * gain, factor)


def norm_back(values, factor, gain, grad_norm):
    scaled = grad_norm * gain
    mean_term = jnp.mean(scaled * values, axis=-1, keepdims=True)
    grad_values = factor * scaled - values * (factor * factor * factor) * mean_term
    return (grad_values, jnp.sum(grad_norm * values * factor, axis=0))


def gelu_grad(preact, grad_hidden):
    _, gelu_back = jax.vjp(jax.nn.gelu, preact)
    return gelu_back(grad_hidden)[0]


def in_sections(advance, running, shards):
    row_count = shards[0].shape[0]
    sections = row_count // SECTION
    stacked = tuple((member.reshape((sections, SECTION) + member.shape[1:]) for member in shards))

    def one_section(inner_state, entry_pair):
        return (advance(inner_state, entry_pair[1], entry_pair[0] * SECTION), None)

    final_state, _ = lax.scan(
        one_section, running, (jnp.arange(sections, dtype=jnp.int32), stacked)
    )
    return final_state


def score_block(queries, key_rows, query_start, key_start, rel_bias, edges):
    query_count = queries.shape[0]
    key_count = key_rows.shape[0]
    distance = (query_start + jnp.arange(query_count, dtype=jnp.int32))[:, None] - (
        key_start + jnp.arange(key_count, dtype=jnp.int32)
    )[None, :]
    allowed = distance >= 0
    bucket_hot = (
        (distance[:, :, None] >= edges[None, None, :-1])
        & (distance[:, :, None] < edges[None, None, 1:])
    ).astype(FLOAT_TYPE)
    bias_term = jnp.einsum("qkb,bh->hqk", bucket_hot, rel_bias, precision=HIGH)
    raw_scores = (
        jnp.einsum("qhd,khd->hqk", queries, key_rows, preferred_element_type=FLOAT_TYPE)
        * queries.shape[2] ** (-0.5)
        + bias_term
    )
    return (raw_scores, allowed, bucket_hot)


def split_three(values):
    upper = lax.optimization_barrier(values.astype(HALF_TYPE))
    remainder = values - upper.astype(FLOAT_TYPE)
    middle = lax.optimization_barrier(remainder.astype(HALF_TYPE))
    bottom = (remainder - middle.astype(FLOAT_TYPE)).astype(HALF_TYPE)
    return jnp.stack([upper, middle, bottom], axis=1)


def join_three(packed):
    as_float = packed.astype(FLOAT_TYPE)
    return as_float[:, 0] + as_float[:, 1] + as_float[:, 2]


def on_device(
    tokens,
    w_qkv,
    w_attn_out,
    gain_attn,
    gain_moe,
    w_router,
    rel_bias,
    w_in,
    w_out,
    teacher,
    routes,
    valid,
    buckets,
):
    tok_rows = tokens.shape[0]
    width = tokens.shape[1]
    seq_count = lax.axis_size("seq")
    my_start = lax.axis_index("seq") * tok_rows
    local_experts = w_in.shape[0]
    experts_all = local_experts * seq_count
    capacity = 4 * tok_rows // experts_all
    slot_rows = seq_count * capacity
    scale = HEAD ** (-0.5)
    qkv_full, attn_full, router_full, gain_one, gain_two, valid_all = (
        lax.all_gather(w_qkv, ("dp", "seq"), axis=0, tiled=True),
        lax.all_gather(w_attn_out, ("dp", "seq"), axis=0, tiled=True),
        lax.all_gather(w_router, ("dp", "seq"), axis=0, tiled=True),
        lax.all_gather(gain_attn, ("dp", "seq"), axis=0, tiled=True),
        lax.all_gather(gain_moe, ("dp", "seq"), axis=0, tiled=True),
        lax.all_gather(valid.astype(HALF_TYPE), ("dp", "seq"), axis=0, tiled=True),
    )
    valid_float = valid.astype(FLOAT_TYPE)
    count_all = jnp.sum(valid_all.astype(FLOAT_TYPE))
    tokens_all = tok_rows * lax.axis_size("dp") * seq_count
    edges = jnp.sum(
        (buckets[None, :] < jnp.arange(BUCKETS + 1, dtype=jnp.int32)[:, None]).astype(jnp.int32),
        axis=1,
    )
    inputs = tokens.astype(FLOAT_TYPE)
    gain_first = gain_one.astype(FLOAT_TYPE)
    gain_second = gain_two.astype(FLOAT_TYPE)
    normed_one, factor_one = normalize(inputs, gain_first)
    normed_in = normed_one.astype(HALF_TYPE)
    qkv_rows = jnp.dot(normed_in, qkv_full, preferred_element_type=FLOAT_TYPE)
    query_low = qkv_rows[:, :width].astype(HALF_TYPE)
    key_low = qkv_rows[:, width : 2 * width].astype(HALF_TYPE)
    value_low = qkv_rows[:, 2 * width :].astype(HALF_TYPE)
    heads_q = query_low.reshape(tok_rows, H, HEAD)
    heads_k = key_low.reshape(tok_rows, H, HEAD)
    heads_v = value_low.reshape(tok_rows, H, HEAD)
    last_row = my_start + tok_rows - 1

    def forward_step(running, shards, offset):
        key_rows = shards[0].reshape(shards[0].shape[0], H, HEAD)
        value_rows = shards[1].reshape(shards[1].shape[0], H, HEAD)

        def work(inner_state):
            maximum, denom, mixture = inner_state
            raw_scores, allowed, _ = score_block(
                heads_q, key_rows, my_start, offset, rel_bias, edges
            )
            masked = jnp.where(allowed[None], raw_scores, NEG)
            new_max = jnp.maximum(maximum, jnp.max(masked, axis=2))
            weights = jnp.where(allowed[None], jnp.exp(masked - new_max[:, :, None]), 0.0)
            rescale = jnp.exp(maximum - new_max)
            addend = jnp.einsum(
                "hqk,khd->hqd",
                weights.astype(HALF_TYPE),
                value_rows,
                preferred_element_type=FLOAT_TYPE,
            )
            return (
                new_max,
                denom * rescale + jnp.sum(weights, axis=2),
                mixture * rescale[:, :, None] + addend,
            )

        return lax.cond(offset <= last_row, work, lambda inner_state: inner_state, running)

    start_state = (
        jnp.full((H, tok_rows), NEG, FLOAT_TYPE),
        jnp.zeros((H, tok_rows), FLOAT_TYPE),
        jnp.zeros((H, tok_rows, HEAD), FLOAT_TYPE),
    )
    maximum, denom, mixture = in_sections(
        forward_step,
        start_state,
        (
            lax.all_gather(key_low, "seq", axis=0, tiled=True),
            lax.all_gather(value_low, "seq", axis=0, tiled=True),
        ),
    )
    log_total = maximum + jnp.log(denom)
    attn_heads = mixture / denom[:, :, None]
    attn_rows = jnp.transpose(attn_heads, (1, 0, 2)).reshape(tok_rows, width)
    attn_low = attn_rows.astype(HALF_TYPE)
    hidden_state = inputs + jnp.dot(attn_low, attn_full, preferred_element_type=FLOAT_TYPE)
    normed_two, factor_two = normalize(hidden_state, gain_second)
    moe_in = normed_two.astype(HALF_TYPE)
    logits = jnp.dot(moe_in, router_full, preferred_element_type=FLOAT_TYPE)
    chosen = jnp.take_along_axis(logits, routes, axis=1)
    gate_weights = jax.nn.softmax(chosen, axis=1)
    flat_routes = routes.reshape(-1)
    matches = (flat_routes[:, None] == jnp.arange(experts_all, dtype=jnp.int32)[None, :]).astype(
        jnp.int32
    )
    slot_index = jnp.sum((jnp.cumsum(matches, axis=0) - matches) * matches, axis=1)
    target_dev = flat_routes // local_experts
    target_local = flat_routes % local_experts
    position = (target_dev * capacity + slot_index) * local_experts + target_local
    dispatch_map = (
        jnp.arange(experts_all * capacity, dtype=jnp.int32)[:, None] == position[None, :]
    ).astype(HALF_TYPE)
    dispatch_map = dispatch_map.reshape(experts_all * capacity, tok_rows, 2)
    outgoing = jnp.einsum(
        "prk,rd->pd", dispatch_map, moe_in, preferred_element_type=FLOAT_TYPE
    ).astype(HALF_TYPE)
    arrived = lax.all_to_all(
        outgoing.reshape(seq_count, capacity * local_experts, width),
        "seq",
        split_axis=0,
        concat_axis=0,
        tiled=True,
    )
    arrived_rows = arrived.reshape(slot_rows, local_experts, width)
    in_full, out_full = (
        lax.all_gather(w_in, "dp", axis=1, tiled=True),
        lax.all_gather(w_out, "dp", axis=1, tiled=True),
    )
    preact = jnp.einsum("mld,ldf->mlf", arrived_rows, in_full, preferred_element_type=FLOAT_TYPE)
    hidden = jax.nn.gelu(preact).astype(HALF_TYPE)
    result = jnp.einsum("mlf,lfd->mld", hidden, out_full, preferred_element_type=FLOAT_TYPE).astype(
        HALF_TYPE
    )
    returned = lax.all_to_all(
        result.reshape(seq_count, capacity * local_experts, width),
        "seq",
        split_axis=0,
        concat_axis=0,
        tiled=True,
    )
    returned = returned.reshape(experts_all * capacity, width)
    combined = jnp.einsum("prk,pd->krd", dispatch_map, returned, preferred_element_type=FLOAT_TYPE)
    output = hidden_state + gate_weights[:, 0:1] * combined[0] + gate_weights[:, 1:2] * combined[1]
    error_rows = output - teacher.astype(FLOAT_TYPE)
    loss_local = jnp.sum(valid_float[:, None] * error_rows * error_rows)
    grad_out = 2.0 * tokens_all / count_all * valid_float[:, None] * error_rows
    grad_gate = jnp.einsum("krd,rd->rk", combined, grad_out)
    grad_chosen = gate_weights * (
        grad_gate - jnp.sum(gate_weights * grad_gate, axis=1, keepdims=True)
    )
    pick = (routes[:, :, None] == jnp.arange(experts_all, dtype=jnp.int32)[None, None, :]).astype(
        FLOAT_TYPE
    )
    grad_logits = jnp.sum(pick * grad_chosen[:, :, None], axis=1).astype(HALF_TYPE)
    grad_router = jnp.einsum("rd,re->de", moe_in, grad_logits, preferred_element_type=FLOAT_TYPE)
    grad_result = (jnp.transpose(gate_weights)[:, :, None] * grad_out[None]).astype(HALF_TYPE)
    grad_slots = jnp.einsum(
        "prk,krd->pd", dispatch_map, grad_result, preferred_element_type=FLOAT_TYPE
    ).astype(HALF_TYPE)
    grad_arrived = lax.all_to_all(
        grad_slots.reshape(seq_count, capacity * local_experts, width),
        "seq",
        split_axis=0,
        concat_axis=0,
        tiled=True,
    )
    grad_rows = grad_arrived.reshape(slot_rows, local_experts, width)
    grad_hidden = jnp.einsum("mld,lfd->mlf", grad_rows, out_full, preferred_element_type=FLOAT_TYPE)
    grad_preact = gelu_grad(preact, grad_hidden).astype(HALF_TYPE)
    grad_out_local = jnp.einsum(
        "mlf,mld->lfd", hidden, grad_rows, preferred_element_type=FLOAT_TYPE
    )
    grad_in_local = jnp.einsum(
        "mld,mlf->ldf", arrived_rows, grad_preact, preferred_element_type=FLOAT_TYPE
    )
    grad_entry = jnp.einsum(
        "mlf,ldf->mld", grad_preact, in_full, preferred_element_type=FLOAT_TYPE
    ).astype(HALF_TYPE)
    grad_w_in, grad_w_out = (
        lax.psum_scatter(
            grad_in_local.astype(jnp.bfloat16), "dp", scatter_dimension=1, tiled=True
        ).astype(jnp.float32),
        lax.psum_scatter(
            grad_out_local.astype(jnp.bfloat16), "dp", scatter_dimension=1, tiled=True
        ).astype(jnp.float32),
    )
    grad_back = lax.all_to_all(
        grad_entry.reshape(seq_count, capacity * local_experts, width),
        "seq",
        split_axis=0,
        concat_axis=0,
        tiled=True,
    )
    grad_back = grad_back.reshape(experts_all * capacity, width)
    grad_moe_in = jnp.einsum(
        "prk,pd->rd", dispatch_map, grad_back, preferred_element_type=FLOAT_TYPE
    )
    grad_moe_in = grad_moe_in + jnp.einsum(
        "re,de->rd", grad_logits, router_full, preferred_element_type=FLOAT_TYPE
    )
    grad_hidden_norm, grad_gain_second = norm_back(
        hidden_state, factor_two, gain_second, grad_moe_in
    )
    grad_state = grad_out + grad_hidden_norm
    grad_state_low = grad_state.astype(HALF_TYPE)
    grad_attn_w = jnp.einsum(
        "rd,re->de", attn_low, grad_state_low, preferred_element_type=FLOAT_TYPE
    )
    grad_attn_low = jnp.einsum(
        "re,de->rd", grad_state_low, attn_full, preferred_element_type=FLOAT_TYPE
    ).astype(HALF_TYPE)
    heads_dout = grad_attn_low.reshape(tok_rows, H, HEAD)
    softmax_dot = jnp.sum(
        jnp.transpose(heads_dout, (1, 0, 2)).astype(FLOAT_TYPE) * attn_heads, axis=2
    )
    row_stats = split_three(
        jnp.stack([jnp.transpose(log_total), jnp.transpose(softmax_dot)], axis=1)
    )

    def backward_step(running, shards, offset):
        key_rows = shards[0].reshape(shards[0].shape[0], H, HEAD)
        value_rows = shards[1].reshape(shards[1].shape[0], H, HEAD)
        query_rows = shards[2].reshape(shards[2].shape[0], H, HEAD)
        dout_rows = shards[3].reshape(shards[3].shape[0], H, HEAD)
        stats_rows = join_three(shards[4])
        piece_total = jnp.transpose(stats_rows[:, 0, :])
        piece_dot = jnp.transpose(stats_rows[:, 1, :])
        grad_query, grad_table, grad_key, grad_value = running

        def query_work(inner_state):
            inner_query, inner_table = inner_state
            raw_scores, allowed, bucket_hot = score_block(
                heads_q, key_rows, my_start, offset, rel_bias, edges
            )
            weights = jnp.where(allowed[None], jnp.exp(raw_scores - log_total[:, :, None]), 0.0)
            grad_prob = jnp.einsum(
                "qhd,khd->hqk", heads_dout, value_rows, preferred_element_type=FLOAT_TYPE
            )
            grad_score = (weights * (grad_prob - softmax_dot[:, :, None])).astype(HALF_TYPE)
            inner_query = (
                inner_query
                + jnp.einsum(
                    "hqk,khd->hqd", grad_score, key_rows, preferred_element_type=FLOAT_TYPE
                )
                * scale
            )
            inner_table = inner_table + jnp.einsum(
                "hqk,qkb->bh", grad_score.astype(FLOAT_TYPE), bucket_hot, precision=HIGH
            )
            return (inner_query, inner_table)

        def key_work(inner_state):
            inner_key, inner_value = inner_state
            raw_scores, allowed, _ = score_block(
                query_rows, heads_k, offset, my_start, rel_bias, edges
            )
            weights = jnp.where(allowed[None], jnp.exp(raw_scores - piece_total[:, :, None]), 0.0)
            inner_value = inner_value + jnp.einsum(
                "hqk,qhd->khd",
                weights.astype(HALF_TYPE),
                dout_rows,
                preferred_element_type=FLOAT_TYPE,
            )
            grad_prob = jnp.einsum(
                "qhd,khd->hqk", dout_rows, heads_v, preferred_element_type=FLOAT_TYPE
            )
            grad_score = (weights * (grad_prob - piece_dot[:, :, None])).astype(HALF_TYPE)
            inner_key = (
                inner_key
                + jnp.einsum(
                    "hqk,qhd->khd", grad_score, query_rows, preferred_element_type=FLOAT_TYPE
                )
                * scale
            )
            return (inner_key, inner_value)

        grad_query, grad_table = lax.cond(
            offset <= last_row,
            query_work,
            lambda inner_state: inner_state,
            (grad_query, grad_table),
        )
        grad_key, grad_value = lax.cond(
            offset + shards[0].shape[0] - 1 >= my_start,
            key_work,
            lambda inner_state: inner_state,
            (grad_key, grad_value),
        )
        return (grad_query, grad_table, grad_key, grad_value)

    back_start = (
        jnp.zeros((H, tok_rows, HEAD), FLOAT_TYPE),
        jnp.zeros((BUCKETS, H), FLOAT_TYPE),
        jnp.zeros((tok_rows, H, HEAD), FLOAT_TYPE),
        jnp.zeros((tok_rows, H, HEAD), FLOAT_TYPE),
    )
    grad_query, grad_table_local, grad_key, grad_value = in_sections(
        backward_step,
        back_start,
        (
            lax.all_gather(key_low, "seq", axis=0, tiled=True),
            lax.all_gather(value_low, "seq", axis=0, tiled=True),
            lax.all_gather(query_low, "seq", axis=0, tiled=True),
            lax.all_gather(grad_attn_low, "seq", axis=0, tiled=True),
            lax.all_gather(row_stats, "seq", axis=0, tiled=True),
        ),
    )
    grad_qkv_low = jnp.concatenate(
        [
            jnp.transpose(grad_query, (1, 0, 2)).reshape(tok_rows, width),
            grad_key.reshape(tok_rows, width),
            grad_value.reshape(tok_rows, width),
        ],
        axis=1,
    ).astype(HALF_TYPE)
    grad_qkv_w = jnp.einsum("rd,re->de", normed_in, grad_qkv_low, preferred_element_type=FLOAT_TYPE)
    grad_normed_one = jnp.einsum(
        "re,de->rd", grad_qkv_low, qkv_full, preferred_element_type=FLOAT_TYPE
    )
    grad_in_norm, grad_gain_first = norm_back(inputs, factor_one, gain_first, grad_normed_one)
    grad_tokens = grad_state + grad_in_norm
    grad_qkv_own, grad_attn_own, grad_router_own, grad_gain_attn, grad_gain_moe = (
        lax.psum_scatter(grad_qkv_w, ("dp", "seq"), scatter_dimension=0, tiled=True),
        lax.psum_scatter(grad_attn_w, ("dp", "seq"), scatter_dimension=0, tiled=True),
        lax.psum_scatter(grad_router, ("dp", "seq"), scatter_dimension=0, tiled=True),
        lax.psum_scatter(grad_gain_first, ("dp", "seq"), scatter_dimension=0, tiled=True),
        lax.psum_scatter(grad_gain_second, ("dp", "seq"), scatter_dimension=0, tiled=True),
    )
    loss_sum, grad_table = lax.psum((loss_local, grad_table_local), ("dp", "seq"))
    loss = loss_sum / (count_all * width)
    return (
        output,
        loss,
        grad_tokens,
        grad_qkv_own,
        grad_attn_own,
        grad_gain_attn,
        grad_gain_moe,
        grad_router_own,
        grad_table,
        grad_w_in,
        grad_w_out,
    )


MESH = pl.DeviceIdType.MESH
ANY = pl.BlockSpec(memory_space=pl.ANY)
VM = pl.BlockSpec(memory_space=pltpu.VMEM)
ROLL = 1280
GW = 1152


def remote(src, dst, send, recv, dev):
    return pltpu.make_async_remote_copy(
        src_ref=src, dst_ref=dst, send_sem=send, recv_sem=recv, device_id=dev, device_id_type=MESH
    )


def place():
    d = lax.axis_index("dp")
    s = lax.axis_index("seq")
    return d, s, s // 2, lax.rem(s, 2)


def comm_call(body, outs, n_in, cid, scratch, name, in_specs=None, out_specs=None, vmem=None):
    return pl.pallas_call(
        body,
        out_shape=outs,
        in_specs=in_specs or [ANY] * n_in,
        out_specs=out_specs or [ANY] * len(outs),
        scratch_shapes=scratch,
        compiler_params=pltpu.CompilerParams(
            collective_id=cid, has_side_effects=True, vmem_limit_bytes=vmem
        ),
        name=name,
    )


def sds(shape, dtype=jnp.bfloat16):
    return jax.ShapeDtypeStruct(shape, dtype)


def head_mask(h):
    lane = lax.broadcasted_iota(jnp.int32, (1, 192), 1)
    return lane // HEAD == h


def dot_t(a, b):
    return lax.dot_general(a, b, (((1,), (1,)), ((), ())), preferred_element_type=jnp.float32)


def dot_l(a, b):
    return lax.dot_general(a, b, (((0,), (0,)), ((), ())), preferred_element_type=jnp.float32)


def dot_n(a, b):
    return jnp.dot(a, b, preferred_element_type=jnp.float32)


def soft_rows(q, keys, g_ref, h, start, width):
    s = dot_t(q, keys) * HEAD ** (-0.5) + g_ref[h, :, pl.ds(start, width)]
    m = jnp.max(s, axis=1, keepdims=True)
    p = jnp.exp(s - m)
    return p / jnp.sum(p, axis=1, keepdims=True)


CHUNK = 768
GELU_A = 0.7978845608028654
GELU_B = 0.044715


class Sems:
    def __init__(self, send, recv):
        self.send, self.recv, self.n = send, recv, 0

    def copy(self, src, dst, dev):
        cp = remote(src, dst, self.send.at[self.n], self.recv.at[self.n], dev)
        self.n += 1
        return cp


def run(copies):
    for cp in copies:
        cp.start()
    return copies


def received(copies):
    for cp in copies:
        cp.wait_recv()


def sent(copies):
    for cp in copies:
        cp.wait_send()


def chips():
    d, s, z, c = place()
    me = z * 4 + d
    numbers = [lax.rem(me + k, 16) for k in range(1, 16)]
    return me, numbers, [(lax.rem(t, 4), 2 * (t // 4) + c) for t in numbers]


def rms(v):
    return lax.rsqrt(jnp.mean(v * v, axis=1, keepdims=True) + EPS)


def step_kernel(
    x,
    w_qkv,
    w_attn,
    w_router,
    gain_a,
    gain_m,
    rel_bias,
    spots,
    routes_t,
    valid_t,
    teacher,
    w_in,
    w_out,
    output,
    grad_tokens,
    grad_qkv,
    grad_rest,
    extra,
    oin,
    oout,
    wq,
    wqf,
    wrf,
    xs,
    n1s,
    q,
    kf,
    vf,
    bias,
    lines,
    out_v,
    attn,
    leave,
    arrived,
    win,
    wout,
    slope,
    hid,
    acc,
    back,
    gback,
    entry,
    gin,
    gout,
    hidden_v,
    gout_v,
    do_out,
    do,
    rest,
    rest_in,
    rest_got,
    kacc,
    vacc,
    gacc,
    dk_out,
    dv_out,
    dk_in,
    dv_in,
    dqkv,
    part,
    parts,
    wpart,
    wpart_in,
    wgot,
    small,
    shared,
    ss,
    rs,
    xe,
    re,
    oe,
    ore,
    ls,
):
    f32, bf16 = jnp.float32, jnp.bfloat16
    d, s, z, c = place()
    sib = (d, s + 1 - 2 * c)
    across = (d + 1 - 2 * lax.rem(d, 2), lax.rem(d + 2, 4), 3 - d)
    plane = [(j, s) for j in across]
    zs = [(d, 2 * lax.rem(z + k, 4) + c) for k in (1, 2, 3)]
    me, numbers, others = chips()
    device = d * 8 + s
    everyone = [(lax.rem(d + k // 8, 4), lax.rem(s + k % 8, 8)) for k in range(1, 32)]
    sems = Sems(ss, rs)
    barrier = pltpu.get_barrier_semaphore()
    for peer in everyone:
        pl.semaphore_signal(barrier, inc=1, device_id=peer, device_id_type=MESH)

    valid_row = valid_t[...].astype(f32)
    diag = lax.broadcasted_iota(jnp.int32, (128, 128), 0) == lax.broadcasted_iota(
        jnp.int32, (128, 128), 1
    )
    lines[...] = jnp.zeros_like(lines)
    lines[0:1, :24] = gain_a[...].astype(f32)
    lines[1:2, :24] = gain_m[...].astype(f32)
    lines[2:3, :24] = jnp.broadcast_to(jnp.sum(valid_row, axis=1, keepdims=True), (1, 24))
    turned = jnp.transpose(lines[:, :128])[:24, :8]
    for zt in range(4):
        for i in range(3):
            at = i * 768 + zt * 192
            wq[zt, :, i * 192 : (i + 1) * 192] = w_qkv[:, at : at + 192]
        wq[zt, :, 576:] = jnp.zeros((24, 128), bf16)
        wq[zt, :, 576:592] = w_router[...]
        wq[zt, :, 592:600] = turned.astype(bf16)
    pl.semaphore_wait(barrier, 31)

    def rows_of(ref, dd, zz, cc):
        return ref.at[pl.ds(pl.multiple_of(((dd * 4 + zz) * 2 + cc) * 24, 8), 24)]

    def column_rows(ref, dd, dev):
        copies = []
        for zz in range(4):
            spot = rows_of(ref, dd, zz, c)
            copies.append(sems.copy(spot, spot, dev))
        return run(copies)

    local = [
        pltpu.make_async_copy(wq.at[z], rows_of(wqf, d, z, c), ls.at[0]),
        pltpu.make_async_copy(w_attn, rows_of(wrf, d, z, c), ls.at[1]),
        pltpu.make_async_copy(x, xs.at[z], ls.at[2]),
    ]
    run(local)
    stage1 = run(
        [
            sems.copy(wq.at[lax.rem(z + k, 4)], rows_of(wqf, d, z, c), zs[i])
            for i, k in enumerate((1, 2, 3))
        ]
    )

    bulk = []

    def piece(m, dd, half):
        if m == 0:
            return win.at[pl.ds(pl.multiple_of(dd * 192 + half * 96, 32), 96)]
        return wout.at[pl.ds(pl.multiple_of(dd * 768 + half * 384, 128), 384)]

    sources = (w_in, w_out)

    def expert_send(m, i, half):
        j = across[i]

        def make():
            return remote(
                sources[m].at[lax.rem(j, 2), half],
                piece(m, d, half),
                xe.at[m, i, half],
                re.at[m, i],
                (j, 2 * z + half),
            )

        @pl.when(j // 2 == c)
        def _():
            make().start()

        bulk.append((j // 2 == c, make))

    def own_here(m, half):
        return pltpu.make_async_copy(
            sources[m].at[lax.rem(d, 2), half], piece(m, d, half), ls.at[3 + 2 * m + half]
        )

    def own_there(m, half):
        return remote(
            sources[m].at[lax.rem(d, 2), half],
            piece(m, d, half),
            xe.at[m, 3, half],
            re.at[m, 3 + half],
            sib,
        )

    def expert_own(m):
        @pl.when(d // 2 == c)
        def _():
            for half in range(2):
                own_here(m, half).start()
                own_there(m, half).start()

    def expert_own_done(m):
        @pl.when(d // 2 == c)
        def _():
            for half in range(2):
                own_here(m, half).wait()
                own_there(m, half).wait_send()

        @pl.when(d // 2 != c)
        def _():
            for half in range(2):
                own_there(m, half).wait_recv()

    def expert_pass(m, i):
        spot = piece(m, across[i], c)
        remote(spot, spot, xe.at[m, i, 0], re.at[m, i], sib).wait_recv()
        return sems.copy(spot, spot, sib)

    expert_send(0, 0, 0)
    expert_send(0, 1, 0)
    rest1 = run([sems.copy(w_attn, rows_of(wrf, d, z, c), zs[i]) for i in range(3)])
    rows = run([sems.copy(x, xs.at[z], zs[i]) for i in range(3)])

    bucket = lax.broadcasted_iota(jnp.int32, (BUCKETS, ROLL), 0)
    hot = (bucket == spots[...]).astype(f32)
    table = lax.dot_general(
        rel_bias[...], hot, (((0,), (0,)), ((), ())), precision=HIGH, preferred_element_type=f32
    )
    lines[:12] = table + jnp.where(spots[...] >= BUCKETS, NEG, 0.0)
    for h in range(3):
        row = jnp.broadcast_to(lines[pl.ds(3 * z + h, 1), :], (128, ROLL))
        bias[h] = pltpu.roll(row, 0, 1, stride=1, stride_axis=0)[:, 128:]
    for cp in local:
        cp.wait()
    received(stage1)
    stage2 = [column_rows(wqf, d, dev) for dev in plane]
    stage3 = column_rows(wqf, d, sib)
    received(rest1)
    rest2 = [column_rows(wrf, d, dev) for dev in plane]
    rest3 = column_rows(wrf, d, sib)
    for i, k in ((0, 1), (1, 1), (2, 0), (2, 1)):
        expert_send(0, i, k)
    expert_own(0)
    expert_own(1)
    for i, dd in enumerate(across):
        received(stage2[i])
        stage3 += column_rows(wqf, dd, sib)
    received(stage3)
    misc = jnp.transpose(wqf[:, 576:704].astype(f32))
    gain_first = misc[16:17]
    gain_second = misc[17:18]
    count = jnp.sum(misc[18:19], axis=1, keepdims=True) / 24.0

    pairs = []
    for i in range(4):
        zb = lax.rem(z + 4 - i, 4)
        if i > 0:
            rows[i - 1].wait_recv()
        xf = xs[zb].astype(f32)
        n1 = (xf * rms(xf) * gain_first).astype(bf16)
        n1s[zb] = n1
        qkv = dot_n(n1, wqf[:, :576]).astype(bf16)
        q[zb] = qkv[:, :192]
        kf[zb, c] = qkv[:, 192:384]
        vf[zb, c] = qkv[:, 384:]
        pairs += run(
            [
                sems.copy(kf.at[zb, c], kf.at[zb, c], sib),
                sems.copy(vf.at[zb, c], vf.at[zb, c], sib),
            ]
        )
    for i, dd in enumerate(across):
        received(rest2[i])
        rest3 += column_rows(wrf, dd, sib)
    expert_send(1, 0, 0)
    expert_send(1, 1, 0)
    received(pairs)
    first = sems.n
    sems.n += 4
    for zb in (3, 2, 1, 0):
        width = 256 * (zb + 1)
        start = pl.multiple_of(128 * (7 - 2 * zb) - 128 * c, 128)
        keys = kf[: zb + 1].reshape(width, 192)
        values = vf[: zb + 1].reshape(width, 192)
        mixed = jnp.zeros((128, 192), f32)
        for h in range(3):
            qh = jnp.where(head_mask(h), q[zb], jnp.zeros((), bf16))
            p = soft_rows(qh, keys, bias, h, start, width).astype(bf16)
            mixed = mixed + jnp.where(head_mask(h), dot_n(p, values), 0.0)
        out_v[zb] = mixed.astype(bf16)

        @pl.when(z != zb)
        def _(zb=zb):
            remote(
                out_v.at[zb], attn.at[z], ss.at[first + zb], rs.at[first + z], (d, 2 * zb + c)
            ).start()

        @pl.when(z == zb)
        def _(zb=zb):
            attn[zb] = out_v[zb]

    received(rest3)
    for zb in range(4):

        @pl.when(z != zb)
        def _(zb=zb):
            remote(
                out_v.at[zb], attn.at[zb], ss.at[first + zb], rs.at[first + zb], (d, 2 * zb + c)
            ).wait()

    hidden = x[...].astype(f32)
    for zb in range(4):
        hidden = hidden + dot_n(attn[zb], wrf[192 * zb : 192 * (zb + 1), :])
    hidden_v[...] = hidden
    n2 = (hidden * rms(hidden) * gain_second).astype(bf16)
    logits = dot_n(n2, wqf[:, 576:704])
    lane = lax.broadcasted_iota(jnp.int32, (128, 128), 1)

    def column(row):
        return jnp.sum(jnp.where(diag, row, jnp.zeros_like(row)), axis=1, keepdims=True)

    route = [column(routes_t[i : i + 1, :]) for i in range(2)]
    picks = [(lane == r).astype(f32) for r in route]
    chosen = [
        jnp.sum(jnp.where(lane == r, logits, 0.0), axis=1, keepdims=True) for r in route
    ]
    top = jnp.maximum(chosen[0], chosen[1])
    powers = [jnp.exp(v - top) for v in chosen]
    gate = [v / (powers[0] + powers[1]) for v in powers]
    lower = (lax.broadcasted_iota(jnp.int32, (128, 128), 0) > lane).astype(bf16)
    before = dot_n(lower, (picks[0] + picks[1]).astype(bf16))
    wide = lax.broadcasted_iota(jnp.int32, (128, 512), 1)
    maps = []
    for i in range(2):
        slot = jnp.sum(picks[i] * before, axis=1, keepdims=True).astype(jnp.int32)
        maps.append((wide == route[i] * 32 + slot).astype(f32).astype(bf16))
    chart = maps[0] + maps[1]
    leave[...] = dot_l(chart, n2).astype(bf16).reshape(16, 32, 768)

    def spread_rows(src, dst):
        copies = run([sems.copy(src.at[t], dst.at[me], dev) for t, dev in zip(numbers, others)])
        dst[pl.ds(me, 1)] = src[pl.ds(me, 1)]
        return copies

    out = spread_rows(leave, arrived)
    for i, k in ((0, 1), (1, 1), (2, 0), (2, 1)):
        expert_send(1, i, k)
    passed = [expert_pass(0, i) for i in range(3)]
    run(passed)
    expert_own_done(0)
    received(passed)
    received(out)
    sent(out)

    def forward_step(f, carry):
        at = pl.multiple_of(f * CHUNK, CHUNK)
        for r in (0, 256):
            pre = dot_n(arrived[r // 32 : r // 32 + 8].reshape(256, 768), win[:, pl.ds(at, CHUNK)])
            t = jnp.tanh(GELU_A * (pre + GELU_B * pre * pre * pre))
            half = 0.5 * (1.0 + t)
            hid[r : r + 256, pl.ds(at, CHUNK)] = (pre * half).astype(bf16)
            slope[r : r + 256, pl.ds(at, CHUNK)] = half + 0.5 * pre * (1.0 - t * t) * (
                GELU_A * (1.0 + 3.0 * GELU_B * pre * pre)
            )
        return carry

    lax.fori_loop(0, 4, forward_step, 0)
    passed_out = [expert_pass(1, i) for i in range(3)]
    run(passed_out)
    expert_own_done(1)
    received(passed_out)
    acc[...] = jnp.zeros_like(acc)

    def result_step(f, carry):
        at = pl.multiple_of(f * CHUNK, CHUNK)
        for r in (0, 256):
            acc[r : r + 256] += dot_n(
                hid[r : r + 256, pl.ds(at, CHUNK)], wout[pl.ds(at, CHUNK), :]
            )
        return carry

    lax.fori_loop(0, 4, result_step, 0)
    leave[...] = acc[...].astype(bf16).reshape(16, 32, 768)
    results = spread_rows(leave, back)
    sent(stage1 + rows + rest1 + stage3 + pairs + rest3 + sum(stage2 + rest2, []))
    sent(passed + passed_out)
    for held, make in bulk:

        @pl.when(held)
        def _(make=make):
            make().wait_send()

    received(results)
    sent(results)

    combined = [dot_n(m, back[...].reshape(512, 768)) for m in maps]
    hidden = hidden_v[...]
    result = hidden + gate[0] * combined[0] + gate[1] * combined[1]
    output[...] = result
    error = result - teacher[...].astype(f32)
    masked = column(valid_row) * error
    loss = jnp.sum(jnp.sum(masked * error, axis=1, keepdims=True), axis=0, keepdims=True)
    grad_out = (2.0 * 4096.0) / count * masked
    gout_v[...] = grad_out
    leave[...] = (
        (
            dot_l(maps[0], (gate[0] * grad_out).astype(bf16))
            + dot_l(maps[1], (gate[1] * grad_out).astype(bf16))
        )
        .astype(bf16)
        .reshape(16, 32, 768)
    )
    grads = spread_rows(leave, gback)
    dgate = [jnp.sum(m * grad_out, axis=1, keepdims=True) for m in combined]
    mean = gate[0] * dgate[0] + gate[1] * dgate[1]
    grad_logits = jnp.zeros((128, 128), f32)
    for i in range(2):
        grad_logits = grad_logits + jnp.where(
            lane == route[i], gate[i] * (dgate[i] - mean), 0.0
        )
    grad_logits = grad_logits.astype(bf16)
    acc[...] = jnp.zeros_like(acc)
    received(grads)
    sent(grads)

    def backward_step(f, carry):
        at = pl.multiple_of(f * CHUNK, CHUNK)
        for r in (0, 256):
            dh = dot_t(gback[r // 32 : r // 32 + 8].reshape(256, 768), wout[pl.ds(at, CHUNK), :])
            dp = (dh * slope[r : r + 256, pl.ds(at, CHUNK)]).astype(bf16)
            slope[r : r + 256, pl.ds(at, CHUNK)] = dp.astype(f32)
            acc[r : r + 256] += dot_t(dp, win[:, pl.ds(at, CHUNK)])
        return carry

    lax.fori_loop(0, 4, backward_step, 0)
    leave[...] = acc[...].astype(bf16).reshape(16, 32, 768)
    entries = spread_rows(leave, entry)

    swap_out = sems.n
    sems.n += 8

    def half_out(f):
        return remote(
            piece(1, f, 1 - c), gout.at[f], ss.at[swap_out + f], rs.at[swap_out + f], sib
        )

    def half_in(f):
        at = swap_out + 4 + f
        return remote(piece(0, f, 1 - c), gin.at[f], ss.at[at], rs.at[at], sib)

    def out_step(f, carry):
        at = pl.multiple_of(f * CHUNK, CHUNK)
        wout[pl.ds(at, CHUNK), :] = dot_l(
            hid[:, pl.ds(at, CHUNK)], gback[...].reshape(512, 768)
        ).astype(bf16)
        half_out(f).start()
        return carry

    lax.fori_loop(0, 4, out_step, 0)

    owned = []

    def owner_send(m, i):
        src, dst = ((gin, oin), (gout, oout))[m]
        cp = remote(
            src.at[across[i]],
            dst.at[lax.rem(d, 2), c],
            oe.at[m, i],
            ore.at[m, lax.rem(d, 2), c],
            (across[i], 2 * z + d // 2),
        )
        cp.start()
        owned.append(cp)

    def owner_here(m):
        src, dst = ((gin, oin), (gout, oout))[m]
        return pltpu.make_async_copy(src.at[d], dst.at[lax.rem(d, 2), c], ls.at[7 + m])

    def owner_there(m):
        src, dst = ((gin, oin), (gout, oout))[m]
        return remote(
            src.at[d], dst.at[lax.rem(d, 2), c], oe.at[m, 3], ore.at[m, lax.rem(d, 2), c], sib
        )

    def owner_local(m):
        @pl.when(d // 2 == c)
        def _():
            owner_here(m).start()

        @pl.when(d // 2 != c)
        def _():
            owner_there(m).start()

    def add_half(m, f):
        ref, rows_n = ((gin, 96), (gout, 384))[m]
        spot = (
            pl.ds(pl.multiple_of(f * 192 + c * 96, 32), 96)
            if m == 0
            else pl.ds(pl.multiple_of(f * 768 + c * 384, 128), 384)
        )
        mine = (win if m == 0 else wout)[spot, :]
        ref[f] = (mine.astype(f32) + ref[f].astype(f32)).astype(bf16)

    for f in range(4):
        half_out(f).wait()
        add_half(1, f)
    for i in range(3):
        owner_send(1, i)
    owner_local(1)

    def in_step(f, carry):
        at = pl.multiple_of(f * CHUNK, CHUNK)
        win[:, pl.ds(at, CHUNK)] = dot_l(
            arrived[...].reshape(512, 768), slope[:, pl.ds(at, CHUNK)].astype(bf16)
        ).astype(bf16)
        return carry

    lax.fori_loop(0, 4, in_step, 0)
    for f in range(4):
        half_in(f).start()
    received(entries)
    sent(entries)

    dn2 = dot_n(chart, entry[...].reshape(512, 768))
    dn2 = dn2 + dot_t(grad_logits, wqf[:, 576:704])
    hidden = hidden_v[...]
    r2 = rms(hidden)
    scaled = dn2 * gain_second
    mean = jnp.mean(scaled * hidden, axis=1, keepdims=True)
    dh = gout_v[...] + r2 * scaled - hidden * (r2 * r2 * r2) * mean
    dh_low = dh.astype(bf16)
    for zb in range(4):
        do_out[zb] = dot_t(dh_low, wrf[192 * zb : 192 * (zb + 1), :]).astype(bf16)
    heads = run(
        [
            sems.copy(do_out.at[lax.rem(z + k, 4)], do.at[z], zs[i])
            for i, k in enumerate((1, 2, 3))
        ]
    )
    do[pl.ds(z, 1)] = do_out[pl.ds(z, 1)]
    grad_tokens[...] = dh

    for zb in range(4):
        rest[192 * zb : 192 * (zb + 1), :768] = dot_l(attn[zb], dh_low).astype(bf16)
    gain_rows = jnp.broadcast_to(jnp.sum(dn2 * hidden * r2, axis=0, keepdims=True), (128, 768))
    n2 = (hidden * r2 * gain_second).astype(bf16)
    tall = lax.broadcasted_iota(jnp.int32, (768, 128), 1)
    rest[:, 768:] = jnp.where(
        tall == 16, jnp.transpose(gain_rows), dot_l(n2, grad_logits)
    ).astype(bf16)
    rest_swap = run([sems.copy(rest, rest_in, sib)])
    for f in range(4):
        half_in(f).wait()
        add_half(0, f)
    received(rest_swap)
    sent(rest_swap)
    rest_in[...] = (rest[...].astype(f32) + rest_in[...].astype(f32)).astype(bf16)

    def chip_rows(ref, t):
        return rows_of(ref, lax.rem(t, 4), t // 4, c)

    here_rows = pl.ds(pl.multiple_of(me * 24, 8), 24)

    def to_owners(src, dst):
        return run(
            [
                sems.copy(chip_rows(src, t), dst.at[here_rows], dev)
                for t, dev in zip(numbers, others)
            ]
        )

    rest_sent = to_owners(rest_in, rest_got)
    for i in range(3):
        owner_send(0, i)
    owner_local(0)
    kacc[...] = jnp.zeros_like(kacc)
    vacc[...] = jnp.zeros_like(vacc)
    gacc[...] = jnp.zeros_like(gacc)
    received(heads)

    scale = HEAD ** (-0.5)
    for zb in (3, 2, 1, 0):
        width = 256 * (zb + 1)
        start = pl.multiple_of(128 * (7 - 2 * zb) - 128 * c, 128)
        keys = kf[: zb + 1].reshape(width, 192)
        values = vf[: zb + 1].reshape(width, 192)
        dq = jnp.zeros((128, 192), f32)
        for h in range(3):
            mask = head_mask(h)
            qh = jnp.where(mask, q[zb], jnp.zeros((), bf16))
            doh = jnp.where(mask, do[zb], jnp.zeros((), bf16))
            p = soft_rows(qh, keys, bias, h, start, width)
            vacc[:width] += dot_l(p.astype(bf16), doh)
            dp = dot_t(doh, values)
            dot = jnp.sum(p * dp, axis=1, keepdims=True)
            ds = (p * (dp - dot)).astype(bf16)
            gacc[h, :, pl.ds(start, width)] += ds.astype(f32)
            dq = dq + jnp.where(mask, dot_n(ds, keys), 0.0)
            kacc[:width] += dot_l(ds, qh)
        dqkv[zb, :, :192] = (dq * scale).astype(bf16)
    for zb in range(4):
        there = pl.ds(pl.multiple_of((2 * zb + 1 - c) * 128, 128), 128)
        dk_out[zb] = (kacc[there] * scale).astype(bf16)
        dv_out[zb] = vacc[there].astype(bf16)
    swaps = run([sems.copy(dk_out, dk_in, sib), sems.copy(dv_out, dv_in, sib)])

    row = lax.broadcasted_iota(jnp.int32, (128, 1), 0)
    sums = []
    for h in range(3):
        y = jnp.concatenate([jnp.zeros((128, ROLL - GW), f32), gacc[h]], axis=1)
        for bit in range(7):
            y = jnp.where((row >> bit) & 1 == 1, pltpu.roll(y, ROLL - (1 << bit), 1), y)
        sums.append(jnp.sum(y, axis=0, keepdims=True))
    bucket = lax.broadcasted_iota(jnp.int32, (128, ROLL), 0)
    hot = (bucket == spots[...]).astype(f32)
    table = lax.dot_general(
        jnp.concatenate(sums + [jnp.zeros((5, ROLL), f32)], axis=0),
        hot,
        (((1,), (1,)), ((), ())),
        precision=HIGH,
        preferred_element_type=f32,
    )
    index = lax.broadcasted_iota(jnp.int32, (8, 128), 0)
    small[...] = jnp.where(index == 3, loss, table)
    shares = run([sems.copy(small, shared.at[device], dev) for dev in everyone])
    shared[pl.ds(device, 1)] = small[...][None]

    received(swaps)
    first_back = sems.n
    sems.n += 4
    gain_part = jnp.zeros((1, 768), f32)
    for zb in (3, 2, 1, 0):
        here = pl.ds(pl.multiple_of((2 * zb + c) * 128, 128), 128)
        dqkv[zb, :, 192:384] = (kacc[here] * scale + dk_in[zb].astype(f32)).astype(bf16)
        dqkv[zb, :, 384:] = (vacc[here] + dv_in[zb].astype(f32)).astype(bf16)
        dn1 = dot_t(dqkv[zb], wqf[:, :576])
        part[zb] = dn1.astype(bf16)

        @pl.when(z != zb)
        def _(zb=zb):
            remote(
                part.at[zb],
                parts.at[z],
                ss.at[first_back + zb],
                rs.at[first_back + z],
                (d, 2 * zb + c),
            ).start()

        @pl.when(z == zb)
        def _(zb=zb):
            parts[zb] = part[zb]

        xf = xs[zb].astype(f32)
        gain_part = gain_part + jnp.sum(dn1 * xf * rms(xf), axis=0, keepdims=True)
    wpart[:, :576] = dot_l(n1s[...].reshape(512, 768), dqkv[...].reshape(512, 576)).astype(bf16)
    wpart[:, 576:] = jnp.transpose(jnp.broadcast_to(gain_part, (128, 768))).astype(bf16)
    wswap = run([sems.copy(wpart, wpart_in, sib)])
    received(wswap)
    sent(wswap)
    wpart_in[...] = (wpart[...].astype(f32) + wpart_in[...].astype(f32)).astype(bf16)
    wsent = to_owners(wpart_in, wgot)

    for zb in range(4):

        @pl.when(z != zb)
        def _(zb=zb):
            remote(
                part.at[zb],
                parts.at[zb],
                ss.at[first_back + zb],
                rs.at[first_back + zb],
                (d, 2 * zb + c),
            ).wait()

    dn1 = (
        parts[0].astype(f32) + parts[1].astype(f32) + parts[2].astype(f32) + parts[3].astype(f32)
    )
    xf = x[...].astype(f32)
    r1 = rms(xf)
    scaled = dn1 * gain_first
    mean = jnp.mean(scaled * xf, axis=1, keepdims=True)
    grad_tokens[...] += r1 * scaled - xf * (r1 * r1 * r1) * mean

    own_rows = [
        pltpu.make_async_copy(chip_rows(rest_in, me), rest_got.at[here_rows], ls.at[9]),
        pltpu.make_async_copy(chip_rows(wpart_in, me), wgot.at[here_rows], ls.at[10]),
    ]
    run(own_rows)

    received(shares)
    by_z = []
    for zb in range(4):
        total = jnp.zeros((8, 128), f32)
        for dd in range(4):
            for cc in range(2):
                total = total + shared[(dd * 4 + zb) * 2 + cc]
        by_z.append(total)
    loss_all = by_z[0] + by_z[1] + by_z[2] + by_z[3]
    extra[0:8] = loss_all[3:4] / (count * 768.0) + jnp.zeros((8, 128), f32)
    for zb in range(4):
        extra[8 + 8 * zb : 16 + 8 * zb] = by_z[zb]

    received(rest_sent)
    received(wsent)
    for cp in own_rows:
        cp.wait()
    total = jnp.zeros((24, 896), f32)
    gain_total = jnp.zeros((24, 128), f32)
    for zb in range(4):
        block = jnp.zeros((24, 576), f32)
        for dd in range(4):
            r = (zb * 4 + dd) * 24
            total = total + rest_got[r : r + 24, :].astype(f32)
            block = block + wgot[r : r + 24, :576].astype(f32)
            gain_total = gain_total + wgot[r : r + 24, 576:].astype(f32)
        for i in range(3):
            at = i * 768 + zb * 192
            grad_qkv[:, at : at + 192] = block[:, i * 192 : (i + 1) * 192]
    grad_rest[:, :896] = total
    grad_rest[:, 896:] = gain_total

    for m, (src, dst) in enumerate(((gin, oin), (gout, oout))):
        for l in range(2):
            for half in range(2):
                here = (2 * c + l == d) & (c == half)

                @pl.when(jnp.logical_not(here))
                def _(src=src, dst=dst, m=m, l=l, half=half):
                    remote(
                        src.at[0], dst.at[l, half], oe.at[m, 3], ore.at[m, l, half], sib
                    ).wait_recv()

        @pl.when(d // 2 == c)
        def _(m=m):
            owner_here(m).wait()

        @pl.when(d // 2 != c)
        def _(m=m):
            owner_there(m).wait_send()

    sent(heads + rest_sent + swaps + shares + wsent + owned)


def finish_kernel(
    oin, oout, output, tokens, qkv, rest, extra, gin, gout, o, t, g, w, r, ga, gm, table, loss
):
    f32 = jnp.float32
    gin[...] = oin[...].astype(f32)
    gout[...] = oout[...].astype(f32)

    @pl.when(pl.program_id(0) == 0)
    def _():
        o[...] = output[...]
        t[...] = tokens[...]
        g[...] = qkv[...]
        w[...] = rest[:, :768]
        r[...] = rest[:, 768:784]
        turned = jnp.transpose(
            jnp.concatenate([rest[:, 768:1024], jnp.zeros((104, 256), f32)], axis=0)
        )
        gm[...] = turned[16:17, :24]
        ga[...] = turned[128:129, :24]
        for zb in range(4):
            tall = jnp.transpose(
                jnp.concatenate(
                    [extra[8 + 8 * zb : 16 + 8 * zb], jnp.zeros((120, 128), f32)], axis=0
                )
            )
            table[:, 3 * zb : 3 * zb + 3] = tall[:BUCKETS, :3]
        loss[...] = extra[0:1, 0:1]


def fast_path(
    tokens,
    w_qkv,
    w_attn_out,
    gain_attn,
    gain_moe,
    w_router,
    rel_bias,
    w_in,
    w_out,
    teacher,
    routes,
    valid,
    buckets,
):
    f32, bf16 = jnp.float32, jnp.bfloat16
    none = BUCKETS + 96
    spots = jnp.concatenate(
        [
            jnp.full((1,), none, jnp.int32),
            buckets[::-1],
            jnp.full((ROLL - 1025,), none, jnp.int32),
        ]
    )[None]
    block = pltpu.VMEM((16, 32, 768), bf16)
    heads = pltpu.VMEM((4, 128, 192), bf16)
    both = pltpu.VMEM((4, 2, 128, 192), bf16)
    wide = pltpu.VMEM((4, 128, 768), bf16)
    output, grad_tokens, grad_qkv, grad_rest, extra, oin, oout = comm_call(
        step_kernel,
        [
            sds((128, 768), f32),
            sds((128, 768), f32),
            sds((24, 2304), f32),
            sds((24, 1024), f32),
            sds((40, 128), f32),
            sds((2, 2, 96, 3072)),
            sds((2, 2, 384, 768)),
        ],
        13,
        1,
        [
            pltpu.VMEM((4, 24, 704), bf16),
            pltpu.VMEM((768, 704), bf16),
            pltpu.VMEM((768, 768), bf16),
            wide,
            wide,
            heads,
            both,
            both,
            pltpu.VMEM((3, 128, GW), f32),
            pltpu.VMEM((16, ROLL), f32),
            heads,
            heads,
            block,
            block,
            pltpu.VMEM((768, 3072), bf16),
            pltpu.VMEM((3072, 768), bf16),
            pltpu.VMEM((512, 3072), f32),
            pltpu.VMEM((512, 3072), bf16),
            pltpu.VMEM((512, 768), f32),
            block,
            block,
            block,
            pltpu.VMEM((4, 96, 3072), bf16),
            pltpu.VMEM((4, 384, 768), bf16),
            pltpu.VMEM((128, 768), f32),
            pltpu.VMEM((128, 768), f32),
            heads,
            heads,
            pltpu.VMEM((768, 896), bf16),
            pltpu.VMEM((768, 896), bf16),
            pltpu.VMEM((384, 896), bf16),
            pltpu.VMEM((1024, 192), f32),
            pltpu.VMEM((1024, 192), f32),
            pltpu.VMEM((3, 128, GW), f32),
            heads,
            heads,
            heads,
            heads,
            pltpu.VMEM((4, 128, 576), bf16),
            wide,
            wide,
            pltpu.VMEM((768, 704), bf16),
            pltpu.VMEM((768, 704), bf16),
            pltpu.VMEM((384, 704), bf16),
            pltpu.VMEM((8, 128), f32),
            pltpu.VMEM((32, 8, 128), f32),
            pltpu.SemaphoreType.DMA((240,)),
            pltpu.SemaphoreType.DMA((240,)),
            pltpu.SemaphoreType.DMA((2, 4, 2)),
            pltpu.SemaphoreType.DMA((2, 5)),
            pltpu.SemaphoreType.DMA((2, 4)),
            pltpu.SemaphoreType.DMA((2, 2, 2)),
            pltpu.SemaphoreType.DMA((11,)),
        ],
        "layer_step",
        in_specs=[VM] * 11 + [ANY] * 2,
        out_specs=[VM] * 5 + [ANY] * 2,
        vmem=63 << 20,
    )(
        tokens,
        w_qkv,
        w_attn_out,
        w_router,
        gain_attn[None],
        gain_moe[None],
        rel_bias,
        spots,
        routes.T,
        valid[None],
        teacher,
        w_in.reshape(2, 2, 96, 3072),
        w_out.reshape(2, 2, 384, 768),
    )

    def whole(shape):
        return pl.BlockSpec(shape, lambda i: (0,) * len(shape))

    small_in = [(128, 768), (128, 768), (24, 2304), (24, 1024), (40, 128)]
    small_out = [
        (128, 768),
        (128, 768),
        (24, 2304),
        (24, 768),
        (24, 16),
        (1, 24),
        (1, 24),
        (BUCKETS, 12),
        (1, 1),
    ]
    blocks = [
        pl.BlockSpec((1, 96, 3072), lambda i: (i, 0, 0)),
        pl.BlockSpec((1, 384, 768), lambda i: (i, 0, 0)),
    ]
    gin, gout, output, grad_tokens, grad_qkv, grad_w, grad_r, grad_ga, grad_gm, table, loss = (
        pl.pallas_call(
            finish_kernel,
            grid=(4,),
            out_shape=[sds((4, 96, 3072), f32), sds((4, 384, 768), f32)]
            + [sds(shape, f32) for shape in small_out],
            in_specs=blocks + [whole(shape) for shape in small_in],
            out_specs=blocks + [whole(shape) for shape in small_out],
            name="finish",
        )(
            oin.reshape(4, 96, 3072),
            oout.reshape(4, 384, 768),
            output,
            grad_tokens,
            grad_qkv,
            grad_rest,
            extra,
        )
    )
    return (
        output,
        loss.reshape(()),
        grad_tokens,
        grad_qkv,
        grad_w,
        grad_ga.reshape(24),
        grad_gm.reshape(24),
        grad_r,
        table,
        gin.reshape(2, 192, 3072),
        gout.reshape(2, 768, 768),
    )


def choose(*arrays):
    tokens, w_in, rel_bias, buckets = arrays[0], arrays[7], arrays[6], arrays[12]
    fits = (
        lax.axis_size("dp") == 4
        and lax.axis_size("seq") == 8
        and tokens.shape == (128, 768)
        and w_in.shape == (2, 192, 3072)
        and rel_bias.shape == (32, 12)
        and buckets.shape == (1024,)
    )
    return fast_path(*arrays) if fits else on_device(*arrays)


def solution(mesh):
    in_specs = (
        P(("dp", "seq"), None),
        P(("dp", "seq"), None),
        P(("dp", "seq"), None),
        P(("dp", "seq")),
        P(("dp", "seq")),
        P(("dp", "seq"), None),
        P(),
        P("seq", "dp", None),
        P("seq", "dp", None),
        P(("dp", "seq"), None),
        P(("dp", "seq"), None),
        P(("dp", "seq")),
        P(),
    )
    out_specs = (
        P(("dp", "seq"), None),
        P(),
        P(("dp", "seq"), None),
        P(("dp", "seq"), None),
        P(("dp", "seq"), None),
        P(("dp", "seq")),
        P(("dp", "seq")),
        P(("dp", "seq"), None),
        P(),
        P("seq", "dp", None),
        P("seq", "dp", None),
    )
    return jax.shard_map(
        choose, mesh=mesh, in_specs=in_specs, out_specs=out_specs, check_vma=False
    )
```

```python
import functools

import jax
import jax.numpy as jnp
from jax import lax
from jax.experimental import pallas as pl
from jax.experimental.pallas import tpu as pltpu
from jax.sharding import PartitionSpec as P

H = 12
HEAD = 64
BUCKETS = 32


EPS = 1e-06
NEG = -1e30
SECTION = 512
HIGH = lax.Precision.HIGHEST
FLOAT_TYPE = jnp.float32
HALF_TYPE = jnp.bfloat16


def normalize(values, gain):
    factor = lax.rsqrt(jnp.mean(values * values, axis=-1, keepdims=True) + EPS)
    return (values * factor * gain, factor)


def norm_back(values, factor, gain, grad_norm):
    scaled = grad_norm * gain
    mean_term = jnp.mean(scaled * values, axis=-1, keepdims=True)
    grad_values = factor * scaled - values * (factor * factor * factor) * mean_term
    return (grad_values, jnp.sum(grad_norm * values * factor, axis=0))


def gelu_grad(preact, grad_hidden):
    _, gelu_back = jax.vjp(jax.nn.gelu, preact)
    return gelu_back(grad_hidden)[0]


def in_sections(advance, running, shards):
    row_count = shards[0].shape[0]
    sections = row_count // SECTION
    stacked = tuple((member.reshape((sections, SECTION) + member.shape[1:]) for member in shards))

    def one_section(inner_state, entry_pair):
        return (advance(inner_state, entry_pair[1], entry_pair[0] * SECTION), None)

    final_state, _ = lax.scan(
        one_section, running, (jnp.arange(sections, dtype=jnp.int32), stacked)
    )
    return final_state


def score_block(queries, key_rows, query_start, key_start, rel_bias, edges):
    query_count = queries.shape[0]
    key_count = key_rows.shape[0]
    distance = (query_start + jnp.arange(query_count, dtype=jnp.int32))[:, None] - (
        key_start + jnp.arange(key_count, dtype=jnp.int32)
    )[None, :]
    allowed = distance >= 0
    bucket_hot = (
        (distance[:, :, None] >= edges[None, None, :-1])
        & (distance[:, :, None] < edges[None, None, 1:])
    ).astype(FLOAT_TYPE)
    bias_term = jnp.einsum("qkb,bh->hqk", bucket_hot, rel_bias, precision=HIGH)
    raw_scores = (
        jnp.einsum("qhd,khd->hqk", queries, key_rows, preferred_element_type=FLOAT_TYPE)
        * queries.shape[2] ** (-0.5)
        + bias_term
    )
    return (raw_scores, allowed, bucket_hot)


def split_three(values):
    upper = lax.optimization_barrier(values.astype(HALF_TYPE))
    remainder = values - upper.astype(FLOAT_TYPE)
    middle = lax.optimization_barrier(remainder.astype(HALF_TYPE))
    bottom = (remainder - middle.astype(FLOAT_TYPE)).astype(HALF_TYPE)
    return jnp.stack([upper, middle, bottom], axis=1)


def join_three(packed):
    as_float = packed.astype(FLOAT_TYPE)
    return as_float[:, 0] + as_float[:, 1] + as_float[:, 2]


def on_device(
    tokens,
    w_qkv,
    w_attn_out,
    gain_attn,
    gain_moe,
    w_router,
    rel_bias,
    w_in,
    w_out,
    teacher,
    routes,
    valid,
    buckets,
):
    tok_rows = tokens.shape[0]
    width = tokens.shape[1]
    seq_count = lax.axis_size("seq")
    my_start = lax.axis_index("seq") * tok_rows
    local_experts = w_in.shape[0]
    experts_all = local_experts * seq_count
    capacity = 4 * tok_rows // experts_all
    slot_rows = seq_count * capacity
    scale = HEAD ** (-0.5)
    qkv_full, attn_full, router_full, gain_one, gain_two, valid_all = (
        lax.all_gather(w_qkv, ("dp", "seq"), axis=0, tiled=True),
        lax.all_gather(w_attn_out, ("dp", "seq"), axis=0, tiled=True),
        lax.all_gather(w_router, ("dp", "seq"), axis=0, tiled=True),
        lax.all_gather(gain_attn, ("dp", "seq"), axis=0, tiled=True),
        lax.all_gather(gain_moe, ("dp", "seq"), axis=0, tiled=True),
        lax.all_gather(valid.astype(HALF_TYPE), ("dp", "seq"), axis=0, tiled=True),
    )
    valid_float = valid.astype(FLOAT_TYPE)
    count_all = jnp.sum(valid_all.astype(FLOAT_TYPE))
    tokens_all = tok_rows * lax.axis_size("dp") * seq_count
    edges = jnp.sum(
        (buckets[None, :] < jnp.arange(BUCKETS + 1, dtype=jnp.int32)[:, None]).astype(jnp.int32),
        axis=1,
    )
    inputs = tokens.astype(FLOAT_TYPE)
    gain_first = gain_one.astype(FLOAT_TYPE)
    gain_second = gain_two.astype(FLOAT_TYPE)
    normed_one, factor_one = normalize(inputs, gain_first)
    normed_in = normed_one.astype(HALF_TYPE)
    qkv_rows = jnp.dot(normed_in, qkv_full, preferred_element_type=FLOAT_TYPE)
    query_low = qkv_rows[:, :width].astype(HALF_TYPE)
    key_low = qkv_rows[:, width : 2 * width].astype(HALF_TYPE)
    value_low = qkv_rows[:, 2 * width :].astype(HALF_TYPE)
    heads_q = query_low.reshape(tok_rows, H, HEAD)
    heads_k = key_low.reshape(tok_rows, H, HEAD)
    heads_v = value_low.reshape(tok_rows, H, HEAD)
    last_row = my_start + tok_rows - 1

    def forward_step(running, shards, offset):
        key_rows = shards[0].reshape(shards[0].shape[0], H, HEAD)
        value_rows = shards[1].reshape(shards[1].shape[0], H, HEAD)

        def work(inner_state):
            maximum, denom, mixture = inner_state
            raw_scores, allowed, _ = score_block(
                heads_q, key_rows, my_start, offset, rel_bias, edges
            )
            masked = jnp.where(allowed[None], raw_scores, NEG)
            new_max = jnp.maximum(maximum, jnp.max(masked, axis=2))
            weights = jnp.where(allowed[None], jnp.exp(masked - new_max[:, :, None]), 0.0)
            rescale = jnp.exp(maximum - new_max)
            addend = jnp.einsum(
                "hqk,khd->hqd",
                weights.astype(HALF_TYPE),
                value_rows,
                preferred_element_type=FLOAT_TYPE,
            )
            return (
                new_max,
                denom * rescale + jnp.sum(weights, axis=2),
                mixture * rescale[:, :, None] + addend,
            )

        return lax.cond(offset <= last_row, work, lambda inner_state: inner_state, running)

    start_state = (
        jnp.full((H, tok_rows), NEG, FLOAT_TYPE),
        jnp.zeros((H, tok_rows), FLOAT_TYPE),
        jnp.zeros((H, tok_rows, HEAD), FLOAT_TYPE),
    )
    maximum, denom, mixture = in_sections(
        forward_step,
        start_state,
        (
            lax.all_gather(key_low, "seq", axis=0, tiled=True),
            lax.all_gather(value_low, "seq", axis=0, tiled=True),
        ),
    )
    log_total = maximum + jnp.log(denom)
    attn_heads = mixture / denom[:, :, None]
    attn_rows = jnp.transpose(attn_heads, (1, 0, 2)).reshape(tok_rows, width)
    attn_low = attn_rows.astype(HALF_TYPE)
    hidden_state = inputs + jnp.dot(attn_low, attn_full, preferred_element_type=FLOAT_TYPE)
    normed_two, factor_two = normalize(hidden_state, gain_second)
    moe_in = normed_two.astype(HALF_TYPE)
    logits = jnp.dot(moe_in, router_full, preferred_element_type=FLOAT_TYPE)
    chosen = jnp.take_along_axis(logits, routes, axis=1)
    gate_weights = jax.nn.softmax(chosen, axis=1)
    flat_routes = routes.reshape(-1)
    matches = (flat_routes[:, None] == jnp.arange(experts_all, dtype=jnp.int32)[None, :]).astype(
        jnp.int32
    )
    slot_index = jnp.sum((jnp.cumsum(matches, axis=0) - matches) * matches, axis=1)
    target_dev = flat_routes // local_experts
    target_local = flat_routes % local_experts
    position = (target_dev * capacity + slot_index) * local_experts + target_local
    dispatch_map = (
        jnp.arange(experts_all * capacity, dtype=jnp.int32)[:, None] == position[None, :]
    ).astype(HALF_TYPE)
    dispatch_map = dispatch_map.reshape(experts_all * capacity, tok_rows, 2)
    outgoing = jnp.einsum(
        "prk,rd->pd", dispatch_map, moe_in, preferred_element_type=FLOAT_TYPE
    ).astype(HALF_TYPE)
    arrived = lax.all_to_all(
        outgoing.reshape(seq_count, capacity * local_experts, width),
        "seq",
        split_axis=0,
        concat_axis=0,
        tiled=True,
    )
    arrived_rows = arrived.reshape(slot_rows, local_experts, width)
    in_full, out_full = (
        lax.all_gather(w_in, "dp", axis=1, tiled=True),
        lax.all_gather(w_out, "dp", axis=1, tiled=True),
    )
    preact = jnp.einsum("mld,ldf->mlf", arrived_rows, in_full, preferred_element_type=FLOAT_TYPE)
    hidden = jax.nn.gelu(preact).astype(HALF_TYPE)
    result = jnp.einsum("mlf,lfd->mld", hidden, out_full, preferred_element_type=FLOAT_TYPE).astype(
        HALF_TYPE
    )
    returned = lax.all_to_all(
        result.reshape(seq_count, capacity * local_experts, width),
        "seq",
        split_axis=0,
        concat_axis=0,
        tiled=True,
    )
    returned = returned.reshape(experts_all * capacity, width)
    combined = jnp.einsum("prk,pd->krd", dispatch_map, returned, preferred_element_type=FLOAT_TYPE)
    output = hidden_state + gate_weights[:, 0:1] * combined[0] + gate_weights[:, 1:2] * combined[1]
    error_rows = output - teacher.astype(FLOAT_TYPE)
    loss_local = jnp.sum(valid_float[:, None] * error_rows * error_rows)
    grad_out = 2.0 * tokens_all / count_all * valid_float[:, None] * error_rows
    grad_gate = jnp.einsum("krd,rd->rk", combined, grad_out)
    grad_chosen = gate_weights * (
        grad_gate - jnp.sum(gate_weights * grad_gate, axis=1, keepdims=True)
    )
    pick = (routes[:, :, None] == jnp.arange(experts_all, dtype=jnp.int32)[None, None, :]).astype(
        FLOAT_TYPE
    )
    grad_logits = jnp.sum(pick * grad_chosen[:, :, None], axis=1).astype(HALF_TYPE)
    grad_router = jnp.einsum("rd,re->de", moe_in, grad_logits, preferred_element_type=FLOAT_TYPE)
    grad_result = (jnp.transpose(gate_weights)[:, :, None] * grad_out[None]).astype(HALF_TYPE)
    grad_slots = jnp.einsum(
        "prk,krd->pd", dispatch_map, grad_result, preferred_element_type=FLOAT_TYPE
    ).astype(HALF_TYPE)
    grad_arrived = lax.all_to_all(
        grad_slots.reshape(seq_count, capacity * local_experts, width),
        "seq",
        split_axis=0,
        concat_axis=0,
        tiled=True,
    )
    grad_rows = grad_arrived.reshape(slot_rows, local_experts, width)
    grad_hidden = jnp.einsum("mld,lfd->mlf", grad_rows, out_full, preferred_element_type=FLOAT_TYPE)
    grad_preact = gelu_grad(preact, grad_hidden).astype(HALF_TYPE)
    grad_out_local = jnp.einsum(
        "mlf,mld->lfd", hidden, grad_rows, preferred_element_type=FLOAT_TYPE
    )
    grad_in_local = jnp.einsum(
        "mld,mlf->ldf", arrived_rows, grad_preact, preferred_element_type=FLOAT_TYPE
    )
    grad_entry = jnp.einsum(
        "mlf,ldf->mld", grad_preact, in_full, preferred_element_type=FLOAT_TYPE
    ).astype(HALF_TYPE)
    grad_w_in, grad_w_out = (
        lax.psum_scatter(
            grad_in_local.astype(jnp.bfloat16), "dp", scatter_dimension=1, tiled=True
        ).astype(jnp.float32),
        lax.psum_scatter(
            grad_out_local.astype(jnp.bfloat16), "dp", scatter_dimension=1, tiled=True
        ).astype(jnp.float32),
    )
    grad_back = lax.all_to_all(
        grad_entry.reshape(seq_count, capacity * local_experts, width),
        "seq",
        split_axis=0,
        concat_axis=0,
        tiled=True,
    )
    grad_back = grad_back.reshape(experts_all * capacity, width)
    grad_moe_in = jnp.einsum(
        "prk,pd->rd", dispatch_map, grad_back, preferred_element_type=FLOAT_TYPE
    )
    grad_moe_in = grad_moe_in + jnp.einsum(
        "re,de->rd", grad_logits, router_full, preferred_element_type=FLOAT_TYPE
    )
    grad_hidden_norm, grad_gain_second = norm_back(
        hidden_state, factor_two, gain_second, grad_moe_in
    )
    grad_state = grad_out + grad_hidden_norm
    grad_state_low = grad_state.astype(HALF_TYPE)
    grad_attn_w = jnp.einsum(
        "rd,re->de", attn_low, grad_state_low, preferred_element_type=FLOAT_TYPE
    )
    grad_attn_low = jnp.einsum(
        "re,de->rd", grad_state_low, attn_full, preferred_element_type=FLOAT_TYPE
    ).astype(HALF_TYPE)
    heads_dout = grad_attn_low.reshape(tok_rows, H, HEAD)
    softmax_dot = jnp.sum(
        jnp.transpose(heads_dout, (1, 0, 2)).astype(FLOAT_TYPE) * attn_heads, axis=2
    )
    row_stats = split_three(
        jnp.stack([jnp.transpose(log_total), jnp.transpose(softmax_dot)], axis=1)
    )

    def backward_step(running, shards, offset):
        key_rows = shards[0].reshape(shards[0].shape[0], H, HEAD)
        value_rows = shards[1].reshape(shards[1].shape[0], H, HEAD)
        query_rows = shards[2].reshape(shards[2].shape[0], H, HEAD)
        dout_rows = shards[3].reshape(shards[3].shape[0], H, HEAD)
        stats_rows = join_three(shards[4])
        piece_total = jnp.transpose(stats_rows[:, 0, :])
        piece_dot = jnp.transpose(stats_rows[:, 1, :])
        grad_query, grad_table, grad_key, grad_value = running

        def query_work(inner_state):
            inner_query, inner_table = inner_state
            raw_scores, allowed, bucket_hot = score_block(
                heads_q, key_rows, my_start, offset, rel_bias, edges
            )
            weights = jnp.where(allowed[None], jnp.exp(raw_scores - log_total[:, :, None]), 0.0)
            grad_prob = jnp.einsum(
                "qhd,khd->hqk", heads_dout, value_rows, preferred_element_type=FLOAT_TYPE
            )
            grad_score = (weights * (grad_prob - softmax_dot[:, :, None])).astype(HALF_TYPE)
            inner_query = (
                inner_query
                + jnp.einsum(
                    "hqk,khd->hqd", grad_score, key_rows, preferred_element_type=FLOAT_TYPE
                )
                * scale
            )
            inner_table = inner_table + jnp.einsum(
                "hqk,qkb->bh", grad_score.astype(FLOAT_TYPE), bucket_hot, precision=HIGH
            )
            return (inner_query, inner_table)

        def key_work(inner_state):
            inner_key, inner_value = inner_state
            raw_scores, allowed, _ = score_block(
                query_rows, heads_k, offset, my_start, rel_bias, edges
            )
            weights = jnp.where(allowed[None], jnp.exp(raw_scores - piece_total[:, :, None]), 0.0)
            inner_value = inner_value + jnp.einsum(
                "hqk,qhd->khd",
                weights.astype(HALF_TYPE),
                dout_rows,
                preferred_element_type=FLOAT_TYPE,
            )
            grad_prob = jnp.einsum(
                "qhd,khd->hqk", dout_rows, heads_v, preferred_element_type=FLOAT_TYPE
            )
            grad_score = (weights * (grad_prob - piece_dot[:, :, None])).astype(HALF_TYPE)
            inner_key = (
                inner_key
                + jnp.einsum(
                    "hqk,qhd->khd", grad_score, query_rows, preferred_element_type=FLOAT_TYPE
                )
                * scale
            )
            return (inner_key, inner_value)

        grad_query, grad_table = lax.cond(
            offset <= last_row,
            query_work,
            lambda inner_state: inner_state,
            (grad_query, grad_table),
        )
        grad_key, grad_value = lax.cond(
            offset + shards[0].shape[0] - 1 >= my_start,
            key_work,
            lambda inner_state: inner_state,
            (grad_key, grad_value),
        )
        return (grad_query, grad_table, grad_key, grad_value)

    back_start = (
        jnp.zeros((H, tok_rows, HEAD), FLOAT_TYPE),
        jnp.zeros((BUCKETS, H), FLOAT_TYPE),
        jnp.zeros((tok_rows, H, HEAD), FLOAT_TYPE),
        jnp.zeros((tok_rows, H, HEAD), FLOAT_TYPE),
    )
    grad_query, grad_table_local, grad_key, grad_value = in_sections(
        backward_step,
        back_start,
        (
            lax.all_gather(key_low, "seq", axis=0, tiled=True),
            lax.all_gather(value_low, "seq", axis=0, tiled=True),
            lax.all_gather(query_low, "seq", axis=0, tiled=True),
            lax.all_gather(grad_attn_low, "seq", axis=0, tiled=True),
            lax.all_gather(row_stats, "seq", axis=0, tiled=True),
        ),
    )
    grad_qkv_low = jnp.concatenate(
        [
            jnp.transpose(grad_query, (1, 0, 2)).reshape(tok_rows, width),
            grad_key.reshape(tok_rows, width),
            grad_value.reshape(tok_rows, width),
        ],
        axis=1,
    ).astype(HALF_TYPE)
    grad_qkv_w = jnp.einsum("rd,re->de", normed_in, grad_qkv_low, preferred_element_type=FLOAT_TYPE)
    grad_normed_one = jnp.einsum(
        "re,de->rd", grad_qkv_low, qkv_full, preferred_element_type=FLOAT_TYPE
    )
    grad_in_norm, grad_gain_first = norm_back(inputs, factor_one, gain_first, grad_normed_one)
    grad_tokens = grad_state + grad_in_norm
    grad_qkv_own, grad_attn_own, grad_router_own, grad_gain_attn, grad_gain_moe = (
        lax.psum_scatter(grad_qkv_w, ("dp", "seq"), scatter_dimension=0, tiled=True),
        lax.psum_scatter(grad_attn_w, ("dp", "seq"), scatter_dimension=0, tiled=True),
        lax.psum_scatter(grad_router, ("dp", "seq"), scatter_dimension=0, tiled=True),
        lax.psum_scatter(grad_gain_first, ("dp", "seq"), scatter_dimension=0, tiled=True),
        lax.psum_scatter(grad_gain_second, ("dp", "seq"), scatter_dimension=0, tiled=True),
    )
    loss_sum, grad_table = lax.psum((loss_local, grad_table_local), ("dp", "seq"))
    loss = loss_sum / (count_all * width)
    return (
        output,
        loss,
        grad_tokens,
        grad_qkv_own,
        grad_attn_own,
        grad_gain_attn,
        grad_gain_moe,
        grad_router_own,
        grad_table,
        grad_w_in,
        grad_w_out,
    )


MESH = pl.DeviceIdType.MESH
ANY = pl.BlockSpec(memory_space=pl.ANY)
VM = pl.BlockSpec(memory_space=pltpu.VMEM)
ROLL = 1280
GW = 1152


def remote(src, dst, send, recv, dev):
    return pltpu.make_async_remote_copy(
        src_ref=src, dst_ref=dst, send_sem=send, recv_sem=recv, device_id=dev, device_id_type=MESH
    )


def place():
    d = lax.axis_index("dp")
    s = lax.axis_index("seq")
    return d, s, s // 2, lax.rem(s, 2)


def comm_call(body, outs, n_in, cid, scratch, name, in_specs=None, out_specs=None, vmem=None):
    return pl.pallas_call(
        body,
        out_shape=outs,
        in_specs=in_specs or [ANY] * n_in,
        out_specs=out_specs or [ANY] * len(outs),
        scratch_shapes=scratch,
        compiler_params=pltpu.CompilerParams(
            collective_id=cid, has_side_effects=True, vmem_limit_bytes=vmem
        ),
        name=name,
    )


def sds(shape, dtype=jnp.bfloat16):
    return jax.ShapeDtypeStruct(shape, dtype)


def head_mask(h):
    lane = lax.broadcasted_iota(jnp.int32, (1, 192), 1)
    return lane // HEAD == h


def dot_t(a, b):
    return lax.dot_general(a, b, (((1,), (1,)), ((), ())), preferred_element_type=jnp.float32)


def dot_l(a, b):
    return lax.dot_general(a, b, (((0,), (0,)), ((), ())), preferred_element_type=jnp.float32)


def dot_n(a, b):
    return jnp.dot(a, b, preferred_element_type=jnp.float32)


def soft_rows(q, keys, g_ref, h, start, width):
    s = dot_t(q, keys) * HEAD ** (-0.5) + g_ref[h, :, pl.ds(start, width)]
    m = jnp.max(s, axis=1, keepdims=True)
    p = jnp.exp(s - m)
    return p / jnp.sum(p, axis=1, keepdims=True)


CHUNK = 768
GELU_A = 0.7978845608028654
GELU_B = 0.044715


class Sems:
    def __init__(self, send, recv):
        self.send, self.recv, self.n = send, recv, 0

    def copy(self, src, dst, dev):
        cp = remote(src, dst, self.send.at[self.n], self.recv.at[self.n], dev)
        self.n += 1
        return cp


def run(copies):
    for cp in copies:
        cp.start()
    return copies


def received(copies):
    for cp in copies:
        cp.wait_recv()


def sent(copies):
    for cp in copies:
        cp.wait_send()


def chips():
    d, s, z, c = place()
    me = z * 4 + d
    half, i = me // 8, lax.rem(me, 8)
    numbers = [(1 - half) * 8 + lax.rem(i + k, 8) for k in range(8)]
    numbers += [half * 8 + lax.rem(i + k, 8) for k in range(1, 8)]
    return me, numbers, [(lax.rem(t, 4), 2 * (t // 4) + c) for t in numbers]


def rms(v):
    return lax.rsqrt(jnp.mean(v * v, axis=1, keepdims=True) + EPS)


def hot_of(buckets, count):
    b = lax.broadcasted_iota(jnp.int32, (count, 1), 0)
    low = jnp.sum((buckets[...] < b).astype(jnp.float32), axis=1, keepdims=True)
    high = jnp.sum((buckets[...] <= b).astype(jnp.float32), axis=1, keepdims=True)
    at = (1024 - lax.broadcasted_iota(jnp.int32, (1, ROLL), 1)).astype(jnp.float32)
    return ((at >= low) & (at < high) & (at < 1024.0)).astype(jnp.float32)


def step_kernel(
    x,
    w_qkv,
    w_attn,
    w_router_t,
    gain_a,
    gain_m,
    rel_bias_t,
    buckets,
    routes_t,
    valid_t,
    teacher,
    w_in,
    w_out,
    output,
    grad_tokens,
    grad_qkv,
    grad_rest,
    extra,
    oin,
    oout,
    wq,
    wqf,
    wrf,
    xs,
    n1s,
    q,
    kf,
    vf,
    bias,
    lines,
    out_v,
    attn,
    leave,
    left,
    arrived,
    win,
    wout,
    slope,
    hid,
    acc,
    back,
    gback,
    entry,
    gin,
    gout,
    hidden_v,
    gout_v,
    do_out,
    do,
    rest,
    rest_in,
    rest_got,
    kacc,
    vacc,
    gacc,
    dk_out,
    dv_out,
    dk_in,
    dv_in,
    dqkv,
    part,
    parts,
    wpart,
    wpart_in,
    wgot,
    small,
    shared,
    gain_rows_v,
    rest_mid,
    wmid,
    ss,
    rs,
    xe,
    re,
    oe,
    ore,
    ls,
):
    f32, bf16 = jnp.float32, jnp.bfloat16
    d, s, z, c = place()
    sib = (d, s + 1 - 2 * c)
    across = (d + 1 - 2 * lax.rem(d, 2), lax.rem(d + 2, 4), 3 - d)
    plane = [(j, s) for j in across]
    zs = [(d, 2 * lax.rem(z + k, 4) + c) for k in (1, 2, 3)]
    me, numbers, others = chips()
    device = d * 8 + s
    everyone = [(lax.rem(d + k // 8, 4), lax.rem(s + k % 8, 8)) for k in range(1, 32)]
    sems = Sems(ss, rs)
    barrier = pltpu.get_barrier_semaphore()
    for peer in everyone:
        pl.semaphore_signal(barrier, inc=1, device_id=peer, device_id_type=MESH)

    valid_row = valid_t[...].astype(f32)
    diag = lax.broadcasted_iota(jnp.int32, (128, 128), 0) == lax.broadcasted_iota(
        jnp.int32, (128, 128), 1
    )
    lines[:, :128] = jnp.zeros((32, 128), f32)
    lines[0:16, :24] = w_router_t[...].astype(f32)
    lines[16:17, :24] = gain_a[...].astype(f32)
    lines[17:18, :24] = gain_m[...].astype(f32)
    lines[18:19, :24] = jnp.broadcast_to(jnp.sum(valid_row, axis=1, keepdims=True), (1, 24))
    turned = jnp.transpose(lines[:, :128])[:24, :]
    for zt in range(4):
        for i in range(3):
            at = i * 768 + zt * 192
            wq[zt, :, i * 192 : (i + 1) * 192] = w_qkv[:, at : at + 192]
        wq[zt, :, 576:] = jnp.zeros((24, 128), bf16)
        wq[zt, :, 576:608] = turned.astype(bf16)
    pl.semaphore_wait(barrier, 31)

    def rows_of(ref, dd, zz, cc):
        return ref.at[pl.ds(pl.multiple_of(((dd * 4 + zz) * 2 + cc) * 24, 8), 24)]

    def column_rows(ref, dd, dev):
        copies = []
        for zz in range(4):
            spot = rows_of(ref, dd, zz, c)
            copies.append(sems.copy(spot, spot, dev))
        return run(copies)

    local = [
        pltpu.make_async_copy(wq.at[z], rows_of(wqf, d, z, c), ls.at[0]),
        pltpu.make_async_copy(w_attn, rows_of(wrf, d, z, c), ls.at[1]),
        pltpu.make_async_copy(x, xs.at[z], ls.at[2]),
    ]
    run(local)
    stage1 = run(
        [
            sems.copy(wq.at[lax.rem(z + k, 4)], rows_of(wqf, d, z, c), zs[i])
            for i, k in enumerate((1, 2, 3))
        ]
    )

    bulk = []

    def piece(m, dd, half):
        if m == 0:
            return win.at[pl.ds(pl.multiple_of(dd * 192 + half * 96, 32), 96)]
        return wout.at[pl.ds(pl.multiple_of(dd * 768 + half * 384, 128), 384)]

    sources = (w_in, w_out)

    def expert_send(m, i, half):
        j = across[i]

        def make():
            return remote(
                sources[m].at[lax.rem(j, 2), half],
                piece(m, d, half),
                xe.at[m, i, half],
                re.at[m, i],
                (j, 2 * z + half),
            )

        @pl.when(j // 2 == c)
        def _():
            make().start()

        bulk.append((j // 2 == c, make))

    def own_here(m, half):
        return pltpu.make_async_copy(
            sources[m].at[lax.rem(d, 2), half], piece(m, d, half), ls.at[3 + 2 * m + half]
        )

    def own_there(m, half):
        return remote(
            sources[m].at[lax.rem(d, 2), half],
            piece(m, d, half),
            xe.at[m, 3, half],
            re.at[m, 3 + half],
            sib,
        )

    def expert_own(m):
        @pl.when(d // 2 == c)
        def _():
            for half in range(2):
                own_here(m, half).start()
                own_there(m, half).start()

    def expert_own_done(m):
        @pl.when(d // 2 == c)
        def _():
            for half in range(2):
                own_here(m, half).wait()
                own_there(m, half).wait_send()

        @pl.when(d // 2 != c)
        def _():
            for half in range(2):
                own_there(m, half).wait_recv()

    def expert_pass(m, i):
        spot = piece(m, across[i], c)
        remote(spot, spot, xe.at[m, i, 0], re.at[m, i], sib).wait_recv()
        return sems.copy(spot, spot, sib)

    expert_send(0, 0, 0)
    expert_send(0, 1, 0)
    rest1 = run([sems.copy(w_attn, rows_of(wrf, d, z, c), zs[i]) for i in range(3)])
    rows = run([sems.copy(x, xs.at[z], zs[i]) for i in range(3)])

    table = jnp.dot(
        rel_bias_t[...], hot_of(buckets, BUCKETS), precision=HIGH, preferred_element_type=f32
    )
    place_of = lax.broadcasted_iota(jnp.int32, (1, ROLL), 1)
    lines[:12] = table + jnp.where((place_of < 1) | (place_of > 1024), NEG, 0.0)
    for h in range(3):
        row = jnp.broadcast_to(lines[pl.ds(3 * z + h, 1), :], (128, ROLL))
        bias[h] = pltpu.roll(row, 0, 1, stride=1, stride_axis=0)[:, 128:]
    for cp in local:
        cp.wait()
    received(stage1)
    stage2 = [column_rows(wqf, d, dev) for dev in plane]
    stage3 = column_rows(wqf, d, sib)
    received(rest1)
    rest2 = [column_rows(wrf, d, dev) for dev in plane]
    rest3 = column_rows(wrf, d, sib)
    for i, k in ((0, 1), (1, 1), (2, 0), (2, 1)):
        expert_send(0, i, k)
    expert_own(0)
    expert_own(1)
    for i, dd in enumerate(across):
        received(stage2[i])
        stage3 += column_rows(wqf, dd, sib)
    received(stage3)
    misc = jnp.transpose(wqf[:, 576:704].astype(f32))
    gain_first = misc[16:17]
    gain_second = misc[17:18]
    count = jnp.sum(misc[18:19], axis=1, keepdims=True) / 24.0

    pairs = []
    for i in range(4):
        zb = lax.rem(z + 4 - i, 4)
        if i > 0:
            rows[i - 1].wait_recv()
        xf = xs[zb].astype(f32)
        n1 = (xf * rms(xf) * gain_first).astype(bf16)
        n1s[zb] = n1
        qkv = dot_n(n1, wqf[:, :576]).astype(bf16)
        q[zb] = qkv[:, :192]
        kf[zb, c] = qkv[:, 192:384]
        vf[zb, c] = qkv[:, 384:]
        pairs += run(
            [
                sems.copy(kf.at[zb, c], kf.at[zb, c], sib),
                sems.copy(vf.at[zb, c], vf.at[zb, c], sib),
            ]
        )
    for i, dd in enumerate(across):
        received(rest2[i])
        rest3 += column_rows(wrf, dd, sib)
    expert_send(1, 0, 0)
    expert_send(1, 1, 0)
    received(pairs)
    first = sems.n
    sems.n += 4
    for zb in (3, 2, 1, 0):
        width = 256 * (zb + 1)
        start = pl.multiple_of(128 * (7 - 2 * zb) - 128 * c, 128)
        keys = kf[: zb + 1].reshape(width, 192)
        values = vf[: zb + 1].reshape(width, 192)
        def one_head(h, mixed, zb=zb, width=width, start=start, keys=keys, values=values):
            qh = jnp.where(head_mask(h), q[zb], jnp.zeros((), bf16))
            p = soft_rows(qh, keys, bias, h, start, width).astype(bf16)
            return mixed + jnp.where(head_mask(h), dot_n(p, values), 0.0)

        mixed = lax.fori_loop(0, 3, one_head, jnp.zeros((128, 192), f32))
        out_v[zb] = mixed.astype(bf16)

        @pl.when(z != zb)
        def _(zb=zb):
            remote(
                out_v.at[zb], attn.at[z], ss.at[first + zb], rs.at[first + z], (d, 2 * zb + c)
            ).start()

        @pl.when(z == zb)
        def _(zb=zb):
            attn[zb] = out_v[zb]

    received(rest3)
    for zb in range(4):

        @pl.when(z != zb)
        def _(zb=zb):
            remote(
                out_v.at[zb], attn.at[zb], ss.at[first + zb], rs.at[first + zb], (d, 2 * zb + c)
            ).wait()

    hidden = x[...].astype(f32)
    for zb in range(4):
        hidden = hidden + dot_n(attn[zb], wrf[192 * zb : 192 * (zb + 1), :])
    hidden_v[...] = hidden
    n2 = (hidden * rms(hidden) * gain_second).astype(bf16)
    logits = dot_n(n2, wqf[:, 576:704])
    lane = lax.broadcasted_iota(jnp.int32, (128, 128), 1)

    def column(row):
        return jnp.sum(jnp.where(diag, row, jnp.zeros_like(row)), axis=1, keepdims=True)

    route = [column(routes_t[i : i + 1, :]) for i in range(2)]
    picks = [(lane == r).astype(f32) for r in route]
    chosen = [
        jnp.sum(jnp.where(lane == r, logits, 0.0), axis=1, keepdims=True) for r in route
    ]
    top = jnp.maximum(chosen[0], chosen[1])
    powers = [jnp.exp(v - top) for v in chosen]
    gate = [v / (powers[0] + powers[1]) for v in powers]
    lower = (lax.broadcasted_iota(jnp.int32, (128, 128), 0) > lane).astype(bf16)
    before = dot_n(lower, (picks[0] + picks[1]).astype(bf16))
    wide = lax.broadcasted_iota(jnp.int32, (128, 512), 1)
    maps = []
    for i in range(2):
        slot = jnp.sum(picks[i] * before, axis=1, keepdims=True).astype(jnp.int32)
        maps.append((wide == route[i] * 32 + slot).astype(f32).astype(bf16))
    chart = maps[0] + maps[1]
    leave[...] = dot_l(chart, n2).astype(bf16).reshape(16, 32, 768)

    def spread_rows(src, dst):
        copies = run([sems.copy(src.at[t], dst.at[me], dev) for t, dev in zip(numbers, others)])
        dst[pl.ds(me, 1)] = src[pl.ds(me, 1)]
        return copies

    def spread_columns(src, dst, at):
        cols = pl.ds(at, 384)
        copies = run(
            [
                sems.copy(src.at[t, :, cols], dst.at[me, :, cols], dev)
                for t, dev in zip(numbers, others)
            ]
        )
        dst[pl.ds(me, 1), :, cols] = src[pl.ds(me, 1), :, cols]
        return copies

    out = spread_rows(leave, arrived)
    for i, k in ((0, 1), (1, 1), (2, 0), (2, 1)):
        expert_send(1, i, k)
    passed = [expert_pass(0, i) for i in range(3)]
    run(passed)
    expert_own_done(0)
    received(passed)
    received(out)
    sent(out)

    def forward_step(i, carry):
        cols = pl.ds(pl.multiple_of((i // 2) * CHUNK, CHUNK), CHUNK)
        these = pl.ds(pl.multiple_of(lax.rem(i, 2) * 256, 256), 256)
        blocks = pl.ds(pl.multiple_of(lax.rem(i, 2) * 8, 8), 8)
        pre = dot_n(arrived[blocks].reshape(256, 768), win[:, cols])
        t = jnp.tanh(GELU_A * (pre + GELU_B * pre * pre * pre))
        half = 0.5 * (1.0 + t)
        hid[these, cols] = (pre * half).astype(bf16)
        slope[these, cols] = half + 0.5 * pre * (1.0 - t * t) * (
            GELU_A * (1.0 + 3.0 * GELU_B * pre * pre)
        )
        return carry

    lax.fori_loop(0, 8, forward_step, 0)
    passed_out = [expert_pass(1, i) for i in range(3)]
    run(passed_out)
    expert_own_done(1)
    received(passed_out)
    results = []
    for at in (0, 384):
        acc[:, :384] = jnp.zeros((512, 384), f32)

        def result_step(i, carry, at=at):
            k = pl.multiple_of((i // 2) * CHUNK, CHUNK)
            these = pl.ds(pl.multiple_of(lax.rem(i, 2) * 256, 256), 256)
            acc[these, :384] += dot_n(hid[these, pl.ds(k, CHUNK)], wout[pl.ds(k, CHUNK), at : at + 384])
            return carry

        lax.fori_loop(0, 8, result_step, 0)
        leave[:, :, at : at + 384] = acc[:, :384].astype(bf16).reshape(16, 32, 384)
        results.append(spread_columns(leave, back, at))
    sent(stage1 + rows + rest1 + stage3 + pairs + rest3 + sum(stage2 + rest2, []))
    sent(passed + passed_out)
    for held, make in bulk:

        @pl.when(held)
        def _(make=make):
            make().wait_send()

    valid_column = column(valid_row)
    loss = jnp.zeros((1, 1), f32)
    dgate = [jnp.zeros((128, 1), f32), jnp.zeros((128, 1), f32)]
    grads = []
    for part_i, at in enumerate((0, 384)):
        cols = slice(at, at + 384)
        received(results[part_i])
        sent(results[part_i])
        combined = [dot_n(m, back[:, :, cols].reshape(512, 384)) for m in maps]
        result = hidden_v[:, cols] + gate[0] * combined[0] + gate[1] * combined[1]
        error = result - teacher[:, cols].astype(f32)
        masked = valid_column * error
        grad_out = (2.0 * 4096.0) / count * masked
        leave[:, :, cols] = (
            (
                dot_l(maps[0], (gate[0] * grad_out).astype(bf16))
                + dot_l(maps[1], (gate[1] * grad_out).astype(bf16))
            )
            .astype(bf16)
            .reshape(16, 32, 384)
        )
        grads.append(spread_columns(leave, gback, at))
        output[:, cols] = result
        gout_v[:, cols] = grad_out
        loss = loss + jnp.sum(
            jnp.sum(masked * error, axis=1, keepdims=True), axis=0, keepdims=True
        )
        dgate = [
            g + jnp.sum(m * grad_out, axis=1, keepdims=True) for g, m in zip(dgate, combined)
        ]
    mean = gate[0] * dgate[0] + gate[1] * dgate[1]
    grad_logits = jnp.zeros((128, 128), f32)
    for i in range(2):
        grad_logits = grad_logits + jnp.where(
            lane == route[i], gate[i] * (dgate[i] - mean), 0.0
        )
    grad_logits = grad_logits.astype(bf16)
    acc[...] = jnp.zeros_like(acc)

    my_half = me // 8
    entries = []
    for near in (True, False):
        members = slice(8, 15) if near else slice(0, 8)
        group = my_half if near else 1 - my_half
        for copies in grads:
            received(copies[members])
        if not near:
            for copies in grads:
                sent(copies)
        blocks = pl.ds(pl.multiple_of(group * 8, 8), 8)
        these = pl.ds(pl.multiple_of(group * 256, 256), 256)

        def backward_step(i, carry, blocks=blocks, these=these):
            cols = pl.ds(pl.multiple_of(i * CHUNK, CHUNK), CHUNK)
            dh = dot_t(gback[blocks].reshape(256, 768), wout[cols, :])
            dp = (dh * slope[these, cols]).astype(bf16)
            slope[these, cols] = dp.astype(f32)
            acc[these] += dot_t(dp, win[:, cols])
            return carry

        lax.fori_loop(0, 4, backward_step, 0)
        left[blocks] = acc[these].astype(bf16).reshape(8, 32, 768)
        entries += run(
            [
                sems.copy(left.at[t], entry.at[me], dev)
                for t, dev in zip(numbers[members], others[members])
            ]
        )
        if near:
            entry[pl.ds(me, 1)] = left[pl.ds(me, 1)]

    swap_out = sems.n
    sems.n += 8

    def half_out(f):
        return remote(
            piece(1, f, 1 - c), gout.at[f], ss.at[swap_out + f], rs.at[swap_out + f], sib
        )

    def half_in(f):
        at = swap_out + 4 + f
        return remote(piece(0, f, 1 - c), gin.at[f], ss.at[at], rs.at[at], sib)

    def out_step(f, carry):
        at = pl.multiple_of(f * CHUNK, CHUNK)
        wout[pl.ds(at, CHUNK), :] = dot_l(
            hid[:, pl.ds(at, CHUNK)], gback[...].reshape(512, 768)
        ).astype(bf16)
        half_out(f).start()
        return carry

    lax.fori_loop(0, 4, out_step, 0)

    owned = []

    def owner_send(m, i):
        src, dst = ((gin, oin), (gout, oout))[m]
        cp = remote(
            src.at[across[i]],
            dst.at[lax.rem(d, 2), c],
            oe.at[m, i],
            ore.at[m, lax.rem(d, 2), c],
            (across[i], 2 * z + d // 2),
        )
        cp.start()
        owned.append(cp)

    def owner_here(m):
        src, dst = ((gin, oin), (gout, oout))[m]
        return pltpu.make_async_copy(src.at[d], dst.at[lax.rem(d, 2), c], ls.at[7 + m])

    def owner_there(m):
        src, dst = ((gin, oin), (gout, oout))[m]
        return remote(
            src.at[d], dst.at[lax.rem(d, 2), c], oe.at[m, 3], ore.at[m, lax.rem(d, 2), c], sib
        )

    def owner_local(m):
        @pl.when(d // 2 == c)
        def _():
            owner_here(m).start()

        @pl.when(d // 2 != c)
        def _():
            owner_there(m).start()

    def add_half(m, f):
        ref, rows_n = ((gin, 96), (gout, 384))[m]
        spot = (
            pl.ds(pl.multiple_of(f * 192 + c * 96, 32), 96)
            if m == 0
            else pl.ds(pl.multiple_of(f * 768 + c * 384, 128), 384)
        )
        mine = (win if m == 0 else wout)[spot, :]
        ref[f] = (mine.astype(f32) + ref[f].astype(f32)).astype(bf16)

    for f in range(4):
        half_out(f).wait()
        add_half(1, f)
    for i in range(3):
        owner_send(1, i)
    owner_local(1)

    def in_step(f, carry):
        at = pl.multiple_of(f * CHUNK, CHUNK)
        win[:, pl.ds(at, CHUNK)] = dot_l(
            arrived[...].reshape(512, 768), slope[:, pl.ds(at, CHUNK)].astype(bf16)
        ).astype(bf16)
        return carry

    lax.fori_loop(0, 4, in_step, 0)
    for f in range(4):
        half_in(f).start()
    received(entries)
    sent(entries)

    dn2 = dot_n(chart, entry[...].reshape(512, 768))
    dn2 = dn2 + dot_t(grad_logits, wqf[:, 576:704])
    hidden = hidden_v[...]
    r2 = rms(hidden)
    scaled = dn2 * gain_second
    mean = jnp.mean(scaled * hidden, axis=1, keepdims=True)
    dh = gout_v[...] + r2 * scaled - hidden * (r2 * r2 * r2) * mean
    dh_low = dh.astype(bf16)
    for zb in range(4):
        do_out[zb] = dot_t(dh_low, wrf[192 * zb : 192 * (zb + 1), :]).astype(bf16)
    heads = run(
        [
            sems.copy(do_out.at[lax.rem(z + k, 4)], do.at[z], zs[i])
            for i, k in enumerate((1, 2, 3))
        ]
    )
    do[pl.ds(z, 1)] = do_out[pl.ds(z, 1)]
    grad_tokens[...] = dh

    for zb in range(4):
        rest[192 * zb : 192 * (zb + 1), :768] = dot_l(attn[zb], dh_low).astype(bf16)
    gain_rows = jnp.broadcast_to(jnp.sum(dn2 * hidden * r2, axis=0, keepdims=True), (128, 768))
    n2 = (hidden * r2 * gain_second).astype(bf16)
    tall = lax.broadcasted_iota(jnp.int32, (768, 128), 1)
    rest[:, 768:] = jnp.where(
        tall == 16, jnp.transpose(gain_rows), dot_l(n2, grad_logits)
    ).astype(bf16)
    rest_swap = run([sems.copy(rest, rest_in, sib)])
    for f in range(4):
        half_in(f).wait()
        add_half(0, f)
    received(rest_swap)
    sent(rest_swap)
    rest_in[...] = (rest[...].astype(f32) + rest_in[...].astype(f32)).astype(bf16)

    def slot(ref, i, j):
        return ref.at[pl.ds(pl.multiple_of((i * 4 + j) * 24, 8), 24)]

    rest_a = []
    for i, k in enumerate((1, 2, 3)):
        zt = lax.rem(z + k, 4)
        for dd in range(4):
            rest_a.append(sems.copy(rows_of(rest_in, dd, zt, c), slot(rest_mid, z, dd), zs[i]))
    run(rest_a)
    for dd in range(4):
        pltpu.make_async_copy(
            rows_of(rest_in, dd, z, c), slot(rest_mid, z, dd), ls.at[11 + dd]
        ).start()
    for i in range(3):
        owner_send(0, i)
    owner_local(0)
    kacc[...] = jnp.zeros_like(kacc)
    vacc[...] = jnp.zeros_like(vacc)
    gacc[...] = jnp.zeros_like(gacc)
    received(heads)

    scale = HEAD ** (-0.5)
    first_back = sems.n
    sems.n += 4
    swaps = []

    def to_tokens(zb, pair):
        received(pair)
        here = pl.ds(pl.multiple_of((2 * zb + c) * 128, 128), 128)
        dqkv[zb, :, 192:384] = (kacc[here] * scale + dk_in[zb].astype(f32)).astype(bf16)
        dqkv[zb, :, 384:] = (vacc[here] + dv_in[zb].astype(f32)).astype(bf16)
        dn1 = dot_t(dqkv[zb], wqf[:, :576])
        part[zb] = dn1.astype(bf16)

        @pl.when(z != zb)
        def _():
            remote(
                part.at[zb],
                parts.at[z],
                ss.at[first_back + zb],
                rs.at[first_back + z],
                (d, 2 * zb + c),
            ).start()

        @pl.when(z == zb)
        def _():
            parts[zb] = part[zb]

        xf = xs[zb].astype(f32)
        gain_rows_v[zb : zb + 1, :] = jnp.sum(dn1 * xf * rms(xf), axis=0, keepdims=True)

    for zb in (3, 2, 1, 0):
        width = 256 * (zb + 1)
        start = pl.multiple_of(128 * (7 - 2 * zb) - 128 * c, 128)
        keys = kf[: zb + 1].reshape(width, 192)
        values = vf[: zb + 1].reshape(width, 192)
        dq = jnp.zeros((128, 192), f32)
        for h in range(3):
            mask = head_mask(h)
            qh = jnp.where(mask, q[zb], jnp.zeros((), bf16))
            doh = jnp.where(mask, do[zb], jnp.zeros((), bf16))
            p = soft_rows(qh, keys, bias, h, start, width)
            vacc[:width] += dot_l(p.astype(bf16), doh)
            dp = dot_t(doh, values)
            dot = jnp.sum(p * dp, axis=1, keepdims=True)
            ds = (p * (dp - dot)).astype(bf16)
            gacc[h, :, pl.ds(start, width)] += ds.astype(f32)
            dq = dq + jnp.where(mask, dot_n(ds, keys), 0.0)
            kacc[:width] += dot_l(ds, qh)
        dqkv[zb, :, :192] = (dq * scale).astype(bf16)
        there = pl.ds(pl.multiple_of((2 * zb + 1 - c) * 128, 128), 128)
        dk_out[zb] = (kacc[there] * scale).astype(bf16)
        dv_out[zb] = vacc[there].astype(bf16)
        swaps.append(
            run(
                [
                    sems.copy(dk_out.at[zb], dk_in.at[zb], sib),
                    sems.copy(dv_out.at[zb], dv_in.at[zb], sib),
                ]
            )
        )
        if zb < 3:
            to_tokens(zb + 1, swaps[-2])
    to_tokens(0, swaps[-1])
    swaps = sum(swaps, [])

    row = lax.broadcasted_iota(jnp.int32, (128, 1), 0)
    sums = []
    for h in range(3):
        y = jnp.concatenate([jnp.zeros((128, ROLL - GW), f32), gacc[h]], axis=1)
        for bit in range(7):
            y = jnp.where((row >> bit) & 1 == 1, pltpu.roll(y, ROLL - (1 << bit), 1), y)
        sums.append(jnp.sum(y, axis=0, keepdims=True))
    hot = hot_of(buckets, 128)
    table = lax.dot_general(
        jnp.concatenate(sums + [jnp.zeros((5, ROLL), f32)], axis=0),
        hot,
        (((1,), (1,)), ((), ())),
        precision=HIGH,
        preferred_element_type=f32,
    )
    index = lax.broadcasted_iota(jnp.int32, (8, 128), 0)
    small[...] = jnp.where(index == 3, loss, table)
    shares = run([sems.copy(small, shared.at[device], dev) for dev in everyone])
    shared[pl.ds(device, 1)] = small[...][None]

    gain_part = jnp.sum(gain_rows_v[...], axis=0, keepdims=True)
    wpart[:, :576] = dot_l(n1s[...].reshape(512, 768), dqkv[...].reshape(512, 576)).astype(bf16)
    wpart[:, 576:] = jnp.transpose(jnp.broadcast_to(gain_part, (128, 768))).astype(bf16)
    wswap = run([sems.copy(wpart, wpart_in, sib)])
    received(wswap)
    sent(wswap)
    wpart_in[...] = (wpart[...].astype(f32) + wpart_in[...].astype(f32)).astype(bf16)
    w_a = []
    for i, dd in enumerate(across):
        for zt in range(4):
            w_a.append(sems.copy(rows_of(wpart_in, dd, zt, c), slot(wmid, d, zt), plane[i]))
    run(w_a)
    for zt in range(4):
        pltpu.make_async_copy(
            rows_of(wpart_in, d, zt, c), slot(wmid, d, zt), ls.at[15 + zt]
        ).start()
    received(rest_a)
    for dd in range(4):
        pltpu.make_async_copy(
            rows_of(rest_in, dd, z, c), slot(rest_mid, z, dd), ls.at[11 + dd]
        ).wait()
    rest[:96] = sum(rest_mid[96 * i : 96 * (i + 1), :].astype(f32) for i in range(4)).astype(bf16)
    rest_b = run(
        [
            sems.copy(
                rest.at[pl.ds(pl.multiple_of(dd * 24, 8), 24)],
                rest_got.at[pl.ds(pl.multiple_of(d * 24, 8), 24)],
                plane[i],
            )
            for i, dd in enumerate(across)
        ]
    )

    for zb in range(4):

        @pl.when(z != zb)
        def _(zb=zb):
            remote(
                part.at[zb],
                parts.at[zb],
                ss.at[first_back + zb],
                rs.at[first_back + zb],
                (d, 2 * zb + c),
            ).wait()

    dn1 = (
        parts[0].astype(f32) + parts[1].astype(f32) + parts[2].astype(f32) + parts[3].astype(f32)
    )
    xf = x[...].astype(f32)
    r1 = rms(xf)
    scaled = dn1 * gain_first
    mean = jnp.mean(scaled * xf, axis=1, keepdims=True)
    grad_tokens[...] += r1 * scaled - xf * (r1 * r1 * r1) * mean

    received(w_a)
    for zt in range(4):
        pltpu.make_async_copy(
            rows_of(wpart_in, d, zt, c), slot(wmid, d, zt), ls.at[15 + zt]
        ).wait()
    wpart[:96] = sum(wmid[96 * i : 96 * (i + 1), :].astype(f32) for i in range(4)).astype(bf16)
    w_b = run(
        [
            sems.copy(
                wpart.at[pl.ds(pl.multiple_of(lax.rem(z + k, 4) * 24, 8), 24)],
                wgot.at[pl.ds(pl.multiple_of(z * 24, 8), 24)],
                zs[i],
            )
            for i, k in enumerate((1, 2, 3))
        ]
    )
    own_rows = [
        pltpu.make_async_copy(
            rest.at[pl.ds(pl.multiple_of(d * 24, 8), 24)],
            rest_got.at[pl.ds(pl.multiple_of(d * 24, 8), 24)],
            ls.at[9],
        ),
        pltpu.make_async_copy(
            wpart.at[pl.ds(pl.multiple_of(z * 24, 8), 24)],
            wgot.at[pl.ds(pl.multiple_of(z * 24, 8), 24)],
            ls.at[10],
        ),
    ]
    run(own_rows)

    received(shares)
    by_z = []
    for zb in range(4):
        total = jnp.zeros((8, 128), f32)
        for dd in range(4):
            for cc in range(2):
                total = total + shared[(dd * 4 + zb) * 2 + cc]
        by_z.append(total)
    loss_all = by_z[0] + by_z[1] + by_z[2] + by_z[3]
    extra[0:8] = loss_all[3:4] / (count * 768.0) + jnp.zeros((8, 128), f32)
    for zb in range(4):
        extra[8 + 8 * zb : 16 + 8 * zb] = by_z[zb]

    received(rest_b)
    received(w_b)
    for cp in own_rows:
        cp.wait()
    total = jnp.zeros((24, 896), f32)
    gain_total = jnp.zeros((24, 128), f32)
    for zb in range(4):
        total = total + rest_got[24 * zb : 24 * (zb + 1), :].astype(f32)
        block = wgot[24 * zb : 24 * (zb + 1), :].astype(f32)
        gain_total = gain_total + block[:, 576:]
        for i in range(3):
            at = i * 768 + zb * 192
            grad_qkv[:, at : at + 192] = block[:, i * 192 : (i + 1) * 192]
    grad_rest[:, :896] = total
    grad_rest[:, 896:] = gain_total

    for m, (src, dst) in enumerate(((gin, oin), (gout, oout))):
        for l in range(2):
            for half in range(2):
                here = (2 * c + l == d) & (c == half)

                @pl.when(jnp.logical_not(here))
                def _(src=src, dst=dst, m=m, l=l, half=half):
                    remote(
                        src.at[0], dst.at[l, half], oe.at[m, 3], ore.at[m, l, half], sib
                    ).wait_recv()

        @pl.when(d // 2 == c)
        def _(m=m):
            owner_here(m).wait()

        @pl.when(d // 2 != c)
        def _(m=m):
            owner_there(m).wait_send()

    sent(heads + rest_a + rest_b + swaps + shares + w_a + w_b + owned)


def finish_kernel(
    oin,
    oout,
    output,
    tokens,
    qkv,
    rest,
    extra,
    gin,
    gout,
    o,
    t,
    g,
    w,
    r,
    ga,
    gm,
    table,
    loss,
    low_in,
    low_out,
    wide_in,
    wide_out,
    o_v,
    t_v,
    g_v,
    sems,
):
    f32 = jnp.float32
    loads, stores = [], []
    for i in range(4):
        loads.append(pltpu.make_async_copy(oin.at[i], low_in.at[i], sems.at[0, i]))
        loads.append(pltpu.make_async_copy(oout.at[i], low_out.at[i], sems.at[1, i]))
        stores.append(pltpu.make_async_copy(wide_in.at[i], gin.at[i], sems.at[2, i]))
        stores.append(pltpu.make_async_copy(wide_out.at[i], gout.at[i], sems.at[3, i]))
    run(loads)
    trios = ((output, o_v, o), (tokens, t_v, t), (qkv, g_v, g))
    moved = run(
        [pltpu.make_async_copy(a, b, sems.at[4, i]) for i, (a, b, _) in enumerate(trios)]
    )
    for i in range(4):
        loads[2 * i].wait()
        wide_in[i] = low_in[i].astype(f32)
        stores[2 * i].start()
        loads[2 * i + 1].wait()
        wide_out[i] = low_out[i].astype(f32)
        stores[2 * i + 1].start()
    for cp in moved:
        cp.wait()
    moved = run(
        [pltpu.make_async_copy(b, e, sems.at[4, i]) for i, (_, b, e) in enumerate(trios)]
    )
    w[...] = rest[:, :768]
    turned = jnp.transpose(
        jnp.concatenate([rest[:, 768:1024], jnp.zeros((104, 256), f32)], axis=0)
    )
    r[...] = turned[:16, :24]
    gm[...] = turned[16:17, :24]
    ga[...] = turned[128:129, :24]
    for zb in range(4):
        table[3 * zb : 3 * zb + 3, :] = extra[8 + 8 * zb : 11 + 8 * zb, :BUCKETS]
    loss[...] = extra[0:1, 0:1]
    for cp in stores + moved:
        cp.wait()


def fast_path(
    tokens,
    w_qkv,
    w_attn_out,
    gain_attn,
    gain_moe,
    w_router,
    rel_bias,
    w_in,
    w_out,
    teacher,
    routes,
    valid,
    buckets,
):
    f32, bf16 = jnp.float32, jnp.bfloat16
    block = pltpu.VMEM((16, 32, 768), bf16)
    heads = pltpu.VMEM((4, 128, 192), bf16)
    both = pltpu.VMEM((4, 2, 128, 192), bf16)
    wide = pltpu.VMEM((4, 128, 768), bf16)
    output, grad_tokens, grad_qkv, grad_rest, extra, oin, oout = comm_call(
        step_kernel,
        [
            sds((128, 768), f32),
            sds((128, 768), f32),
            sds((24, 2304), f32),
            sds((24, 1024), f32),
            sds((40, 128), f32),
            sds((2, 2, 96, 3072)),
            sds((2, 2, 384, 768)),
        ],
        13,
        1,
        [
            pltpu.VMEM((4, 24, 704), bf16),
            pltpu.VMEM((768, 704), bf16),
            pltpu.VMEM((768, 768), bf16),
            wide,
            wide,
            heads,
            both,
            both,
            pltpu.VMEM((3, 128, GW), f32),
            pltpu.VMEM((32, ROLL), f32),
            heads,
            heads,
            block,
            block,
            block,
            pltpu.VMEM((768, 3072), bf16),
            pltpu.VMEM((3072, 768), bf16),
            pltpu.VMEM((512, 3072), f32),
            pltpu.VMEM((512, 3072), bf16),
            pltpu.VMEM((512, 768), f32),
            block,
            block,
            block,
            pltpu.VMEM((4, 96, 3072), bf16),
            pltpu.VMEM((4, 384, 768), bf16),
            pltpu.VMEM((128, 768), f32),
            pltpu.VMEM((128, 768), f32),
            heads,
            heads,
            pltpu.VMEM((768, 896), bf16),
            pltpu.VMEM((768, 896), bf16),
            pltpu.VMEM((96, 896), bf16),
            pltpu.VMEM((1024, 192), f32),
            pltpu.VMEM((1024, 192), f32),
            pltpu.VMEM((3, 128, GW), f32),
            heads,
            heads,
            heads,
            heads,
            pltpu.VMEM((4, 128, 576), bf16),
            wide,
            wide,
            pltpu.VMEM((768, 704), bf16),
            pltpu.VMEM((768, 704), bf16),
            pltpu.VMEM((96, 704), bf16),
            pltpu.VMEM((8, 128), f32),
            pltpu.VMEM((32, 8, 128), f32),
            pltpu.VMEM((4, 768), f32),
            pltpu.VMEM((384, 896), bf16),
            pltpu.VMEM((384, 704), bf16),
            pltpu.SemaphoreType.DMA((300,)),
            pltpu.SemaphoreType.DMA((300,)),
            pltpu.SemaphoreType.DMA((2, 4, 2)),
            pltpu.SemaphoreType.DMA((2, 5)),
            pltpu.SemaphoreType.DMA((2, 4)),
            pltpu.SemaphoreType.DMA((2, 2, 2)),
            pltpu.SemaphoreType.DMA((19,)),
        ],
        "layer_step",
        in_specs=[VM] * 11 + [ANY] * 2,
        out_specs=[VM] * 5 + [ANY] * 2,
        vmem=63 << 20,
    )(
        tokens,
        w_qkv,
        w_attn_out,
        w_router.T,
        gain_attn[None],
        gain_moe[None],
        rel_bias.T,
        buckets[None],
        routes.T,
        valid[None],
        teacher,
        w_in.reshape(2, 2, 96, 3072),
        w_out.reshape(2, 2, 384, 768),
    )

    small_out = [
        (128, 768),
        (128, 768),
        (24, 2304),
        (24, 768),
        (16, 24),
        (1, 24),
        (1, 24),
        (12, BUCKETS),
        (1, 1),
    ]
    gin, gout, output, grad_tokens, grad_qkv, grad_w, grad_r, grad_ga, grad_gm, table, loss = (
        pl.pallas_call(
            finish_kernel,
            out_shape=[sds((4, 96, 3072), f32), sds((4, 384, 768), f32)]
            + [sds(shape, f32) for shape in small_out],
            in_specs=[ANY] * 5 + [VM] * 2,
            out_specs=[ANY] * 5 + [VM] * 6,
            scratch_shapes=[
                pltpu.VMEM((4, 96, 3072), bf16),
                pltpu.VMEM((4, 384, 768), bf16),
                pltpu.VMEM((4, 96, 3072), f32),
                pltpu.VMEM((4, 384, 768), f32),
                pltpu.VMEM((128, 768), f32),
                pltpu.VMEM((128, 768), f32),
                pltpu.VMEM((24, 2304), f32),
                pltpu.SemaphoreType.DMA((5, 4)),
            ],
            compiler_params=pltpu.CompilerParams(vmem_limit_bytes=63 << 20),
            name="finish",
        )(
            oin.reshape(4, 96, 3072),
            oout.reshape(4, 384, 768),
            output,
            grad_tokens,
            grad_qkv,
            grad_rest,
            extra,
        )
    )
    return (
        output,
        loss.reshape(()),
        grad_tokens,
        grad_qkv,
        grad_w,
        grad_ga.reshape(24),
        grad_gm.reshape(24),
        grad_r.T,
        table.T,
        gin.reshape(2, 192, 3072),
        gout.reshape(2, 768, 768),
    )


def choose(*arrays):
    tokens, w_in, rel_bias, buckets = arrays[0], arrays[7], arrays[6], arrays[12]
    fits = (
        lax.axis_size("dp") == 4
        and lax.axis_size("seq") == 8
        and tokens.shape == (128, 768)
        and w_in.shape == (2, 192, 3072)
        and rel_bias.shape == (32, 12)
        and buckets.shape == (1024,)
    )
    return fast_path(*arrays) if fits else on_device(*arrays)


def solution(mesh):
    in_specs = (
        P(("dp", "seq"), None),
        P(("dp", "seq"), None),
        P(("dp", "seq"), None),
        P(("dp", "seq")),
        P(("dp", "seq")),
        P(("dp", "seq"), None),
        P(),
        P("seq", "dp", None),
        P("seq", "dp", None),
        P(("dp", "seq"), None),
        P(("dp", "seq"), None),
        P(("dp", "seq")),
        P(),
    )
    out_specs = (
        P(("dp", "seq"), None),
        P(),
        P(("dp", "seq"), None),
        P(("dp", "seq"), None),
        P(("dp", "seq"), None),
        P(("dp", "seq")),
        P(("dp", "seq")),
        P(("dp", "seq"), None),
        P(),
        P("seq", "dp", None),
        P("seq", "dp", None),
    )
    return jax.shard_map(
        choose, mesh=mesh, in_specs=in_specs, out_specs=out_specs, check_vma=False
    )
```

```python
import functools

import jax
import jax.numpy as jnp
from jax import lax
from jax.experimental import pallas as pl
from jax.experimental.pallas import tpu as pltpu
from jax.sharding import PartitionSpec as P

H = 12
HEAD = 64
BUCKETS = 32


EPS = 1e-06
NEG = -1e30
SECTION = 512
HIGH = lax.Precision.HIGHEST
FLOAT_TYPE = jnp.float32
HALF_TYPE = jnp.bfloat16


def normalize(values, gain):
    factor = lax.rsqrt(jnp.mean(values * values, axis=-1, keepdims=True) + EPS)
    return (values * factor * gain, factor)


def norm_back(values, factor, gain, grad_norm):
    scaled = grad_norm * gain
    mean_term = jnp.mean(scaled * values, axis=-1, keepdims=True)
    grad_values = factor * scaled - values * (factor * factor * factor) * mean_term
    return (grad_values, jnp.sum(grad_norm * values * factor, axis=0))


def gelu_grad(preact, grad_hidden):
    _, gelu_back = jax.vjp(jax.nn.gelu, preact)
    return gelu_back(grad_hidden)[0]


def in_sections(advance, running, shards):
    row_count = shards[0].shape[0]
    sections = row_count // SECTION
    stacked = tuple((member.reshape((sections, SECTION) + member.shape[1:]) for member in shards))

    def one_section(inner_state, entry_pair):
        return (advance(inner_state, entry_pair[1], entry_pair[0] * SECTION), None)

    final_state, _ = lax.scan(
        one_section, running, (jnp.arange(sections, dtype=jnp.int32), stacked)
    )
    return final_state


def score_block(queries, key_rows, query_start, key_start, rel_bias, edges):
    query_count = queries.shape[0]
    key_count = key_rows.shape[0]
    distance = (query_start + jnp.arange(query_count, dtype=jnp.int32))[:, None] - (
        key_start + jnp.arange(key_count, dtype=jnp.int32)
    )[None, :]
    allowed = distance >= 0
    bucket_hot = (
        (distance[:, :, None] >= edges[None, None, :-1])
        & (distance[:, :, None] < edges[None, None, 1:])
    ).astype(FLOAT_TYPE)
    bias_term = jnp.einsum("qkb,bh->hqk", bucket_hot, rel_bias, precision=HIGH)
    raw_scores = (
        jnp.einsum("qhd,khd->hqk", queries, key_rows, preferred_element_type=FLOAT_TYPE)
        * queries.shape[2] ** (-0.5)
        + bias_term
    )
    return (raw_scores, allowed, bucket_hot)


def split_three(values):
    upper = lax.optimization_barrier(values.astype(HALF_TYPE))
    remainder = values - upper.astype(FLOAT_TYPE)
    middle = lax.optimization_barrier(remainder.astype(HALF_TYPE))
    bottom = (remainder - middle.astype(FLOAT_TYPE)).astype(HALF_TYPE)
    return jnp.stack([upper, middle, bottom], axis=1)


def join_three(packed):
    as_float = packed.astype(FLOAT_TYPE)
    return as_float[:, 0] + as_float[:, 1] + as_float[:, 2]


def on_device(
    tokens,
    w_qkv,
    w_attn_out,
    gain_attn,
    gain_moe,
    w_router,
    rel_bias,
    w_in,
    w_out,
    teacher,
    routes,
    valid,
    buckets,
):
    tok_rows = tokens.shape[0]
    width = tokens.shape[1]
    seq_count = lax.axis_size("seq")
    my_start = lax.axis_index("seq") * tok_rows
    local_experts = w_in.shape[0]
    experts_all = local_experts * seq_count
    capacity = 4 * tok_rows // experts_all
    slot_rows = seq_count * capacity
    scale = HEAD ** (-0.5)
    qkv_full, attn_full, router_full, gain_one, gain_two, valid_all = (
        lax.all_gather(w_qkv, ("dp", "seq"), axis=0, tiled=True),
        lax.all_gather(w_attn_out, ("dp", "seq"), axis=0, tiled=True),
        lax.all_gather(w_router, ("dp", "seq"), axis=0, tiled=True),
        lax.all_gather(gain_attn, ("dp", "seq"), axis=0, tiled=True),
        lax.all_gather(gain_moe, ("dp", "seq"), axis=0, tiled=True),
        lax.all_gather(valid.astype(HALF_TYPE), ("dp", "seq"), axis=0, tiled=True),
    )
    valid_float = valid.astype(FLOAT_TYPE)
    count_all = jnp.sum(valid_all.astype(FLOAT_TYPE))
    tokens_all = tok_rows * lax.axis_size("dp") * seq_count
    edges = jnp.sum(
        (buckets[None, :] < jnp.arange(BUCKETS + 1, dtype=jnp.int32)[:, None]).astype(jnp.int32),
        axis=1,
    )
    inputs = tokens.astype(FLOAT_TYPE)
    gain_first = gain_one.astype(FLOAT_TYPE)
    gain_second = gain_two.astype(FLOAT_TYPE)
    normed_one, factor_one = normalize(inputs, gain_first)
    normed_in = normed_one.astype(HALF_TYPE)
    qkv_rows = jnp.dot(normed_in, qkv_full, preferred_element_type=FLOAT_TYPE)
    query_low = qkv_rows[:, :width].astype(HALF_TYPE)
    key_low = qkv_rows[:, width : 2 * width].astype(HALF_TYPE)
    value_low = qkv_rows[:, 2 * width :].astype(HALF_TYPE)
    heads_q = query_low.reshape(tok_rows, H, HEAD)
    heads_k = key_low.reshape(tok_rows, H, HEAD)
    heads_v = value_low.reshape(tok_rows, H, HEAD)
    last_row = my_start + tok_rows - 1

    def forward_step(running, shards, offset):
        key_rows = shards[0].reshape(shards[0].shape[0], H, HEAD)
        value_rows = shards[1].reshape(shards[1].shape[0], H, HEAD)

        def work(inner_state):
            maximum, denom, mixture = inner_state
            raw_scores, allowed, _ = score_block(
                heads_q, key_rows, my_start, offset, rel_bias, edges
            )
            masked = jnp.where(allowed[None], raw_scores, NEG)
            new_max = jnp.maximum(maximum, jnp.max(masked, axis=2))
            weights = jnp.where(allowed[None], jnp.exp(masked - new_max[:, :, None]), 0.0)
            rescale = jnp.exp(maximum - new_max)
            addend = jnp.einsum(
                "hqk,khd->hqd",
                weights.astype(HALF_TYPE),
                value_rows,
                preferred_element_type=FLOAT_TYPE,
            )
            return (
                new_max,
                denom * rescale + jnp.sum(weights, axis=2),
                mixture * rescale[:, :, None] + addend,
            )

        return lax.cond(offset <= last_row, work, lambda inner_state: inner_state, running)

    start_state = (
        jnp.full((H, tok_rows), NEG, FLOAT_TYPE),
        jnp.zeros((H, tok_rows), FLOAT_TYPE),
        jnp.zeros((H, tok_rows, HEAD), FLOAT_TYPE),
    )
    maximum, denom, mixture = in_sections(
        forward_step,
        start_state,
        (
            lax.all_gather(key_low, "seq", axis=0, tiled=True),
            lax.all_gather(value_low, "seq", axis=0, tiled=True),
        ),
    )
    log_total = maximum + jnp.log(denom)
    attn_heads = mixture / denom[:, :, None]
    attn_rows = jnp.transpose(attn_heads, (1, 0, 2)).reshape(tok_rows, width)
    attn_low = attn_rows.astype(HALF_TYPE)
    hidden_state = inputs + jnp.dot(attn_low, attn_full, preferred_element_type=FLOAT_TYPE)
    normed_two, factor_two = normalize(hidden_state, gain_second)
    moe_in = normed_two.astype(HALF_TYPE)
    logits = jnp.dot(moe_in, router_full, preferred_element_type=FLOAT_TYPE)
    chosen = jnp.take_along_axis(logits, routes, axis=1)
    gate_weights = jax.nn.softmax(chosen, axis=1)
    flat_routes = routes.reshape(-1)
    matches = (flat_routes[:, None] == jnp.arange(experts_all, dtype=jnp.int32)[None, :]).astype(
        jnp.int32
    )
    slot_index = jnp.sum((jnp.cumsum(matches, axis=0) - matches) * matches, axis=1)
    target_dev = flat_routes // local_experts
    target_local = flat_routes % local_experts
    position = (target_dev * capacity + slot_index) * local_experts + target_local
    dispatch_map = (
        jnp.arange(experts_all * capacity, dtype=jnp.int32)[:, None] == position[None, :]
    ).astype(HALF_TYPE)
    dispatch_map = dispatch_map.reshape(experts_all * capacity, tok_rows, 2)
    outgoing = jnp.einsum(
        "prk,rd->pd", dispatch_map, moe_in, preferred_element_type=FLOAT_TYPE
    ).astype(HALF_TYPE)
    arrived = lax.all_to_all(
        outgoing.reshape(seq_count, capacity * local_experts, width),
        "seq",
        split_axis=0,
        concat_axis=0,
        tiled=True,
    )
    arrived_rows = arrived.reshape(slot_rows, local_experts, width)
    in_full, out_full = (
        lax.all_gather(w_in, "dp", axis=1, tiled=True),
        lax.all_gather(w_out, "dp", axis=1, tiled=True),
    )
    preact = jnp.einsum("mld,ldf->mlf", arrived_rows, in_full, preferred_element_type=FLOAT_TYPE)
    hidden = jax.nn.gelu(preact).astype(HALF_TYPE)
    result = jnp.einsum("mlf,lfd->mld", hidden, out_full, preferred_element_type=FLOAT_TYPE).astype(
        HALF_TYPE
    )
    returned = lax.all_to_all(
        result.reshape(seq_count, capacity * local_experts, width),
        "seq",
        split_axis=0,
        concat_axis=0,
        tiled=True,
    )
    returned = returned.reshape(experts_all * capacity, width)
    combined = jnp.einsum("prk,pd->krd", dispatch_map, returned, preferred_element_type=FLOAT_TYPE)
    output = hidden_state + gate_weights[:, 0:1] * combined[0] + gate_weights[:, 1:2] * combined[1]
    error_rows = output - teacher.astype(FLOAT_TYPE)
    loss_local = jnp.sum(valid_float[:, None] * error_rows * error_rows)
    grad_out = 2.0 * tokens_all / count_all * valid_float[:, None] * error_rows
    grad_gate = jnp.einsum("krd,rd->rk", combined, grad_out)
    grad_chosen = gate_weights * (
        grad_gate - jnp.sum(gate_weights * grad_gate, axis=1, keepdims=True)
    )
    pick = (routes[:, :, None] == jnp.arange(experts_all, dtype=jnp.int32)[None, None, :]).astype(
        FLOAT_TYPE
    )
    grad_logits = jnp.sum(pick * grad_chosen[:, :, None], axis=1).astype(HALF_TYPE)
    grad_router = jnp.einsum("rd,re->de", moe_in, grad_logits, preferred_element_type=FLOAT_TYPE)
    grad_result = (jnp.transpose(gate_weights)[:, :, None] * grad_out[None]).astype(HALF_TYPE)
    grad_slots = jnp.einsum(
        "prk,krd->pd", dispatch_map, grad_result, preferred_element_type=FLOAT_TYPE
    ).astype(HALF_TYPE)
    grad_arrived = lax.all_to_all(
        grad_slots.reshape(seq_count, capacity * local_experts, width),
        "seq",
        split_axis=0,
        concat_axis=0,
        tiled=True,
    )
    grad_rows = grad_arrived.reshape(slot_rows, local_experts, width)
    grad_hidden = jnp.einsum("mld,lfd->mlf", grad_rows, out_full, preferred_element_type=FLOAT_TYPE)
    grad_preact = gelu_grad(preact, grad_hidden).astype(HALF_TYPE)
    grad_out_local = jnp.einsum(
        "mlf,mld->lfd", hidden, grad_rows, preferred_element_type=FLOAT_TYPE
    )
    grad_in_local = jnp.einsum(
        "mld,mlf->ldf", arrived_rows, grad_preact, preferred_element_type=FLOAT_TYPE
    )
    grad_entry = jnp.einsum(
        "mlf,ldf->mld", grad_preact, in_full, preferred_element_type=FLOAT_TYPE
    ).astype(HALF_TYPE)
    grad_w_in, grad_w_out = (
        lax.psum_scatter(
            grad_in_local.astype(jnp.bfloat16), "dp", scatter_dimension=1, tiled=True
        ).astype(jnp.float32),
        lax.psum_scatter(
            grad_out_local.astype(jnp.bfloat16), "dp", scatter_dimension=1, tiled=True
        ).astype(jnp.float32),
    )
    grad_back = lax.all_to_all(
        grad_entry.reshape(seq_count, capacity * local_experts, width),
        "seq",
        split_axis=0,
        concat_axis=0,
        tiled=True,
    )
    grad_back = grad_back.reshape(experts_all * capacity, width)
    grad_moe_in = jnp.einsum(
        "prk,pd->rd", dispatch_map, grad_back, preferred_element_type=FLOAT_TYPE
    )
    grad_moe_in = grad_moe_in + jnp.einsum(
        "re,de->rd", grad_logits, router_full, preferred_element_type=FLOAT_TYPE
    )
    grad_hidden_norm, grad_gain_second = norm_back(
        hidden_state, factor_two, gain_second, grad_moe_in
    )
    grad_state = grad_out + grad_hidden_norm
    grad_state_low = grad_state.astype(HALF_TYPE)
    grad_attn_w = jnp.einsum(
        "rd,re->de", attn_low, grad_state_low, preferred_element_type=FLOAT_TYPE
    )
    grad_attn_low = jnp.einsum(
        "re,de->rd", grad_state_low, attn_full, preferred_element_type=FLOAT_TYPE
    ).astype(HALF_TYPE)
    heads_dout = grad_attn_low.reshape(tok_rows, H, HEAD)
    softmax_dot = jnp.sum(
        jnp.transpose(heads_dout, (1, 0, 2)).astype(FLOAT_TYPE) * attn_heads, axis=2
    )
    row_stats = split_three(
        jnp.stack([jnp.transpose(log_total), jnp.transpose(softmax_dot)], axis=1)
    )

    def backward_step(running, shards, offset):
        key_rows = shards[0].reshape(shards[0].shape[0], H, HEAD)
        value_rows = shards[1].reshape(shards[1].shape[0], H, HEAD)
        query_rows = shards[2].reshape(shards[2].shape[0], H, HEAD)
        dout_rows = shards[3].reshape(shards[3].shape[0], H, HEAD)
        stats_rows = join_three(shards[4])
        piece_total = jnp.transpose(stats_rows[:, 0, :])
        piece_dot = jnp.transpose(stats_rows[:, 1, :])
        grad_query, grad_table, grad_key, grad_value = running

        def query_work(inner_state):
            inner_query, inner_table = inner_state
            raw_scores, allowed, bucket_hot = score_block(
                heads_q, key_rows, my_start, offset, rel_bias, edges
            )
            weights = jnp.where(allowed[None], jnp.exp(raw_scores - log_total[:, :, None]), 0.0)
            grad_prob = jnp.einsum(
                "qhd,khd->hqk", heads_dout, value_rows, preferred_element_type=FLOAT_TYPE
            )
            grad_score = (weights * (grad_prob - softmax_dot[:, :, None])).astype(HALF_TYPE)
            inner_query = (
                inner_query
                + jnp.einsum(
                    "hqk,khd->hqd", grad_score, key_rows, preferred_element_type=FLOAT_TYPE
                )
                * scale
            )
            inner_table = inner_table + jnp.einsum(
                "hqk,qkb->bh", grad_score.astype(FLOAT_TYPE), bucket_hot, precision=HIGH
            )
            return (inner_query, inner_table)

        def key_work(inner_state):
            inner_key, inner_value = inner_state
            raw_scores, allowed, _ = score_block(
                query_rows, heads_k, offset, my_start, rel_bias, edges
            )
            weights = jnp.where(allowed[None], jnp.exp(raw_scores - piece_total[:, :, None]), 0.0)
            inner_value = inner_value + jnp.einsum(
                "hqk,qhd->khd",
                weights.astype(HALF_TYPE),
                dout_rows,
                preferred_element_type=FLOAT_TYPE,
            )
            grad_prob = jnp.einsum(
                "qhd,khd->hqk", dout_rows, heads_v, preferred_element_type=FLOAT_TYPE
            )
            grad_score = (weights * (grad_prob - piece_dot[:, :, None])).astype(HALF_TYPE)
            inner_key = (
                inner_key
                + jnp.einsum(
                    "hqk,qhd->khd", grad_score, query_rows, preferred_element_type=FLOAT_TYPE
                )
                * scale
            )
            return (inner_key, inner_value)

        grad_query, grad_table = lax.cond(
            offset <= last_row,
            query_work,
            lambda inner_state: inner_state,
            (grad_query, grad_table),
        )
        grad_key, grad_value = lax.cond(
            offset + shards[0].shape[0] - 1 >= my_start,
            key_work,
            lambda inner_state: inner_state,
            (grad_key, grad_value),
        )
        return (grad_query, grad_table, grad_key, grad_value)

    back_start = (
        jnp.zeros((H, tok_rows, HEAD), FLOAT_TYPE),
        jnp.zeros((BUCKETS, H), FLOAT_TYPE),
        jnp.zeros((tok_rows, H, HEAD), FLOAT_TYPE),
        jnp.zeros((tok_rows, H, HEAD), FLOAT_TYPE),
    )
    grad_query, grad_table_local, grad_key, grad_value = in_sections(
        backward_step,
        back_start,
        (
            lax.all_gather(key_low, "seq", axis=0, tiled=True),
            lax.all_gather(value_low, "seq", axis=0, tiled=True),
            lax.all_gather(query_low, "seq", axis=0, tiled=True),
            lax.all_gather(grad_attn_low, "seq", axis=0, tiled=True),
            lax.all_gather(row_stats, "seq", axis=0, tiled=True),
        ),
    )
    grad_qkv_low = jnp.concatenate(
        [
            jnp.transpose(grad_query, (1, 0, 2)).reshape(tok_rows, width),
            grad_key.reshape(tok_rows, width),
            grad_value.reshape(tok_rows, width),
        ],
        axis=1,
    ).astype(HALF_TYPE)
    grad_qkv_w = jnp.einsum("rd,re->de", normed_in, grad_qkv_low, preferred_element_type=FLOAT_TYPE)
    grad_normed_one = jnp.einsum(
        "re,de->rd", grad_qkv_low, qkv_full, preferred_element_type=FLOAT_TYPE
    )
    grad_in_norm, grad_gain_first = norm_back(inputs, factor_one, gain_first, grad_normed_one)
    grad_tokens = grad_state + grad_in_norm
    grad_qkv_own, grad_attn_own, grad_router_own, grad_gain_attn, grad_gain_moe = (
        lax.psum_scatter(grad_qkv_w, ("dp", "seq"), scatter_dimension=0, tiled=True),
        lax.psum_scatter(grad_attn_w, ("dp", "seq"), scatter_dimension=0, tiled=True),
        lax.psum_scatter(grad_router, ("dp", "seq"), scatter_dimension=0, tiled=True),
        lax.psum_scatter(grad_gain_first, ("dp", "seq"), scatter_dimension=0, tiled=True),
        lax.psum_scatter(grad_gain_second, ("dp", "seq"), scatter_dimension=0, tiled=True),
    )
    loss_sum, grad_table = lax.psum((loss_local, grad_table_local), ("dp", "seq"))
    loss = loss_sum / (count_all * width)
    return (
        output,
        loss,
        grad_tokens,
        grad_qkv_own,
        grad_attn_own,
        grad_gain_attn,
        grad_gain_moe,
        grad_router_own,
        grad_table,
        grad_w_in,
        grad_w_out,
    )


MESH = pl.DeviceIdType.MESH
ANY = pl.BlockSpec(memory_space=pl.ANY)
VM = pl.BlockSpec(memory_space=pltpu.VMEM)
ROLL = 1280
GW = 1152


def remote(src, dst, send, recv, dev):
    return pltpu.make_async_remote_copy(
        src_ref=src, dst_ref=dst, send_sem=send, recv_sem=recv, device_id=dev, device_id_type=MESH
    )


def place():
    d = lax.axis_index("dp")
    s = lax.axis_index("seq")
    return d, s, s // 2, lax.rem(s, 2)


def comm_call(body, outs, n_in, cid, scratch, name, in_specs=None, out_specs=None, vmem=None):
    return pl.pallas_call(
        body,
        out_shape=outs,
        in_specs=in_specs or [ANY] * n_in,
        out_specs=out_specs or [ANY] * len(outs),
        scratch_shapes=scratch,
        compiler_params=pltpu.CompilerParams(
            collective_id=cid, has_side_effects=True, vmem_limit_bytes=vmem
        ),
        name=name,
    )


def sds(shape, dtype=jnp.bfloat16):
    return jax.ShapeDtypeStruct(shape, dtype)


def head_mask(h):
    lane = lax.broadcasted_iota(jnp.int32, (1, 192), 1)
    return lane // HEAD == h


def dot_t(a, b):
    return lax.dot_general(a, b, (((1,), (1,)), ((), ())), preferred_element_type=jnp.float32)


def dot_l(a, b):
    return lax.dot_general(a, b, (((0,), (0,)), ((), ())), preferred_element_type=jnp.float32)


def dot_n(a, b):
    return jnp.dot(a, b, preferred_element_type=jnp.float32)


def soft_rows(q, keys, g_ref, h, start, width):
    s = dot_t(q, keys) * HEAD ** (-0.5) + g_ref[h, :, pl.ds(start, width)]
    m = jnp.max(s, axis=1, keepdims=True)
    p = jnp.exp(s - m)
    return p / jnp.sum(p, axis=1, keepdims=True)


CHUNK = 768
GELU_A = 0.7978845608028654
GELU_B = 0.044715


class Sems:
    def __init__(self, send, recv):
        self.send, self.recv, self.n = send, recv, 0

    def copy(self, src, dst, dev):
        cp = remote(src, dst, self.send.at[self.n], self.recv.at[self.n], dev)
        self.n += 1
        return cp


def run(copies):
    for cp in copies:
        cp.start()
    return copies


def received(copies):
    for cp in copies:
        cp.wait_recv()


def sent(copies):
    for cp in copies:
        cp.wait_send()


def chips():
    d, s, z, c = place()
    me = z * 4 + d
    half, i = me // 8, lax.rem(me, 8)
    numbers = [(1 - half) * 8 + lax.rem(i + k, 8) for k in range(8)]
    numbers += [half * 8 + lax.rem(i + k, 8) for k in range(1, 8)]
    return me, numbers, [(lax.rem(t, 4), 2 * (t // 4) + c) for t in numbers]


def rms(v):
    return lax.rsqrt(jnp.mean(v * v, axis=1, keepdims=True) + EPS)


def hot_of(buckets, count):
    b = lax.broadcasted_iota(jnp.int32, (count, 1), 0)
    low = jnp.sum((buckets[...] < b).astype(jnp.float32), axis=1, keepdims=True)
    high = jnp.sum((buckets[...] <= b).astype(jnp.float32), axis=1, keepdims=True)
    at = (1024 - lax.broadcasted_iota(jnp.int32, (1, ROLL), 1)).astype(jnp.float32)
    return ((at >= low) & (at < high) & (at < 1024.0)).astype(jnp.float32)


def step_kernel(
    x,
    w_qkv,
    w_attn,
    w_router_t,
    gain_a,
    gain_m,
    rel_bias_t,
    buckets,
    routes_t,
    valid_t,
    teacher,
    w_in,
    w_out,
    output,
    grad_tokens,
    grad_qkv,
    grad_rest,
    extra,
    oin,
    oout,
    wq,
    wqf,
    wrf,
    xs,
    n1s,
    q,
    kf,
    vf,
    bias,
    lines,
    out_v,
    attn,
    leave,
    left,
    arrived,
    win,
    wout,
    slope,
    hid,
    acc,
    back,
    gback,
    entry,
    gin,
    gout,
    hidden_v,
    gout_v,
    do_out,
    do,
    rest,
    rest_in,
    rest_got,
    kacc,
    vacc,
    gacc,
    dk_out,
    dv_out,
    dk_in,
    dv_in,
    dqkv,
    part,
    parts,
    wpart,
    wpart_in,
    wgot,
    small,
    shared,
    gain_rows_v,
    rest_mid,
    wmid,
    ss,
    rs,
    xe,
    re,
    oe,
    ore,
    ls,
):
    f32, bf16 = jnp.float32, jnp.bfloat16
    d, s, z, c = place()
    sib = (d, s + 1 - 2 * c)
    across = (d + 1 - 2 * lax.rem(d, 2), lax.rem(d + 2, 4), 3 - d)
    plane = [(j, s) for j in across]
    zs = [(d, 2 * lax.rem(z + k, 4) + c) for k in (1, 2, 3)]
    me, numbers, others = chips()
    device = d * 8 + s
    everyone = [(lax.rem(d + k // 8, 4), lax.rem(s + k % 8, 8)) for k in range(1, 32)]
    sems = Sems(ss, rs)
    barrier = pltpu.get_barrier_semaphore()
    for peer in everyone:
        pl.semaphore_signal(barrier, inc=1, device_id=peer, device_id_type=MESH)

    valid_row = valid_t[...].astype(f32)
    diag = lax.broadcasted_iota(jnp.int32, (128, 128), 0) == lax.broadcasted_iota(
        jnp.int32, (128, 128), 1
    )
    lines[:, :128] = jnp.zeros((32, 128), f32)
    lines[0:16, :24] = w_router_t[...].astype(f32)
    lines[16:17, :24] = gain_a[...].astype(f32)
    lines[17:18, :24] = gain_m[...].astype(f32)
    lines[18:19, :24] = jnp.broadcast_to(jnp.sum(valid_row, axis=1, keepdims=True), (1, 24))
    turned = jnp.transpose(lines[:, :128])[:24, :]
    for zt in range(4):
        for i in range(3):
            at = i * 768 + zt * 192
            wq[zt, :, i * 192 : (i + 1) * 192] = w_qkv[:, at : at + 192]
        wq[zt, :, 576:] = jnp.zeros((24, 128), bf16)
        wq[zt, :, 576:608] = turned.astype(bf16)
    pl.semaphore_wait(barrier, 31)

    def rows_of(ref, dd, zz, cc):
        return ref.at[pl.ds(pl.multiple_of(((dd * 4 + zz) * 2 + cc) * 24, 8), 24)]

    def column_rows(ref, dd, dev):
        copies = []
        for zz in range(4):
            spot = rows_of(ref, dd, zz, c)
            copies.append(sems.copy(spot, spot, dev))
        return run(copies)

    local = [
        pltpu.make_async_copy(wq.at[z], rows_of(wqf, d, z, c), ls.at[0]),
        pltpu.make_async_copy(w_attn, rows_of(wrf, d, z, c), ls.at[1]),
        pltpu.make_async_copy(x, xs.at[z], ls.at[2]),
    ]
    run(local)
    stage1 = run(
        [
            sems.copy(wq.at[lax.rem(z + k, 4)], rows_of(wqf, d, z, c), zs[i])
            for i, k in enumerate((1, 2, 3))
        ]
    )

    bulk = []

    def piece(m, dd, half):
        if m == 0:
            return win.at[pl.ds(pl.multiple_of(dd * 192 + half * 96, 32), 96)]
        return wout.at[pl.ds(pl.multiple_of(dd * 768 + half * 384, 128), 384)]

    sources = (w_in, w_out)

    def expert_send(m, i, half):
        j = across[i]

        def make():
            return remote(
                sources[m].at[lax.rem(j, 2), half],
                piece(m, d, half),
                xe.at[m, i, half],
                re.at[m, i],
                (j, 2 * z + half),
            )

        @pl.when(j // 2 == c)
        def _():
            make().start()

        bulk.append((j // 2 == c, make))

    def own_here(m, half):
        return pltpu.make_async_copy(
            sources[m].at[lax.rem(d, 2), half], piece(m, d, half), ls.at[3 + 2 * m + half]
        )

    def own_there(m, half):
        return remote(
            sources[m].at[lax.rem(d, 2), half],
            piece(m, d, half),
            xe.at[m, 3, half],
            re.at[m, 3 + half],
            sib,
        )

    def expert_own(m):
        @pl.when(d // 2 == c)
        def _():
            for half in range(2):
                own_here(m, half).start()
                own_there(m, half).start()

    def expert_own_done(m):
        @pl.when(d // 2 == c)
        def _():
            for half in range(2):
                own_here(m, half).wait()
                own_there(m, half).wait_send()

        @pl.when(d // 2 != c)
        def _():
            for half in range(2):
                own_there(m, half).wait_recv()

    def expert_pass(m, i):
        spot = piece(m, across[i], c)
        remote(spot, spot, xe.at[m, i, 0], re.at[m, i], sib).wait_recv()
        return sems.copy(spot, spot, sib)

    expert_send(0, 0, 0)
    expert_send(0, 1, 0)
    rest1 = run([sems.copy(w_attn, rows_of(wrf, d, z, c), zs[i]) for i in range(3)])
    rows = run([sems.copy(x, xs.at[z], zs[i]) for i in range(3)])

    table = jnp.dot(
        rel_bias_t[...], hot_of(buckets, BUCKETS), precision=HIGH, preferred_element_type=f32
    )
    place_of = lax.broadcasted_iota(jnp.int32, (1, ROLL), 1)
    lines[:12] = table + jnp.where((place_of < 1) | (place_of > 1024), NEG, 0.0)
    for h in range(3):
        row = jnp.broadcast_to(lines[pl.ds(3 * z + h, 1), :], (128, ROLL))
        bias[h] = pltpu.roll(row, 0, 1, stride=1, stride_axis=0)[:, 128:]
    for cp in local:
        cp.wait()
    received(stage1)
    stage2 = [column_rows(wqf, d, dev) for dev in plane]
    stage3 = column_rows(wqf, d, sib)
    received(rest1)
    rest2 = [column_rows(wrf, d, dev) for dev in plane]
    rest3 = column_rows(wrf, d, sib)
    for i, k in ((0, 1), (1, 1), (2, 0), (2, 1)):
        expert_send(0, i, k)
    expert_own(0)
    expert_own(1)
    for i, dd in enumerate(across):
        received(stage2[i])
        stage3 += column_rows(wqf, dd, sib)
    received(stage3)
    misc = jnp.transpose(wqf[:, 576:704].astype(f32))
    gain_first = misc[16:17]
    gain_second = misc[17:18]
    count = jnp.sum(misc[18:19], axis=1, keepdims=True) / 24.0

    pairs = []
    for i in range(4):
        zb = lax.rem(z + 4 - i, 4)
        if i > 0:
            rows[i - 1].wait_recv()
        xf = xs[zb].astype(f32)
        n1 = (xf * rms(xf) * gain_first).astype(bf16)
        n1s[zb] = n1
        qkv = dot_n(n1, wqf[:, :576]).astype(bf16)
        q[zb] = qkv[:, :192]
        kf[zb, c] = qkv[:, 192:384]
        vf[zb, c] = qkv[:, 384:]
        pairs += run(
            [
                sems.copy(kf.at[zb, c], kf.at[zb, c], sib),
                sems.copy(vf.at[zb, c], vf.at[zb, c], sib),
            ]
        )
    for i, dd in enumerate(across):
        received(rest2[i])
        rest3 += column_rows(wrf, dd, sib)
    expert_send(1, 0, 0)
    expert_send(1, 1, 0)
    received(pairs)
    first = sems.n
    sems.n += 4
    for zb in (3, 2, 1, 0):
        width = 256 * (zb + 1)
        start = pl.multiple_of(128 * (7 - 2 * zb) - 128 * c, 128)
        keys = kf[: zb + 1].reshape(width, 192)
        values = vf[: zb + 1].reshape(width, 192)
        def one_head(h, mixed, zb=zb, width=width, start=start, keys=keys, values=values):
            qh = jnp.where(head_mask(h), q[zb], jnp.zeros((), bf16))
            p = soft_rows(qh, keys, bias, h, start, width).astype(bf16)
            return mixed + jnp.where(head_mask(h), dot_n(p, values), 0.0)

        mixed = lax.fori_loop(0, 3, one_head, jnp.zeros((128, 192), f32))
        out_v[zb] = mixed.astype(bf16)

        @pl.when(z != zb)
        def _(zb=zb):
            remote(
                out_v.at[zb], attn.at[z], ss.at[first + zb], rs.at[first + z], (d, 2 * zb + c)
            ).start()

        @pl.when(z == zb)
        def _(zb=zb):
            attn[zb] = out_v[zb]

    received(rest3)
    for zb in range(4):

        @pl.when(z != zb)
        def _(zb=zb):
            remote(
                out_v.at[zb], attn.at[zb], ss.at[first + zb], rs.at[first + zb], (d, 2 * zb + c)
            ).wait()

    hidden = x[...].astype(f32)
    for zb in range(4):
        hidden = hidden + dot_n(attn[zb], wrf[192 * zb : 192 * (zb + 1), :])
    hidden_v[...] = hidden
    n2 = (hidden * rms(hidden) * gain_second).astype(bf16)
    logits = dot_n(n2, wqf[:, 576:704])
    lane = lax.broadcasted_iota(jnp.int32, (128, 128), 1)

    def column(row):
        return jnp.sum(jnp.where(diag, row, jnp.zeros_like(row)), axis=1, keepdims=True)

    route = [column(routes_t[i : i + 1, :]) for i in range(2)]
    picks = [(lane == r).astype(f32) for r in route]
    chosen = [
        jnp.sum(jnp.where(lane == r, logits, 0.0), axis=1, keepdims=True) for r in route
    ]
    top = jnp.maximum(chosen[0], chosen[1])
    powers = [jnp.exp(v - top) for v in chosen]
    gate = [v / (powers[0] + powers[1]) for v in powers]
    lower = (lax.broadcasted_iota(jnp.int32, (128, 128), 0) > lane).astype(bf16)
    before = dot_n(lower, (picks[0] + picks[1]).astype(bf16))
    wide = lax.broadcasted_iota(jnp.int32, (128, 512), 1)
    maps = []
    for i in range(2):
        slot = jnp.sum(picks[i] * before, axis=1, keepdims=True).astype(jnp.int32)
        maps.append((wide == route[i] * 32 + slot).astype(f32).astype(bf16))
    chart = maps[0] + maps[1]
    leave[...] = dot_l(chart, n2).astype(bf16).reshape(16, 32, 768)

    def spread_rows(src, dst, targets, devices):
        copies = run([sems.copy(src.at[t], dst.at[me], dev) for t, dev in zip(targets, devices)])
        dst[pl.ds(me, 1)] = src[pl.ds(me, 1)]
        return copies

    def spread_columns(src, dst, at):
        cols = pl.ds(at, 384)
        copies = run(
            [
                sems.copy(src.at[t, :, cols], dst.at[me, :, cols], dev)
                for t, dev in zip(numbers, others)
            ]
        )
        dst[pl.ds(me, 1), :, cols] = src[pl.ds(me, 1), :, cols]
        return copies

    out = spread_rows(leave, arrived, numbers[8:] + numbers[:8], others[8:] + others[:8])
    for i, k in ((0, 1), (1, 1), (2, 0), (2, 1)):
        expert_send(1, i, k)
    passed = [expert_pass(0, i) for i in range(3)]
    run(passed)
    expert_own_done(0)
    received(passed)
    received(out)
    sent(out)

    def forward_step(i, carry):
        cols = pl.ds(pl.multiple_of((i // 2) * CHUNK, CHUNK), CHUNK)
        these = pl.ds(pl.multiple_of(lax.rem(i, 2) * 256, 256), 256)
        blocks = pl.ds(pl.multiple_of(lax.rem(i, 2) * 8, 8), 8)
        pre = dot_n(arrived[blocks].reshape(256, 768), win[:, cols])
        t = jnp.tanh(GELU_A * (pre + GELU_B * pre * pre * pre))
        half = 0.5 * (1.0 + t)
        hid[these, cols] = (pre * half).astype(bf16)
        slope[these, cols] = half + 0.5 * pre * (1.0 - t * t) * (
            GELU_A * (1.0 + 3.0 * GELU_B * pre * pre)
        )
        return carry

    lax.fori_loop(0, 8, forward_step, 0)
    acc[...] = jnp.zeros_like(acc)

    def quarter(dd):
        k = pl.ds(pl.multiple_of(dd * 768, 768), 768)

        def result_step(i, carry):
            these = pl.ds(pl.multiple_of(i * 256, 256), 256)
            acc[these] += dot_n(hid[these, k], wout[k, :])
            return carry

        lax.fori_loop(0, 2, result_step, 0)

    expert_own_done(1)
    passed_out = []
    quarters = (d,) + across
    for i in range(3):
        passed_out += run([expert_pass(1, i)])
        quarter(quarters[i])
        received(passed_out[-1:])
    results = []
    k = pl.ds(pl.multiple_of(across[2] * 768, 768), 768)
    for at in (0, 384):
        half = acc[:, at : at + 384] + dot_n(hid[:, k], wout[k, at : at + 384])
        leave[:, :, at : at + 384] = half.astype(bf16).reshape(16, 32, 384)
        results.append(spread_columns(leave, back, at))
    sent(stage1 + rows + rest1 + stage3 + pairs + rest3 + sum(stage2 + rest2, []))
    sent(passed + passed_out)
    for held, make in bulk:

        @pl.when(held)
        def _(make=make):
            make().wait_send()

    valid_column = column(valid_row)
    loss = jnp.zeros((1, 1), f32)
    dgate = [jnp.zeros((128, 1), f32), jnp.zeros((128, 1), f32)]
    grads = []
    for part_i, at in enumerate((0, 384)):
        cols = slice(at, at + 384)
        received(results[part_i])
        sent(results[part_i])
        combined = [dot_n(m, back[:, :, cols].reshape(512, 384)) for m in maps]
        result = hidden_v[:, cols] + gate[0] * combined[0] + gate[1] * combined[1]
        error = result - teacher[:, cols].astype(f32)
        masked = valid_column * error
        grad_out = (2.0 * 4096.0) / count * masked
        leave[:, :, cols] = (
            (
                dot_l(maps[0], (gate[0] * grad_out).astype(bf16))
                + dot_l(maps[1], (gate[1] * grad_out).astype(bf16))
            )
            .astype(bf16)
            .reshape(16, 32, 384)
        )
        grads.append(spread_columns(leave, gback, at))
        output[:, cols] = result
        gout_v[:, cols] = grad_out
        loss = loss + jnp.sum(
            jnp.sum(masked * error, axis=1, keepdims=True), axis=0, keepdims=True
        )
        dgate = [
            g + jnp.sum(m * grad_out, axis=1, keepdims=True) for g, m in zip(dgate, combined)
        ]
    mean = gate[0] * dgate[0] + gate[1] * dgate[1]
    grad_logits = jnp.zeros((128, 128), f32)
    for i in range(2):
        grad_logits = grad_logits + jnp.where(
            lane == route[i], gate[i] * (dgate[i] - mean), 0.0
        )
    grad_logits = grad_logits.astype(bf16)
    acc[...] = jnp.zeros_like(acc)

    my_half = me // 8
    entries = []
    for near in (True, False):
        members = slice(8, 15) if near else slice(0, 8)
        group = my_half if near else 1 - my_half
        for copies in grads:
            received(copies[members])
        if not near:
            for copies in grads:
                sent(copies)
        blocks = pl.ds(pl.multiple_of(group * 8, 8), 8)
        these = pl.ds(pl.multiple_of(group * 256, 256), 256)

        def backward_step(i, carry, blocks=blocks, these=these):
            cols = pl.ds(pl.multiple_of(i * CHUNK, CHUNK), CHUNK)
            dh = dot_t(gback[blocks].reshape(256, 768), wout[cols, :])
            dp = (dh * slope[these, cols]).astype(bf16)
            slope[these, cols] = dp.astype(f32)
            acc[these] += dot_t(dp, win[:, cols])
            return carry

        lax.fori_loop(0, 4, backward_step, 0)
        left[blocks] = acc[these].astype(bf16).reshape(8, 32, 768)
        entries += run(
            [
                sems.copy(left.at[t], entry.at[me], dev)
                for t, dev in zip(numbers[members], others[members])
            ]
        )
        if near:
            entry[pl.ds(me, 1)] = left[pl.ds(me, 1)]

    swap_out = sems.n
    sems.n += 8

    def turn(i):
        m = lax.rem(i + 1, 4)
        return lax.rem(d + m, 2) + 2 * lax.rem(d // 2 + m // 2, 2)

    def half_out(i):
        f = turn(i)
        return remote(
            piece(1, f, 1 - c), gout.at[f], ss.at[swap_out + i], rs.at[swap_out + i], sib
        )

    def half_in(f):
        at = swap_out + 4 + f
        return remote(piece(0, f, 1 - c), gin.at[f], ss.at[at], rs.at[at], sib)

    owned = []

    def owner_send(m, i):
        src, dst = ((gin, oin), (gout, oout))[m]
        cp = remote(
            src.at[across[i]],
            dst.at[lax.rem(d, 2), c],
            oe.at[m, i],
            ore.at[m, lax.rem(d, 2), c],
            (across[i], 2 * z + d // 2),
        )
        cp.start()
        owned.append(cp)

    def owner_here(m):
        src, dst = ((gin, oin), (gout, oout))[m]
        return pltpu.make_async_copy(src.at[d], dst.at[lax.rem(d, 2), c], ls.at[7 + m])

    def owner_there(m):
        src, dst = ((gin, oin), (gout, oout))[m]
        return remote(
            src.at[d], dst.at[lax.rem(d, 2), c], oe.at[m, 3], ore.at[m, lax.rem(d, 2), c], sib
        )

    def owner_local(m):
        @pl.when(d // 2 == c)
        def _():
            owner_here(m).start()

        @pl.when(d // 2 != c)
        def _():
            owner_there(m).start()

    def add_half(m, f):
        ref, rows_n = ((gin, 96), (gout, 384))[m]
        spot = (
            pl.ds(pl.multiple_of(f * 192 + c * 96, 32), 96)
            if m == 0
            else pl.ds(pl.multiple_of(f * 768 + c * 384, 128), 384)
        )
        mine = (win if m == 0 else wout)[spot, :]
        ref[f] = (mine.astype(f32) + ref[f].astype(f32)).astype(bf16)

    def out_done(i):
        half_out(i).wait()
        add_half(1, turn(i))

    def out_owner(i):
        return remote(
            gout.at[turn(i)],
            oout.at[lax.rem(d, 2), c],
            oe.at[1, i],
            ore.at[1, lax.rem(d, 2), c],
            (turn(i), 2 * z + d // 2),
        )

    def out_step(i, carry):
        at = pl.multiple_of(turn(i) * CHUNK, CHUNK)
        wout[pl.ds(at, CHUNK), :] = dot_l(
            hid[:, pl.ds(at, CHUNK)], gback[...].reshape(512, 768)
        ).astype(bf16)
        half_out(i).start()

        @pl.when(i > 0)
        def _():
            out_done(i - 1)
            out_owner(i - 1).start()

        return carry

    lax.fori_loop(0, 4, out_step, 0)
    out_done(3)
    owner_local(1)
    owned += [out_owner(i) for i in range(3)]

    def in_step(f, carry):
        at = pl.multiple_of(f * CHUNK, CHUNK)
        win[:, pl.ds(at, CHUNK)] = dot_l(
            arrived[...].reshape(512, 768), slope[:, pl.ds(at, CHUNK)].astype(bf16)
        ).astype(bf16)
        return carry

    lax.fori_loop(0, 4, in_step, 0)
    for f in range(4):
        half_in(f).start()
    kacc[...] = jnp.zeros_like(kacc)
    vacc[...] = jnp.zeros_like(vacc)
    gacc[...] = jnp.zeros_like(gacc)
    for f in range(4):
        half_in(f).wait()
        add_half(0, f)
    for i in range(3):
        owner_send(0, i)
    owner_local(0)
    received(entries)
    sent(entries)

    dn2 = dot_n(chart, entry[...].reshape(512, 768))
    dn2 = dn2 + dot_t(grad_logits, wqf[:, 576:704])
    hidden = hidden_v[...]
    r2 = rms(hidden)
    scaled = dn2 * gain_second
    mean = jnp.mean(scaled * hidden, axis=1, keepdims=True)
    dh = gout_v[...] + r2 * scaled - hidden * (r2 * r2 * r2) * mean
    dh_low = dh.astype(bf16)
    for zb in range(4):
        do_out[zb] = dot_t(dh_low, wrf[192 * zb : 192 * (zb + 1), :]).astype(bf16)
    heads = run(
        [
            sems.copy(do_out.at[lax.rem(z + k, 4)], do.at[z], zs[i])
            for i, k in enumerate((1, 2, 3))
        ]
    )
    do[pl.ds(z, 1)] = do_out[pl.ds(z, 1)]
    grad_tokens[...] = dh

    for zb in range(4):
        rest[192 * zb : 192 * (zb + 1), :768] = dot_l(attn[zb], dh_low).astype(bf16)
    gain_rows = jnp.broadcast_to(jnp.sum(dn2 * hidden * r2, axis=0, keepdims=True), (128, 768))
    n2 = (hidden * r2 * gain_second).astype(bf16)
    tall = lax.broadcasted_iota(jnp.int32, (768, 128), 1)
    rest[:, 768:] = jnp.where(
        tall == 16, jnp.transpose(gain_rows), dot_l(n2, grad_logits)
    ).astype(bf16)
    rest_swap = run([sems.copy(rest, rest_in, sib)])
    received(rest_swap)
    sent(rest_swap)
    rest_in[...] = (rest[...].astype(f32) + rest_in[...].astype(f32)).astype(bf16)

    def slot(ref, i, j):
        return ref.at[pl.ds(pl.multiple_of((i * 4 + j) * 24, 8), 24)]

    rest_a = []
    for i, k in enumerate((1, 2, 3)):
        zt = lax.rem(z + k, 4)
        for dd in range(4):
            rest_a.append(sems.copy(rows_of(rest_in, dd, zt, c), slot(rest_mid, z, dd), zs[i]))
    run(rest_a)
    for dd in range(4):
        pltpu.make_async_copy(
            rows_of(rest_in, dd, z, c), slot(rest_mid, z, dd), ls.at[11 + dd]
        ).start()
    received(heads)

    scale = HEAD ** (-0.5)
    first_back = sems.n
    sems.n += 4
    swaps = []

    def to_tokens(zb, pair):
        received(pair)
        here = pl.ds(pl.multiple_of((2 * zb + c) * 128, 128), 128)
        dqkv[zb, :, 192:384] = (kacc[here] * scale + dk_in[zb].astype(f32)).astype(bf16)
        dqkv[zb, :, 384:] = (vacc[here] + dv_in[zb].astype(f32)).astype(bf16)
        dn1 = dot_t(dqkv[zb], wqf[:, :576])
        part[zb] = dn1.astype(bf16)

        @pl.when(z != zb)
        def _():
            remote(
                part.at[zb],
                parts.at[z],
                ss.at[first_back + zb],
                rs.at[first_back + z],
                (d, 2 * zb + c),
            ).start()

        @pl.when(z == zb)
        def _():
            parts[zb] = part[zb]

        xf = xs[zb].astype(f32)
        gain_rows_v[zb : zb + 1, :] = jnp.sum(dn1 * xf * rms(xf), axis=0, keepdims=True)

    for zb in (3, 2, 1, 0):
        width = 256 * (zb + 1)
        start = pl.multiple_of(128 * (7 - 2 * zb) - 128 * c, 128)
        keys = kf[: zb + 1].reshape(width, 192)
        values = vf[: zb + 1].reshape(width, 192)
        dq = jnp.zeros((128, 192), f32)
        for h in range(3):
            mask = head_mask(h)
            qh = jnp.where(mask, q[zb], jnp.zeros((), bf16))
            doh = jnp.where(mask, do[zb], jnp.zeros((), bf16))
            p = soft_rows(qh, keys, bias, h, start, width)
            vacc[:width] += dot_l(p.astype(bf16), doh)
            dp = dot_t(doh, values)
            dot = jnp.sum(p * dp, axis=1, keepdims=True)
            ds = (p * (dp - dot)).astype(bf16)
            gacc[h, :, pl.ds(start, width)] += ds.astype(f32)
            dq = dq + jnp.where(mask, dot_n(ds, keys), 0.0)
            kacc[:width] += dot_l(ds, qh)
        dqkv[zb, :, :192] = (dq * scale).astype(bf16)
        there = pl.ds(pl.multiple_of((2 * zb + 1 - c) * 128, 128), 128)
        dk_out[zb] = (kacc[there] * scale).astype(bf16)
        dv_out[zb] = vacc[there].astype(bf16)
        swaps.append(
            run(
                [
                    sems.copy(dk_out.at[zb], dk_in.at[zb], sib),
                    sems.copy(dv_out.at[zb], dv_in.at[zb], sib),
                ]
            )
        )
        if zb < 3:
            to_tokens(zb + 1, swaps[-2])
    to_tokens(0, swaps[-1])
    swaps = sum(swaps, [])

    gain_part = jnp.sum(gain_rows_v[...], axis=0, keepdims=True)
    wpart[:, :576] = dot_l(n1s[...].reshape(512, 768), dqkv[...].reshape(512, 576)).astype(bf16)
    wpart[:, 576:] = jnp.transpose(jnp.broadcast_to(gain_part, (128, 768))).astype(bf16)
    wswap = run([sems.copy(wpart, wpart_in, sib)])
    received(wswap)
    sent(wswap)
    wpart_in[...] = (wpart[...].astype(f32) + wpart_in[...].astype(f32)).astype(bf16)
    w_a = []
    for i, dd in enumerate(across):
        for zt in range(4):
            w_a.append(sems.copy(rows_of(wpart_in, dd, zt, c), slot(wmid, d, zt), plane[i]))
    run(w_a)
    for zt in range(4):
        pltpu.make_async_copy(
            rows_of(wpart_in, d, zt, c), slot(wmid, d, zt), ls.at[15 + zt]
        ).start()
    received(rest_a)
    for dd in range(4):
        pltpu.make_async_copy(
            rows_of(rest_in, dd, z, c), slot(rest_mid, z, dd), ls.at[11 + dd]
        ).wait()
    rest[:96] = sum(rest_mid[96 * i : 96 * (i + 1), :].astype(f32) for i in range(4)).astype(bf16)
    rest_b = run(
        [
            sems.copy(
                rest.at[pl.ds(pl.multiple_of(dd * 24, 8), 24)],
                rest_got.at[pl.ds(pl.multiple_of(d * 24, 8), 24)],
                plane[i],
            )
            for i, dd in enumerate(across)
        ]
    )

    row = lax.broadcasted_iota(jnp.int32, (128, 1), 0)
    sums = []
    for h in range(3):
        y = jnp.concatenate([jnp.zeros((128, ROLL - GW), f32), gacc[h]], axis=1)
        for bit in range(7):
            y = jnp.where((row >> bit) & 1 == 1, pltpu.roll(y, ROLL - (1 << bit), 1), y)
        sums.append(jnp.sum(y, axis=0, keepdims=True))
    hot = hot_of(buckets, 128)
    table = lax.dot_general(
        jnp.concatenate(sums + [jnp.zeros((5, ROLL), f32)], axis=0),
        hot,
        (((1,), (1,)), ((), ())),
        precision=HIGH,
        preferred_element_type=f32,
    )
    index = lax.broadcasted_iota(jnp.int32, (8, 128), 0)
    small[...] = jnp.where(index == 3, loss, table)
    shares = run([sems.copy(small, shared.at[device], dev) for dev in everyone])
    shared[pl.ds(device, 1)] = small[...][None]

    for zb in range(4):

        @pl.when(z != zb)
        def _(zb=zb):
            remote(
                part.at[zb],
                parts.at[zb],
                ss.at[first_back + zb],
                rs.at[first_back + zb],
                (d, 2 * zb + c),
            ).wait()

    dn1 = (
        parts[0].astype(f32) + parts[1].astype(f32) + parts[2].astype(f32) + parts[3].astype(f32)
    )
    xf = x[...].astype(f32)
    r1 = rms(xf)
    scaled = dn1 * gain_first
    mean = jnp.mean(scaled * xf, axis=1, keepdims=True)
    grad_tokens[...] += r1 * scaled - xf * (r1 * r1 * r1) * mean

    received(w_a)
    for zt in range(4):
        pltpu.make_async_copy(
            rows_of(wpart_in, d, zt, c), slot(wmid, d, zt), ls.at[15 + zt]
        ).wait()
    wpart[:96] = sum(wmid[96 * i : 96 * (i + 1), :].astype(f32) for i in range(4)).astype(bf16)
    w_b = run(
        [
            sems.copy(
                wpart.at[pl.ds(pl.multiple_of(lax.rem(z + k, 4) * 24, 8), 24)],
                wgot.at[pl.ds(pl.multiple_of(z * 24, 8), 24)],
                zs[i],
            )
            for i, k in enumerate((1, 2, 3))
        ]
    )
    own_rows = [
        pltpu.make_async_copy(
            rest.at[pl.ds(pl.multiple_of(d * 24, 8), 24)],
            rest_got.at[pl.ds(pl.multiple_of(d * 24, 8), 24)],
            ls.at[9],
        ),
        pltpu.make_async_copy(
            wpart.at[pl.ds(pl.multiple_of(z * 24, 8), 24)],
            wgot.at[pl.ds(pl.multiple_of(z * 24, 8), 24)],
            ls.at[10],
        ),
    ]
    run(own_rows)

    received(shares)
    by_z = []
    for zb in range(4):
        total = jnp.zeros((8, 128), f32)
        for dd in range(4):
            for cc in range(2):
                total = total + shared[(dd * 4 + zb) * 2 + cc]
        by_z.append(total)
    loss_all = by_z[0] + by_z[1] + by_z[2] + by_z[3]
    extra[0:8] = loss_all[3:4] / (count * 768.0) + jnp.zeros((8, 128), f32)
    for zb in range(4):
        extra[8 + 8 * zb : 16 + 8 * zb] = by_z[zb]

    received(rest_b)
    received(w_b)
    for cp in own_rows:
        cp.wait()
    total = jnp.zeros((24, 896), f32)
    gain_total = jnp.zeros((24, 128), f32)
    for zb in range(4):
        total = total + rest_got[24 * zb : 24 * (zb + 1), :].astype(f32)
        block = wgot[24 * zb : 24 * (zb + 1), :].astype(f32)
        gain_total = gain_total + block[:, 576:]
        for i in range(3):
            at = i * 768 + zb * 192
            grad_qkv[:, at : at + 192] = block[:, i * 192 : (i + 1) * 192]
    grad_rest[:, :896] = total
    grad_rest[:, 896:] = gain_total

    for m, (src, dst) in enumerate(((gin, oin), (gout, oout))):
        for l in range(2):
            for half in range(2):
                here = (2 * c + l == d) & (c == half)

                @pl.when(jnp.logical_not(here))
                def _(src=src, dst=dst, m=m, l=l, half=half):
                    remote(
                        src.at[0], dst.at[l, half], oe.at[m, 3], ore.at[m, l, half], sib
                    ).wait_recv()

        @pl.when(d // 2 == c)
        def _(m=m):
            owner_here(m).wait()

        @pl.when(d // 2 != c)
        def _(m=m):
            owner_there(m).wait_send()

    sent(heads + rest_a + rest_b + swaps + shares + w_a + w_b + owned)


def finish_kernel(
    oin,
    oout,
    output,
    tokens,
    qkv,
    rest,
    extra,
    gin,
    gout,
    o,
    t,
    g,
    w,
    r,
    ga,
    gm,
    table,
    loss,
    low_in,
    low_out,
    wide_in,
    wide_out,
    o_v,
    t_v,
    g_v,
    sems,
):
    f32 = jnp.float32
    loads, stores = [], []
    for i in range(4):
        loads.append(pltpu.make_async_copy(oin.at[i], low_in.at[i], sems.at[0, i]))
        loads.append(pltpu.make_async_copy(oout.at[i], low_out.at[i], sems.at[1, i]))
        stores.append(pltpu.make_async_copy(wide_in.at[i], gin.at[i], sems.at[2, i]))
        stores.append(pltpu.make_async_copy(wide_out.at[i], gout.at[i], sems.at[3, i]))
    run(loads)
    trios = ((output, o_v, o), (tokens, t_v, t), (qkv, g_v, g))
    moved = run(
        [pltpu.make_async_copy(a, b, sems.at[4, i]) for i, (a, b, _) in enumerate(trios)]
    )
    for i in range(4):
        loads[2 * i].wait()
        wide_in[i] = low_in[i].astype(f32)
        stores[2 * i].start()
        loads[2 * i + 1].wait()
        wide_out[i] = low_out[i].astype(f32)
        stores[2 * i + 1].start()
    for cp in moved:
        cp.wait()
    moved = run(
        [pltpu.make_async_copy(b, e, sems.at[4, i]) for i, (_, b, e) in enumerate(trios)]
    )
    w[...] = rest[:, :768]
    turned = jnp.transpose(
        jnp.concatenate([rest[:, 768:1024], jnp.zeros((104, 256), f32)], axis=0)
    )
    r[...] = turned[:16, :24]
    gm[...] = turned[16:17, :24]
    ga[...] = turned[128:129, :24]
    for zb in range(4):
        table[3 * zb : 3 * zb + 3, :] = extra[8 + 8 * zb : 11 + 8 * zb, :BUCKETS]
    loss[...] = extra[0:1, 0:1]
    for cp in stores + moved:
        cp.wait()


def fast_path(
    tokens,
    w_qkv,
    w_attn_out,
    gain_attn,
    gain_moe,
    w_router,
    rel_bias,
    w_in,
    w_out,
    teacher,
    routes,
    valid,
    buckets,
):
    f32, bf16 = jnp.float32, jnp.bfloat16
    block = pltpu.VMEM((16, 32, 768), bf16)
    heads = pltpu.VMEM((4, 128, 192), bf16)
    both = pltpu.VMEM((4, 2, 128, 192), bf16)
    wide = pltpu.VMEM((4, 128, 768), bf16)
    output, grad_tokens, grad_qkv, grad_rest, extra, oin, oout = comm_call(
        step_kernel,
        [
            sds((128, 768), f32),
            sds((128, 768), f32),
            sds((24, 2304), f32),
            sds((24, 1024), f32),
            sds((40, 128), f32),
            sds((2, 2, 96, 3072)),
            sds((2, 2, 384, 768)),
        ],
        13,
        1,
        [
            pltpu.VMEM((4, 24, 704), bf16),
            pltpu.VMEM((768, 704), bf16),
            pltpu.VMEM((768, 768), bf16),
            wide,
            wide,
            heads,
            both,
            both,
            pltpu.VMEM((3, 128, GW), f32),
            pltpu.VMEM((32, ROLL), f32),
            heads,
            heads,
            block,
            block,
            block,
            pltpu.VMEM((768, 3072), bf16),
            pltpu.VMEM((3072, 768), bf16),
            pltpu.VMEM((512, 3072), f32),
            pltpu.VMEM((512, 3072), bf16),
            pltpu.VMEM((512, 768), f32),
            block,
            block,
            block,
            pltpu.VMEM((4, 96, 3072), bf16),
            pltpu.VMEM((4, 384, 768), bf16),
            pltpu.VMEM((128, 768), f32),
            pltpu.VMEM((128, 768), f32),
            heads,
            heads,
            pltpu.VMEM((768, 896), bf16),
            pltpu.VMEM((768, 896), bf16),
            pltpu.VMEM((96, 896), bf16),
            pltpu.VMEM((1024, 192), f32),
            pltpu.VMEM((1024, 192), f32),
            pltpu.VMEM((3, 128, GW), f32),
            heads,
            heads,
            heads,
            heads,
            pltpu.VMEM((4, 128, 576), bf16),
            wide,
            wide,
            pltpu.VMEM((768, 704), bf16),
            pltpu.VMEM((768, 704), bf16),
            pltpu.VMEM((96, 704), bf16),
            pltpu.VMEM((8, 128), f32),
            pltpu.VMEM((32, 8, 128), f32),
            pltpu.VMEM((4, 768), f32),
            pltpu.VMEM((384, 896), bf16),
            pltpu.VMEM((384, 704), bf16),
            pltpu.SemaphoreType.DMA((300,)),
            pltpu.SemaphoreType.DMA((300,)),
            pltpu.SemaphoreType.DMA((2, 4, 2)),
            pltpu.SemaphoreType.DMA((2, 5)),
            pltpu.SemaphoreType.DMA((2, 5)),
            pltpu.SemaphoreType.DMA((2, 2, 2)),
            pltpu.SemaphoreType.DMA((19,)),
        ],
        "layer_step",
        in_specs=[VM] * 11 + [ANY] * 2,
        out_specs=[VM] * 5 + [ANY] * 2,
        vmem=63 << 20,
    )(
        tokens,
        w_qkv,
        w_attn_out,
        w_router.T,
        gain_attn[None],
        gain_moe[None],
        rel_bias.T,
        buckets[None],
        routes.T,
        valid[None],
        teacher,
        w_in.reshape(2, 2, 96, 3072),
        w_out.reshape(2, 2, 384, 768),
    )

    small_out = [
        (128, 768),
        (128, 768),
        (24, 2304),
        (24, 768),
        (16, 24),
        (1, 24),
        (1, 24),
        (12, BUCKETS),
        (1, 1),
    ]
    gin, gout, output, grad_tokens, grad_qkv, grad_w, grad_r, grad_ga, grad_gm, table, loss = (
        pl.pallas_call(
            finish_kernel,
            out_shape=[sds((4, 96, 3072), f32), sds((4, 384, 768), f32)]
            + [sds(shape, f32) for shape in small_out],
            in_specs=[ANY] * 5 + [VM] * 2,
            out_specs=[ANY] * 5 + [VM] * 6,
            scratch_shapes=[
                pltpu.VMEM((4, 96, 3072), bf16),
                pltpu.VMEM((4, 384, 768), bf16),
                pltpu.VMEM((4, 96, 3072), f32),
                pltpu.VMEM((4, 384, 768), f32),
                pltpu.VMEM((128, 768), f32),
                pltpu.VMEM((128, 768), f32),
                pltpu.VMEM((24, 2304), f32),
                pltpu.SemaphoreType.DMA((5, 4)),
            ],
            compiler_params=pltpu.CompilerParams(vmem_limit_bytes=63 << 20),
            name="finish",
        )(
            oin.reshape(4, 96, 3072),
            oout.reshape(4, 384, 768),
            output,
            grad_tokens,
            grad_qkv,
            grad_rest,
            extra,
        )
    )
    return (
        output,
        loss.reshape(()),
        grad_tokens,
        grad_qkv,
        grad_w,
        grad_ga.reshape(24),
        grad_gm.reshape(24),
        grad_r.T,
        table.T,
        gin.reshape(2, 192, 3072),
        gout.reshape(2, 768, 768),
    )


def choose(*arrays):
    tokens, w_in, rel_bias, buckets = arrays[0], arrays[7], arrays[6], arrays[12]
    fits = (
        lax.axis_size("dp") == 4
        and lax.axis_size("seq") == 8
        and tokens.shape == (128, 768)
        and w_in.shape == (2, 192, 3072)
        and rel_bias.shape == (32, 12)
        and buckets.shape == (1024,)
    )
    return fast_path(*arrays) if fits else on_device(*arrays)


def solution(mesh):
    in_specs = (
        P(("dp", "seq"), None),
        P(("dp", "seq"), None),
        P(("dp", "seq"), None),
        P(("dp", "seq")),
        P(("dp", "seq")),
        P(("dp", "seq"), None),
        P(),
        P("seq", "dp", None),
        P("seq", "dp", None),
        P(("dp", "seq"), None),
        P(("dp", "seq"), None),
        P(("dp", "seq")),
        P(),
    )
    out_specs = (
        P(("dp", "seq"), None),
        P(),
        P(("dp", "seq"), None),
        P(("dp", "seq"), None),
        P(("dp", "seq"), None),
        P(("dp", "seq")),
        P(("dp", "seq")),
        P(("dp", "seq"), None),
        P(),
        P("seq", "dp", None),
        P("seq", "dp", None),
    )
    return jax.shard_map(
        choose, mesh=mesh, in_specs=in_specs, out_specs=out_specs, check_vma=False
    )
```

```python
import functools

import jax
import jax.numpy as jnp
from jax import lax
from jax.experimental import pallas as pl
from jax.experimental.pallas import tpu as pltpu
from jax.sharding import PartitionSpec as P

H = 12
HEAD = 64
BUCKETS = 32


EPS = 1e-06
NEG = -1e30
SECTION = 512
HIGH = lax.Precision.HIGHEST
FLOAT_TYPE = jnp.float32
HALF_TYPE = jnp.bfloat16


def normalize(values, gain):
    factor = lax.rsqrt(jnp.mean(values * values, axis=-1, keepdims=True) + EPS)
    return (values * factor * gain, factor)


def norm_back(values, factor, gain, grad_norm):
    scaled = grad_norm * gain
    mean_term = jnp.mean(scaled * values, axis=-1, keepdims=True)
    grad_values = factor * scaled - values * (factor * factor * factor) * mean_term
    return (grad_values, jnp.sum(grad_norm * values * factor, axis=0))


def gelu_grad(preact, grad_hidden):
    _, gelu_back = jax.vjp(jax.nn.gelu, preact)
    return gelu_back(grad_hidden)[0]


def in_sections(advance, running, shards):
    row_count = shards[0].shape[0]
    sections = row_count // SECTION
    stacked = tuple((member.reshape((sections, SECTION) + member.shape[1:]) for member in shards))

    def one_section(inner_state, entry_pair):
        return (advance(inner_state, entry_pair[1], entry_pair[0] * SECTION), None)

    final_state, _ = lax.scan(
        one_section, running, (jnp.arange(sections, dtype=jnp.int32), stacked)
    )
    return final_state


def score_block(queries, key_rows, query_start, key_start, rel_bias, edges):
    query_count = queries.shape[0]
    key_count = key_rows.shape[0]
    distance = (query_start + jnp.arange(query_count, dtype=jnp.int32))[:, None] - (
        key_start + jnp.arange(key_count, dtype=jnp.int32)
    )[None, :]
    allowed = distance >= 0
    bucket_hot = (
        (distance[:, :, None] >= edges[None, None, :-1])
        & (distance[:, :, None] < edges[None, None, 1:])
    ).astype(FLOAT_TYPE)
    bias_term = jnp.einsum("qkb,bh->hqk", bucket_hot, rel_bias, precision=HIGH)
    raw_scores = (
        jnp.einsum("qhd,khd->hqk", queries, key_rows, preferred_element_type=FLOAT_TYPE)
        * queries.shape[2] ** (-0.5)
        + bias_term
    )
    return (raw_scores, allowed, bucket_hot)


def split_three(values):
    upper = lax.optimization_barrier(values.astype(HALF_TYPE))
    remainder = values - upper.astype(FLOAT_TYPE)
    middle = lax.optimization_barrier(remainder.astype(HALF_TYPE))
    bottom = (remainder - middle.astype(FLOAT_TYPE)).astype(HALF_TYPE)
    return jnp.stack([upper, middle, bottom], axis=1)


def join_three(packed):
    as_float = packed.astype(FLOAT_TYPE)
    return as_float[:, 0] + as_float[:, 1] + as_float[:, 2]


def on_device(
    tokens,
    w_qkv,
    w_attn_out,
    gain_attn,
    gain_moe,
    w_router,
    rel_bias,
    w_in,
    w_out,
    teacher,
    routes,
    valid,
    buckets,
):
    tok_rows = tokens.shape[0]
    width = tokens.shape[1]
    seq_count = lax.axis_size("seq")
    my_start = lax.axis_index("seq") * tok_rows
    local_experts = w_in.shape[0]
    experts_all = local_experts * seq_count
    capacity = 4 * tok_rows // experts_all
    slot_rows = seq_count * capacity
    scale = HEAD ** (-0.5)
    qkv_full, attn_full, router_full, gain_one, gain_two, valid_all = (
        lax.all_gather(w_qkv, ("dp", "seq"), axis=0, tiled=True),
        lax.all_gather(w_attn_out, ("dp", "seq"), axis=0, tiled=True),
        lax.all_gather(w_router, ("dp", "seq"), axis=0, tiled=True),
        lax.all_gather(gain_attn, ("dp", "seq"), axis=0, tiled=True),
        lax.all_gather(gain_moe, ("dp", "seq"), axis=0, tiled=True),
        lax.all_gather(valid.astype(HALF_TYPE), ("dp", "seq"), axis=0, tiled=True),
    )
    valid_float = valid.astype(FLOAT_TYPE)
    count_all = jnp.sum(valid_all.astype(FLOAT_TYPE))
    tokens_all = tok_rows * lax.axis_size("dp") * seq_count
    edges = jnp.sum(
        (buckets[None, :] < jnp.arange(BUCKETS + 1, dtype=jnp.int32)[:, None]).astype(jnp.int32),
        axis=1,
    )
    inputs = tokens.astype(FLOAT_TYPE)
    gain_first = gain_one.astype(FLOAT_TYPE)
    gain_second = gain_two.astype(FLOAT_TYPE)
    normed_one, factor_one = normalize(inputs, gain_first)
    normed_in = normed_one.astype(HALF_TYPE)
    qkv_rows = jnp.dot(normed_in, qkv_full, preferred_element_type=FLOAT_TYPE)
    query_low = qkv_rows[:, :width].astype(HALF_TYPE)
    key_low = qkv_rows[:, width : 2 * width].astype(HALF_TYPE)
    value_low = qkv_rows[:, 2 * width :].astype(HALF_TYPE)
    heads_q = query_low.reshape(tok_rows, H, HEAD)
    heads_k = key_low.reshape(tok_rows, H, HEAD)
    heads_v = value_low.reshape(tok_rows, H, HEAD)
    last_row = my_start + tok_rows - 1

    def forward_step(running, shards, offset):
        key_rows = shards[0].reshape(shards[0].shape[0], H, HEAD)
        value_rows = shards[1].reshape(shards[1].shape[0], H, HEAD)

        def work(inner_state):
            maximum, denom, mixture = inner_state
            raw_scores, allowed, _ = score_block(
                heads_q, key_rows, my_start, offset, rel_bias, edges
            )
            masked = jnp.where(allowed[None], raw_scores, NEG)
            new_max = jnp.maximum(maximum, jnp.max(masked, axis=2))
            weights = jnp.where(allowed[None], jnp.exp(masked - new_max[:, :, None]), 0.0)
            rescale = jnp.exp(maximum - new_max)
            addend = jnp.einsum(
                "hqk,khd->hqd",
                weights.astype(HALF_TYPE),
                value_rows,
                preferred_element_type=FLOAT_TYPE,
            )
            return (
                new_max,
                denom * rescale + jnp.sum(weights, axis=2),
                mixture * rescale[:, :, None] + addend,
            )

        return lax.cond(offset <= last_row, work, lambda inner_state: inner_state, running)

    start_state = (
        jnp.full((H, tok_rows), NEG, FLOAT_TYPE),
        jnp.zeros((H, tok_rows), FLOAT_TYPE),
        jnp.zeros((H, tok_rows, HEAD), FLOAT_TYPE),
    )
    maximum, denom, mixture = in_sections(
        forward_step,
        start_state,
        (
            lax.all_gather(key_low, "seq", axis=0, tiled=True),
            lax.all_gather(value_low, "seq", axis=0, tiled=True),
        ),
    )
    log_total = maximum + jnp.log(denom)
    attn_heads = mixture / denom[:, :, None]
    attn_rows = jnp.transpose(attn_heads, (1, 0, 2)).reshape(tok_rows, width)
    attn_low = attn_rows.astype(HALF_TYPE)
    hidden_state = inputs + jnp.dot(attn_low, attn_full, preferred_element_type=FLOAT_TYPE)
    normed_two, factor_two = normalize(hidden_state, gain_second)
    moe_in = normed_two.astype(HALF_TYPE)
    logits = jnp.dot(moe_in, router_full, preferred_element_type=FLOAT_TYPE)
    chosen = jnp.take_along_axis(logits, routes, axis=1)
    gate_weights = jax.nn.softmax(chosen, axis=1)
    flat_routes = routes.reshape(-1)
    matches = (flat_routes[:, None] == jnp.arange(experts_all, dtype=jnp.int32)[None, :]).astype(
        jnp.int32
    )
    slot_index = jnp.sum((jnp.cumsum(matches, axis=0) - matches) * matches, axis=1)
    target_dev = flat_routes // local_experts
    target_local = flat_routes % local_experts
    position = (target_dev * capacity + slot_index) * local_experts + target_local
    dispatch_map = (
        jnp.arange(experts_all * capacity, dtype=jnp.int32)[:, None] == position[None, :]
    ).astype(HALF_TYPE)
    dispatch_map = dispatch_map.reshape(experts_all * capacity, tok_rows, 2)
    outgoing = jnp.einsum(
        "prk,rd->pd", dispatch_map, moe_in, preferred_element_type=FLOAT_TYPE
    ).astype(HALF_TYPE)
    arrived = lax.all_to_all(
        outgoing.reshape(seq_count, capacity * local_experts, width),
        "seq",
        split_axis=0,
        concat_axis=0,
        tiled=True,
    )
    arrived_rows = arrived.reshape(slot_rows, local_experts, width)
    in_full, out_full = (
        lax.all_gather(w_in, "dp", axis=1, tiled=True),
        lax.all_gather(w_out, "dp", axis=1, tiled=True),
    )
    preact = jnp.einsum("mld,ldf->mlf", arrived_rows, in_full, preferred_element_type=FLOAT_TYPE)
    hidden = jax.nn.gelu(preact).astype(HALF_TYPE)
    result = jnp.einsum("mlf,lfd->mld", hidden, out_full, preferred_element_type=FLOAT_TYPE).astype(
        HALF_TYPE
    )
    returned = lax.all_to_all(
        result.reshape(seq_count, capacity * local_experts, width),
        "seq",
        split_axis=0,
        concat_axis=0,
        tiled=True,
    )
    returned = returned.reshape(experts_all * capacity, width)
    combined = jnp.einsum("prk,pd->krd", dispatch_map, returned, preferred_element_type=FLOAT_TYPE)
    output = hidden_state + gate_weights[:, 0:1] * combined[0] + gate_weights[:, 1:2] * combined[1]
    error_rows = output - teacher.astype(FLOAT_TYPE)
    loss_local = jnp.sum(valid_float[:, None] * error_rows * error_rows)
    grad_out = 2.0 * tokens_all / count_all * valid_float[:, None] * error_rows
    grad_gate = jnp.einsum("krd,rd->rk", combined, grad_out)
    grad_chosen = gate_weights * (
        grad_gate - jnp.sum(gate_weights * grad_gate, axis=1, keepdims=True)
    )
    pick = (routes[:, :, None] == jnp.arange(experts_all, dtype=jnp.int32)[None, None, :]).astype(
        FLOAT_TYPE
    )
    grad_logits = jnp.sum(pick * grad_chosen[:, :, None], axis=1).astype(HALF_TYPE)
    grad_router = jnp.einsum("rd,re->de", moe_in, grad_logits, preferred_element_type=FLOAT_TYPE)
    grad_result = (jnp.transpose(gate_weights)[:, :, None] * grad_out[None]).astype(HALF_TYPE)
    grad_slots = jnp.einsum(
        "prk,krd->pd", dispatch_map, grad_result, preferred_element_type=FLOAT_TYPE
    ).astype(HALF_TYPE)
    grad_arrived = lax.all_to_all(
        grad_slots.reshape(seq_count, capacity * local_experts, width),
        "seq",
        split_axis=0,
        concat_axis=0,
        tiled=True,
    )
    grad_rows = grad_arrived.reshape(slot_rows, local_experts, width)
    grad_hidden = jnp.einsum("mld,lfd->mlf", grad_rows, out_full, preferred_element_type=FLOAT_TYPE)
    grad_preact = gelu_grad(preact, grad_hidden).astype(HALF_TYPE)
    grad_out_local = jnp.einsum(
        "mlf,mld->lfd", hidden, grad_rows, preferred_element_type=FLOAT_TYPE
    )
    grad_in_local = jnp.einsum(
        "mld,mlf->ldf", arrived_rows, grad_preact, preferred_element_type=FLOAT_TYPE
    )
    grad_entry = jnp.einsum(
        "mlf,ldf->mld", grad_preact, in_full, preferred_element_type=FLOAT_TYPE
    ).astype(HALF_TYPE)
    grad_w_in, grad_w_out = (
        lax.psum_scatter(
            grad_in_local.astype(jnp.bfloat16), "dp", scatter_dimension=1, tiled=True
        ).astype(jnp.float32),
        lax.psum_scatter(
            grad_out_local.astype(jnp.bfloat16), "dp", scatter_dimension=1, tiled=True
        ).astype(jnp.float32),
    )
    grad_back = lax.all_to_all(
        grad_entry.reshape(seq_count, capacity * local_experts, width),
        "seq",
        split_axis=0,
        concat_axis=0,
        tiled=True,
    )
    grad_back = grad_back.reshape(experts_all * capacity, width)
    grad_moe_in = jnp.einsum(
        "prk,pd->rd", dispatch_map, grad_back, preferred_element_type=FLOAT_TYPE
    )
    grad_moe_in = grad_moe_in + jnp.einsum(
        "re,de->rd", grad_logits, router_full, preferred_element_type=FLOAT_TYPE
    )
    grad_hidden_norm, grad_gain_second = norm_back(
        hidden_state, factor_two, gain_second, grad_moe_in
    )
    grad_state = grad_out + grad_hidden_norm
    grad_state_low = grad_state.astype(HALF_TYPE)
    grad_attn_w = jnp.einsum(
        "rd,re->de", attn_low, grad_state_low, preferred_element_type=FLOAT_TYPE
    )
    grad_attn_low = jnp.einsum(
        "re,de->rd", grad_state_low, attn_full, preferred_element_type=FLOAT_TYPE
    ).astype(HALF_TYPE)
    heads_dout = grad_attn_low.reshape(tok_rows, H, HEAD)
    softmax_dot = jnp.sum(
        jnp.transpose(heads_dout, (1, 0, 2)).astype(FLOAT_TYPE) * attn_heads, axis=2
    )
    row_stats = split_three(
        jnp.stack([jnp.transpose(log_total), jnp.transpose(softmax_dot)], axis=1)
    )

    def backward_step(running, shards, offset):
        key_rows = shards[0].reshape(shards[0].shape[0], H, HEAD)
        value_rows = shards[1].reshape(shards[1].shape[0], H, HEAD)
        query_rows = shards[2].reshape(shards[2].shape[0], H, HEAD)
        dout_rows = shards[3].reshape(shards[3].shape[0], H, HEAD)
        stats_rows = join_three(shards[4])
        piece_total = jnp.transpose(stats_rows[:, 0, :])
        piece_dot = jnp.transpose(stats_rows[:, 1, :])
        grad_query, grad_table, grad_key, grad_value = running

        def query_work(inner_state):
            inner_query, inner_table = inner_state
            raw_scores, allowed, bucket_hot = score_block(
                heads_q, key_rows, my_start, offset, rel_bias, edges
            )
            weights = jnp.where(allowed[None], jnp.exp(raw_scores - log_total[:, :, None]), 0.0)
            grad_prob = jnp.einsum(
                "qhd,khd->hqk", heads_dout, value_rows, preferred_element_type=FLOAT_TYPE
            )
            grad_score = (weights * (grad_prob - softmax_dot[:, :, None])).astype(HALF_TYPE)
            inner_query = (
                inner_query
                + jnp.einsum(
                    "hqk,khd->hqd", grad_score, key_rows, preferred_element_type=FLOAT_TYPE
                )
                * scale
            )
            inner_table = inner_table + jnp.einsum(
                "hqk,qkb->bh", grad_score.astype(FLOAT_TYPE), bucket_hot, precision=HIGH
            )
            return (inner_query, inner_table)

        def key_work(inner_state):
            inner_key, inner_value = inner_state
            raw_scores, allowed, _ = score_block(
                query_rows, heads_k, offset, my_start, rel_bias, edges
            )
            weights = jnp.where(allowed[None], jnp.exp(raw_scores - piece_total[:, :, None]), 0.0)
            inner_value = inner_value + jnp.einsum(
                "hqk,qhd->khd",
                weights.astype(HALF_TYPE),
                dout_rows,
                preferred_element_type=FLOAT_TYPE,
            )
            grad_prob = jnp.einsum(
                "qhd,khd->hqk", dout_rows, heads_v, preferred_element_type=FLOAT_TYPE
            )
            grad_score = (weights * (grad_prob - piece_dot[:, :, None])).astype(HALF_TYPE)
            inner_key = (
                inner_key
                + jnp.einsum(
                    "hqk,qhd->khd", grad_score, query_rows, preferred_element_type=FLOAT_TYPE
                )
                * scale
            )
            return (inner_key, inner_value)

        grad_query, grad_table = lax.cond(
            offset <= last_row,
            query_work,
            lambda inner_state: inner_state,
            (grad_query, grad_table),
        )
        grad_key, grad_value = lax.cond(
            offset + shards[0].shape[0] - 1 >= my_start,
            key_work,
            lambda inner_state: inner_state,
            (grad_key, grad_value),
        )
        return (grad_query, grad_table, grad_key, grad_value)

    back_start = (
        jnp.zeros((H, tok_rows, HEAD), FLOAT_TYPE),
        jnp.zeros((BUCKETS, H), FLOAT_TYPE),
        jnp.zeros((tok_rows, H, HEAD), FLOAT_TYPE),
        jnp.zeros((tok_rows, H, HEAD), FLOAT_TYPE),
    )
    grad_query, grad_table_local, grad_key, grad_value = in_sections(
        backward_step,
        back_start,
        (
            lax.all_gather(key_low, "seq", axis=0, tiled=True),
            lax.all_gather(value_low, "seq", axis=0, tiled=True),
            lax.all_gather(query_low, "seq", axis=0, tiled=True),
            lax.all_gather(grad_attn_low, "seq", axis=0, tiled=True),
            lax.all_gather(row_stats, "seq", axis=0, tiled=True),
        ),
    )
    grad_qkv_low = jnp.concatenate(
        [
            jnp.transpose(grad_query, (1, 0, 2)).reshape(tok_rows, width),
            grad_key.reshape(tok_rows, width),
            grad_value.reshape(tok_rows, width),
        ],
        axis=1,
    ).astype(HALF_TYPE)
    grad_qkv_w = jnp.einsum("rd,re->de", normed_in, grad_qkv_low, preferred_element_type=FLOAT_TYPE)
    grad_normed_one = jnp.einsum(
        "re,de->rd", grad_qkv_low, qkv_full, preferred_element_type=FLOAT_TYPE
    )
    grad_in_norm, grad_gain_first = norm_back(inputs, factor_one, gain_first, grad_normed_one)
    grad_tokens = grad_state + grad_in_norm
    grad_qkv_own, grad_attn_own, grad_router_own, grad_gain_attn, grad_gain_moe = (
        lax.psum_scatter(grad_qkv_w, ("dp", "seq"), scatter_dimension=0, tiled=True),
        lax.psum_scatter(grad_attn_w, ("dp", "seq"), scatter_dimension=0, tiled=True),
        lax.psum_scatter(grad_router, ("dp", "seq"), scatter_dimension=0, tiled=True),
        lax.psum_scatter(grad_gain_first, ("dp", "seq"), scatter_dimension=0, tiled=True),
        lax.psum_scatter(grad_gain_second, ("dp", "seq"), scatter_dimension=0, tiled=True),
    )
    loss_sum, grad_table = lax.psum((loss_local, grad_table_local), ("dp", "seq"))
    loss = loss_sum / (count_all * width)
    return (
        output,
        loss,
        grad_tokens,
        grad_qkv_own,
        grad_attn_own,
        grad_gain_attn,
        grad_gain_moe,
        grad_router_own,
        grad_table,
        grad_w_in,
        grad_w_out,
    )


MESH = pl.DeviceIdType.MESH
ANY = pl.BlockSpec(memory_space=pl.ANY)
VM = pl.BlockSpec(memory_space=pltpu.VMEM)
ROLL = 1280
GW = 1152


def remote(src, dst, send, recv, dev):
    return pltpu.make_async_remote_copy(
        src_ref=src, dst_ref=dst, send_sem=send, recv_sem=recv, device_id=dev, device_id_type=MESH
    )


def place():
    d = lax.axis_index("dp")
    s = lax.axis_index("seq")
    return d, s, s // 2, lax.rem(s, 2)


def comm_call(body, outs, n_in, cid, scratch, name, in_specs=None, out_specs=None, vmem=None):
    return pl.pallas_call(
        body,
        out_shape=outs,
        in_specs=in_specs or [ANY] * n_in,
        out_specs=out_specs or [ANY] * len(outs),
        scratch_shapes=scratch,
        compiler_params=pltpu.CompilerParams(
            collective_id=cid, has_side_effects=True, vmem_limit_bytes=vmem
        ),
        name=name,
    )


def sds(shape, dtype=jnp.bfloat16):
    return jax.ShapeDtypeStruct(shape, dtype)


def head_mask(h):
    lane = lax.broadcasted_iota(jnp.int32, (1, 192), 1)
    return lane // HEAD == h


def dot_t(a, b):
    return lax.dot_general(a, b, (((1,), (1,)), ((), ())), preferred_element_type=jnp.float32)


def dot_l(a, b):
    return lax.dot_general(a, b, (((0,), (0,)), ((), ())), preferred_element_type=jnp.float32)


def dot_n(a, b):
    return jnp.dot(a, b, preferred_element_type=jnp.float32)


def soft_rows(q, keys, g_ref, h, start, width):
    s = dot_t(q, keys) * HEAD ** (-0.5) + g_ref[h, :, pl.ds(start, width)]
    m = jnp.max(s, axis=1, keepdims=True)
    p = jnp.exp(s - m)
    return p / jnp.sum(p, axis=1, keepdims=True)


CHUNK = 768
GELU_A = 0.7978845608028654
GELU_B = 0.044715


class Sems:
    def __init__(self, send, recv):
        self.send, self.recv, self.n = send, recv, 0

    def copy(self, src, dst, dev):
        cp = remote(src, dst, self.send.at[self.n], self.recv.at[self.n], dev)
        self.n += 1
        return cp


def run(copies):
    for cp in copies:
        cp.start()
    return copies


def received(copies):
    for cp in copies:
        cp.wait_recv()


def sent(copies):
    for cp in copies:
        cp.wait_send()


def chips():
    d, s, z, c = place()
    me = z * 4 + d
    half, i = me // 8, lax.rem(me, 8)
    numbers = [(1 - half) * 8 + lax.rem(i + k, 8) for k in range(8)]
    numbers += [half * 8 + lax.rem(i + k, 8) for k in range(1, 8)]
    return me, numbers, [(lax.rem(t, 4), 2 * (t // 4) + c) for t in numbers]


def rms(v):
    return lax.rsqrt(jnp.mean(v * v, axis=1, keepdims=True) + EPS)


def hot_of(buckets, count):
    b = lax.broadcasted_iota(jnp.int32, (count, 1), 0)
    low = jnp.sum((buckets[...] < b).astype(jnp.float32), axis=1, keepdims=True)
    high = jnp.sum((buckets[...] <= b).astype(jnp.float32), axis=1, keepdims=True)
    at = (1024 - lax.broadcasted_iota(jnp.int32, (1, ROLL), 1)).astype(jnp.float32)
    return ((at >= low) & (at < high) & (at < 1024.0)).astype(jnp.float32)


def step_kernel(
    x,
    w_qkv,
    w_attn,
    w_router_t,
    gain_a,
    gain_m,
    rel_bias_t,
    buckets,
    routes_t,
    valid_t,
    teacher,
    w_in,
    w_out,
    output,
    grad_tokens,
    grad_qkv,
    grad_rest,
    extra,
    oin,
    oout,
    wq,
    wqf,
    wrf,
    xs,
    n1s,
    q,
    kf,
    vf,
    bias,
    lines,
    out_v,
    attn,
    leave,
    left,
    arrived,
    win,
    wout,
    slope,
    hid,
    acc,
    back,
    gback,
    entry,
    gin,
    gout,
    hidden_v,
    gout_v,
    do_out,
    do,
    rest,
    rest_in,
    rest_got,
    kacc,
    vacc,
    gacc,
    dk_out,
    dv_out,
    dk_in,
    dv_in,
    dqkv,
    part,
    parts,
    wpart,
    wpart_in,
    wgot,
    small,
    shared,
    gain_rows_v,
    rest_mid,
    wmid,
    ss,
    rs,
    xe,
    re,
    oe,
    ore,
    ls,
):
    f32, bf16 = jnp.float32, jnp.bfloat16
    d, s, z, c = place()
    sib = (d, s + 1 - 2 * c)
    across = (d + 1 - 2 * lax.rem(d, 2), lax.rem(d + 2, 4), 3 - d)
    plane = [(j, s) for j in across]
    zs = [(d, 2 * lax.rem(z + k, 4) + c) for k in (1, 2, 3)]
    me, numbers, others = chips()
    device = d * 8 + s
    everyone = [(lax.rem(d + k // 8, 4), lax.rem(s + k % 8, 8)) for k in range(1, 32)]
    sems = Sems(ss, rs)
    barrier = pltpu.get_barrier_semaphore()
    for peer in everyone:
        pl.semaphore_signal(barrier, inc=1, device_id=peer, device_id_type=MESH)

    valid_row = valid_t[...].astype(f32)
    diag = lax.broadcasted_iota(jnp.int32, (128, 128), 0) == lax.broadcasted_iota(
        jnp.int32, (128, 128), 1
    )
    lines[:, :128] = jnp.zeros((32, 128), f32)
    lines[0:16, :24] = w_router_t[...].astype(f32)
    lines[16:17, :24] = gain_a[...].astype(f32)
    lines[17:18, :24] = gain_m[...].astype(f32)
    lines[18:19, :24] = jnp.broadcast_to(jnp.sum(valid_row, axis=1, keepdims=True), (1, 24))
    turned = jnp.transpose(lines[:, :128])[:24, :]
    for zt in range(4):
        for i in range(3):
            at = i * 768 + zt * 192
            wq[zt, :, i * 192 : (i + 1) * 192] = w_qkv[:, at : at + 192]
        wq[zt, :, 576:] = jnp.zeros((24, 128), bf16)
        wq[zt, :, 576:608] = turned.astype(bf16)
    pl.semaphore_wait(barrier, 31)

    def rows_of(ref, dd, zz, cc):
        return ref.at[pl.ds(pl.multiple_of(((dd * 4 + zz) * 2 + cc) * 24, 8), 24)]

    def column_rows(ref, dd, dev):
        copies = []
        for zz in range(4):
            spot = rows_of(ref, dd, zz, c)
            copies.append(sems.copy(spot, spot, dev))
        return run(copies)

    local = [
        pltpu.make_async_copy(wq.at[z], rows_of(wqf, d, z, c), ls.at[0]),
        pltpu.make_async_copy(w_attn, rows_of(wrf, d, z, c), ls.at[1]),
        pltpu.make_async_copy(x, xs.at[z], ls.at[2]),
    ]
    run(local)
    stage1 = run(
        [
            sems.copy(wq.at[lax.rem(z + k, 4)], rows_of(wqf, d, z, c), zs[i])
            for i, k in enumerate((1, 2, 3))
        ]
    )

    bulk = []

    def piece(m, dd, half):
        if m == 0:
            return win.at[pl.ds(pl.multiple_of(dd * 192 + half * 96, 32), 96)]
        return wout.at[pl.ds(pl.multiple_of(dd * 768 + half * 384, 128), 384)]

    sources = (w_in, w_out)

    def expert_send(m, i, half):
        j = across[i]
        parts = ((0, None),) if (m, i) != (1, 2) else ((0, 2), (192, 4))

        @pl.when(j // 2 == c)
        def _():
            for at, n in parts:
                expert_copy(m, i, half, at, n).start()

        for at, n in parts:
            bulk.append(
                (j // 2 == c, functools.partial(expert_copy, m, i, half, at, n))
            )

    def expert_copy(m, i, half, at, n):
        j = across[i]
        src, dst = sources[m].at[lax.rem(j, 2), half], piece(m, d, half)
        if n is None:
            return remote(src, dst, xe.at[m, i, half], re.at[m, i], (j, 2 * z + half))
        return remote(
            src.at[pl.ds(at, 192)],
            last_part(d, half, at),
            xe.at[m, n, half],
            re.at[m, n + 1 if n > 2 else n],
            (j, 2 * z + half),
        )

    def last_part(dd, half, at):
        return wout.at[pl.ds(pl.multiple_of(dd * 768 + half * 384 + at, 64), 192)]

    def last_pass(at, n):
        spot = last_part(across[2], c, at)
        remote(
            spot, spot, xe.at[1, n, 0], re.at[1, n + 1 if n > 2 else n], sib
        ).wait_recv()
        return sems.copy(spot, spot, sib)

    def own_here(m, half):
        return pltpu.make_async_copy(
            sources[m].at[lax.rem(d, 2), half], piece(m, d, half), ls.at[3 + 2 * m + half]
        )

    def own_there(m, half):
        return remote(
            sources[m].at[lax.rem(d, 2), half],
            piece(m, d, half),
            xe.at[m, 3, half],
            re.at[m, 3 + half],
            sib,
        )

    def expert_own(m):
        @pl.when(d // 2 == c)
        def _():
            for half in range(2):
                own_here(m, half).start()
                own_there(m, half).start()

    def expert_own_done(m):
        @pl.when(d // 2 == c)
        def _():
            for half in range(2):
                own_here(m, half).wait()
                own_there(m, half).wait_send()

        @pl.when(d // 2 != c)
        def _():
            for half in range(2):
                own_there(m, half).wait_recv()

    def expert_pass(m, i):
        spot = piece(m, across[i], c)
        remote(spot, spot, xe.at[m, i, 0], re.at[m, i], sib).wait_recv()
        return sems.copy(spot, spot, sib)

    expert_send(0, 0, 0)
    expert_send(0, 1, 0)
    rest1 = run([sems.copy(w_attn, rows_of(wrf, d, z, c), zs[i]) for i in range(3)])
    rows = run([sems.copy(x, xs.at[z], zs[i]) for i in range(3)])

    table = jnp.dot(
        rel_bias_t[...], hot_of(buckets, BUCKETS), precision=HIGH, preferred_element_type=f32
    )
    place_of = lax.broadcasted_iota(jnp.int32, (1, ROLL), 1)
    lines[:12] = table + jnp.where((place_of < 1) | (place_of > 1024), NEG, 0.0)
    for h in range(3):
        row = jnp.broadcast_to(lines[pl.ds(3 * z + h, 1), :], (128, ROLL))
        bias[h] = pltpu.roll(row, 0, 1, stride=1, stride_axis=0)[:, 128:]
    for cp in local:
        cp.wait()
    received(stage1)
    stage2 = [column_rows(wqf, d, dev) for dev in plane]
    stage3 = column_rows(wqf, d, sib)
    received(rest1)
    rest2 = [column_rows(wrf, d, dev) for dev in plane]
    rest3 = column_rows(wrf, d, sib)
    for i, k in ((0, 1), (1, 1), (2, 0), (2, 1)):
        expert_send(0, i, k)
    expert_own(0)
    expert_own(1)
    for i, dd in enumerate(across):
        received(stage2[i])
        stage3 += column_rows(wqf, dd, sib)
    received(stage3)
    misc = jnp.transpose(wqf[:, 576:704].astype(f32))
    gain_first = misc[16:17]
    gain_second = misc[17:18]
    count = jnp.sum(misc[18:19], axis=1, keepdims=True) / 24.0

    pairs = []
    for i in range(4):
        zb = lax.rem(z + 4 - i, 4)
        if i > 0:
            rows[i - 1].wait_recv()
        xf = xs[zb].astype(f32)
        n1 = (xf * rms(xf) * gain_first).astype(bf16)
        n1s[zb] = n1
        qkv = dot_n(n1, wqf[:, :576]).astype(bf16)
        q[zb] = qkv[:, :192]
        kf[zb, c] = qkv[:, 192:384]
        vf[zb, c] = qkv[:, 384:]
        pairs += run(
            [
                sems.copy(kf.at[zb, c], kf.at[zb, c], sib),
                sems.copy(vf.at[zb, c], vf.at[zb, c], sib),
            ]
        )
    for i, dd in enumerate(across):
        received(rest2[i])
        rest3 += column_rows(wrf, dd, sib)
    expert_send(1, 0, 0)
    expert_send(1, 1, 0)
    received(pairs)
    first = sems.n
    sems.n += 4
    for zb in (3, 2, 1, 0):
        width = 256 * (zb + 1)
        start = pl.multiple_of(128 * (7 - 2 * zb) - 128 * c, 128)
        keys = kf[: zb + 1].reshape(width, 192)
        values = vf[: zb + 1].reshape(width, 192)
        def one_head(h, mixed, zb=zb, width=width, start=start, keys=keys, values=values):
            qh = jnp.where(head_mask(h), q[zb], jnp.zeros((), bf16))
            p = soft_rows(qh, keys, bias, h, start, width).astype(bf16)
            return mixed + jnp.where(head_mask(h), dot_n(p, values), 0.0)

        mixed = lax.fori_loop(0, 3, one_head, jnp.zeros((128, 192), f32))
        out_v[zb] = mixed.astype(bf16)

        @pl.when(z != zb)
        def _(zb=zb):
            remote(
                out_v.at[zb], attn.at[z], ss.at[first + zb], rs.at[first + z], (d, 2 * zb + c)
            ).start()

        @pl.when(z == zb)
        def _(zb=zb):
            attn[zb] = out_v[zb]

    received(rest3)
    for zb in range(4):

        @pl.when(z != zb)
        def _(zb=zb):
            remote(
                out_v.at[zb], attn.at[zb], ss.at[first + zb], rs.at[first + zb], (d, 2 * zb + c)
            ).wait()

    hidden = x[...].astype(f32)
    for zb in range(4):
        hidden = hidden + dot_n(attn[zb], wrf[192 * zb : 192 * (zb + 1), :])
    hidden_v[...] = hidden
    n2 = (hidden * rms(hidden) * gain_second).astype(bf16)
    logits = dot_n(n2, wqf[:, 576:704])
    lane = lax.broadcasted_iota(jnp.int32, (128, 128), 1)

    def column(row):
        return jnp.sum(jnp.where(diag, row, jnp.zeros_like(row)), axis=1, keepdims=True)

    route = [column(routes_t[i : i + 1, :]) for i in range(2)]
    picks = [(lane == r).astype(f32) for r in route]
    chosen = [
        jnp.sum(jnp.where(lane == r, logits, 0.0), axis=1, keepdims=True) for r in route
    ]
    top = jnp.maximum(chosen[0], chosen[1])
    powers = [jnp.exp(v - top) for v in chosen]
    gate = [v / (powers[0] + powers[1]) for v in powers]
    lower = (lax.broadcasted_iota(jnp.int32, (128, 128), 0) > lane).astype(bf16)
    before = dot_n(lower, (picks[0] + picks[1]).astype(bf16))
    wide = lax.broadcasted_iota(jnp.int32, (128, 512), 1)
    maps = []
    for i in range(2):
        slot = jnp.sum(picks[i] * before, axis=1, keepdims=True).astype(jnp.int32)
        maps.append((wide == route[i] * 32 + slot).astype(f32).astype(bf16))
    chart = maps[0] + maps[1]
    leave[...] = dot_l(chart, n2).astype(bf16).reshape(16, 32, 768)

    def spread_rows(src, dst, targets, devices):
        copies = run([sems.copy(src.at[t], dst.at[me], dev) for t, dev in zip(targets, devices)])
        dst[pl.ds(me, 1)] = src[pl.ds(me, 1)]
        return copies

    def spread_columns(src, dst, at):
        cols = pl.ds(at, 384)
        copies = run(
            [
                sems.copy(src.at[t, :, cols], dst.at[me, :, cols], dev)
                for t, dev in zip(numbers, others)
            ]
        )
        dst[pl.ds(me, 1), :, cols] = src[pl.ds(me, 1), :, cols]
        return copies

    out = spread_rows(leave, arrived, numbers[8:] + numbers[:8], others[8:] + others[:8])
    for i, k in ((0, 1), (1, 1), (2, 0), (2, 1)):
        expert_send(1, i, k)
    passed = [expert_pass(0, i) for i in range(3)]
    run(passed)
    expert_own_done(0)
    received(passed)
    received(out)
    sent(out)

    def forward_step(i, carry):
        cols = pl.ds(pl.multiple_of((i // 2) * CHUNK, CHUNK), CHUNK)
        these = pl.ds(pl.multiple_of(lax.rem(i, 2) * 256, 256), 256)
        blocks = pl.ds(pl.multiple_of(lax.rem(i, 2) * 8, 8), 8)
        pre = dot_n(arrived[blocks].reshape(256, 768), win[:, cols])
        t = jnp.tanh(GELU_A * (pre + GELU_B * pre * pre * pre))
        half = 0.5 * (1.0 + t)
        hid[these, cols] = (pre * half).astype(bf16)
        slope[these, cols] = half + 0.5 * pre * (1.0 - t * t) * (
            GELU_A * (1.0 + 3.0 * GELU_B * pre * pre)
        )
        return carry

    lax.fori_loop(0, 8, forward_step, 0)
    acc[...] = jnp.zeros_like(acc)

    def quarter(dd):
        k = pl.ds(pl.multiple_of(dd * 768, 768), 768)

        def result_step(i, carry):
            these = pl.ds(pl.multiple_of(i * 256, 256), 256)
            acc[these] += dot_n(hid[these, k], wout[k, :])
            return carry

        lax.fori_loop(0, 2, result_step, 0)

    expert_own_done(1)
    passed_out = []
    quarters = (d,) + across
    for i in range(2):
        passed_out += run([expert_pass(1, i)])
        quarter(quarters[i])
        received(passed_out[-1:])
    passed_out += run([last_pass(0, 2)])
    quarter(quarters[2])
    passed_out += run([last_pass(192, 4)])

    def eighth(core):
        return pl.ds(pl.multiple_of(across[2] * 768 + core * 384, 384), 384)

    k = eighth(c)
    acc[...] += dot_n(hid[:, k], wout[k, :])
    received(passed_out[-2:])
    results = []
    k = eighth(1 - c)
    for at in (0, 384):
        half = acc[:, at : at + 384] + dot_n(hid[:, k], wout[k, at : at + 384])
        leave[:, :, at : at + 384] = half.astype(bf16).reshape(16, 32, 384)
        results.append(spread_columns(leave, back, at))
    sent(stage1 + rows + rest1 + stage3 + pairs + rest3 + sum(stage2 + rest2, []))
    sent(passed + passed_out)
    for held, make in bulk:

        @pl.when(held)
        def _(make=make):
            make().wait_send()

    valid_column = column(valid_row)
    loss = jnp.zeros((1, 1), f32)
    dgate = [jnp.zeros((128, 1), f32), jnp.zeros((128, 1), f32)]
    grads = []
    for part_i, at in enumerate((0, 384)):
        cols = slice(at, at + 384)
        received(results[part_i])
        sent(results[part_i])
        combined = [dot_n(m, back[:, :, cols].reshape(512, 384)) for m in maps]
        result = hidden_v[:, cols] + gate[0] * combined[0] + gate[1] * combined[1]
        error = result - teacher[:, cols].astype(f32)
        masked = valid_column * error
        grad_out = (2.0 * 4096.0) / count * masked
        leave[:, :, cols] = (
            (
                dot_l(maps[0], (gate[0] * grad_out).astype(bf16))
                + dot_l(maps[1], (gate[1] * grad_out).astype(bf16))
            )
            .astype(bf16)
            .reshape(16, 32, 384)
        )
        grads.append(spread_columns(leave, gback, at))
        output[:, cols] = result
        gout_v[:, cols] = grad_out
        loss = loss + jnp.sum(
            jnp.sum(masked * error, axis=1, keepdims=True), axis=0, keepdims=True
        )
        dgate = [
            g + jnp.sum(m * grad_out, axis=1, keepdims=True) for g, m in zip(dgate, combined)
        ]
    mean = gate[0] * dgate[0] + gate[1] * dgate[1]
    grad_logits = jnp.zeros((128, 128), f32)
    for i in range(2):
        grad_logits = grad_logits + jnp.where(
            lane == route[i], gate[i] * (dgate[i] - mean), 0.0
        )
    grad_logits = grad_logits.astype(bf16)
    acc[...] = jnp.zeros_like(acc)

    my_half = me // 8
    entries = []
    for near in (True, False):
        members = slice(8, 15) if near else slice(0, 8)
        group = my_half if near else 1 - my_half
        for copies in grads:
            received(copies[members])
        if not near:
            for copies in grads:
                sent(copies)
        blocks = pl.ds(pl.multiple_of(group * 8, 8), 8)
        these = pl.ds(pl.multiple_of(group * 256, 256), 256)

        def backward_step(i, carry, blocks=blocks, these=these):
            cols = pl.ds(pl.multiple_of(i * CHUNK, CHUNK), CHUNK)
            dh = dot_t(gback[blocks].reshape(256, 768), wout[cols, :])
            dp = (dh * slope[these, cols]).astype(bf16)
            slope[these, cols] = dp.astype(f32)
            acc[these] += dot_t(dp, win[:, cols])
            return carry

        lax.fori_loop(0, 4, backward_step, 0)
        left[blocks] = acc[these].astype(bf16).reshape(8, 32, 768)
        entries += run(
            [
                sems.copy(left.at[t], entry.at[me], dev)
                for t, dev in zip(numbers[members], others[members])
            ]
        )
        if near:
            entry[pl.ds(me, 1)] = left[pl.ds(me, 1)]

    swap_out = sems.n
    sems.n += 8

    def turn(i):
        m = lax.rem(i + 1, 4)
        return lax.rem(d + m, 2) + 2 * lax.rem(d // 2 + m // 2, 2)

    def half_out(i):
        f = turn(i)
        return remote(
            piece(1, f, 1 - c), gout.at[f], ss.at[swap_out + i], rs.at[swap_out + i], sib
        )

    def half_in(f):
        at = swap_out + 4 + f
        return remote(piece(0, f, 1 - c), gin.at[f], ss.at[at], rs.at[at], sib)

    owned = []

    def owner_send(m, i):
        src, dst = ((gin, oin), (gout, oout))[m]
        cp = remote(
            src.at[across[i]],
            dst.at[lax.rem(d, 2), c],
            oe.at[m, i],
            ore.at[m, lax.rem(d, 2), c],
            (across[i], 2 * z + d // 2),
        )
        cp.start()
        owned.append(cp)

    def last_rows(at, count, send):
        rows = pl.ds(at, count)
        cp = remote(
            gin.at[across[2], rows],
            oin.at[lax.rem(d, 2), c, rows],
            oe.at[0, send],
            ore.at[0, lax.rem(d, 2), c],
            (across[2], 2 * z + d // 2),
        )
        cp.start()
        owned.append(cp)

    def owner_here(m):
        src, dst = ((gin, oin), (gout, oout))[m]
        return pltpu.make_async_copy(src.at[d], dst.at[lax.rem(d, 2), c], ls.at[7 + m])

    def owner_there(m):
        src, dst = ((gin, oin), (gout, oout))[m]
        return remote(
            src.at[d], dst.at[lax.rem(d, 2), c], oe.at[m, 3], ore.at[m, lax.rem(d, 2), c], sib
        )

    def owner_local(m):
        @pl.when(d // 2 == c)
        def _():
            owner_here(m).start()

        @pl.when(d // 2 != c)
        def _():
            owner_there(m).start()

    def add_half(m, f):
        ref, rows_n = ((gin, 96), (gout, 384))[m]
        spot = (
            pl.ds(pl.multiple_of(f * 192 + c * 96, 32), 96)
            if m == 0
            else pl.ds(pl.multiple_of(f * 768 + c * 384, 128), 384)
        )
        mine = (win if m == 0 else wout)[spot, :]
        ref[f] = (mine.astype(f32) + ref[f].astype(f32)).astype(bf16)

    def out_done(i):
        half_out(i).wait()
        add_half(1, turn(i))

    def out_owner(i):
        return remote(
            gout.at[turn(i)],
            oout.at[lax.rem(d, 2), c],
            oe.at[1, i],
            ore.at[1, lax.rem(d, 2), c],
            (turn(i), 2 * z + d // 2),
        )

    def out_step(i, carry):
        at = pl.multiple_of(turn(i) * CHUNK, CHUNK)
        wout[pl.ds(at, CHUNK), :] = dot_l(
            hid[:, pl.ds(at, CHUNK)], gback[...].reshape(512, 768)
        ).astype(bf16)
        half_out(i).start()

        @pl.when(i > 0)
        def _():
            out_done(i - 1)
            out_owner(i - 1).start()

        return carry

    lax.fori_loop(0, 4, out_step, 0)
    out_done(3)
    owner_local(1)
    owned += [out_owner(i) for i in range(3)]

    def in_step(f, carry):
        at = pl.multiple_of(f * CHUNK, CHUNK)
        win[:, pl.ds(at, CHUNK)] = dot_l(
            arrived[...].reshape(512, 768), slope[:, pl.ds(at, CHUNK)].astype(bf16)
        ).astype(bf16)
        return carry

    lax.fori_loop(0, 4, in_step, 0)
    for f in range(4):
        half_in(f).start()
    kacc[...] = jnp.zeros_like(kacc)
    vacc[...] = jnp.zeros_like(vacc)
    gacc[...] = jnp.zeros_like(gacc)
    for f in range(4):
        half_in(f).wait()
        add_half(0, f)
    for i in range(2):
        owner_send(0, i)
    last_rows(0, 64, 2)
    owner_local(0)
    received(entries)
    sent(entries)

    dn2 = dot_n(chart, entry[...].reshape(512, 768))
    dn2 = dn2 + dot_t(grad_logits, wqf[:, 576:704])
    hidden = hidden_v[...]
    r2 = rms(hidden)
    scaled = dn2 * gain_second
    mean = jnp.mean(scaled * hidden, axis=1, keepdims=True)
    dh = gout_v[...] + r2 * scaled - hidden * (r2 * r2 * r2) * mean
    dh_low = dh.astype(bf16)
    for zb in range(4):
        do_out[zb] = dot_t(dh_low, wrf[192 * zb : 192 * (zb + 1), :]).astype(bf16)
    heads = run(
        [
            sems.copy(do_out.at[lax.rem(z + k, 4)], do.at[z], zs[i])
            for i, k in enumerate((1, 2, 3))
        ]
    )
    do[pl.ds(z, 1)] = do_out[pl.ds(z, 1)]
    grad_tokens[...] = dh

    for zb in range(4):
        rest[192 * zb : 192 * (zb + 1), :768] = dot_l(attn[zb], dh_low).astype(bf16)
    gain_rows = jnp.broadcast_to(jnp.sum(dn2 * hidden * r2, axis=0, keepdims=True), (128, 768))
    n2 = (hidden * r2 * gain_second).astype(bf16)
    tall = lax.broadcasted_iota(jnp.int32, (768, 128), 1)
    rest[:, 768:] = jnp.where(
        tall == 16, jnp.transpose(gain_rows), dot_l(n2, grad_logits)
    ).astype(bf16)
    rest_swap = run([sems.copy(rest, rest_in, sib)])
    received(rest_swap)
    sent(rest_swap)
    rest_in[...] = (rest[...].astype(f32) + rest_in[...].astype(f32)).astype(bf16)

    def slot(ref, i, j):
        return ref.at[pl.ds(pl.multiple_of((i * 4 + j) * 24, 8), 24)]

    rest_a = []
    for i, k in enumerate((1, 2, 3)):
        zt = lax.rem(z + k, 4)
        for dd in range(4):
            rest_a.append(sems.copy(rows_of(rest_in, dd, zt, c), slot(rest_mid, z, dd), zs[i]))
    run(rest_a)
    for dd in range(4):
        pltpu.make_async_copy(
            rows_of(rest_in, dd, z, c), slot(rest_mid, z, dd), ls.at[11 + dd]
        ).start()
    received(heads)

    scale = HEAD ** (-0.5)
    first_back = sems.n
    sems.n += 4
    swaps = []

    def to_tokens(zb, pair):
        received(pair)
        here = pl.ds(pl.multiple_of((2 * zb + c) * 128, 128), 128)
        dqkv[zb, :, 192:384] = (kacc[here] * scale + dk_in[zb].astype(f32)).astype(bf16)
        dqkv[zb, :, 384:] = (vacc[here] + dv_in[zb].astype(f32)).astype(bf16)
        dn1 = dot_t(dqkv[zb], wqf[:, :576])
        part[zb] = dn1.astype(bf16)

        @pl.when(z != zb)
        def _():
            remote(
                part.at[zb],
                parts.at[z],
                ss.at[first_back + zb],
                rs.at[first_back + z],
                (d, 2 * zb + c),
            ).start()

        @pl.when(z == zb)
        def _():
            parts[zb] = part[zb]

        xf = xs[zb].astype(f32)
        gain_rows_v[zb : zb + 1, :] = jnp.sum(dn1 * xf * rms(xf), axis=0, keepdims=True)

    for zb in (3, 2, 1, 0):
        width = 256 * (zb + 1)
        start = pl.multiple_of(128 * (7 - 2 * zb) - 128 * c, 128)
        keys = kf[: zb + 1].reshape(width, 192)
        values = vf[: zb + 1].reshape(width, 192)
        dq = jnp.zeros((128, 192), f32)
        for h in range(3):
            mask = head_mask(h)
            qh = jnp.where(mask, q[zb], jnp.zeros((), bf16))
            doh = jnp.where(mask, do[zb], jnp.zeros((), bf16))
            p = soft_rows(qh, keys, bias, h, start, width)
            vacc[:width] += dot_l(p.astype(bf16), doh)
            dp = dot_t(doh, values)
            dot = jnp.sum(p * dp, axis=1, keepdims=True)
            ds = (p * (dp - dot)).astype(bf16)
            gacc[h, :, pl.ds(start, width)] += ds.astype(f32)
            dq = dq + jnp.where(mask, dot_n(ds, keys), 0.0)
            kacc[:width] += dot_l(ds, qh)
        dqkv[zb, :, :192] = (dq * scale).astype(bf16)
        there = pl.ds(pl.multiple_of((2 * zb + 1 - c) * 128, 128), 128)
        dk_out[zb] = (kacc[there] * scale).astype(bf16)
        dv_out[zb] = vacc[there].astype(bf16)
        swaps.append(
            run(
                [
                    sems.copy(dk_out.at[zb], dk_in.at[zb], sib),
                    sems.copy(dv_out.at[zb], dv_in.at[zb], sib),
                ]
            )
        )
        if zb < 3:
            to_tokens(zb + 1, swaps[-2])
    to_tokens(0, swaps[-1])
    swaps = sum(swaps, [])

    gain_part = jnp.sum(gain_rows_v[...], axis=0, keepdims=True)
    wpart[:, :576] = dot_l(n1s[...].reshape(512, 768), dqkv[...].reshape(512, 576)).astype(bf16)
    wpart[:, 576:] = jnp.transpose(jnp.broadcast_to(gain_part, (128, 768))).astype(bf16)
    wswap = run([sems.copy(wpart, wpart_in, sib)])
    received(wswap)
    sent(wswap)
    wpart_in[...] = (wpart[...].astype(f32) + wpart_in[...].astype(f32)).astype(bf16)
    w_a = []
    for i, dd in enumerate(across):
        for zt in range(4):
            w_a.append(sems.copy(rows_of(wpart_in, dd, zt, c), slot(wmid, d, zt), plane[i]))
    run(w_a)
    last_rows(64, 32, 4)
    for zt in range(4):
        pltpu.make_async_copy(
            rows_of(wpart_in, d, zt, c), slot(wmid, d, zt), ls.at[15 + zt]
        ).start()
    received(rest_a)
    for dd in range(4):
        pltpu.make_async_copy(
            rows_of(rest_in, dd, z, c), slot(rest_mid, z, dd), ls.at[11 + dd]
        ).wait()
    rest[:96] = sum(rest_mid[96 * i : 96 * (i + 1), :].astype(f32) for i in range(4)).astype(bf16)
    rest_b = run(
        [
            sems.copy(
                rest.at[pl.ds(pl.multiple_of(dd * 24, 8), 24)],
                rest_got.at[pl.ds(pl.multiple_of(d * 24, 8), 24)],
                plane[i],
            )
            for i, dd in enumerate(across)
        ]
    )

    row = lax.broadcasted_iota(jnp.int32, (128, 1), 0)
    sums = []
    for h in range(3):
        y = jnp.concatenate([jnp.zeros((128, ROLL - GW), f32), gacc[h]], axis=1)
        for bit in range(7):
            y = jnp.where((row >> bit) & 1 == 1, pltpu.roll(y, ROLL - (1 << bit), 1), y)
        sums.append(jnp.sum(y, axis=0, keepdims=True))
    hot = hot_of(buckets, 128)
    table = lax.dot_general(
        jnp.concatenate(sums + [jnp.zeros((5, ROLL), f32)], axis=0),
        hot,
        (((1,), (1,)), ((), ())),
        precision=HIGH,
        preferred_element_type=f32,
    )
    index = lax.broadcasted_iota(jnp.int32, (8, 128), 0)
    small[...] = jnp.where(index == 3, loss, table)
    shares = run([sems.copy(small, shared.at[device], dev) for dev in everyone])
    shared[pl.ds(device, 1)] = small[...][None]

    for zb in range(4):

        @pl.when(z != zb)
        def _(zb=zb):
            remote(
                part.at[zb],
                parts.at[zb],
                ss.at[first_back + zb],
                rs.at[first_back + zb],
                (d, 2 * zb + c),
            ).wait()

    dn1 = (
        parts[0].astype(f32) + parts[1].astype(f32) + parts[2].astype(f32) + parts[3].astype(f32)
    )
    xf = x[...].astype(f32)
    r1 = rms(xf)
    scaled = dn1 * gain_first
    mean = jnp.mean(scaled * xf, axis=1, keepdims=True)
    grad_tokens[...] += r1 * scaled - xf * (r1 * r1 * r1) * mean

    received(w_a)
    for zt in range(4):
        pltpu.make_async_copy(
            rows_of(wpart_in, d, zt, c), slot(wmid, d, zt), ls.at[15 + zt]
        ).wait()
    wpart[:96] = sum(wmid[96 * i : 96 * (i + 1), :].astype(f32) for i in range(4)).astype(bf16)
    w_b = run(
        [
            sems.copy(
                wpart.at[pl.ds(pl.multiple_of(lax.rem(z + k, 4) * 24, 8), 24)],
                wgot.at[pl.ds(pl.multiple_of(z * 24, 8), 24)],
                zs[i],
            )
            for i, k in enumerate((1, 2, 3))
        ]
    )
    own_rows = [
        pltpu.make_async_copy(
            rest.at[pl.ds(pl.multiple_of(d * 24, 8), 24)],
            rest_got.at[pl.ds(pl.multiple_of(d * 24, 8), 24)],
            ls.at[9],
        ),
        pltpu.make_async_copy(
            wpart.at[pl.ds(pl.multiple_of(z * 24, 8), 24)],
            wgot.at[pl.ds(pl.multiple_of(z * 24, 8), 24)],
            ls.at[10],
        ),
    ]
    run(own_rows)

    received(shares)
    by_z = []
    for zb in range(4):
        total = jnp.zeros((8, 128), f32)
        for dd in range(4):
            for cc in range(2):
                total = total + shared[(dd * 4 + zb) * 2 + cc]
        by_z.append(total)
    loss_all = by_z[0] + by_z[1] + by_z[2] + by_z[3]
    extra[0:8] = loss_all[3:4] / (count * 768.0) + jnp.zeros((8, 128), f32)
    for zb in range(4):
        extra[8 + 8 * zb : 16 + 8 * zb] = by_z[zb]

    received(rest_b)
    received(w_b)
    for cp in own_rows:
        cp.wait()
    total = jnp.zeros((24, 896), f32)
    gain_total = jnp.zeros((24, 128), f32)
    for zb in range(4):
        total = total + rest_got[24 * zb : 24 * (zb + 1), :].astype(f32)
        block = wgot[24 * zb : 24 * (zb + 1), :].astype(f32)
        gain_total = gain_total + block[:, 576:]
        for i in range(3):
            at = i * 768 + zb * 192
            grad_qkv[:, at : at + 192] = block[:, i * 192 : (i + 1) * 192]
    grad_rest[:, :896] = total
    grad_rest[:, 896:] = gain_total

    for m, (src, dst) in enumerate(((gin, oin), (gout, oout))):
        for l in range(2):
            for half in range(2):
                here = (2 * c + l == d) & (c == half)

                @pl.when(jnp.logical_not(here))
                def _(src=src, dst=dst, m=m, l=l, half=half):
                    remote(
                        src.at[0], dst.at[l, half], oe.at[m, 3], ore.at[m, l, half], sib
                    ).wait_recv()

        @pl.when(d // 2 == c)
        def _(m=m):
            owner_here(m).wait()

        @pl.when(d // 2 != c)
        def _(m=m):
            owner_there(m).wait_send()

    sent(heads + rest_a + rest_b + swaps + shares + w_a + w_b + owned)


def finish_kernel(
    oin,
    oout,
    output,
    tokens,
    qkv,
    rest,
    extra,
    gin,
    gout,
    o,
    t,
    g,
    w,
    r,
    ga,
    gm,
    table,
    loss,
    low_in,
    low_out,
    wide_in,
    wide_out,
    o_v,
    t_v,
    g_v,
    sems,
):
    f32 = jnp.float32
    loads, stores = [], []
    for i in range(4):
        loads.append(pltpu.make_async_copy(oin.at[i], low_in.at[i], sems.at[0, i]))
        loads.append(pltpu.make_async_copy(oout.at[i], low_out.at[i], sems.at[1, i]))
        stores.append(pltpu.make_async_copy(wide_in.at[i], gin.at[i], sems.at[2, i]))
        stores.append(pltpu.make_async_copy(wide_out.at[i], gout.at[i], sems.at[3, i]))
    run(loads)
    trios = ((output, o_v, o), (tokens, t_v, t), (qkv, g_v, g))
    moved = run(
        [pltpu.make_async_copy(a, b, sems.at[4, i]) for i, (a, b, _) in enumerate(trios)]
    )
    for i in range(4):
        loads[2 * i].wait()
        wide_in[i] = low_in[i].astype(f32)
        stores[2 * i].start()
        loads[2 * i + 1].wait()
        wide_out[i] = low_out[i].astype(f32)
        stores[2 * i + 1].start()
    for cp in moved:
        cp.wait()
    moved = run(
        [pltpu.make_async_copy(b, e, sems.at[4, i]) for i, (_, b, e) in enumerate(trios)]
    )
    w[...] = rest[:, :768]
    turned = jnp.transpose(
        jnp.concatenate([rest[:, 768:1024], jnp.zeros((104, 256), f32)], axis=0)
    )
    r[...] = turned[:16, :24]
    gm[...] = turned[16:17, :24]
    ga[...] = turned[128:129, :24]
    for zb in range(4):
        table[3 * zb : 3 * zb + 3, :] = extra[8 + 8 * zb : 11 + 8 * zb, :BUCKETS]
    loss[...] = extra[0:1, 0:1]
    for cp in stores + moved:
        cp.wait()


def fast_path(
    tokens,
    w_qkv,
    w_attn_out,
    gain_attn,
    gain_moe,
    w_router,
    rel_bias,
    w_in,
    w_out,
    teacher,
    routes,
    valid,
    buckets,
):
    f32, bf16 = jnp.float32, jnp.bfloat16
    block = pltpu.VMEM((16, 32, 768), bf16)
    heads = pltpu.VMEM((4, 128, 192), bf16)
    both = pltpu.VMEM((4, 2, 128, 192), bf16)
    wide = pltpu.VMEM((4, 128, 768), bf16)
    output, grad_tokens, grad_qkv, grad_rest, extra, oin, oout = comm_call(
        step_kernel,
        [
            sds((128, 768), f32),
            sds((128, 768), f32),
            sds((24, 2304), f32),
            sds((24, 1024), f32),
            sds((40, 128), f32),
            sds((2, 2, 96, 3072)),
            sds((2, 2, 384, 768)),
        ],
        13,
        1,
        [
            pltpu.VMEM((4, 24, 704), bf16),
            pltpu.VMEM((768, 704), bf16),
            pltpu.VMEM((768, 768), bf16),
            wide,
            wide,
            heads,
            both,
            both,
            pltpu.VMEM((3, 128, GW), f32),
            pltpu.VMEM((32, ROLL), f32),
            heads,
            heads,
            block,
            block,
            block,
            pltpu.VMEM((768, 3072), bf16),
            pltpu.VMEM((3072, 768), bf16),
            pltpu.VMEM((512, 3072), f32),
            pltpu.VMEM((512, 3072), bf16),
            pltpu.VMEM((512, 768), f32),
            block,
            block,
            block,
            pltpu.VMEM((4, 96, 3072), bf16),
            pltpu.VMEM((4, 384, 768), bf16),
            pltpu.VMEM((128, 768), f32),
            pltpu.VMEM((128, 768), f32),
            heads,
            heads,
            pltpu.VMEM((768, 896), bf16),
            pltpu.VMEM((768, 896), bf16),
            pltpu.VMEM((96, 896), bf16),
            pltpu.VMEM((1024, 192), f32),
            pltpu.VMEM((1024, 192), f32),
            pltpu.VMEM((3, 128, GW), f32),
            heads,
            heads,
            heads,
            heads,
            pltpu.VMEM((4, 128, 576), bf16),
            wide,
            wide,
            pltpu.VMEM((768, 704), bf16),
            pltpu.VMEM((768, 704), bf16),
            pltpu.VMEM((96, 704), bf16),
            pltpu.VMEM((8, 128), f32),
            pltpu.VMEM((32, 8, 128), f32),
            pltpu.VMEM((4, 768), f32),
            pltpu.VMEM((384, 896), bf16),
            pltpu.VMEM((384, 704), bf16),
            pltpu.SemaphoreType.DMA((300,)),
            pltpu.SemaphoreType.DMA((300,)),
            pltpu.SemaphoreType.DMA((2, 5, 2)),
            pltpu.SemaphoreType.DMA((2, 6)),
            pltpu.SemaphoreType.DMA((2, 5)),
            pltpu.SemaphoreType.DMA((2, 2, 2)),
            pltpu.SemaphoreType.DMA((19,)),
        ],
        "layer_step",
        in_specs=[VM] * 11 + [ANY] * 2,
        out_specs=[VM] * 5 + [ANY] * 2,
        vmem=63 << 20,
    )(
        tokens,
        w_qkv,
        w_attn_out,
        w_router.T,
        gain_attn[None],
        gain_moe[None],
        rel_bias.T,
        buckets[None],
        routes.T,
        valid[None],
        teacher,
        w_in.reshape(2, 2, 96, 3072),
        w_out.reshape(2, 2, 384, 768),
    )

    small_out = [
        (128, 768),
        (128, 768),
        (24, 2304),
        (24, 768),
        (16, 24),
        (1, 24),
        (1, 24),
        (12, BUCKETS),
        (1, 1),
    ]
    gin, gout, output, grad_tokens, grad_qkv, grad_w, grad_r, grad_ga, grad_gm, table, loss = (
        pl.pallas_call(
            finish_kernel,
            out_shape=[sds((4, 96, 3072), f32), sds((4, 384, 768), f32)]
            + [sds(shape, f32) for shape in small_out],
            in_specs=[ANY] * 5 + [VM] * 2,
            out_specs=[ANY] * 5 + [VM] * 6,
            scratch_shapes=[
                pltpu.VMEM((4, 96, 3072), bf16),
                pltpu.VMEM((4, 384, 768), bf16),
                pltpu.VMEM((4, 96, 3072), f32),
                pltpu.VMEM((4, 384, 768), f32),
                pltpu.VMEM((128, 768), f32),
                pltpu.VMEM((128, 768), f32),
                pltpu.VMEM((24, 2304), f32),
                pltpu.SemaphoreType.DMA((5, 4)),
            ],
            compiler_params=pltpu.CompilerParams(vmem_limit_bytes=63 << 20),
            name="finish",
        )(
            oin.reshape(4, 96, 3072),
            oout.reshape(4, 384, 768),
            output,
            grad_tokens,
            grad_qkv,
            grad_rest,
            extra,
        )
    )
    return (
        output,
        loss.reshape(()),
        grad_tokens,
        grad_qkv,
        grad_w,
        grad_ga.reshape(24),
        grad_gm.reshape(24),
        grad_r.T,
        table.T,
        gin.reshape(2, 192, 3072),
        gout.reshape(2, 768, 768),
    )


def choose(*arrays):
    tokens, w_in, rel_bias, buckets = arrays[0], arrays[7], arrays[6], arrays[12]
    fits = (
        lax.axis_size("dp") == 4
        and lax.axis_size("seq") == 8
        and tokens.shape == (128, 768)
        and w_in.shape == (2, 192, 3072)
        and rel_bias.shape == (32, 12)
        and buckets.shape == (1024,)
    )
    return fast_path(*arrays) if fits else on_device(*arrays)


def solution(mesh):
    in_specs = (
        P(("dp", "seq"), None),
        P(("dp", "seq"), None),
        P(("dp", "seq"), None),
        P(("dp", "seq")),
        P(("dp", "seq")),
        P(("dp", "seq"), None),
        P(),
        P("seq", "dp", None),
        P("seq", "dp", None),
        P(("dp", "seq"), None),
        P(("dp", "seq"), None),
        P(("dp", "seq")),
        P(),
    )
    out_specs = (
        P(("dp", "seq"), None),
        P(),
        P(("dp", "seq"), None),
        P(("dp", "seq"), None),
        P(("dp", "seq"), None),
        P(("dp", "seq")),
        P(("dp", "seq")),
        P(("dp", "seq"), None),
        P(),
        P("seq", "dp", None),
        P("seq", "dp", None),
    )
    return jax.shard_map(
        choose, mesh=mesh, in_specs=in_specs, out_specs=out_specs, check_vma=False
    )
```

```python
import functools

import jax
import jax.numpy as jnp
from jax import lax
from jax.experimental import pallas as pl
from jax.experimental.pallas import tpu as pltpu
from jax.sharding import PartitionSpec as P

H = 12
HEAD = 64
BUCKETS = 32


EPS = 1e-06
NEG = -1e30
SECTION = 512
HIGH = lax.Precision.HIGHEST
FLOAT_TYPE = jnp.float32
HALF_TYPE = jnp.bfloat16


def normalize(values, gain):
    factor = lax.rsqrt(jnp.mean(values * values, axis=-1, keepdims=True) + EPS)
    return (values * factor * gain, factor)


def norm_back(values, factor, gain, grad_norm):
    scaled = grad_norm * gain
    mean_term = jnp.mean(scaled * values, axis=-1, keepdims=True)
    grad_values = factor * scaled - values * (factor * factor * factor) * mean_term
    return (grad_values, jnp.sum(grad_norm * values * factor, axis=0))


def gelu_grad(preact, grad_hidden):
    _, gelu_back = jax.vjp(jax.nn.gelu, preact)
    return gelu_back(grad_hidden)[0]


def in_sections(advance, running, shards):
    row_count = shards[0].shape[0]
    sections = row_count // SECTION
    stacked = tuple((member.reshape((sections, SECTION) + member.shape[1:]) for member in shards))

    def one_section(inner_state, entry_pair):
        return (advance(inner_state, entry_pair[1], entry_pair[0] * SECTION), None)

    final_state, _ = lax.scan(
        one_section, running, (jnp.arange(sections, dtype=jnp.int32), stacked)
    )
    return final_state


def score_block(queries, key_rows, query_start, key_start, rel_bias, edges):
    query_count = queries.shape[0]
    key_count = key_rows.shape[0]
    distance = (query_start + jnp.arange(query_count, dtype=jnp.int32))[:, None] - (
        key_start + jnp.arange(key_count, dtype=jnp.int32)
    )[None, :]
    allowed = distance >= 0
    bucket_hot = (
        (distance[:, :, None] >= edges[None, None, :-1])
        & (distance[:, :, None] < edges[None, None, 1:])
    ).astype(FLOAT_TYPE)
    bias_term = jnp.einsum("qkb,bh->hqk", bucket_hot, rel_bias, precision=HIGH)
    raw_scores = (
        jnp.einsum("qhd,khd->hqk", queries, key_rows, preferred_element_type=FLOAT_TYPE)
        * queries.shape[2] ** (-0.5)
        + bias_term
    )
    return (raw_scores, allowed, bucket_hot)


def split_three(values):
    upper = lax.optimization_barrier(values.astype(HALF_TYPE))
    remainder = values - upper.astype(FLOAT_TYPE)
    middle = lax.optimization_barrier(remainder.astype(HALF_TYPE))
    bottom = (remainder - middle.astype(FLOAT_TYPE)).astype(HALF_TYPE)
    return jnp.stack([upper, middle, bottom], axis=1)


def join_three(packed):
    as_float = packed.astype(FLOAT_TYPE)
    return as_float[:, 0] + as_float[:, 1] + as_float[:, 2]


def on_device(
    tokens,
    w_qkv,
    w_attn_out,
    gain_attn,
    gain_moe,
    w_router,
    rel_bias,
    w_in,
    w_out,
    teacher,
    routes,
    valid,
    buckets,
):
    tok_rows = tokens.shape[0]
    width = tokens.shape[1]
    seq_count = lax.axis_size("seq")
    my_start = lax.axis_index("seq") * tok_rows
    local_experts = w_in.shape[0]
    experts_all = local_experts * seq_count
    capacity = 4 * tok_rows // experts_all
    slot_rows = seq_count * capacity
    scale = HEAD ** (-0.5)
    qkv_full, attn_full, router_full, gain_one, gain_two, valid_all = (
        lax.all_gather(w_qkv, ("dp", "seq"), axis=0, tiled=True),
        lax.all_gather(w_attn_out, ("dp", "seq"), axis=0, tiled=True),
        lax.all_gather(w_router, ("dp", "seq"), axis=0, tiled=True),
        lax.all_gather(gain_attn, ("dp", "seq"), axis=0, tiled=True),
        lax.all_gather(gain_moe, ("dp", "seq"), axis=0, tiled=True),
        lax.all_gather(valid.astype(HALF_TYPE), ("dp", "seq"), axis=0, tiled=True),
    )
    valid_float = valid.astype(FLOAT_TYPE)
    count_all = jnp.sum(valid_all.astype(FLOAT_TYPE))
    tokens_all = tok_rows * lax.axis_size("dp") * seq_count
    edges = jnp.sum(
        (buckets[None, :] < jnp.arange(BUCKETS + 1, dtype=jnp.int32)[:, None]).astype(jnp.int32),
        axis=1,
    )
    inputs = tokens.astype(FLOAT_TYPE)
    gain_first = gain_one.astype(FLOAT_TYPE)
    gain_second = gain_two.astype(FLOAT_TYPE)
    normed_one, factor_one = normalize(inputs, gain_first)
    normed_in = normed_one.astype(HALF_TYPE)
    qkv_rows = jnp.dot(normed_in, qkv_full, preferred_element_type=FLOAT_TYPE)
    query_low = qkv_rows[:, :width].astype(HALF_TYPE)
    key_low = qkv_rows[:, width : 2 * width].astype(HALF_TYPE)
    value_low = qkv_rows[:, 2 * width :].astype(HALF_TYPE)
    heads_q = query_low.reshape(tok_rows, H, HEAD)
    heads_k = key_low.reshape(tok_rows, H, HEAD)
    heads_v = value_low.reshape(tok_rows, H, HEAD)
    last_row = my_start + tok_rows - 1

    def forward_step(running, shards, offset):
        key_rows = shards[0].reshape(shards[0].shape[0], H, HEAD)
        value_rows = shards[1].reshape(shards[1].shape[0], H, HEAD)

        def work(inner_state):
            maximum, denom, mixture = inner_state
            raw_scores, allowed, _ = score_block(
                heads_q, key_rows, my_start, offset, rel_bias, edges
            )
            masked = jnp.where(allowed[None], raw_scores, NEG)
            new_max = jnp.maximum(maximum, jnp.max(masked, axis=2))
            weights = jnp.where(allowed[None], jnp.exp(masked - new_max[:, :, None]), 0.0)
            rescale = jnp.exp(maximum - new_max)
            addend = jnp.einsum(
                "hqk,khd->hqd",
                weights.astype(HALF_TYPE),
                value_rows,
                preferred_element_type=FLOAT_TYPE,
            )
            return (
                new_max,
                denom * rescale + jnp.sum(weights, axis=2),
                mixture * rescale[:, :, None] + addend,
            )

        return lax.cond(offset <= last_row, work, lambda inner_state: inner_state, running)

    start_state = (
        jnp.full((H, tok_rows), NEG, FLOAT_TYPE),
        jnp.zeros((H, tok_rows), FLOAT_TYPE),
        jnp.zeros((H, tok_rows, HEAD), FLOAT_TYPE),
    )
    maximum, denom, mixture = in_sections(
        forward_step,
        start_state,
        (
            lax.all_gather(key_low, "seq", axis=0, tiled=True),
            lax.all_gather(value_low, "seq", axis=0, tiled=True),
        ),
    )
    log_total = maximum + jnp.log(denom)
    attn_heads = mixture / denom[:, :, None]
    attn_rows = jnp.transpose(attn_heads, (1, 0, 2)).reshape(tok_rows, width)
    attn_low = attn_rows.astype(HALF_TYPE)
    hidden_state = inputs + jnp.dot(attn_low, attn_full, preferred_element_type=FLOAT_TYPE)
    normed_two, factor_two = normalize(hidden_state, gain_second)
    moe_in = normed_two.astype(HALF_TYPE)
    logits = jnp.dot(moe_in, router_full, preferred_element_type=FLOAT_TYPE)
    chosen = jnp.take_along_axis(logits, routes, axis=1)
    gate_weights = jax.nn.softmax(chosen, axis=1)
    flat_routes = routes.reshape(-1)
    matches = (flat_routes[:, None] == jnp.arange(experts_all, dtype=jnp.int32)[None, :]).astype(
        jnp.int32
    )
    slot_index = jnp.sum((jnp.cumsum(matches, axis=0) - matches) * matches, axis=1)
    target_dev = flat_routes // local_experts
    target_local = flat_routes % local_experts
    position = (target_dev * capacity + slot_index) * local_experts + target_local
    dispatch_map = (
        jnp.arange(experts_all * capacity, dtype=jnp.int32)[:, None] == position[None, :]
    ).astype(HALF_TYPE)
    dispatch_map = dispatch_map.reshape(experts_all * capacity, tok_rows, 2)
    outgoing = jnp.einsum(
        "prk,rd->pd", dispatch_map, moe_in, preferred_element_type=FLOAT_TYPE
    ).astype(HALF_TYPE)
    arrived = lax.all_to_all(
        outgoing.reshape(seq_count, capacity * local_experts, width),
        "seq",
        split_axis=0,
        concat_axis=0,
        tiled=True,
    )
    arrived_rows = arrived.reshape(slot_rows, local_experts, width)
    in_full, out_full = (
        lax.all_gather(w_in, "dp", axis=1, tiled=True),
        lax.all_gather(w_out, "dp", axis=1, tiled=True),
    )
    preact = jnp.einsum("mld,ldf->mlf", arrived_rows, in_full, preferred_element_type=FLOAT_TYPE)
    hidden = jax.nn.gelu(preact).astype(HALF_TYPE)
    result = jnp.einsum("mlf,lfd->mld", hidden, out_full, preferred_element_type=FLOAT_TYPE).astype(
        HALF_TYPE
    )
    returned = lax.all_to_all(
        result.reshape(seq_count, capacity * local_experts, width),
        "seq",
        split_axis=0,
        concat_axis=0,
        tiled=True,
    )
    returned = returned.reshape(experts_all * capacity, width)
    combined = jnp.einsum("prk,pd->krd", dispatch_map, returned, preferred_element_type=FLOAT_TYPE)
    output = hidden_state + gate_weights[:, 0:1] * combined[0] + gate_weights[:, 1:2] * combined[1]
    error_rows = output - teacher.astype(FLOAT_TYPE)
    loss_local = jnp.sum(valid_float[:, None] * error_rows * error_rows)
    grad_out = 2.0 * tokens_all / count_all * valid_float[:, None] * error_rows
    grad_gate = jnp.einsum("krd,rd->rk", combined, grad_out)
    grad_chosen = gate_weights * (
        grad_gate - jnp.sum(gate_weights * grad_gate, axis=1, keepdims=True)
    )
    pick = (routes[:, :, None] == jnp.arange(experts_all, dtype=jnp.int32)[None, None, :]).astype(
        FLOAT_TYPE
    )
    grad_logits = jnp.sum(pick * grad_chosen[:, :, None], axis=1).astype(HALF_TYPE)
    grad_router = jnp.einsum("rd,re->de", moe_in, grad_logits, preferred_element_type=FLOAT_TYPE)
    grad_result = (jnp.transpose(gate_weights)[:, :, None] * grad_out[None]).astype(HALF_TYPE)
    grad_slots = jnp.einsum(
        "prk,krd->pd", dispatch_map, grad_result, preferred_element_type=FLOAT_TYPE
    ).astype(HALF_TYPE)
    grad_arrived = lax.all_to_all(
        grad_slots.reshape(seq_count, capacity * local_experts, width),
        "seq",
        split_axis=0,
        concat_axis=0,
        tiled=True,
    )
    grad_rows = grad_arrived.reshape(slot_rows, local_experts, width)
    grad_hidden = jnp.einsum("mld,lfd->mlf", grad_rows, out_full, preferred_element_type=FLOAT_TYPE)
    grad_preact = gelu_grad(preact, grad_hidden).astype(HALF_TYPE)
    grad_out_local = jnp.einsum(
        "mlf,mld->lfd", hidden, grad_rows, preferred_element_type=FLOAT_TYPE
    )
    grad_in_local = jnp.einsum(
        "mld,mlf->ldf", arrived_rows, grad_preact, preferred_element_type=FLOAT_TYPE
    )
    grad_entry = jnp.einsum(
        "mlf,ldf->mld", grad_preact, in_full, preferred_element_type=FLOAT_TYPE
    ).astype(HALF_TYPE)
    grad_w_in, grad_w_out = (
        lax.psum_scatter(
            grad_in_local.astype(jnp.bfloat16), "dp", scatter_dimension=1, tiled=True
        ).astype(jnp.float32),
        lax.psum_scatter(
            grad_out_local.astype(jnp.bfloat16), "dp", scatter_dimension=1, tiled=True
        ).astype(jnp.float32),
    )
    grad_back = lax.all_to_all(
        grad_entry.reshape(seq_count, capacity * local_experts, width),
        "seq",
        split_axis=0,
        concat_axis=0,
        tiled=True,
    )
    grad_back = grad_back.reshape(experts_all * capacity, width)
    grad_moe_in = jnp.einsum(
        "prk,pd->rd", dispatch_map, grad_back, preferred_element_type=FLOAT_TYPE
    )
    grad_moe_in = grad_moe_in + jnp.einsum(
        "re,de->rd", grad_logits, router_full, preferred_element_type=FLOAT_TYPE
    )
    grad_hidden_norm, grad_gain_second = norm_back(
        hidden_state, factor_two, gain_second, grad_moe_in
    )
    grad_state = grad_out + grad_hidden_norm
    grad_state_low = grad_state.astype(HALF_TYPE)
    grad_attn_w = jnp.einsum(
        "rd,re->de", attn_low, grad_state_low, preferred_element_type=FLOAT_TYPE
    )
    grad_attn_low = jnp.einsum(
        "re,de->rd", grad_state_low, attn_full, preferred_element_type=FLOAT_TYPE
    ).astype(HALF_TYPE)
    heads_dout = grad_attn_low.reshape(tok_rows, H, HEAD)
    softmax_dot = jnp.sum(
        jnp.transpose(heads_dout, (1, 0, 2)).astype(FLOAT_TYPE) * attn_heads, axis=2
    )
    row_stats = split_three(
        jnp.stack([jnp.transpose(log_total), jnp.transpose(softmax_dot)], axis=1)
    )

    def backward_step(running, shards, offset):
        key_rows = shards[0].reshape(shards[0].shape[0], H, HEAD)
        value_rows = shards[1].reshape(shards[1].shape[0], H, HEAD)
        query_rows = shards[2].reshape(shards[2].shape[0], H, HEAD)
        dout_rows = shards[3].reshape(shards[3].shape[0], H, HEAD)
        stats_rows = join_three(shards[4])
        piece_total = jnp.transpose(stats_rows[:, 0, :])
        piece_dot = jnp.transpose(stats_rows[:, 1, :])
        grad_query, grad_table, grad_key, grad_value = running

        def query_work(inner_state):
            inner_query, inner_table = inner_state
            raw_scores, allowed, bucket_hot = score_block(
                heads_q, key_rows, my_start, offset, rel_bias, edges
            )
            weights = jnp.where(allowed[None], jnp.exp(raw_scores - log_total[:, :, None]), 0.0)
            grad_prob = jnp.einsum(
                "qhd,khd->hqk", heads_dout, value_rows, preferred_element_type=FLOAT_TYPE
            )
            grad_score = (weights * (grad_prob - softmax_dot[:, :, None])).astype(HALF_TYPE)
            inner_query = (
                inner_query
                + jnp.einsum(
                    "hqk,khd->hqd", grad_score, key_rows, preferred_element_type=FLOAT_TYPE
                )
                * scale
            )
            inner_table = inner_table + jnp.einsum(
                "hqk,qkb->bh", grad_score.astype(FLOAT_TYPE), bucket_hot, precision=HIGH
            )
            return (inner_query, inner_table)

        def key_work(inner_state):
            inner_key, inner_value = inner_state
            raw_scores, allowed, _ = score_block(
                query_rows, heads_k, offset, my_start, rel_bias, edges
            )
            weights = jnp.where(allowed[None], jnp.exp(raw_scores - piece_total[:, :, None]), 0.0)
            inner_value = inner_value + jnp.einsum(
                "hqk,qhd->khd",
                weights.astype(HALF_TYPE),
                dout_rows,
                preferred_element_type=FLOAT_TYPE,
            )
            grad_prob = jnp.einsum(
                "qhd,khd->hqk", dout_rows, heads_v, preferred_element_type=FLOAT_TYPE
            )
            grad_score = (weights * (grad_prob - piece_dot[:, :, None])).astype(HALF_TYPE)
            inner_key = (
                inner_key
                + jnp.einsum(
                    "hqk,qhd->khd", grad_score, query_rows, preferred_element_type=FLOAT_TYPE
                )
                * scale
            )
            return (inner_key, inner_value)

        grad_query, grad_table = lax.cond(
            offset <= last_row,
            query_work,
            lambda inner_state: inner_state,
            (grad_query, grad_table),
        )
        grad_key, grad_value = lax.cond(
            offset + shards[0].shape[0] - 1 >= my_start,
            key_work,
            lambda inner_state: inner_state,
            (grad_key, grad_value),
        )
        return (grad_query, grad_table, grad_key, grad_value)

    back_start = (
        jnp.zeros((H, tok_rows, HEAD), FLOAT_TYPE),
        jnp.zeros((BUCKETS, H), FLOAT_TYPE),
        jnp.zeros((tok_rows, H, HEAD), FLOAT_TYPE),
        jnp.zeros((tok_rows, H, HEAD), FLOAT_TYPE),
    )
    grad_query, grad_table_local, grad_key, grad_value = in_sections(
        backward_step,
        back_start,
        (
            lax.all_gather(key_low, "seq", axis=0, tiled=True),
            lax.all_gather(value_low, "seq", axis=0, tiled=True),
            lax.all_gather(query_low, "seq", axis=0, tiled=True),
            lax.all_gather(grad_attn_low, "seq", axis=0, tiled=True),
            lax.all_gather(row_stats, "seq", axis=0, tiled=True),
        ),
    )
    grad_qkv_low = jnp.concatenate(
        [
            jnp.transpose(grad_query, (1, 0, 2)).reshape(tok_rows, width),
            grad_key.reshape(tok_rows, width),
            grad_value.reshape(tok_rows, width),
        ],
        axis=1,
    ).astype(HALF_TYPE)
    grad_qkv_w = jnp.einsum("rd,re->de", normed_in, grad_qkv_low, preferred_element_type=FLOAT_TYPE)
    grad_normed_one = jnp.einsum(
        "re,de->rd", grad_qkv_low, qkv_full, preferred_element_type=FLOAT_TYPE
    )
    grad_in_norm, grad_gain_first = norm_back(inputs, factor_one, gain_first, grad_normed_one)
    grad_tokens = grad_state + grad_in_norm
    grad_qkv_own, grad_attn_own, grad_router_own, grad_gain_attn, grad_gain_moe = (
        lax.psum_scatter(grad_qkv_w, ("dp", "seq"), scatter_dimension=0, tiled=True),
        lax.psum_scatter(grad_attn_w, ("dp", "seq"), scatter_dimension=0, tiled=True),
        lax.psum_scatter(grad_router, ("dp", "seq"), scatter_dimension=0, tiled=True),
        lax.psum_scatter(grad_gain_first, ("dp", "seq"), scatter_dimension=0, tiled=True),
        lax.psum_scatter(grad_gain_second, ("dp", "seq"), scatter_dimension=0, tiled=True),
    )
    loss_sum, grad_table = lax.psum((loss_local, grad_table_local), ("dp", "seq"))
    loss = loss_sum / (count_all * width)
    return (
        output,
        loss,
        grad_tokens,
        grad_qkv_own,
        grad_attn_own,
        grad_gain_attn,
        grad_gain_moe,
        grad_router_own,
        grad_table,
        grad_w_in,
        grad_w_out,
    )


MESH = pl.DeviceIdType.MESH
ANY = pl.BlockSpec(memory_space=pl.ANY)
VM = pl.BlockSpec(memory_space=pltpu.VMEM)
ROLL = 1280
GW = 1152


def remote(src, dst, send, recv, dev):
    return pltpu.make_async_remote_copy(
        src_ref=src, dst_ref=dst, send_sem=send, recv_sem=recv, device_id=dev, device_id_type=MESH
    )


def place():
    d = lax.axis_index("dp")
    s = lax.axis_index("seq")
    return d, s, s // 2, lax.rem(s, 2)


def comm_call(body, outs, n_in, cid, scratch, name, in_specs=None, out_specs=None, vmem=None):
    return pl.pallas_call(
        body,
        out_shape=outs,
        in_specs=in_specs or [ANY] * n_in,
        out_specs=out_specs or [ANY] * len(outs),
        scratch_shapes=scratch,
        compiler_params=pltpu.CompilerParams(
            collective_id=cid, has_side_effects=True, vmem_limit_bytes=vmem
        ),
        name=name,
    )


def sds(shape, dtype=jnp.bfloat16):
    return jax.ShapeDtypeStruct(shape, dtype)


def head_mask(h):
    lane = lax.broadcasted_iota(jnp.int32, (1, 192), 1)
    return lane // HEAD == h


def dot_t(a, b):
    return lax.dot_general(a, b, (((1,), (1,)), ((), ())), preferred_element_type=jnp.float32)


def dot_l(a, b):
    return lax.dot_general(a, b, (((0,), (0,)), ((), ())), preferred_element_type=jnp.float32)


def dot_n(a, b):
    return jnp.dot(a, b, preferred_element_type=jnp.float32)


def soft_rows(q, keys, g_ref, h, start, width):
    s = dot_t(q, keys) * HEAD ** (-0.5) + g_ref[h, :, pl.ds(start, width)]
    m = jnp.max(s, axis=1, keepdims=True)
    p = jnp.exp(s - m)
    return p / jnp.sum(p, axis=1, keepdims=True)


CHUNK = 768
GELU_A = 0.7978845608028654
GELU_B = 0.044715


class Sems:
    def __init__(self, send, recv):
        self.send, self.recv, self.n = send, recv, 0

    def copy(self, src, dst, dev):
        cp = remote(src, dst, self.send.at[self.n], self.recv.at[self.n], dev)
        self.n += 1
        return cp


def run(copies):
    for cp in copies:
        cp.start()
    return copies


def received(copies):
    for cp in copies:
        cp.wait_recv()


def sent(copies):
    for cp in copies:
        cp.wait_send()


def chips():
    d, s, z, c = place()
    me = z * 4 + d
    half, i = me // 8, lax.rem(me, 8)
    numbers = [(1 - half) * 8 + lax.rem(i + k, 8) for k in range(8)]
    numbers += [half * 8 + lax.rem(i + k, 8) for k in range(1, 8)]
    return me, numbers, [(lax.rem(t, 4), 2 * (t // 4) + c) for t in numbers]


def rms(v):
    return lax.rsqrt(jnp.mean(v * v, axis=1, keepdims=True) + EPS)


def hot_of(buckets, count):
    b = lax.broadcasted_iota(jnp.int32, (count, 1), 0)
    low = jnp.sum((buckets[...] < b).astype(jnp.float32), axis=1, keepdims=True)
    high = jnp.sum((buckets[...] <= b).astype(jnp.float32), axis=1, keepdims=True)
    at = (1024 - lax.broadcasted_iota(jnp.int32, (1, ROLL), 1)).astype(jnp.float32)
    return ((at >= low) & (at < high) & (at < 1024.0)).astype(jnp.float32)


def step_kernel(
    x,
    w_qkv,
    w_attn,
    w_router_t,
    gain_a,
    gain_m,
    rel_bias_t,
    buckets,
    routes_t,
    valid_t,
    teacher,
    w_in,
    w_out,
    output,
    grad_tokens,
    grad_qkv,
    grad_rest,
    extra,
    oin,
    oout,
    wq,
    wqf,
    wrf,
    xs,
    n1s,
    q,
    kf,
    vf,
    bias,
    lines,
    out_v,
    attn,
    leave,
    left,
    arrived,
    win,
    wout,
    slope,
    hid,
    acc,
    back,
    gback,
    entry,
    gin,
    gout,
    hidden_v,
    gout_v,
    do_out,
    do,
    rest,
    rest_in,
    rest_got,
    kacc,
    vacc,
    gacc,
    dk_out,
    dv_out,
    dk_in,
    dv_in,
    dqkv,
    part,
    parts,
    wpart,
    wpart_in,
    wgot,
    small,
    shared,
    gain_rows_v,
    rest_mid,
    wmid,
    ss,
    rs,
    xe,
    re,
    oe,
    ore,
    ls,
):
    f32, bf16 = jnp.float32, jnp.bfloat16
    d, s, z, c = place()
    sib = (d, s + 1 - 2 * c)
    across = (d + 1 - 2 * lax.rem(d, 2), lax.rem(d + 2, 4), 3 - d)
    plane = [(j, s) for j in across]
    zs = [(d, 2 * lax.rem(z + k, 4) + c) for k in (1, 2, 3)]
    me, numbers, others = chips()
    device = d * 8 + s
    everyone = [(lax.rem(d + k // 8, 4), lax.rem(s + k % 8, 8)) for k in range(1, 32)]
    sems = Sems(ss, rs)
    barrier = pltpu.get_barrier_semaphore()
    for peer in everyone:
        pl.semaphore_signal(barrier, inc=1, device_id=peer, device_id_type=MESH)

    valid_row = valid_t[...].astype(f32)
    diag = lax.broadcasted_iota(jnp.int32, (128, 128), 0) == lax.broadcasted_iota(
        jnp.int32, (128, 128), 1
    )
    lines[:, :128] = jnp.zeros((32, 128), f32)
    lines[0:16, :24] = w_router_t[...].astype(f32)
    lines[16:17, :24] = gain_a[...].astype(f32)
    lines[17:18, :24] = gain_m[...].astype(f32)
    lines[18:19, :24] = jnp.broadcast_to(jnp.sum(valid_row, axis=1, keepdims=True), (1, 24))
    turned = jnp.transpose(lines[:, :128])[:24, :]
    for zt in range(4):
        for i in range(3):
            at = i * 768 + zt * 192
            wq[zt, :, i * 192 : (i + 1) * 192] = w_qkv[:, at : at + 192]
        wq[zt, :, 576:] = jnp.zeros((24, 128), bf16)
        wq[zt, :, 576:608] = turned.astype(bf16)
    pl.semaphore_wait(barrier, 31)

    def rows_of(ref, dd, zz, cc):
        return ref.at[pl.ds(pl.multiple_of(((dd * 4 + zz) * 2 + cc) * 24, 8), 24)]

    def column_rows(ref, dd, dev):
        copies = []
        for zz in range(4):
            spot = rows_of(ref, dd, zz, c)
            copies.append(sems.copy(spot, spot, dev))
        return run(copies)

    local = [
        pltpu.make_async_copy(wq.at[z], rows_of(wqf, d, z, c), ls.at[0]),
        pltpu.make_async_copy(w_attn, rows_of(wrf, d, z, c), ls.at[1]),
        pltpu.make_async_copy(x, xs.at[z], ls.at[2]),
    ]
    run(local)
    stage1 = run(
        [
            sems.copy(wq.at[lax.rem(z + k, 4)], rows_of(wqf, d, z, c), zs[i])
            for i, k in enumerate((1, 2, 3))
        ]
    )

    bulk = []

    def piece(m, dd, half):
        if m == 0:
            return win.at[pl.ds(pl.multiple_of(dd * 192 + half * 96, 32), 96)]
        return wout.at[pl.ds(pl.multiple_of(dd * 768 + half * 384, 128), 384)]

    sources = (w_in, w_out)

    def expert_send(m, i, half):
        j = across[i]
        parts = ((0, None),) if (m, i) != (1, 2) else ((0, 2), (192, 4))

        @pl.when(j // 2 == c)
        def _():
            for at, n in parts:
                expert_copy(m, i, half, at, n).start()

        for at, n in parts:
            bulk.append(
                (j // 2 == c, functools.partial(expert_copy, m, i, half, at, n))
            )

    def expert_copy(m, i, half, at, n):
        j = across[i]
        src, dst = sources[m].at[lax.rem(j, 2), half], piece(m, d, half)
        if n is None:
            return remote(src, dst, xe.at[m, i, half], re.at[m, i], (j, 2 * z + half))
        return remote(
            src.at[pl.ds(at, 192)],
            last_part(d, half, at),
            xe.at[m, n, half],
            re.at[m, n + 1 if n > 2 else n],
            (j, 2 * z + half),
        )

    def last_part(dd, half, at):
        return wout.at[pl.ds(pl.multiple_of(dd * 768 + half * 384 + at, 64), 192)]

    def last_pass(at, n):
        spot = last_part(across[2], c, at)
        remote(
            spot, spot, xe.at[1, n, 0], re.at[1, n + 1 if n > 2 else n], sib
        ).wait_recv()
        return sems.copy(spot, spot, sib)

    def own_here(m, half):
        return pltpu.make_async_copy(
            sources[m].at[lax.rem(d, 2), half], piece(m, d, half), ls.at[3 + 2 * m + half]
        )

    def own_there(m, half):
        return remote(
            sources[m].at[lax.rem(d, 2), half],
            piece(m, d, half),
            xe.at[m, 3, half],
            re.at[m, 3 + half],
            sib,
        )

    def expert_own(m):
        @pl.when(d // 2 == c)
        def _():
            for half in range(2):
                own_here(m, half).start()
                own_there(m, half).start()

    def expert_own_done(m):
        @pl.when(d // 2 == c)
        def _():
            for half in range(2):
                own_here(m, half).wait()
                own_there(m, half).wait_send()

        @pl.when(d // 2 != c)
        def _():
            for half in range(2):
                own_there(m, half).wait_recv()

    def expert_pass(m, i):
        spot = piece(m, across[i], c)
        remote(spot, spot, xe.at[m, i, 0], re.at[m, i], sib).wait_recv()
        return sems.copy(spot, spot, sib)

    expert_send(0, 0, 0)
    expert_send(0, 1, 0)
    rest1 = run([sems.copy(w_attn, rows_of(wrf, d, z, c), zs[i]) for i in range(3)])
    rows = run([sems.copy(x, xs.at[z], zs[i]) for i in range(3)])

    table = jnp.dot(
        rel_bias_t[...], hot_of(buckets, BUCKETS), precision=HIGH, preferred_element_type=f32
    )
    place_of = lax.broadcasted_iota(jnp.int32, (1, ROLL), 1)
    lines[:12] = table + jnp.where((place_of < 1) | (place_of > 1024), NEG, 0.0)
    for h in range(3):
        row = jnp.broadcast_to(lines[pl.ds(3 * z + h, 1), :], (128, ROLL))
        bias[h] = pltpu.roll(row, 0, 1, stride=1, stride_axis=0)[:, 128:]
    for cp in local:
        cp.wait()
    received(stage1)
    stage2 = [column_rows(wqf, d, dev) for dev in plane]
    stage3 = column_rows(wqf, d, sib)
    received(rest1)
    rest2 = [column_rows(wrf, d, dev) for dev in plane]
    rest3 = column_rows(wrf, d, sib)
    for i, k in ((0, 1), (1, 1), (2, 0), (2, 1)):
        expert_send(0, i, k)
    expert_own(0)
    expert_own(1)
    for i, dd in enumerate(across):
        received(stage2[i])
        stage3 += column_rows(wqf, dd, sib)
    received(stage3)
    misc = jnp.transpose(wqf[:, 576:704].astype(f32))
    gain_first = misc[16:17]
    gain_second = misc[17:18]
    count = jnp.sum(misc[18:19], axis=1, keepdims=True) / 24.0

    pairs = []
    for i in range(4):
        zb = lax.rem(z + 4 - i, 4)
        if i > 0:
            rows[i - 1].wait_recv()
        xf = xs[zb].astype(f32)
        n1 = (xf * rms(xf) * gain_first).astype(bf16)
        n1s[zb] = n1
        qkv = dot_n(n1, wqf[:, :576]).astype(bf16)
        q[zb] = qkv[:, :192]
        kf[zb, c] = qkv[:, 192:384]
        vf[zb, c] = qkv[:, 384:]
        pairs += run(
            [
                sems.copy(kf.at[zb, c], kf.at[zb, c], sib),
                sems.copy(vf.at[zb, c], vf.at[zb, c], sib),
            ]
        )
    for i, dd in enumerate(across):
        received(rest2[i])
        rest3 += column_rows(wrf, dd, sib)
    expert_send(1, 0, 0)
    expert_send(1, 1, 0)
    received(pairs)
    first = sems.n
    sems.n += 4
    for zb in (3, 2, 1, 0):
        width = 256 * (zb + 1)
        start = pl.multiple_of(128 * (7 - 2 * zb) - 128 * c, 128)
        keys = kf[: zb + 1].reshape(width, 192)
        values = vf[: zb + 1].reshape(width, 192)
        def one_head(h, mixed, zb=zb, width=width, start=start, keys=keys, values=values):
            qh = jnp.where(head_mask(h), q[zb], jnp.zeros((), bf16))
            p = soft_rows(qh, keys, bias, h, start, width).astype(bf16)
            return mixed + jnp.where(head_mask(h), dot_n(p, values), 0.0)

        mixed = lax.fori_loop(0, 3, one_head, jnp.zeros((128, 192), f32))
        out_v[zb] = mixed.astype(bf16)

        @pl.when(z != zb)
        def _(zb=zb):
            remote(
                out_v.at[zb], attn.at[z], ss.at[first + zb], rs.at[first + z], (d, 2 * zb + c)
            ).start()

        @pl.when(z == zb)
        def _(zb=zb):
            attn[zb] = out_v[zb]

    received(rest3)
    for zb in range(4):

        @pl.when(z != zb)
        def _(zb=zb):
            remote(
                out_v.at[zb], attn.at[zb], ss.at[first + zb], rs.at[first + zb], (d, 2 * zb + c)
            ).wait()

    hidden = x[...].astype(f32)
    for zb in range(4):
        hidden = hidden + dot_n(attn[zb], wrf[192 * zb : 192 * (zb + 1), :])
    hidden_v[...] = hidden
    n2 = (hidden * rms(hidden) * gain_second).astype(bf16)
    logits = dot_n(n2, wqf[:, 576:704])
    lane = lax.broadcasted_iota(jnp.int32, (128, 128), 1)

    def column(row):
        return jnp.sum(jnp.where(diag, row, jnp.zeros_like(row)), axis=1, keepdims=True)

    route = [column(routes_t[i : i + 1, :]) for i in range(2)]
    picks = [(lane == r).astype(f32) for r in route]
    chosen = [
        jnp.sum(jnp.where(lane == r, logits, 0.0), axis=1, keepdims=True) for r in route
    ]
    top = jnp.maximum(chosen[0], chosen[1])
    powers = [jnp.exp(v - top) for v in chosen]
    gate = [v / (powers[0] + powers[1]) for v in powers]
    lower = (lax.broadcasted_iota(jnp.int32, (128, 128), 0) > lane).astype(bf16)
    before = dot_n(lower, (picks[0] + picks[1]).astype(bf16))
    wide = lax.broadcasted_iota(jnp.int32, (128, 512), 1)
    maps = []
    for i in range(2):
        slot = jnp.sum(picks[i] * before, axis=1, keepdims=True).astype(jnp.int32)
        maps.append((wide == route[i] * 32 + slot).astype(f32).astype(bf16))
    chart = maps[0] + maps[1]
    leave[...] = dot_l(chart, n2).astype(bf16).reshape(16, 32, 768)

    def spread_rows(src, dst, targets, devices):
        copies = run([sems.copy(src.at[t], dst.at[me], dev) for t, dev in zip(targets, devices)])
        dst[pl.ds(me, 1)] = src[pl.ds(me, 1)]
        return copies

    def spread_columns(src, dst, at):
        cols = pl.ds(at, 384)
        copies = run(
            [
                sems.copy(src.at[t, :, cols], dst.at[me, :, cols], dev)
                for t, dev in zip(numbers, others)
            ]
        )
        dst[pl.ds(me, 1), :, cols] = src[pl.ds(me, 1), :, cols]
        return copies

    out = spread_rows(leave, arrived, numbers[8:] + numbers[:8], others[8:] + others[:8])
    for i, k in ((0, 1), (1, 1), (2, 0), (2, 1)):
        expert_send(1, i, k)
    passed = [expert_pass(0, i) for i in range(3)]
    run(passed)
    expert_own_done(0)
    received(passed)
    received(out)
    sent(out)

    def forward_step(i, carry):
        cols = pl.ds(pl.multiple_of((i // 2) * CHUNK, CHUNK), CHUNK)
        these = pl.ds(pl.multiple_of(lax.rem(i, 2) * 256, 256), 256)
        blocks = pl.ds(pl.multiple_of(lax.rem(i, 2) * 8, 8), 8)
        pre = dot_n(arrived[blocks].reshape(256, 768), win[:, cols])
        t = jnp.tanh(GELU_A * (pre + GELU_B * pre * pre * pre))
        half = 0.5 * (1.0 + t)
        hid[these, cols] = (pre * half).astype(bf16)
        slope[these, cols] = half + 0.5 * pre * (1.0 - t * t) * (
            GELU_A * (1.0 + 3.0 * GELU_B * pre * pre)
        )
        return carry

    lax.fori_loop(0, 8, forward_step, 0)
    acc[...] = jnp.zeros_like(acc)

    def quarter(dd):
        k = pl.ds(pl.multiple_of(dd * 768, 768), 768)

        def result_step(i, carry):
            these = pl.ds(pl.multiple_of(i * 256, 256), 256)
            acc[these] += dot_n(hid[these, k], wout[k, :])
            return carry

        lax.fori_loop(0, 2, result_step, 0)

    expert_own_done(1)
    passed_out = []
    quarters = (d,) + across
    for i in range(2):
        passed_out += run([expert_pass(1, i)])
        quarter(quarters[i])
        received(passed_out[-1:])
    passed_out += run([last_pass(0, 2)])
    quarter(quarters[2])
    passed_out += run([last_pass(192, 4)])

    def eighth(core):
        return pl.ds(pl.multiple_of(across[2] * 768 + core * 384, 384), 384)

    k = eighth(c)
    acc[...] += dot_n(hid[:, k], wout[k, :])
    received(passed_out[-2:])
    results = []
    k = eighth(1 - c)
    for at in (0, 384):
        half = acc[:, at : at + 384] + dot_n(hid[:, k], wout[k, at : at + 384])
        leave[:, :, at : at + 384] = half.astype(bf16).reshape(16, 32, 384)
        results.append(spread_columns(leave, back, at))
    sent(stage1 + rows + rest1 + stage3 + pairs + rest3 + sum(stage2 + rest2, []))
    sent(passed + passed_out)
    for held, make in bulk:

        @pl.when(held)
        def _(make=make):
            make().wait_send()

    valid_column = column(valid_row)
    loss = jnp.zeros((1, 1), f32)
    dgate = [jnp.zeros((128, 1), f32), jnp.zeros((128, 1), f32)]
    grads = []
    for part_i, at in enumerate((0, 384)):
        cols = slice(at, at + 384)
        received(results[part_i])
        sent(results[part_i])
        combined = [dot_n(m, back[:, :, cols].reshape(512, 384)) for m in maps]
        result = hidden_v[:, cols] + gate[0] * combined[0] + gate[1] * combined[1]
        error = result - teacher[:, cols].astype(f32)
        masked = valid_column * error
        grad_out = (2.0 * 4096.0) / count * masked
        leave[:, :, cols] = (
            (
                dot_l(maps[0], (gate[0] * grad_out).astype(bf16))
                + dot_l(maps[1], (gate[1] * grad_out).astype(bf16))
            )
            .astype(bf16)
            .reshape(16, 32, 384)
        )
        grads.append(spread_columns(leave, gback, at))
        output[:, cols] = result
        gout_v[:, cols] = grad_out
        loss = loss + jnp.sum(
            jnp.sum(masked * error, axis=1, keepdims=True), axis=0, keepdims=True
        )
        dgate = [
            g + jnp.sum(m * grad_out, axis=1, keepdims=True) for g, m in zip(dgate, combined)
        ]
    mean = gate[0] * dgate[0] + gate[1] * dgate[1]
    grad_logits = jnp.zeros((128, 128), f32)
    for i in range(2):
        grad_logits = grad_logits + jnp.where(
            lane == route[i], gate[i] * (dgate[i] - mean), 0.0
        )
    grad_logits = grad_logits.astype(bf16)
    acc[...] = jnp.zeros_like(acc)

    my_half = me // 8
    entries = []
    for near in (True, False):
        members = slice(8, 15) if near else slice(0, 8)
        group = my_half if near else 1 - my_half
        for copies in grads:
            received(copies[members])
        if not near:
            for copies in grads:
                sent(copies)
        blocks = pl.ds(pl.multiple_of(group * 8, 8), 8)
        these = pl.ds(pl.multiple_of(group * 256, 256), 256)

        def backward_step(i, carry, blocks=blocks, these=these):
            cols = pl.ds(pl.multiple_of(i * CHUNK, CHUNK), CHUNK)
            dh = dot_t(gback[blocks].reshape(256, 768), wout[cols, :])
            dp = (dh * slope[these, cols]).astype(bf16)
            slope[these, cols] = dp.astype(f32)
            acc[these] += dot_t(dp, win[:, cols])
            return carry

        lax.fori_loop(0, 4, backward_step, 0)
        left[blocks] = acc[these].astype(bf16).reshape(8, 32, 768)
        entries += run(
            [
                sems.copy(left.at[t], entry.at[me], dev)
                for t, dev in zip(numbers[members], others[members])
            ]
        )
        if near:
            entry[pl.ds(me, 1)] = left[pl.ds(me, 1)]

    swap_out = sems.n
    sems.n += 8

    def turn(i):
        m = lax.rem(i + 1, 4)
        return lax.rem(d + m, 2) + 2 * lax.rem(d // 2 + m // 2, 2)

    def half_out(i):
        f = turn(i)
        return remote(
            piece(1, f, 1 - c), gout.at[f], ss.at[swap_out + i], rs.at[swap_out + i], sib
        )

    def half_in(f):
        at = swap_out + 4 + f
        return remote(piece(0, f, 1 - c), gin.at[f], ss.at[at], rs.at[at], sib)

    owned = []

    def owner_send(m, i):
        src, dst = ((gin, oin), (gout, oout))[m]
        cp = remote(
            src.at[across[i]],
            dst.at[lax.rem(d, 2), c],
            oe.at[m, i],
            ore.at[m, lax.rem(d, 2), c],
            (across[i], 2 * z + d // 2),
        )
        cp.start()
        owned.append(cp)

    def last_rows(at, count, send):
        rows = pl.ds(at, count)
        cp = remote(
            gin.at[across[2], rows],
            oin.at[lax.rem(d, 2), c, rows],
            oe.at[0, send],
            ore.at[0, lax.rem(d, 2), c],
            (across[2], 2 * z + d // 2),
        )
        cp.start()
        owned.append(cp)

    def owner_here(m):
        src, dst = ((gin, oin), (gout, oout))[m]
        return pltpu.make_async_copy(src.at[d], dst.at[lax.rem(d, 2), c], ls.at[7 + m])

    def owner_there(m):
        src, dst = ((gin, oin), (gout, oout))[m]
        return remote(
            src.at[d], dst.at[lax.rem(d, 2), c], oe.at[m, 3], ore.at[m, lax.rem(d, 2), c], sib
        )

    def owner_local(m):
        @pl.when(d // 2 == c)
        def _():
            owner_here(m).start()

        @pl.when(d // 2 != c)
        def _():
            owner_there(m).start()

    def add_half(m, f):
        ref, rows_n = ((gin, 96), (gout, 384))[m]
        spot = (
            pl.ds(pl.multiple_of(f * 192 + c * 96, 32), 96)
            if m == 0
            else pl.ds(pl.multiple_of(f * 768 + c * 384, 128), 384)
        )
        mine = (win if m == 0 else wout)[spot, :]
        ref[f] = (mine.astype(f32) + ref[f].astype(f32)).astype(bf16)

    def out_done(i):
        half_out(i).wait()
        add_half(1, turn(i))

    def out_owner(i):
        return remote(
            gout.at[turn(i)],
            oout.at[lax.rem(d, 2), c],
            oe.at[1, i],
            ore.at[1, lax.rem(d, 2), c],
            (turn(i), 2 * z + d // 2),
        )

    def out_step(i, carry):
        at = pl.multiple_of(turn(i) * CHUNK, CHUNK)
        wout[pl.ds(at, CHUNK), :] = dot_l(
            hid[:, pl.ds(at, CHUNK)], gback[...].reshape(512, 768)
        ).astype(bf16)
        half_out(i).start()

        @pl.when(i > 0)
        def _():
            out_done(i - 1)
            out_owner(i - 1).start()

        return carry

    lax.fori_loop(0, 4, out_step, 0)
    out_done(3)
    owner_local(1)
    owned += [out_owner(i) for i in range(3)]

    def in_step(f, carry):
        at = pl.multiple_of(f * CHUNK, CHUNK)
        win[:, pl.ds(at, CHUNK)] = dot_l(
            arrived[...].reshape(512, 768), slope[:, pl.ds(at, CHUNK)].astype(bf16)
        ).astype(bf16)
        return carry

    lax.fori_loop(0, 4, in_step, 0)
    for f in range(4):
        half_in(f).start()
    kacc[...] = jnp.zeros_like(kacc)
    vacc[...] = jnp.zeros_like(vacc)
    gacc[...] = jnp.zeros_like(gacc)
    for f in range(4):
        half_in(f).wait()
        add_half(0, f)
    for i in range(2):
        owner_send(0, i)
    last_rows(0, 64, 2)
    owner_local(0)
    received(entries)
    sent(entries)

    dn2 = dot_n(chart, entry[...].reshape(512, 768))
    dn2 = dn2 + dot_t(grad_logits, wqf[:, 576:704])
    hidden = hidden_v[...]
    r2 = rms(hidden)
    scaled = dn2 * gain_second
    mean = jnp.mean(scaled * hidden, axis=1, keepdims=True)
    dh = gout_v[...] + r2 * scaled - hidden * (r2 * r2 * r2) * mean
    dh_low = dh.astype(bf16)
    for zb in range(4):
        do_out[zb] = dot_t(dh_low, wrf[192 * zb : 192 * (zb + 1), :]).astype(bf16)
    heads = run(
        [
            sems.copy(do_out.at[lax.rem(z + k, 4)], do.at[z], zs[i])
            for i, k in enumerate((1, 2, 3))
        ]
    )
    do[pl.ds(z, 1)] = do_out[pl.ds(z, 1)]
    grad_tokens[...] = dh

    for zb in range(4):
        rest[192 * zb : 192 * (zb + 1), :768] = dot_l(attn[zb], dh_low).astype(bf16)
    gain_rows = jnp.broadcast_to(jnp.sum(dn2 * hidden * r2, axis=0, keepdims=True), (128, 768))
    n2 = (hidden * r2 * gain_second).astype(bf16)
    tall = lax.broadcasted_iota(jnp.int32, (768, 128), 1)
    rest[:, 768:] = jnp.where(
        tall == 16, jnp.transpose(gain_rows), dot_l(n2, grad_logits)
    ).astype(bf16)
    rest_swap = run([sems.copy(rest, rest_in, sib)])
    received(rest_swap)
    sent(rest_swap)
    rest_in[...] = (rest[...].astype(f32) + rest_in[...].astype(f32)).astype(bf16)

    def slot(ref, i, j):
        return ref.at[pl.ds(pl.multiple_of((i * 4 + j) * 24, 8), 24)]

    rest_a = []
    for i, k in enumerate((1, 2, 3)):
        zt = lax.rem(z + k, 4)
        for dd in range(4):
            rest_a.append(sems.copy(rows_of(rest_in, dd, zt, c), slot(rest_mid, z, dd), zs[i]))
    run(rest_a)
    for dd in range(4):
        pltpu.make_async_copy(
            rows_of(rest_in, dd, z, c), slot(rest_mid, z, dd), ls.at[11 + dd]
        ).start()
    received(heads)

    scale = HEAD ** (-0.5)
    first_back = sems.n
    sems.n += 4
    swaps = []

    def to_tokens(zb, pair):
        received(pair)
        here = pl.ds(pl.multiple_of((2 * zb + c) * 128, 128), 128)
        dqkv[zb, :, 192:384] = (kacc[here] * scale + dk_in[zb].astype(f32)).astype(bf16)
        dqkv[zb, :, 384:] = (vacc[here] + dv_in[zb].astype(f32)).astype(bf16)
        dn1 = dot_t(dqkv[zb], wqf[:, :576])
        part[zb] = dn1.astype(bf16)

        @pl.when(z != zb)
        def _():
            remote(
                part.at[zb],
                parts.at[z],
                ss.at[first_back + zb],
                rs.at[first_back + z],
                (d, 2 * zb + c),
            ).start()

        @pl.when(z == zb)
        def _():
            parts[zb] = part[zb]

        xf = xs[zb].astype(f32)
        gain_rows_v[zb : zb + 1, :] = jnp.sum(dn1 * xf * rms(xf), axis=0, keepdims=True)

    for zb in (3, 2, 1, 0):
        width = 256 * (zb + 1)
        start = pl.multiple_of(128 * (7 - 2 * zb) - 128 * c, 128)
        keys = kf[: zb + 1].reshape(width, 192)
        values = vf[: zb + 1].reshape(width, 192)
        dq = jnp.zeros((128, 192), f32)
        for h in range(3):
            mask = head_mask(h)
            qh = jnp.where(mask, q[zb], jnp.zeros((), bf16))
            doh = jnp.where(mask, do[zb], jnp.zeros((), bf16))
            p = soft_rows(qh, keys, bias, h, start, width)
            vacc[:width] += dot_l(p.astype(bf16), doh)
            dp = dot_t(doh, values)
            dot = jnp.sum(p * dp, axis=1, keepdims=True)
            ds = (p * (dp - dot)).astype(bf16)
            gacc[h, :, pl.ds(start, width)] += ds.astype(f32)
            dq = dq + jnp.where(mask, dot_n(ds, keys), 0.0)
            kacc[:width] += dot_l(ds, qh)
        dqkv[zb, :, :192] = (dq * scale).astype(bf16)
        there = pl.ds(pl.multiple_of((2 * zb + 1 - c) * 128, 128), 128)
        dk_out[zb] = (kacc[there] * scale).astype(bf16)
        dv_out[zb] = vacc[there].astype(bf16)
        swaps.append(
            run(
                [
                    sems.copy(dk_out.at[zb], dk_in.at[zb], sib),
                    sems.copy(dv_out.at[zb], dv_in.at[zb], sib),
                ]
            )
        )
        if zb < 3:
            to_tokens(zb + 1, swaps[-2])
    to_tokens(0, swaps[-1])
    swaps = sum(swaps, [])

    gain_part = jnp.sum(gain_rows_v[...], axis=0, keepdims=True)
    wpart[:, :576] = dot_l(n1s[...].reshape(512, 768), dqkv[...].reshape(512, 576)).astype(bf16)
    wpart[:, 576:] = jnp.transpose(jnp.broadcast_to(gain_part, (128, 768))).astype(bf16)
    wswap = run([sems.copy(wpart, wpart_in, sib)])
    received(wswap)
    sent(wswap)
    wpart_in[...] = (wpart[...].astype(f32) + wpart_in[...].astype(f32)).astype(bf16)
    w_a = []
    for i, dd in enumerate(across):
        for zt in range(4):
            w_a.append(sems.copy(rows_of(wpart_in, dd, zt, c), slot(wmid, d, zt), plane[i]))
    run(w_a)
    last_rows(64, 32, 4)
    for zt in range(4):
        pltpu.make_async_copy(
            rows_of(wpart_in, d, zt, c), slot(wmid, d, zt), ls.at[15 + zt]
        ).start()
    received(rest_a)
    for dd in range(4):
        pltpu.make_async_copy(
            rows_of(rest_in, dd, z, c), slot(rest_mid, z, dd), ls.at[11 + dd]
        ).wait()
    rest[:96] = sum(rest_mid[96 * i : 96 * (i + 1), :].astype(f32) for i in range(4)).astype(bf16)
    rest_b = run(
        [
            sems.copy(
                rest.at[pl.ds(pl.multiple_of(dd * 24, 8), 24)],
                rest_got.at[pl.ds(pl.multiple_of(d * 24, 8), 24)],
                plane[i],
            )
            for i, dd in enumerate(across)
        ]
    )

    row = lax.broadcasted_iota(jnp.int32, (128, 1), 0)
    sums = []
    for h in range(3):
        y = jnp.concatenate([jnp.zeros((128, ROLL - GW), f32), gacc[h]], axis=1)
        for bit in range(7):
            y = jnp.where((row >> bit) & 1 == 1, pltpu.roll(y, ROLL - (1 << bit), 1), y)
        sums.append(jnp.sum(y, axis=0, keepdims=True))
    hot = hot_of(buckets, 128)
    table = lax.dot_general(
        jnp.concatenate(sums + [jnp.zeros((5, ROLL), f32)], axis=0),
        hot,
        (((1,), (1,)), ((), ())),
        precision=HIGH,
        preferred_element_type=f32,
    )
    index = lax.broadcasted_iota(jnp.int32, (8, 128), 0)
    small[...] = jnp.where(index == 3, loss, table)
    shares = run([sems.copy(small, shared.at[device], dev) for dev in everyone])
    shared[pl.ds(device, 1)] = small[...][None]

    for zb in range(4):

        @pl.when(z != zb)
        def _(zb=zb):
            remote(
                part.at[zb],
                parts.at[zb],
                ss.at[first_back + zb],
                rs.at[first_back + zb],
                (d, 2 * zb + c),
            ).wait()

    dn1 = (
        parts[0].astype(f32) + parts[1].astype(f32) + parts[2].astype(f32) + parts[3].astype(f32)
    )
    xf = x[...].astype(f32)
    r1 = rms(xf)
    scaled = dn1 * gain_first
    mean = jnp.mean(scaled * xf, axis=1, keepdims=True)
    grad_tokens[...] += r1 * scaled - xf * (r1 * r1 * r1) * mean

    received(w_a)
    for zt in range(4):
        pltpu.make_async_copy(
            rows_of(wpart_in, d, zt, c), slot(wmid, d, zt), ls.at[15 + zt]
        ).wait()
    wpart[:96] = sum(wmid[96 * i : 96 * (i + 1), :].astype(f32) for i in range(4)).astype(bf16)
    w_b = run(
        [
            sems.copy(
                wpart.at[pl.ds(pl.multiple_of(lax.rem(z + k, 4) * 24, 8), 24)],
                wgot.at[pl.ds(pl.multiple_of(z * 24, 8), 24)],
                zs[i],
            )
            for i, k in enumerate((1, 2, 3))
        ]
    )
    own_rows = [
        pltpu.make_async_copy(
            rest.at[pl.ds(pl.multiple_of(d * 24, 8), 24)],
            rest_got.at[pl.ds(pl.multiple_of(d * 24, 8), 24)],
            ls.at[9],
        ),
        pltpu.make_async_copy(
            wpart.at[pl.ds(pl.multiple_of(z * 24, 8), 24)],
            wgot.at[pl.ds(pl.multiple_of(z * 24, 8), 24)],
            ls.at[10],
        ),
    ]
    run(own_rows)

    received(shares)
    by_z = []
    for zb in range(4):
        total = jnp.zeros((8, 128), f32)
        for dd in range(4):
            for cc in range(2):
                total = total + shared[(dd * 4 + zb) * 2 + cc]
        by_z.append(total)
    loss_all = by_z[0] + by_z[1] + by_z[2] + by_z[3]
    extra[0:8] = loss_all[3:4] / (count * 768.0) + jnp.zeros((8, 128), f32)
    for zb in range(4):
        extra[8 + 8 * zb : 16 + 8 * zb] = by_z[zb]

    received(rest_b)
    received(w_b)
    for cp in own_rows:
        cp.wait()
    total = jnp.zeros((24, 896), f32)
    gain_total = jnp.zeros((24, 128), f32)
    for zb in range(4):
        total = total + rest_got[24 * zb : 24 * (zb + 1), :].astype(f32)
        block = wgot[24 * zb : 24 * (zb + 1), :].astype(f32)
        gain_total = gain_total + block[:, 576:]
        for i in range(3):
            at = i * 768 + zb * 192
            grad_qkv[:, at : at + 192] = block[:, i * 192 : (i + 1) * 192]
    grad_rest[:, :896] = total
    grad_rest[:, 896:] = gain_total

    for m, (src, dst) in enumerate(((gin, oin), (gout, oout))):
        for l in range(2):
            for half in range(2):
                here = (2 * c + l == d) & (c == half)

                @pl.when(jnp.logical_not(here))
                def _(src=src, dst=dst, m=m, l=l, half=half):
                    remote(
                        src.at[0], dst.at[l, half], oe.at[m, 3], ore.at[m, l, half], sib
                    ).wait_recv()

        @pl.when(d // 2 == c)
        def _(m=m):
            owner_here(m).wait()

        @pl.when(d // 2 != c)
        def _(m=m):
            owner_there(m).wait_send()

    sent(heads + rest_a + rest_b + swaps + shares + w_a + w_b + owned)


def finish_kernel(
    oin, oout, output, tokens, qkv, rest, extra, gin, gout, o, t, g, w, r, ga, gm, table, loss
):
    f32 = jnp.float32
    gin[...] = oin[...].astype(f32)
    gout[...] = oout[...].astype(f32)

    @pl.when(pl.program_id(0) == 0)
    def _():
        o[...] = output[...]
        t[...] = tokens[...]
        g[...] = qkv[...]
        w[...] = rest[:, :768]
        turned = jnp.transpose(
            jnp.concatenate([rest[:, 768:1024], jnp.zeros((104, 256), f32)], axis=0)
        )
        r[...] = turned[:16, :24]
        gm[...] = turned[16:17, :24]
        ga[...] = turned[128:129, :24]
        for zb in range(4):
            table[3 * zb : 3 * zb + 3, :] = extra[8 + 8 * zb : 11 + 8 * zb, :BUCKETS]
        loss[...] = extra[0:1, 0:1]


def fast_path(
    tokens,
    w_qkv,
    w_attn_out,
    gain_attn,
    gain_moe,
    w_router,
    rel_bias,
    w_in,
    w_out,
    teacher,
    routes,
    valid,
    buckets,
):
    f32, bf16 = jnp.float32, jnp.bfloat16
    block = pltpu.VMEM((16, 32, 768), bf16)
    heads = pltpu.VMEM((4, 128, 192), bf16)
    both = pltpu.VMEM((4, 2, 128, 192), bf16)
    wide = pltpu.VMEM((4, 128, 768), bf16)
    output, grad_tokens, grad_qkv, grad_rest, extra, oin, oout = comm_call(
        step_kernel,
        [
            sds((128, 768), f32),
            sds((128, 768), f32),
            sds((24, 2304), f32),
            sds((24, 1024), f32),
            sds((40, 128), f32),
            sds((2, 2, 96, 3072)),
            sds((2, 2, 384, 768)),
        ],
        13,
        1,
        [
            pltpu.VMEM((4, 24, 704), bf16),
            pltpu.VMEM((768, 704), bf16),
            pltpu.VMEM((768, 768), bf16),
            wide,
            wide,
            heads,
            both,
            both,
            pltpu.VMEM((3, 128, GW), f32),
            pltpu.VMEM((32, ROLL), f32),
            heads,
            heads,
            block,
            block,
            block,
            pltpu.VMEM((768, 3072), bf16),
            pltpu.VMEM((3072, 768), bf16),
            pltpu.VMEM((512, 3072), f32),
            pltpu.VMEM((512, 3072), bf16),
            pltpu.VMEM((512, 768), f32),
            block,
            block,
            block,
            pltpu.VMEM((4, 96, 3072), bf16),
            pltpu.VMEM((4, 384, 768), bf16),
            pltpu.VMEM((128, 768), f32),
            pltpu.VMEM((128, 768), f32),
            heads,
            heads,
            pltpu.VMEM((768, 896), bf16),
            pltpu.VMEM((768, 896), bf16),
            pltpu.VMEM((96, 896), bf16),
            pltpu.VMEM((1024, 192), f32),
            pltpu.VMEM((1024, 192), f32),
            pltpu.VMEM((3, 128, GW), f32),
            heads,
            heads,
            heads,
            heads,
            pltpu.VMEM((4, 128, 576), bf16),
            wide,
            wide,
            pltpu.VMEM((768, 704), bf16),
            pltpu.VMEM((768, 704), bf16),
            pltpu.VMEM((96, 704), bf16),
            pltpu.VMEM((8, 128), f32),
            pltpu.VMEM((32, 8, 128), f32),
            pltpu.VMEM((4, 768), f32),
            pltpu.VMEM((384, 896), bf16),
            pltpu.VMEM((384, 704), bf16),
            pltpu.SemaphoreType.DMA((300,)),
            pltpu.SemaphoreType.DMA((300,)),
            pltpu.SemaphoreType.DMA((2, 5, 2)),
            pltpu.SemaphoreType.DMA((2, 6)),
            pltpu.SemaphoreType.DMA((2, 5)),
            pltpu.SemaphoreType.DMA((2, 2, 2)),
            pltpu.SemaphoreType.DMA((19,)),
        ],
        "layer_step",
        in_specs=[VM] * 11 + [ANY] * 2,
        out_specs=[VM] * 5 + [ANY] * 2,
        vmem=63 << 20,
    )(
        tokens,
        w_qkv,
        w_attn_out,
        w_router.T,
        gain_attn[None],
        gain_moe[None],
        rel_bias.T,
        buckets[None],
        routes.T,
        valid[None],
        teacher,
        w_in.reshape(2, 2, 96, 3072),
        w_out.reshape(2, 2, 384, 768),
    )

    def whole(shape):
        return pl.BlockSpec(shape, lambda i: (0,) * len(shape))

    small_in = [(128, 768), (128, 768), (24, 2304), (24, 1024), (40, 128)]
    small_out = [
        (128, 768),
        (128, 768),
        (24, 2304),
        (24, 768),
        (16, 24),
        (1, 24),
        (1, 24),
        (12, BUCKETS),
        (1, 1),
    ]
    blocks = [
        pl.BlockSpec((2, 96, 3072), lambda i: (i, 0, 0)),
        pl.BlockSpec((2, 384, 768), lambda i: (i, 0, 0)),
    ]
    gin, gout, output, grad_tokens, grad_qkv, grad_w, grad_r, grad_ga, grad_gm, table, loss = (
        pl.pallas_call(
            finish_kernel,
            grid=(2,),
            out_shape=[sds((4, 96, 3072), f32), sds((4, 384, 768), f32)]
            + [sds(shape, f32) for shape in small_out],
            in_specs=blocks + [whole(shape) for shape in small_in],
            out_specs=blocks + [whole(shape) for shape in small_out],
            name="finish",
        )(
            oin.reshape(4, 96, 3072),
            oout.reshape(4, 384, 768),
            output,
            grad_tokens,
            grad_qkv,
            grad_rest,
            extra,
        )
    )
    return (
        output,
        loss.reshape(()),
        grad_tokens,
        grad_qkv,
        grad_w,
        grad_ga.reshape(24),
        grad_gm.reshape(24),
        grad_r.T,
        table.T,
        gin.reshape(2, 192, 3072),
        gout.reshape(2, 768, 768),
    )


def choose(*arrays):
    tokens, w_in, rel_bias, buckets = arrays[0], arrays[7], arrays[6], arrays[12]
    fits = (
        lax.axis_size("dp") == 4
        and lax.axis_size("seq") == 8
        and tokens.shape == (128, 768)
        and w_in.shape == (2, 192, 3072)
        and rel_bias.shape == (32, 12)
        and buckets.shape == (1024,)
    )
    return fast_path(*arrays) if fits else on_device(*arrays)


def solution(mesh):
    in_specs = (
        P(("dp", "seq"), None),
        P(("dp", "seq"), None),
        P(("dp", "seq"), None),
        P(("dp", "seq")),
        P(("dp", "seq")),
        P(("dp", "seq"), None),
        P(),
        P("seq", "dp", None),
        P("seq", "dp", None),
        P(("dp", "seq"), None),
        P(("dp", "seq"), None),
        P(("dp", "seq")),
        P(),
    )
    out_specs = (
        P(("dp", "seq"), None),
        P(),
        P(("dp", "seq"), None),
        P(("dp", "seq"), None),
        P(("dp", "seq"), None),
        P(("dp", "seq")),
        P(("dp", "seq")),
        P(("dp", "seq"), None),
        P(),
        P("seq", "dp", None),
        P("seq", "dp", None),
    )
    return jax.shard_map(
        choose, mesh=mesh, in_specs=in_specs, out_specs=out_specs, check_vma=False
    )
```
